32 devices in a mesh: rep: 4 (over y, x), fsdp: 4 (over z), ctx: 2 (over core).
Axes of the slice: x: 2, y: 2, z: 4, core: 2. Of those that a mesh axis runs over, the one named last changes fastest.
Arguments:
- inputs: bfloat16 [2, 16, 1024, 768], P(None, ('rep', 'fsdp'), 'ctx'), may hold values from -6 to 6
- weight_qkv: bfloat16 [768, 2304], P('fsdp'), may hold values from -0.21875 to 0.21875
- bias_query: bfloat16 [768], P('fsdp'), may hold values from -3 to 3
- bias_value: bfloat16 [768], P('fsdp'), may hold values from -3 to 3
- weight_mix: bfloat16 [768, 768], P('fsdp'), may hold values from -1.75 to 1.75
- bias_mix: bfloat16 [768], P('fsdp'), may hold values from -2 to 2
- gain_attn: bfloat16 [768], P('fsdp'), may hold values from 0.099609375 to 1.8984375
- shift_attn: bfloat16 [768], P('fsdp'), may hold values from -2 to 2
- gain_mlp: bfloat16 [768], P('fsdp'), may hold values from 0.099609375 to 1.8984375
- shift_mlp: bfloat16 [768], P('fsdp'), may hold values from -2 to 2
- weight_up: bfloat16 [768, 3072], P('fsdp'), may hold values from -0.21875 to 0.21875
- bias_up: bfloat16 [3072], P('fsdp'), may hold values from -3 to 3
- weight_down: bfloat16 [3072, 768], P('fsdp'), may hold values from -0.109375 to 0.109375
- bias_down: bfloat16 [768], P('fsdp'), may hold values from -2 to 2
- cotangent: bfloat16 [2, 16, 1024, 768], P(None, ('rep', 'fsdp'), 'ctx'), may hold values from -6 to 6
Outputs:
- outputs: bfloat16 [2, 16, 1024, 768], P(None, ('rep', 'fsdp'), 'ctx')
- grad_inputs: float32 [2, 16, 1024, 768], P(None, ('rep', 'fsdp'), 'ctx')
- weight_qkv_grad: float32 [768, 2304], P('fsdp')
- bias_query_grad: float32 [768], P('fsdp')
- bias_value_grad: float32 [768], P('fsdp')
- weight_mix_grad: float32 [768, 768], P('fsdp')
- bias_mix_grad: float32 [768], P('fsdp')
- gain_attn_grad: float32 [768], P('fsdp')
- shift_attn_grad: float32 [768], P('fsdp')
- gain_mlp_grad: float32 [768], P('fsdp')
- shift_mlp_grad: float32 [768], P('fsdp')
- weight_up_grad: float32 [768, 3072], P('fsdp')
- bias_up_grad: float32 [3072], P('fsdp')
- weight_down_grad: float32 [3072, 768], P('fsdp')
- bias_down_grad: float32 [768], P('fsdp')
The draws below stay inside these ranges and needn't reach their ends.
All inputs are finite; a program needn't handle non-finite values.
Results may differ from the reference program's by a relative error of at most 0.018.
Values may be sent and summed in bfloat16 or wider, within the bound.
A program may use at most 320 MiB of HBM per device.

```python
import jax
import jax.numpy as jnp
from jax import lax

D = 768
H = 12
HD = 64
FF = 3072
LEN = 1024
MB = 2
SEQS = 16


def shard_levels(stream_key, extent, split, least, top_value):
    def one(axis_at, shards_of):
        steps = jax.random.uniform(jax.random.fold_in(jax.random.fold_in(stream_key, 6), axis_at), (shards_of,), jnp.float32, least / len(split), top_value / len(split))
        return jnp.repeat(jnp.exp(steps), extent[axis_at] // shards_of).reshape((-1,) + (1,) * (len(extent) - axis_at - 1))

    level = one(*split[0])
    for cut in split[1:]:
        level = level * one(*cut)
    return level


def noise(stream_key, extent, width, most, cuts=(), kind=jnp.bfloat16):
    values = width * jax.random.normal(stream_key, extent, jnp.float32)
    if cuts:
        values = values * shard_levels(stream_key, extent, cuts, -0.22, 0.18)
    return jnp.clip(values, -most, most).astype(kind)


def setup_inputs(seed: int = 0) -> dict:
    arg_keys = jax.random.split(jax.random.key(seed), 16)
    return {
        "inputs": noise(arg_keys[0], (MB, SEQS, LEN, D), 1.0, 6.0, ((1, 16), (2, 2))),
        "weight_qkv": noise(arg_keys[1], (D, 3 * D), D ** -0.5, 0.21875, ((0, 4),)),
        "bias_query": noise(arg_keys[2], (D,), 0.5, 3.0, ((0, 4),)),
        "bias_value": noise(arg_keys[3], (D,), 0.5, 3.0, ((0, 4),)),
        "weight_mix": noise(arg_keys[4], (D, D), (D // 64) ** -0.5, 1.75, ((0, 4),)),
        "bias_mix": noise(arg_keys[5], (D,), 0.3, 2.0, ((0, 4),)),
        "gain_attn": jnp.clip(1.0 + 0.18 * jax.random.normal(arg_keys[6], (D,), jnp.float32), 0.099609375, 1.8984375).astype(jnp.bfloat16),
        "shift_attn": noise(arg_keys[7], (D,), 0.3, 2.0, ((0, 4),)),
        "gain_mlp": jnp.clip(1.0 + 0.18 * jax.random.normal(arg_keys[8], (D,), jnp.float32), 0.099609375, 1.8984375).astype(jnp.bfloat16),
        "shift_mlp": noise(arg_keys[9], (D,), 0.3, 2.0, ((0, 4),)),
        "weight_up": noise(arg_keys[10], (D, FF), D ** -0.5, 0.21875, ((0, 4),)),
        "bias_up": noise(arg_keys[11], (FF,), 0.5, 3.0, ((0, 4),)),
        "weight_down": noise(arg_keys[12], (FF, D), FF ** -0.5, 0.109375, ((0, 4),)),
        "bias_down": noise(arg_keys[13], (D,), 0.3, 2.0, ((0, 4),)),
        "cotangent": noise(arg_keys[14], (MB, SEQS, LEN, D), 1.0, 6.0, ((1, 16), (2, 2))),
    }


EPS = 1e-05

@jax.custom_vjp
def low(v):
    return lax.optimization_barrier(v.astype(jnp.bfloat16)).astype(jnp.float32)

@jax.custom_vjp
def low_back(v):
    return v

def low_keep(v):
    return (low(v), None)

def low_pass(kept, grad):
    return (grad,)

def back_keep(v):
    return (v, None)

def back_low(kept, grad):
    return (low(grad),)
low.defvjp(low_keep, low_pass)
low_back.defvjp(back_keep, back_low)

def layer_norm(values, gain, shift):
    center = values - lax.optimization_barrier(jnp.mean(values, axis=-1, keepdims=True))
    spread = lax.optimization_barrier(jnp.mean(center * center, axis=-1, keepdims=True))
    return center * lax.rsqrt(spread + EPS) * gain + shift

def matmul(left, right):
    return jnp.dot(left, right, precision=lax.Precision.HIGHEST)

def sequence_block(tokens, params):
    weight_qkv, bias_query, bias_value, weight_mix, bias_mix, gain_attn, shift_attn, gain_mlp, shift_mlp, weight_up, bias_up, weight_down, bias_down = params
    first = low(layer_norm(tokens, gain_attn, shift_attn))
    joined = matmul(first, weight_qkv)
    query = low(low_back(joined[:, :D] + bias_query)).reshape(LEN, H, HD)
    key_rows = low(low_back(joined[:, D:2 * D])).reshape(LEN, H, HD)
    value_rows = low(low_back(joined[:, 2 * D:] + bias_value)).reshape(LEN, H, HD)
    raw = low_back(jnp.einsum('qhd,khd->hqk', query, key_rows, precision=lax.Precision.HIGHEST))
    row_pos = lax.broadcasted_iota(jnp.int32, (LEN, LEN), 0)
    col_pos = lax.broadcasted_iota(jnp.int32, (LEN, LEN), 1)
    scaled = jnp.where(col_pos <= row_pos, raw * HD ** (-0.5), -1e+30)
    probs = low(jax.nn.softmax(scaled, axis=-1))
    mixed = jnp.einsum('hqk,khd->qhd', probs, value_rows, precision=lax.Precision.HIGHEST)
    mixed = low(low_back(mixed.reshape(LEN, D)))
    middle = tokens + low_back(matmul(mixed, weight_mix) + bias_mix)
    second = low(layer_norm(middle, gain_mlp, shift_mlp))
    before = low_back(matmul(second, weight_up) + bias_up)
    active = low(jax.nn.gelu(before, approximate=True))
    return middle + low_back(matmul(active, weight_down) + bias_down)

def reference(inputs, weight_qkv, bias_query, bias_value, weight_mix, bias_mix, gain_attn, shift_attn, gain_mlp, shift_mlp, weight_up, bias_up, weight_down, bias_down, cotangent):
    params = tuple((item.astype(jnp.float32) for item in (weight_qkv, bias_query, bias_value, weight_mix, bias_mix, gain_attn, shift_attn, gain_mlp, shift_mlp, weight_up, bias_up, weight_down, bias_down)))
    tokens = inputs.astype(jnp.float32).reshape(MB * SEQS, LEN, D)
    grad_out = cotangent.astype(jnp.float32).reshape(MB * SEQS, LEN, D)
    step = jax.checkpoint(sequence_block)

    def forward(all_tokens, all_params):
        return lax.map(lambda row: step(row, all_params), all_tokens)
    results, pullback = jax.vjp(forward, tokens, params)
    grad_tokens, grad_params = pullback(grad_out)
    return (results.reshape(inputs.shape).astype(jnp.bfloat16), grad_tokens.reshape(inputs.shape), grad_params[0], grad_params[1], grad_params[2], grad_params[3], grad_params[4], grad_params[5], grad_params[6], grad_params[7], grad_params[8], grad_params[9], grad_params[10], grad_params[11], grad_params[12])
```

```python
from functools import partial

import jax
import jax.numpy as jnp
from jax import lax
from jax.experimental import pallas as pl
from jax.experimental.pallas import tpu as pltpu
from jax.sharding import PartitionSpec as P

H = 12
EPS = 1e-05
BF16 = jnp.bfloat16
F32 = jnp.float32
QB = 256


def norm_stats(values):
    center = values - jnp.mean(values, axis=-1, keepdims=True)
    inverse = lax.rsqrt(jnp.mean(center * center, axis=-1, keepdims=True) + EPS)
    return (center * inverse, inverse)


def norm_back(grad_norm, normal, inverse, gain):
    scaled = grad_norm * gain
    return inverse * (
        scaled
        - jnp.mean(scaled, axis=-1, keepdims=True)
        - normal * jnp.mean(scaled * normal, axis=-1, keepdims=True)
    )


def outer_sum(left, right):
    return jnp.einsum("sri,srj->ij", left, right, preferred_element_type=F32)


def project(left, weight):
    return jnp.einsum("sri,ij->srj", left, weight, preferred_element_type=F32)


def project_back(grad_rows, weight):
    return jnp.einsum("srj,ij->sri", grad_rows, weight, preferred_element_type=F32)


def dot_nt(a, b):
    return lax.dot_general(a, b, (((1,), (1,)), ((), ())), preferred_element_type=F32)


def dot_nn(a, b):
    return lax.dot_general(a, b, (((1,), (0,)), ((), ())), preferred_element_type=F32)


def head_mask(x, head, size):
    lane = lax.broadcasted_iota(jnp.int32, x.shape, 1)
    keep = (lane >= head * size) & (lane < (head + 1) * size)
    return jnp.where(keep, x, jnp.zeros_like(x))


def causal(scores_t, qb):
    n = scores_t.shape[0]
    bottom = scores_t[n - QB :]
    key = lax.broadcasted_iota(jnp.int32, bottom.shape, 0)
    query = lax.broadcasted_iota(jnp.int32, bottom.shape, 1)
    bottom = jnp.where(key <= query, bottom, -1e30)
    return bottom if n == QB else jnp.concatenate([scores_t[: n - QB], bottom], axis=0)


def attention_forward_kernel(factor, size, q_ref, k_ref, v_ref, o_ref, lse_ref):
    length = q_ref.shape[1]
    k = k_ref[0]
    vt = jnp.transpose(v_ref[0])
    for qb in range(length // QB):
        n = (qb + 1) * QB
        rows = pl.ds(qb * QB, QB)
        q = q_ref[0, rows, :]
        outs = []
        for head in range(2):
            s = causal(dot_nt(k[:n], head_mask(q, head, size)) * factor, qb)
            top = jnp.max(s, axis=0, keepdims=True)
            p = jnp.exp(s - top)
            total = jnp.sum(p, axis=0, keepdims=True)
            o = dot_nn(vt[head * size : (head + 1) * size, :n], p.astype(BF16))
            outs.append(o * (1.0 / total))
            lse_ref[0, 0, head : head + 1, rows] = top + jnp.log(total)
        o_ref[0, rows, :] = jnp.transpose(jnp.concatenate(outs, axis=0)).astype(o_ref.dtype)


def attention_forward(q, k, v, factor, size):
    mbs, length, width = q.shape
    lanes = 2 * size
    pairs = width // lanes
    block = pl.BlockSpec((1, length, lanes), lambda m, p: (m, 0, p))
    area = mbs * pairs * 2 * length * (length + QB) // 2
    return pl.pallas_call(
        partial(attention_forward_kernel, factor, size),
        grid=(mbs, pairs),
        in_specs=[block] * 3,
        out_specs=[block, pl.BlockSpec((1, 1, 8, length), lambda m, p: (m, p, 0, 0))],
        out_shape=[
            jax.ShapeDtypeStruct(q.shape, BF16),
            jax.ShapeDtypeStruct((mbs, pairs, 8, length), F32),
        ],
        compiler_params=pltpu.CompilerParams(vmem_limit_bytes=48 << 20),
        cost_estimate=pl.CostEstimate(
            flops=16 * area * size, bytes_accessed=8 * q.size, transcendentals=area
        ),
        name="attention_forward",
    )(q, k, v)


def attention_backward_kernel(factor, size, q_ref, k_ref, v_ref, do_ref, lse_ref, dq_ref, dk_ref, dv_ref, dk_sum, dv_sum):
    length = q_ref.shape[1]
    k = k_ref[0]
    v = v_ref[0]
    kt = jnp.transpose(k)
    for qb in reversed(range(length // QB)):
        n = (qb + 1) * QB
        rows = pl.ds(qb * QB, QB)
        q = q_ref[0, rows, :]
        do = do_ref[0, rows, :]
        dqs, dk, dv = [], None, None
        for head in range(2):
            qh = head_mask(q, head, size)
            doh = head_mask(do, head, size)
            s = causal(dot_nt(k[:n], qh) * factor, qb)
            p = jnp.exp(s - lse_ref[0, 0, head : head + 1, rows])
            dp = dot_nt(v[:n], doh)
            mean = jnp.sum(dp * p, axis=0, keepdims=True)
            ds = (p * (dp - mean) * factor).astype(BF16)
            dvh = dot_nn(p.astype(BF16), doh)
            dkh = dot_nn(ds, qh)
            dv = dvh if dv is None else dv + dvh
            dk = dkh if dk is None else dk + dkh
            dqs.append(dot_nn(kt[head * size : (head + 1) * size, :n], ds))
        dq_ref[0, rows, :] = jnp.transpose(jnp.concatenate(dqs, axis=0)).astype(BF16)
        if n == length:
            dk_sum[...] = dk
            dv_sum[...] = dv
        else:
            dk_sum[:n] += dk
            dv_sum[:n] += dv
    dk_ref[0] = dk_sum[...].astype(BF16)
    dv_ref[0] = dv_sum[...].astype(BF16)


def attention_backward(q, k, v, do, lse, factor, size):
    mbs, length, width = q.shape
    lanes = 2 * size
    pairs = width // lanes
    block = pl.BlockSpec((1, length, lanes), lambda m, p: (m, 0, p))
    area = mbs * pairs * 2 * length * (length + QB) // 2
    return pl.pallas_call(
        partial(attention_backward_kernel, factor, size),
        grid=(mbs, pairs),
        in_specs=[block] * 4 + [pl.BlockSpec((1, 1, 8, length), lambda m, p: (m, p, 0, 0))],
        out_specs=[block] * 3,
        out_shape=[jax.ShapeDtypeStruct(q.shape, BF16)] * 3,
        scratch_shapes=[pltpu.VMEM((length, lanes), F32)] * 2,
        compiler_params=pltpu.CompilerParams(vmem_limit_bytes=48 << 20),
        cost_estimate=pl.CostEstimate(
            flops=40 * area * size, bytes_accessed=14 * q.size, transcendentals=area
        ),
        name="attention_backward",
    )(q, k, v, do, lse)


def local(
    inputs,
    weight_qkv,
    bias_query,
    bias_value,
    weight_mix,
    bias_mix,
    gain_attn,
    shift_attn,
    gain_mlp,
    shift_mlp,
    weight_up,
    bias_up,
    weight_down,
    bias_down,
    cotangent,
):
    width = weight_qkv.shape[1] // 3
    half = width // 2
    size = width // H
    factor = size ** (-0.5)
    rows = inputs.shape[2]
    owners = lax.axis_size("fsdp")
    reps = lax.axis_size("rep")
    ctx = lax.axis_index("ctx")
    rep = lax.axis_index("rep")
    own = weight_qkv.shape[0]

    def swap(x):
        return lax.ppermute(x, "ctx", [(0, 1), (1, 0)])

    def order(mine, other, axis):
        return jnp.where(
            ctx == 0,
            jnp.concatenate([mine, other], axis=axis),
            jnp.concatenate([other, mine], axis=axis),
        )

    def columns(x, axis, which):
        return lax.dynamic_slice_in_dim(x, which * half, half, axis)

    flat = jnp.concatenate(
        [bias_query, bias_value, bias_mix, gain_attn, shift_attn, gain_mlp, shift_mlp, bias_down, bias_up]
    )
    small = lax.all_gather(flat.reshape(1, -1), "fsdp", axis=0, tiled=True).astype(F32)
    b_query, b_value, b_mix, g_attn, s_attn, g_mlp, s_mlp, b_down = (
        small[:, i * own : (i + 1) * own].reshape(-1) for i in range(8)
    )
    b_up = small[:, 8 * own :].reshape(-1)

    part = own // reps
    mine = lax.dynamic_slice_in_dim(weight_qkv, rep * part, part, 0)
    mine = jnp.concatenate([columns(mine[:, i * width : (i + 1) * width], 1, ctx) for i in range(3)], axis=1)
    w_qkv = lax.all_gather(mine, ("fsdp", "rep"), axis=0, tiled=True)

    def gather(shard):
        piece = shard.shape[0] // (2 * reps)
        mine = lax.dynamic_slice_in_dim(shard, (rep * 2 + ctx) * piece, piece, 0)
        return lax.all_gather(mine, ("fsdp", "rep", "ctx"), axis=0, tiled=True)

    w_mix = gather(weight_mix)
    w_up = gather(weight_up)
    w_down = gather(weight_down)

    tokens = inputs[:, 0].astype(F32)
    normal_one, inverse_one = norm_stats(tokens)
    first_own = (normal_one * g_attn + s_attn).astype(BF16)
    first = order(first_own, swap(first_own), 1)
    joined = project(first, w_qkv)
    query = (joined[..., :half] + columns(b_query, 0, ctx)).astype(BF16)
    key = joined[..., half : 2 * half].astype(BF16)
    value = (joined[..., 2 * half :] + columns(b_value, 0, ctx)).astype(BF16)
    mixed_heads, lse = attention_forward(query, key, value, factor, size)

    def my_rows(x):
        return lax.dynamic_slice_in_dim(x, ctx * rows, rows, 1)

    def their_rows(x):
        return lax.dynamic_slice_in_dim(x, (1 - ctx) * rows, rows, 1)

    mixed = order(my_rows(mixed_heads), swap(their_rows(mixed_heads)), 2)
    middle = tokens + project(mixed, w_mix) + b_mix
    normal_two, inverse_two = norm_stats(middle)
    second = (normal_two * g_mlp + s_mlp).astype(BF16)
    before = project(second, w_up) + b_up
    active, gelu_back = jax.vjp(partial(jax.nn.gelu, approximate=True), before)
    active = active.astype(BF16)
    result = (middle + project(active, w_down) + b_down).astype(BF16)

    d_down = cotangent[:, 0]
    grad_out = d_down.astype(F32)
    g_wdown = outer_sum(active, d_down)
    g_bdown = jnp.sum(grad_out, axis=(0, 1))
    d_before_f = gelu_back(project_back(d_down, w_down))[0]
    d_before = d_before_f.astype(BF16)
    g_wup = outer_sum(second, d_before)
    g_bup = jnp.sum(d_before.astype(F32), axis=(0, 1))
    d_second = project_back(d_before, w_up)
    g_gmlp = jnp.sum(d_second * normal_two, axis=(0, 1))
    g_smlp = jnp.sum(d_second, axis=(0, 1))
    d_middle = grad_out + norm_back(d_second, normal_two, inverse_two, g_mlp)
    d_branch = d_middle.astype(BF16)
    g_wmix = outer_sum(mixed, d_branch)
    g_bmix = jnp.sum(d_branch.astype(F32), axis=(0, 1))
    d_mixed = project_back(d_branch, w_mix).astype(BF16)
    d_heads = order(columns(d_mixed, 2, ctx), swap(columns(d_mixed, 2, 1 - ctx)), 1)
    d_query, d_key, d_value = attention_backward(query, key, value, d_heads, lse, factor, size)
    d_joined = jnp.concatenate([d_query, d_key, d_value], axis=-1)
    g_wqkv = outer_sum(first, d_joined)
    g_bquery = jnp.sum(d_query.astype(F32), axis=(0, 1))
    g_bvalue = jnp.sum(d_value.astype(F32), axis=(0, 1))
    d_first = project_back(d_joined, w_qkv)
    d_first = my_rows(d_first) + swap(their_rows(d_first).astype(BF16)).astype(F32)
    g_gattn = jnp.sum(d_first * normal_one, axis=(0, 1))
    g_sattn = jnp.sum(d_first, axis=(0, 1))
    d_tokens = d_middle + norm_back(d_first, normal_one, inverse_one, g_attn)

    def reduce(grad):
        piece = lax.psum_scatter(
            grad.astype(BF16), ("fsdp", "rep", "ctx"), scatter_dimension=0, tiled=True
        )
        return lax.all_gather(piece, ("rep", "ctx"), axis=0, tiled=True).astype(F32)

    o_wdown = reduce(g_wdown)
    o_wup = reduce(g_wup)
    o_wmix = reduce(g_wmix)
    piece = lax.psum_scatter(g_wqkv.astype(BF16), ("fsdp", "rep"), scatter_dimension=0, tiled=True)
    piece = lax.all_gather(piece, "rep", axis=0, tiled=True)
    other = swap(piece)
    low, high = jnp.where(ctx == 0, piece, other), jnp.where(ctx == 0, other, piece)
    o_wqkv = jnp.concatenate(
        [t for i in range(3) for t in (low[:, i * half : (i + 1) * half], high[:, i * half : (i + 1) * half])],
        axis=1,
    ).astype(F32)

    zeros = jnp.zeros((width,), F32)

    def place(v):
        return lax.dynamic_update_slice_in_dim(zeros, v, ctx * half, 0)

    vectors = (place(g_bquery), place(g_bvalue), g_bmix, g_gattn, g_sattn, g_gmlp, g_smlp, g_bdown)
    stacked = jnp.concatenate([v.reshape(owners, own) for v in vectors] + [g_bup.reshape(owners, -1)], axis=1)
    summed = lax.psum(stacked, ("rep", "fsdp", "ctx"))
    summed = lax.dynamic_slice_in_dim(summed, lax.axis_index("fsdp"), 1, 0)[0]
    o_bq, o_bv, o_bmix, o_ga, o_sa, o_gm, o_sm, o_bd = (summed[i * own : (i + 1) * own] for i in range(8))
    o_bup = summed[8 * own :]
    return (
        result[:, None],
        d_tokens[:, None],
        o_wqkv,
        o_bq,
        o_bv,
        o_wmix,
        o_bmix,
        o_ga,
        o_sa,
        o_gm,
        o_sm,
        o_wup,
        o_bup,
        o_wdown,
        o_bd,
    )


def solution(mesh):
    row = P(None, ("rep", "fsdp"), "ctx", None)
    mat = P("fsdp", None)
    vec = P("fsdp")
    params = (mat, vec, vec, mat, vec, vec, vec, vec, vec, mat, vec, mat, vec)
    in_specs = (row,) + params + (row,)
    out_specs = (row, row) + params
    return jax.shard_map(local, mesh=mesh, in_specs=in_specs, out_specs=out_specs, check_vma=False)
```

```python
from functools import partial

import jax
import jax.numpy as jnp
from jax import lax
from jax.experimental import pallas as pl
from jax.experimental.pallas import tpu as pltpu
from jax.sharding import PartitionSpec as P

H = 12
EPS = 1e-05
BF16 = jnp.bfloat16
F32 = jnp.float32
QB = 256


def norm_stats(values):
    center = values - jnp.mean(values, axis=-1, keepdims=True)
    inverse = lax.rsqrt(jnp.mean(center * center, axis=-1, keepdims=True) + EPS)
    return (center * inverse, inverse)


def norm_back(grad_norm, normal, inverse, gain):
    scaled = grad_norm * gain
    return inverse * (
        scaled
        - jnp.mean(scaled, axis=-1, keepdims=True)
        - normal * jnp.mean(scaled * normal, axis=-1, keepdims=True)
    )


def outer_sum(left, right):
    return jnp.einsum("sri,srj->ij", left, right, preferred_element_type=F32)


def project(left, weight):
    return jnp.einsum("sri,ij->srj", left, weight, preferred_element_type=F32)


def project_back(grad_rows, weight):
    return jnp.einsum("srj,ij->sri", grad_rows, weight, preferred_element_type=F32)


def dot_nt(a, b):
    return lax.dot_general(a, b, (((1,), (1,)), ((), ())), preferred_element_type=F32)


def dot_nn(a, b):
    return lax.dot_general(a, b, (((1,), (0,)), ((), ())), preferred_element_type=F32)


def head_mask(x, head, size):
    lane = lax.broadcasted_iota(jnp.int32, x.shape, 1)
    keep = (lane >= head * size) & (lane < (head + 1) * size)
    return jnp.where(keep, x, jnp.zeros_like(x))


def causal(scores_t, qb):
    n = scores_t.shape[0]
    bottom = scores_t[n - QB :]
    key = lax.broadcasted_iota(jnp.int32, bottom.shape, 0)
    query = lax.broadcasted_iota(jnp.int32, bottom.shape, 1)
    bottom = jnp.where(key <= query, bottom, -1e30)
    return bottom if n == QB else jnp.concatenate([scores_t[: n - QB], bottom], axis=0)


def attention_forward_kernel(factor, size, q_ref, k_ref, v_ref, o_ref, lse_ref):
    length = q_ref.shape[1]
    k = k_ref[0]
    vt = jnp.transpose(v_ref[0])
    for qb in range(length // QB):
        n = (qb + 1) * QB
        rows = pl.ds(qb * QB, QB)
        q = q_ref[0, rows, :]
        outs = []
        for head in range(2):
            s = causal(dot_nt(k[:n], head_mask(q, head, size)) * factor, qb)
            top = jnp.max(s, axis=0, keepdims=True)
            p = jnp.exp(s - top)
            total = jnp.sum(p, axis=0, keepdims=True)
            o = dot_nn(vt[head * size : (head + 1) * size, :n], p.astype(BF16))
            outs.append(o * (1.0 / total))
            lse_ref[0, 0, head : head + 1, rows] = top + jnp.log(total)
        o_ref[0, rows, :] = jnp.transpose(jnp.concatenate(outs, axis=0)).astype(o_ref.dtype)


def attention_forward(q, k, v, factor, size):
    mbs, length, width = q.shape
    lanes = 2 * size
    pairs = width // lanes
    block = pl.BlockSpec((1, length, lanes), lambda m, p: (m, 0, p))
    area = mbs * pairs * 2 * length * (length + QB) // 2
    return pl.pallas_call(
        partial(attention_forward_kernel, factor, size),
        grid=(mbs, pairs),
        in_specs=[block] * 3,
        out_specs=[block, pl.BlockSpec((1, 1, 8, length), lambda m, p: (m, p, 0, 0))],
        out_shape=[
            jax.ShapeDtypeStruct(q.shape, BF16),
            jax.ShapeDtypeStruct((mbs, pairs, 8, length), F32),
        ],
        compiler_params=pltpu.CompilerParams(vmem_limit_bytes=48 << 20),
        cost_estimate=pl.CostEstimate(
            flops=16 * area * size, bytes_accessed=8 * q.size, transcendentals=area
        ),
        name="attention_forward",
    )(q, k, v)


def attention_backward_kernel(factor, size, q_ref, k_ref, v_ref, do_ref, lse_ref, dq_ref, dk_ref, dv_ref, dk_sum, dv_sum):
    length = q_ref.shape[1]
    k = k_ref[0]
    v = v_ref[0]
    kt = jnp.transpose(k)
    for qb in reversed(range(length // QB)):
        n = (qb + 1) * QB
        rows = pl.ds(qb * QB, QB)
        q = q_ref[0, rows, :]
        do = do_ref[0, rows, :]
        dqs, dk, dv = [], None, None
        for head in range(2):
            qh = head_mask(q, head, size)
            doh = head_mask(do, head, size)
            s = causal(dot_nt(k[:n], qh) * factor, qb)
            p = jnp.exp(s - lse_ref[0, 0, head : head + 1, rows])
            dp = dot_nt(v[:n], doh)
            mean = jnp.sum(dp * p, axis=0, keepdims=True)
            ds = (p * (dp - mean) * factor).astype(BF16)
            dvh = dot_nn(p.astype(BF16), doh)
            dkh = dot_nn(ds, qh)
            dv = dvh if dv is None else dv + dvh
            dk = dkh if dk is None else dk + dkh
            dqs.append(dot_nn(kt[head * size : (head + 1) * size, :n], ds))
        dq_ref[0, rows, :] = jnp.transpose(jnp.concatenate(dqs, axis=0)).astype(BF16)
        if n == length:
            dk_sum[...] = dk
            dv_sum[...] = dv
        else:
            dk_sum[:n] += dk
            dv_sum[:n] += dv
    dk_ref[0] = dk_sum[...].astype(BF16)
    dv_ref[0] = dv_sum[...].astype(BF16)


def attention_backward(q, k, v, do, lse, factor, size):
    mbs, length, width = q.shape
    lanes = 2 * size
    pairs = width // lanes
    block = pl.BlockSpec((1, length, lanes), lambda m, p: (m, 0, p))
    area = mbs * pairs * 2 * length * (length + QB) // 2
    return pl.pallas_call(
        partial(attention_backward_kernel, factor, size),
        grid=(mbs, pairs),
        in_specs=[block] * 4 + [pl.BlockSpec((1, 1, 8, length), lambda m, p: (m, p, 0, 0))],
        out_specs=[block] * 3,
        out_shape=[jax.ShapeDtypeStruct(q.shape, BF16)] * 3,
        scratch_shapes=[pltpu.VMEM((length, lanes), F32)] * 2,
        compiler_params=pltpu.CompilerParams(vmem_limit_bytes=48 << 20),
        cost_estimate=pl.CostEstimate(
            flops=40 * area * size, bytes_accessed=14 * q.size, transcendentals=area
        ),
        name="attention_backward",
    )(q, k, v, do, lse)


MESH = pl.DeviceIdType.MESH


def position():
    return lax.axis_index("fsdp"), lax.axis_index("rep"), lax.axis_index("ctx")


def greet(owners, reps):
    z, r, c = position()
    barrier = pltpu.get_barrier_semaphore()
    peers = [{"fsdp": lax.rem(z + j, owners)} for j in range(1, owners)]
    peers += [{"rep": r ^ j} for j in range(1, reps)]
    peers += [{"ctx": 1 - c}]
    for peer in peers:
        pl.semaphore_signal(barrier, inc=1, device_id=peer, device_id_type=MESH)
    pl.semaphore_wait(barrier, len(peers))


class Copies:
    def __init__(self, send, recv, local):
        self.send, self.recv, self.local = send, recv, local
        self.slots, self.locals = 0, 0
        self.sent, self.kept = [], []

    def remote(self, src, dst, peer):
        copy = pltpu.make_async_remote_copy(
            src_ref=src,
            dst_ref=dst,
            send_sem=self.send.at[self.slots],
            recv_sem=self.recv.at[self.slots],
            device_id=peer,
            device_id_type=MESH,
        )
        self.slots += 1
        copy.start()
        self.sent.append(copy)
        return copy

    def keep(self, src, dst):
        copy = pltpu.make_async_copy(src, dst, self.local.at[self.locals])
        self.locals += 1
        copy.start()
        self.kept.append(copy)
        return copy

    def close(self):
        for copy in self.sent:
            copy.wait_send()


def slab(i, half):
    return pl.ds(pl.multiple_of(i * half, 128), half)


def gather_kernel(owners, reps, qkv_ref, mix_ref, up_ref, down_ref, small_ref, w_qkv, w_mix, w_up, w_down, w_small, send, recv, kept):
    z, r, c = position()
    greet(owners, reps)
    copies = Copies(send, recv, kept)
    items = [(mix_ref, w_mix), (up_ref, w_up), (down_ref, w_down)]
    half = w_qkv.shape[-1] // 3
    peers_z = [{"fsdp": lax.rem(z + j, owners)} for j in range(1, owners)]
    origins = [lax.rem(z - j + owners, owners) for j in range(1, owners)]
    peers_r = [{"rep": r ^ k} for k in range(1, reps)]

    small = [copies.remote(small_ref, w_small.at[z], to) for to in peers_z]
    first = [
        [
            copies.remote(qkv_ref.at[r, :, slab(2 * i + c, half)], w_qkv.at[z, r, :, slab(i, half)], to)
            for i in range(3)
        ]
        for to in peers_z
    ]
    rest = [[copies.remote(shard.at[c, r], whole.at[z, c, r], to) for to in peers_z] for shard, whole in items]
    copies.keep(small_ref, w_small.at[z])
    for i in range(3):
        copies.keep(qkv_ref.at[:, :, slab(2 * i + c, half)], w_qkv.at[z, :, :, slab(i, half)])
    for shard, whole in items:
        copies.keep(shard, whole.at[z])

    spread = []
    for arrived, origin in zip(first, origins):
        for copy in arrived:
            copy.wait_recv()
        piece = w_qkv.at[origin, r]
        spread += [copies.remote(piece, piece, to) for to in peers_r]
    spread_rest = []
    for (shard, whole), arrived in zip(items, rest):
        for copy, origin in zip(arrived, origins):
            copy.wait_recv()
            piece = whole.at[origin, c, r]
            spread_rest.append((whole.at[origin, c], [copies.remote(piece, piece, to) for to in peers_r]))
    last = []
    for side, arrived in spread_rest:
        for copy in arrived:
            copy.wait_recv()
        last.append(copies.remote(side, side, {"ctx": 1 - c}))
    for copy in small + spread + last:
        copy.wait_recv()
    copies.close()
    for copy in copies.kept:
        copy.wait()


def gather_weights(owners, reps, weight_qkv, weight_mix, weight_up, weight_down, small):
    own, wide = weight_qkv.shape

    def cut(shard):
        return shard.reshape(2, reps, shard.shape[0] // (2 * reps), shard.shape[1])

    ins = (
        weight_qkv.reshape(reps, own // reps, wide),
        cut(weight_mix),
        cut(weight_up),
        cut(weight_down),
        small,
    )
    shapes = [(owners, reps, own // reps, wide // 2)] + [(owners,) + x.shape for x in ins[1:]]
    remotes = (owners - 1) * (4 + 3 + 4 * (reps - 1) + 3)
    whole = pl.pallas_call(
        partial(gather_kernel, owners, reps),
        in_specs=[pl.BlockSpec(memory_space=pl.ANY)] * 5,
        out_specs=[pl.BlockSpec(memory_space=pl.ANY)] * 5,
        out_shape=[jax.ShapeDtypeStruct(s, BF16) for s in shapes],
        scratch_shapes=[
            pltpu.SemaphoreType.DMA((remotes,)),
            pltpu.SemaphoreType.DMA((remotes,)),
            pltpu.SemaphoreType.DMA((7,)),
        ],
        compiler_params=pltpu.CompilerParams(collective_id=1, has_side_effects=True),
        name="gather_weights",
    )(*ins)
    return (
        whole[0].reshape(owners * own, wide // 2),
        whole[1].reshape(owners * own, -1),
        whole[2].reshape(owners * own, -1),
        whole[3].reshape(owners * weight_down.shape[0], -1),
        whole[4],
    )


def add_blocks(out, parts, dtype):
    lead = out.shape[:-2]
    count = 1
    for n in lead:
        count *= n

    def body(i, _):
        at = []
        for n in reversed(lead):
            at.append(lax.rem(i, n))
            i = lax.div(i, n)
        at = tuple(reversed(at))
        terms = [p[at].astype(F32) for p in parts]
        while len(terms) > 1:
            terms = [a + b for a, b in zip(terms[::2], terms[1::2])]
        out[at] = terms[0].astype(dtype)
        return 0

    lax.fori_loop(0, count, body, 0)


def reduce_kernel(owners, reps, *refs):
    z, r, c = position()
    n = 4
    ins, vec = refs[:n], refs[n]
    outs, vec_out = refs[n + 1 : 2 * n + 1], refs[2 * n + 1]
    refs = refs[2 * n + 2 :]
    sums, from_core, from_reps, from_owners, finals = (refs[i * n : (i + 1) * n] for i in range(5))
    v_core, v_reps, v_mid, v_late, v_owners, send, recv, kept = refs[5 * n :]
    greet(owners, reps)
    copies = Copies(send, recv, kept)
    peers_z = [lax.rem(z + j, owners) for j in range(1, owners)]
    peers_r = [r ^ k for k in range(1, reps)]
    other = {"ctx": 1 - c}
    halved = [len(x.shape) == 5 for x in ins]

    loads, cores = [], []
    v_first = copies.remote(vec, v_core, other)
    for x, mine, theirs, split in zip(ins, sums, from_core, halved):
        if split:
            cores.append(copies.remote(x.at[:, 1 - c], theirs, other))
            loads.append(copies.keep(x.at[:, c], mine))
        else:
            cores.append(None)
            loads.append(copies.keep(x, mine))
    v_first.wait_recv()
    v_mid[...] = vec[...] + v_core[...]
    v_second = [copies.remote(v_mid, v_reps.at[k], {"rep": p}) for k, p in enumerate(peers_r)]
    seconds = []
    for mine, theirs, load, core, gets in zip(sums, from_core, loads, cores, from_reps):
        load.wait()
        if core is not None:
            core.wait_recv()
            add_blocks(mine, [mine, theirs], BF16)
        seconds.append([copies.remote(mine.at[:, p], gets.at[k], {"rep": p}) for k, p in enumerate(peers_r)])
    for copy in v_second:
        copy.wait_recv()
    v_late[...] = (v_mid[...] + v_reps[0]) + (v_reps[1] + v_reps[2])
    v_third = [copies.remote(v_late.at[p], v_owners.at[j], {"fsdp": p}) for j, p in enumerate(peers_z)]
    thirds = []
    for mine, arrived, gets, at_owner in zip(sums, seconds, from_reps, from_owners):
        for copy in arrived:
            copy.wait_recv()
        add_blocks(gets.at[0], [mine.at[:, r]] + [gets.at[k] for k in range(reps - 1)], BF16)
        thirds.append([copies.remote(gets.at[0, p], at_owner.at[j], {"fsdp": p}) for j, p in enumerate(peers_z)])
    fourths = []
    for arrived, gets, at_owner, final in zip(thirds, from_reps, from_owners, finals):
        for copy in arrived:
            copy.wait_recv()
        terms = [gets[0, z].astype(F32)] + [at_owner[j].astype(F32) for j in range(owners - 1)]
        while len(terms) > 1:
            terms = [a + b for a, b in zip(terms[::2], terms[1::2])]
        final[c, r] = terms[0].astype(BF16)
        piece = final.at[c, r]
        fourths.append([copies.remote(piece, piece, {"rep": p}) for p in peers_r])
    for copy in v_third:
        copy.wait_recv()
    vec_out[...] = (v_late[z] + v_owners[0]) + (v_owners[1] + v_owners[2])
    fifths = []
    for arrived, final in zip(fourths, finals):
        for copy in arrived:
            copy.wait_recv()
        fifths.append(copies.remote(final.at[c], final.at[c], other))
    for copy, final, out, split in zip(fifths, finals, outs, halved):
        copy.wait_recv()
        if split:
            for k in range(2):
                for j in range(reps):
                    out[k, j] = final[k, j].astype(F32)
        else:
            half = final.shape[-1] // 3
            for k in range(2):
                for j in range(reps):
                    whole = final[k, j].astype(F32)
                    for i in range(3):
                        out[j, :, (2 * i + k) * half : (2 * i + k + 1) * half] = whole[:, i * half : (i + 1) * half]
    copies.close()


def reduce_grads(owners, reps, g_wdown, g_wup, g_wmix, g_wqkv, vectors):
    def cut(grad):
        rows = grad.shape[0] // (owners * 2 * reps)
        return grad.reshape(owners, 2, reps, rows, grad.shape[1])

    own = g_wqkv.shape[0] // owners
    ins = [cut(g_wdown), cut(g_wup), cut(g_wmix), g_wqkv.reshape(owners, reps, own // reps, g_wqkv.shape[1])]
    pieces = [x.shape[-2:] for x in ins]
    outs = [(2, reps) + p for p in pieces[:3]] + [(reps, pieces[3][0], 2 * pieces[3][1])]
    spread = [(owners, reps) + p for p in pieces]
    scratch = [pltpu.VMEM(s, BF16) for s in spread]
    scratch += [pltpu.VMEM(s, BF16) for s in spread[:3]] + [pltpu.VMEM((8, 128), BF16)]
    scratch += [pltpu.VMEM((reps - 1, owners) + p, BF16) for p in pieces]
    scratch += [pltpu.VMEM((owners - 1,) + p, BF16) for p in pieces]
    scratch += [pltpu.VMEM((2, reps) + p, BF16) for p in pieces]
    block = vectors.shape[1:]
    scratch += [
        pltpu.VMEM((owners,) + block, F32),
        pltpu.VMEM((reps - 1, owners) + block, F32),
        pltpu.VMEM((owners,) + block, F32),
        pltpu.VMEM((owners,) + block, F32),
        pltpu.VMEM((owners - 1,) + block, F32),
    ]
    remotes = 3 + 4 * 2 * (reps - 1) + 4 * (owners - 1) + 4 + 1 + (reps - 1) + (owners - 1)
    scratch += [
        pltpu.SemaphoreType.DMA((remotes,)),
        pltpu.SemaphoreType.DMA((remotes,)),
        pltpu.SemaphoreType.DMA((4,)),
    ]
    vmem = pl.BlockSpec(memory_space=pltpu.VMEM)
    o_wdown, o_wup, o_wmix, o_wqkv, o_vec = pl.pallas_call(
        partial(reduce_kernel, owners, reps),
        in_specs=[pl.BlockSpec(memory_space=pl.ANY)] * 4 + [vmem],
        out_specs=[vmem] * 5,
        out_shape=[jax.ShapeDtypeStruct(s, F32) for s in outs] + [jax.ShapeDtypeStruct(block, F32)],
        scratch_shapes=scratch,
        compiler_params=pltpu.CompilerParams(collective_id=2, has_side_effects=True, vmem_limit_bytes=60 << 20),
        name="reduce_grads",
    )(*ins, vectors)
    return (
        o_wdown.reshape(-1, g_wdown.shape[1]),
        o_wup.reshape(-1, g_wup.shape[1]),
        o_wmix.reshape(-1, g_wmix.shape[1]),
        o_wqkv.reshape(own, -1),
        o_vec,
    )


def local(
    inputs,
    weight_qkv,
    bias_query,
    bias_value,
    weight_mix,
    bias_mix,
    gain_attn,
    shift_attn,
    gain_mlp,
    shift_mlp,
    weight_up,
    bias_up,
    weight_down,
    bias_down,
    cotangent,
):
    width = weight_qkv.shape[1] // 3
    half = width // 2
    size = width // H
    factor = size ** (-0.5)
    rows = inputs.shape[2]
    owners = lax.axis_size("fsdp")
    reps = lax.axis_size("rep")
    ctx = lax.axis_index("ctx")
    rep = lax.axis_index("rep")
    own = weight_qkv.shape[0]

    def swap(x):
        return lax.ppermute(x, "ctx", [(0, 1), (1, 0)])

    def order(mine, other, axis):
        return jnp.where(
            ctx == 0,
            jnp.concatenate([mine, other], axis=axis),
            jnp.concatenate([other, mine], axis=axis),
        )

    def columns(x, axis, which):
        return lax.dynamic_slice_in_dim(x, which * half, half, axis)

    direct = own % (16 * reps) == 0 and owners == 4 and reps == 4
    rows8 = jnp.stack(
        [bias_query, bias_value, bias_mix, gain_attn, shift_attn, gain_mlp, shift_mlp, bias_down]
    )
    small = jnp.concatenate([rows8, bias_up.reshape(-1, own), jnp.zeros((4, own), BF16)], axis=0)
    if direct:
        w_qkv, w_mix, w_up, w_down, small = gather_weights(
            owners, reps, weight_qkv, weight_mix, weight_up, weight_down, small
        )
    else:
        part = own // reps
        mine = lax.dynamic_slice_in_dim(weight_qkv, rep * part, part, 0)
        mine = jnp.concatenate([columns(mine[:, i * width : (i + 1) * width], 1, ctx) for i in range(3)], axis=1)
        w_qkv = lax.all_gather(mine, ("fsdp", "rep"), axis=0, tiled=True)

        def gather(shard):
            piece = shard.shape[0] // (2 * reps)
            mine = lax.dynamic_slice_in_dim(shard, (rep * 2 + ctx) * piece, piece, 0)
            return lax.all_gather(mine, ("fsdp", "rep", "ctx"), axis=0, tiled=True)

        w_mix = gather(weight_mix)
        w_up = gather(weight_up)
        w_down = gather(weight_down)
        small = lax.all_gather(small, "fsdp")
    small = small.astype(F32)
    b_query, b_value, b_mix, g_attn, s_attn, g_mlp, s_mlp, b_down = (small[:, i].reshape(-1) for i in range(8))
    b_up = small[:, 8:-4].reshape(-1)

    tokens = inputs[:, 0].astype(F32)
    normal_one, inverse_one = norm_stats(tokens)
    first_own = (normal_one * g_attn + s_attn).astype(BF16)
    first = order(first_own, swap(first_own), 1)
    joined = project(first, w_qkv)
    query = (joined[..., :half] + columns(b_query, 0, ctx)).astype(BF16)
    key = joined[..., half : 2 * half].astype(BF16)
    value = (joined[..., 2 * half :] + columns(b_value, 0, ctx)).astype(BF16)
    mixed_heads, lse = attention_forward(query, key, value, factor, size)

    def my_rows(x):
        return lax.dynamic_slice_in_dim(x, ctx * rows, rows, 1)

    def their_rows(x):
        return lax.dynamic_slice_in_dim(x, (1 - ctx) * rows, rows, 1)

    mixed = order(my_rows(mixed_heads), swap(their_rows(mixed_heads)), 2)
    middle = tokens + project(mixed, w_mix) + b_mix
    normal_two, inverse_two = norm_stats(middle)
    second = (normal_two * g_mlp + s_mlp).astype(BF16)
    before = project(second, w_up) + b_up
    active, gelu_back = jax.vjp(partial(jax.nn.gelu, approximate=True), before)
    active = active.astype(BF16)
    result = (middle + project(active, w_down) + b_down).astype(BF16)

    d_down = cotangent[:, 0]
    grad_out = d_down.astype(F32)
    g_wdown = outer_sum(active, d_down)
    g_bdown = jnp.sum(grad_out, axis=(0, 1))
    d_before_f = gelu_back(project_back(d_down, w_down))[0]
    d_before = d_before_f.astype(BF16)
    g_wup = outer_sum(second, d_before)
    g_bup = jnp.sum(d_before.astype(F32), axis=(0, 1))
    d_second = project_back(d_before, w_up)
    g_gmlp = jnp.sum(d_second * normal_two, axis=(0, 1))
    g_smlp = jnp.sum(d_second, axis=(0, 1))
    d_middle = grad_out + norm_back(d_second, normal_two, inverse_two, g_mlp)
    d_branch = d_middle.astype(BF16)
    g_wmix = outer_sum(mixed, d_branch)
    g_bmix = jnp.sum(d_branch.astype(F32), axis=(0, 1))
    d_mixed = project_back(d_branch, w_mix).astype(BF16)
    d_heads = order(columns(d_mixed, 2, ctx), swap(columns(d_mixed, 2, 1 - ctx)), 1)
    d_query, d_key, d_value = attention_backward(query, key, value, d_heads, lse, factor, size)
    d_joined = jnp.concatenate([d_query, d_key, d_value], axis=-1)
    g_wqkv = outer_sum(first, d_joined)
    g_bquery = jnp.sum(d_query.astype(F32), axis=(0, 1))
    g_bvalue = jnp.sum(d_value.astype(F32), axis=(0, 1))
    d_first = project_back(d_joined, w_qkv)
    d_first = my_rows(d_first) + swap(their_rows(d_first).astype(BF16)).astype(F32)
    g_gattn = jnp.sum(d_first * normal_one, axis=(0, 1))
    g_sattn = jnp.sum(d_first, axis=(0, 1))
    d_tokens = d_middle + norm_back(d_first, normal_one, inverse_one, g_attn)

    zeros = jnp.zeros((width,), F32)

    def place(v):
        return lax.dynamic_update_slice_in_dim(zeros, v, ctx * half, 0)

    vectors = (place(g_bquery), place(g_bvalue), g_bmix, g_gattn, g_sattn, g_gmlp, g_smlp, g_bdown)
    stacked = jnp.concatenate(
        [jnp.stack([v.reshape(owners, own) for v in vectors], axis=1), g_bup.reshape(owners, -1, own), jnp.zeros((owners, 4, own), F32)],
        axis=1,
    )
    if direct:
        o_wdown, o_wup, o_wmix, o_wqkv, summed = reduce_grads(
            owners, reps, g_wdown.astype(BF16), g_wup.astype(BF16), g_wmix.astype(BF16), g_wqkv.astype(BF16), stacked
        )
    else:

        def reduce(grad):
            piece = lax.psum_scatter(
                grad.astype(BF16), ("fsdp", "rep", "ctx"), scatter_dimension=0, tiled=True
            )
            return lax.all_gather(piece, ("rep", "ctx"), axis=0, tiled=True).astype(F32)

        o_wdown = reduce(g_wdown)
        o_wup = reduce(g_wup)
        o_wmix = reduce(g_wmix)
        piece = lax.psum_scatter(g_wqkv.astype(BF16), ("fsdp", "rep"), scatter_dimension=0, tiled=True)
        piece = lax.all_gather(piece, "rep", axis=0, tiled=True)
        other = swap(piece)
        low, high = jnp.where(ctx == 0, piece, other), jnp.where(ctx == 0, other, piece)
        o_wqkv = jnp.concatenate(
            [t for i in range(3) for t in (low[:, i * half : (i + 1) * half], high[:, i * half : (i + 1) * half])],
            axis=1,
        ).astype(F32)
        summed = lax.psum(stacked, ("rep", "fsdp", "ctx"))
        summed = lax.dynamic_index_in_dim(summed, lax.axis_index("fsdp"), 0, keepdims=False)
    o_bq, o_bv, o_bmix, o_ga, o_sa, o_gm, o_sm, o_bd = (summed[i] for i in range(8))
    o_bup = summed[8:-4].reshape(-1)
    return (
        result[:, None],
        d_tokens[:, None],
        o_wqkv,
        o_bq,
        o_bv,
        o_wmix,
        o_bmix,
        o_ga,
        o_sa,
        o_gm,
        o_sm,
        o_wup,
        o_bup,
        o_wdown,
        o_bd,
    )


def solution(mesh):
    row = P(None, ("rep", "fsdp"), "ctx", None)
    mat = P("fsdp", None)
    vec = P("fsdp")
    params = (mat, vec, vec, mat, vec, vec, vec, vec, vec, mat, vec, mat, vec)
    in_specs = (row,) + params + (row,)
    out_specs = (row, row) + params
    return jax.shard_map(local, mesh=mesh, in_specs=in_specs, out_specs=out_specs, check_vma=False)
```

```python
from functools import partial

import jax
import jax.numpy as jnp
from jax import lax
from jax.experimental import pallas as pl
from jax.experimental.pallas import tpu as pltpu
from jax.sharding import PartitionSpec as P

H = 12
EPS = 1e-05
BF16 = jnp.bfloat16
F32 = jnp.float32
QB = 256
TB = 256
FB = 512
GELU_A = 0.7978845608028654
GELU_B = 0.044715


def norm_stats(values):
    center = values - jnp.mean(values, axis=-1, keepdims=True)
    inverse = lax.rsqrt(jnp.mean(center * center, axis=-1, keepdims=True) + EPS)
    return (center * inverse, inverse)


def norm_back(grad_norm, normal, inverse, gain):
    scaled = grad_norm * gain
    return inverse * (
        scaled
        - jnp.mean(scaled, axis=-1, keepdims=True)
        - normal * jnp.mean(scaled * normal, axis=-1, keepdims=True)
    )


def outer_sum(left, right):
    return jnp.einsum("sri,srj->ij", left, right, preferred_element_type=F32)


def project(left, weight):
    return jnp.einsum("sri,ij->srj", left, weight, preferred_element_type=F32)


def project_back(grad_rows, weight):
    return jnp.einsum("srj,ij->sri", grad_rows, weight, preferred_element_type=F32)


def dot_nt(a, b):
    return lax.dot_general(a, b, (((1,), (1,)), ((), ())), preferred_element_type=F32)


def dot_nn(a, b):
    return lax.dot_general(a, b, (((1,), (0,)), ((), ())), preferred_element_type=F32)


def head_mask(x, head, size):
    lane = lax.broadcasted_iota(jnp.int32, x.shape, 1)
    keep = (lane >= head * size) & (lane < (head + 1) * size)
    return jnp.where(keep, x, jnp.zeros_like(x))


def causal(scores_t, qb):
    n = scores_t.shape[0]
    bottom = scores_t[n - QB :]
    key = lax.broadcasted_iota(jnp.int32, bottom.shape, 0)
    query = lax.broadcasted_iota(jnp.int32, bottom.shape, 1)
    bottom = jnp.where(key <= query, bottom, -1e30)
    return bottom if n == QB else jnp.concatenate([scores_t[: n - QB], bottom], axis=0)


def attention_forward_kernel(factor, size, q_ref, k_ref, v_ref, o_ref, lse_ref):
    attention_forward_block(factor, size, q_ref.at[0], k_ref.at[0], v_ref.at[0], o_ref.at[0], lse_ref.at[0, 0])


def attention_forward_block(factor, size, q_ref, k_ref, v_ref, o_ref, lse_ref):
    length = q_ref.shape[0]
    k = k_ref[...]
    vt = jnp.transpose(v_ref[...])
    for qb in range(length // QB):
        n = (qb + 1) * QB
        rows = pl.ds(qb * QB, QB)
        q = q_ref[rows, :]
        outs = []
        for head in range(2):
            s = causal(dot_nt(k[:n], head_mask(q, head, size)) * factor, qb)
            top = jnp.max(s, axis=0, keepdims=True)
            p = jnp.exp(s - top)
            total = jnp.sum(p, axis=0, keepdims=True)
            o = dot_nn(vt[head * size : (head + 1) * size, :n], p.astype(BF16))
            outs.append(o * (1.0 / total))
            lse_ref[head : head + 1, rows] = top + jnp.log(total)
        o_ref[rows, :] = jnp.transpose(jnp.concatenate(outs, axis=0)).astype(o_ref.dtype)


def attention_forward(q, k, v, factor, size):
    mbs, length, width = q.shape
    lanes = 2 * size
    pairs = width // lanes
    block = pl.BlockSpec((1, length, lanes), lambda m, p: (m, 0, p))
    area = mbs * pairs * 2 * length * (length + QB) // 2
    return pl.pallas_call(
        partial(attention_forward_kernel, factor, size),
        grid=(mbs, pairs),
        in_specs=[block] * 3,
        out_specs=[block, pl.BlockSpec((1, 1, 8, length), lambda m, p: (m, p, 0, 0))],
        out_shape=[
            jax.ShapeDtypeStruct(q.shape, BF16),
            jax.ShapeDtypeStruct((mbs, pairs, 8, length), F32),
        ],
        compiler_params=pltpu.CompilerParams(vmem_limit_bytes=48 << 20),
        cost_estimate=pl.CostEstimate(
            flops=16 * area * size, bytes_accessed=8 * q.size, transcendentals=area
        ),
        name="attention_forward",
    )(q, k, v)


def attention_backward_kernel(factor, size, q_ref, k_ref, v_ref, do_ref, lse_ref, dq_ref, dk_ref, dv_ref, dk_sum, dv_sum):
    length = q_ref.shape[1]
    k = k_ref[0]
    v = v_ref[0]
    kt = jnp.transpose(k)
    for qb in reversed(range(length // QB)):
        n = (qb + 1) * QB
        rows = pl.ds(qb * QB, QB)
        q = q_ref[0, rows, :]
        do = do_ref[0, rows, :]
        dqs, dk, dv = [], None, None
        for head in range(2):
            qh = head_mask(q, head, size)
            doh = head_mask(do, head, size)
            s = causal(dot_nt(k[:n], qh) * factor, qb)
            p = jnp.exp(s - lse_ref[0, 0, head : head + 1, rows])
            dp = dot_nt(v[:n], doh)
            mean = jnp.sum(dp * p, axis=0, keepdims=True)
            ds = (p * (dp - mean) * factor).astype(BF16)
            dvh = dot_nn(p.astype(BF16), doh)
            dkh = dot_nn(ds, qh)
            dv = dvh if dv is None else dv + dvh
            dk = dkh if dk is None else dk + dkh
            dqs.append(dot_nn(kt[head * size : (head + 1) * size, :n], ds))
        dq_ref[0, rows, :] = jnp.transpose(jnp.concatenate(dqs, axis=0)).astype(BF16)
        if n == length:
            dk_sum[...] = dk
            dv_sum[...] = dv
        else:
            dk_sum[:n] += dk
            dv_sum[:n] += dv
    dk_ref[0] = dk_sum[...].astype(BF16)
    dv_ref[0] = dv_sum[...].astype(BF16)


def attention_backward(q, k, v, do, lse, factor, size):
    mbs, length, width = q.shape
    lanes = 2 * size
    pairs = width // lanes
    block = pl.BlockSpec((1, length, lanes), lambda m, p: (m, 0, p))
    area = mbs * pairs * 2 * length * (length + QB) // 2
    return pl.pallas_call(
        partial(attention_backward_kernel, factor, size),
        grid=(mbs, pairs),
        in_specs=[block] * 4 + [pl.BlockSpec((1, 1, 8, length), lambda m, p: (m, p, 0, 0))],
        out_specs=[block] * 3,
        out_shape=[jax.ShapeDtypeStruct(q.shape, BF16)] * 3,
        scratch_shapes=[pltpu.VMEM((length, lanes), F32)] * 2,
        compiler_params=pltpu.CompilerParams(vmem_limit_bytes=48 << 20),
        cost_estimate=pl.CostEstimate(
            flops=40 * area * size, bytes_accessed=14 * q.size, transcendentals=area
        ),
        name="attention_backward",
    )(q, k, v, do, lse)


def gelu_parts(b):
    square = b * b
    inner = GELU_A * b * (1.0 + GELU_B * square)
    t = jnp.tanh(inner)
    rise = 0.5 * (1.0 + t)
    slope = rise + 0.5 * b * (1.0 - t * t) * (GELU_A * (1.0 + 3.0 * GELU_B * square))
    return b * rise, slope


def middle_kernel(
    x_ref, mixed_ref, d_ref, wmix_ref, wup_ref, wdown_ref, vec_ref, bup_ref,
    result_ref, dmid_ref, dmixed_ref, gmix_ref, gup_ref, gdown_ref, gvec_ref, gbup_ref,
    middle, second, second_t, mixed_t, out_sum, ds_sum, active_t, d_before,
):
    step = pl.program_id(0)
    last = pl.num_programs(0) - 1
    rows = x_ref.shape[0]
    chunks = [slice(i, i + TB) for i in range(0, rows, TB)]
    b_mix, gain, shift, b_down = (vec_ref[i : i + 1, :] for i in range(4))

    @pl.when(step == 0)
    def _():
        for at in chunks:
            mixed = mixed_ref[at]
            mixed_t[:, at] = jnp.transpose(mixed)
            mid = x_ref[at].astype(F32) + (dot_nn(mixed, wmix_ref[...]) + b_mix)
            middle[at] = mid
            normal, _ = norm_stats(mid)
            low = (normal * gain + shift).astype(BF16)
            second[at] = low
            second_t[:, at] = jnp.transpose(low)

    d_bup = None
    for at in chunks:
        act, slope = gelu_parts(dot_nn(second[at], wup_ref[...]) + bup_ref[...])
        act = act.astype(BF16)
        active_t[:, at] = jnp.transpose(act)
        db = (dot_nt(d_ref[at], wdown_ref[...]) * slope).astype(BF16)
        d_before[at] = db
        part = jnp.sum(db.astype(F32), axis=0, keepdims=True)
        d_bup = part if d_bup is None else d_bup + part
        out = dot_nn(act, wdown_ref[...])
        ds = dot_nt(db, wup_ref[...])

        @pl.when(step == 0)
        def _():
            out_sum[at] = out
            ds_sum[at] = ds

        @pl.when(step > 0)
        def _():
            out_sum[at] += out
            ds_sum[at] += ds

    gbup_ref[...] = d_bup
    gdown_ref[...] = dot_nn(active_t[...], d_ref[...]).astype(BF16)
    gup_ref[...] = dot_nn(second_t[...], d_before[...]).astype(BF16)

    @pl.when(step == last)
    def _():
        sums = [None] * 4
        for at in chunks:
            mid = middle[at]
            result_ref[at] = (mid + (out_sum[at] + b_down)).astype(BF16)
            normal, inverse = norm_stats(mid)
            ds = ds_sum[at]
            grad_out = d_ref[at].astype(F32)
            d_mid = grad_out + norm_back(ds, normal, inverse, gain)
            dmid_ref[at] = d_mid
            branch = d_mid.astype(BF16)
            second[at] = branch
            dmixed_ref[at] = dot_nt(branch, wmix_ref[...]).astype(BF16)
            parts = (branch.astype(F32), ds * normal, ds, grad_out)
            for i, part in enumerate(parts):
                part = jnp.sum(part, axis=0, keepdims=True)
                sums[i] = part if sums[i] is None else sums[i] + part
        for i in range(4):
            gvec_ref[i : i + 1, :] = sums[i]
        gmix_ref[...] = dot_nn(mixed_t[...], second[...]).astype(BF16)


def middle_block(x, mixed, d_out, w_mix, w_up, w_down, vecs, b_up):
    rows, width = x.shape
    ff = w_up.shape[1]
    whole = lambda shape: pl.BlockSpec(shape, lambda f: (0, 0), pipeline_mode=pl.Buffered(1))
    out = jax.ShapeDtypeStruct
    return pl.pallas_call(
        middle_kernel,
        grid=(ff // FB,),
        in_specs=[whole((rows, width))] * 3
        + [
            whole((width, width)),
            pl.BlockSpec((width, FB), lambda f: (0, f)),
            pl.BlockSpec((FB, width), lambda f: (f, 0)),
            whole(vecs.shape),
            pl.BlockSpec((1, FB), lambda f: (0, f)),
        ],
        out_specs=[
            whole((rows, width)),
            whole((rows, width)),
            whole((rows, width)),
            whole((width, width)),
            pl.BlockSpec((width, FB), lambda f: (0, f)),
            pl.BlockSpec((FB, width), lambda f: (f, 0)),
            whole((4, width)),
            pl.BlockSpec((1, FB), lambda f: (0, f)),
        ],
        out_shape=[
            out((rows, width), BF16),
            out((rows, width), F32),
            out((rows, width), BF16),
            out((width, width), BF16),
            out((width, ff), BF16),
            out((ff, width), BF16),
            out((4, width), F32),
            out((1, ff), F32),
        ],
        scratch_shapes=[
            pltpu.VMEM((rows, width), F32),
            pltpu.VMEM((rows, width), BF16),
            pltpu.VMEM((width, rows), BF16),
            pltpu.VMEM((width, rows), BF16),
            pltpu.VMEM((rows, width), F32),
            pltpu.VMEM((rows, width), F32),
            pltpu.VMEM((FB, rows), BF16),
            pltpu.VMEM((rows, FB), BF16),
        ],
        compiler_params=pltpu.CompilerParams(vmem_limit_bytes=56 << 20),
        cost_estimate=pl.CostEstimate(
            flops=12 * rows * width * ff + 6 * rows * width * width,
            bytes_accessed=8 * width * ff + 16 * rows * width,
            transcendentals=rows * ff,
        ),
        name="middle_block",
    )(x, mixed, d_out, w_mix, w_up, w_down, vecs, b_up)


MESH = pl.DeviceIdType.MESH


def position():
    return lax.axis_index("fsdp"), lax.axis_index("rep"), lax.axis_index("ctx")


def greet(owners, reps):
    z, r, c = position()
    barrier = pltpu.get_barrier_semaphore()
    peers = [{"fsdp": lax.rem(z + j, owners)} for j in range(1, owners)]
    peers += [{"rep": r ^ j} for j in range(1, reps)]
    peers += [{"ctx": 1 - c}]
    for peer in peers:
        pl.semaphore_signal(barrier, inc=1, device_id=peer, device_id_type=MESH)
    pl.semaphore_wait(barrier, len(peers))


class Copies:
    def __init__(self, send, recv, local):
        self.send, self.recv, self.local = send, recv, local
        self.slots, self.locals = 0, 0
        self.sent, self.kept = [], []

    def remote(self, src, dst, peer):
        copy = pltpu.make_async_remote_copy(
            src_ref=src,
            dst_ref=dst,
            send_sem=self.send.at[self.slots],
            recv_sem=self.recv.at[self.slots],
            device_id=peer,
            device_id_type=MESH,
        )
        self.slots += 1
        copy.start()
        self.sent.append(copy)
        return copy

    def keep(self, src, dst):
        copy = pltpu.make_async_copy(src, dst, self.local.at[self.locals])
        self.locals += 1
        copy.start()
        self.kept.append(copy)
        return copy

    def close(self):
        for copy in self.sent:
            copy.wait_send()


def slab(i, half):
    return pl.ds(pl.multiple_of(i * half, 128), half)


def add_blocks(out, parts, dtype):
    lead = out.shape[:-2]
    count = 1
    for n in lead:
        count *= n

    def body(i, _):
        at = []
        for n in reversed(lead):
            at.append(lax.rem(i, n))
            i = lax.div(i, n)
        at = tuple(reversed(at))
        terms = [p[at].astype(F32) for p in parts]
        while len(terms) > 1:
            terms = [a + b for a, b in zip(terms[::2], terms[1::2])]
        out[at] = terms[0].astype(dtype)
        return 0

    lax.fori_loop(0, count, body, 0)


def reduce_kernel(owners, reps, *refs):
    z, r, c = position()
    n = 4
    ins, vec = refs[:n], refs[n]
    outs, vec_out = refs[n + 1 : 2 * n + 1], refs[2 * n + 1]
    refs = refs[2 * n + 2 :]
    sums, from_core, from_reps, from_owners, finals = (refs[i * n : (i + 1) * n] for i in range(5))
    v_core, v_reps, v_mid, v_late, v_owners, send, recv, kept = refs[5 * n :]
    greet(owners, reps)
    copies = Copies(send, recv, kept)
    peers_z = [lax.rem(z + j, owners) for j in range(1, owners)]
    peers_r = [r ^ k for k in range(1, reps)]
    other = {"ctx": 1 - c}
    halved = [len(x.shape) == 5 for x in ins]

    loads, cores = [], []
    v_first = copies.remote(vec, v_core, other)
    for x, mine, theirs, split in zip(ins, sums, from_core, halved):
        if split:
            cores.append(copies.remote(x.at[:, 1 - c], theirs, other))
            loads.append(copies.keep(x.at[:, c], mine))
        else:
            cores.append(None)
            loads.append(copies.keep(x, mine))
    v_first.wait_recv()
    v_mid[...] = vec[...] + v_core[...]
    v_second = [copies.remote(v_mid, v_reps.at[k], {"rep": p}) for k, p in enumerate(peers_r)]
    seconds = []
    for mine, theirs, load, core, gets in zip(sums, from_core, loads, cores, from_reps):
        load.wait()
        if core is not None:
            core.wait_recv()
            add_blocks(mine, [mine, theirs], BF16)
        seconds.append([copies.remote(mine.at[:, p], gets.at[k], {"rep": p}) for k, p in enumerate(peers_r)])
    for copy in v_second:
        copy.wait_recv()
    v_late[...] = (v_mid[...] + v_reps[0]) + (v_reps[1] + v_reps[2])
    v_third = [copies.remote(v_late.at[p], v_owners.at[j], {"fsdp": p}) for j, p in enumerate(peers_z)]
    thirds = []
    for mine, arrived, gets, at_owner in zip(sums, seconds, from_reps, from_owners):
        for copy in arrived:
            copy.wait_recv()
        add_blocks(gets.at[0], [mine.at[:, r]] + [gets.at[k] for k in range(reps - 1)], BF16)
        thirds.append([copies.remote(gets.at[0, p], at_owner.at[j], {"fsdp": p}) for j, p in enumerate(peers_z)])
    fourths = []
    for arrived, gets, at_owner, final in zip(thirds, from_reps, from_owners, finals):
        for copy in arrived:
            copy.wait_recv()
        terms = [gets[0, z].astype(F32)] + [at_owner[j].astype(F32) for j in range(owners - 1)]
        while len(terms) > 1:
            terms = [a + b for a, b in zip(terms[::2], terms[1::2])]
        final[c, r] = terms[0].astype(BF16)
        piece = final.at[c, r]
        fourths.append([copies.remote(piece, piece, {"rep": p}) for p in peers_r])
    for copy in v_third:
        copy.wait_recv()
    vec_out[...] = (v_late[z] + v_owners[0]) + (v_owners[1] + v_owners[2])
    fifths = []
    for arrived, final in zip(fourths, finals):
        for copy in arrived:
            copy.wait_recv()
        fifths.append(copies.remote(final.at[c], final.at[c], other))
    for copy, final, out, split in zip(fifths, finals, outs, halved):
        copy.wait_recv()
        if split:
            for k in range(2):
                for j in range(reps):
                    out[k, j] = final[k, j].astype(F32)
        else:
            half = final.shape[-1] // 3
            for k in range(2):
                for j in range(reps):
                    whole = final[k, j].astype(F32)
                    for i in range(3):
                        out[j, :, (2 * i + k) * half : (2 * i + k + 1) * half] = whole[:, i * half : (i + 1) * half]
    copies.close()


def reduce_grads(owners, reps, g_wdown, g_wup, g_wmix, g_wqkv, vectors):
    def cut(grad):
        rows = grad.shape[0] // (owners * 2 * reps)
        return grad.reshape(owners, 2, reps, rows, grad.shape[1])

    own = g_wqkv.shape[0] // owners
    ins = [cut(g_wdown), cut(g_wup), cut(g_wmix), g_wqkv.reshape(owners, reps, own // reps, g_wqkv.shape[1])]
    pieces = [x.shape[-2:] for x in ins]
    outs = [(2, reps) + p for p in pieces[:3]] + [(reps, pieces[3][0], 2 * pieces[3][1])]
    spread = [(owners, reps) + p for p in pieces]
    scratch = [pltpu.VMEM(s, BF16) for s in spread]
    scratch += [pltpu.VMEM(s, BF16) for s in spread[:3]] + [pltpu.VMEM((8, 128), BF16)]
    scratch += [pltpu.VMEM((reps - 1, owners) + p, BF16) for p in pieces]
    scratch += [pltpu.VMEM((owners - 1,) + p, BF16) for p in pieces]
    scratch += [pltpu.VMEM((2, reps) + p, BF16) for p in pieces]
    block = vectors.shape[1:]
    scratch += [
        pltpu.VMEM((owners,) + block, F32),
        pltpu.VMEM((reps - 1, owners) + block, F32),
        pltpu.VMEM((owners,) + block, F32),
        pltpu.VMEM((owners,) + block, F32),
        pltpu.VMEM((owners - 1,) + block, F32),
    ]
    remotes = 3 + 4 * 2 * (reps - 1) + 4 * (owners - 1) + 4 + 1 + (reps - 1) + (owners - 1)
    scratch += [
        pltpu.SemaphoreType.DMA((remotes,)),
        pltpu.SemaphoreType.DMA((remotes,)),
        pltpu.SemaphoreType.DMA((4,)),
    ]
    vmem = pl.BlockSpec(memory_space=pltpu.VMEM)
    o_wdown, o_wup, o_wmix, o_wqkv, o_vec = pl.pallas_call(
        partial(reduce_kernel, owners, reps),
        in_specs=[pl.BlockSpec(memory_space=pl.ANY)] * 4 + [vmem],
        out_specs=[vmem] * 5,
        out_shape=[jax.ShapeDtypeStruct(s, F32) for s in outs] + [jax.ShapeDtypeStruct(block, F32)],
        scratch_shapes=scratch,
        compiler_params=pltpu.CompilerParams(collective_id=2, has_side_effects=True, vmem_limit_bytes=60 << 20),
        name="reduce_grads",
    )(*ins, vectors)
    return (
        o_wdown.reshape(-1, g_wdown.shape[1]),
        o_wup.reshape(-1, g_wup.shape[1]),
        o_wmix.reshape(-1, g_wmix.shape[1]),
        o_wqkv.reshape(own, -1),
        o_vec,
    )


class Plan:
    def __init__(self, send, recv):
        self.send, self.recv = send, recv
        self.made = {}

    def add(self, name, src, dst, peer):
        self.made[name] = (len(self.made), src, dst, peer)

    def copy(self, name):
        slot, src, dst, peer = self.made[name]
        return pltpu.make_async_remote_copy(
            src_ref=src(),
            dst_ref=dst(),
            send_sem=self.send.at[slot],
            recv_sem=self.recv.at[slot],
            device_id=peer,
            device_id_type=MESH,
        )

    def start(self, *names):
        for name in names:
            self.copy(name).start()

    def arrive(self, *names):
        for name in names:
            self.copy(name).wait_recv()

    def close(self):
        for name in self.made:
            self.copy(name).wait_send()


def spread_plan(plan, tag, owners, reps, z, r, c, src, dst, halves, core=None):
    for j in range(1, owners):
        origin = lax.rem(z - j + owners, owners)
        plan.add((tag, "z", j), src, lambda: dst(z, r), {"fsdp": lax.rem(z + j, owners)})
        here = partial(dst, origin, r)
        plan.add((tag, "x", j), here, here, {"rep": r ^ 1})
        plan.add((tag, "y", j), here, here, {"rep": r ^ 2})
        by_y = lambda origin=origin: halves(dst(origin, r ^ 2))[0]
        by_x = lambda origin=origin: halves(dst(origin, r ^ 1))[1]
        plan.add((tag, "xx", j), by_y, by_y, {"rep": r ^ 1})
        plan.add((tag, "yy", j), by_x, by_x, {"rep": r ^ 2})
        if core is not None:
            side = partial(core, origin)
            plan.add((tag, "c", j), side, side, {"ctx": 1 - c})


def spread_step(plan, tag, owners, stage):
    for j in range(1, owners):
        if stage == 0:
            plan.start((tag, "z", j))
        elif stage == 1:
            plan.arrive((tag, "z", j))
            plan.start((tag, "x", j), (tag, "y", j))
        elif stage == 2:
            plan.arrive((tag, "y", j))
            plan.start((tag, "xx", j))
            plan.arrive((tag, "x", j))
            plan.start((tag, "yy", j))
        elif stage == 3:
            plan.arrive((tag, "xx", j), (tag, "yy", j))
            if (tag, "c", j) in plan.made:
                plan.start((tag, "c", j))
        else:
            plan.arrive((tag, "c", j))


def forward_kernel(owners, reps, pairs, factor, size,
                   x_ref, qkv_ref, mix_ref, up_ref, down_ref, small_ref,
                   mixed, qkv_out, first_t_out, w_qkv_out, w_mix, w_up, w_down, vec_ref, lse_ref,
                   first, first_t, w_qkv, qkv, heads, small, send, recv, kept):
    step = pl.program_id(0)
    last = pl.num_programs(0) - 1
    z, r, c = position()
    mbs, rows, width = x_ref.shape
    half = width // 2
    lanes = 2 * size
    plan = Plan(send, recv)
    own_rows = pl.ds(pl.multiple_of(c * rows, rows), rows)
    their_rows = pl.ds(pl.multiple_of((1 - c) * rows, rows), rows)

    for j in range(1, owners):
        plan.add(("small", j), lambda: small_ref, lambda: small.at[z], {"fsdp": lax.rem(z + j, owners)})
    for m in range(mbs):
        plan.add(("first", m), lambda m=m: first.at[m, own_rows], lambda m=m: first.at[m, own_rows], {"ctx": 1 - c})
    for j in range(1, owners):
        for i in range(3):
            plan.add(
                ("qkv", "z", i, j),
                lambda i=i: qkv_ref.at[r, :, slab(2 * i + c, half)],
                lambda i=i: w_qkv.at[z, r, :, slab(i, half)],
                {"fsdp": lax.rem(z + j, owners)},
            )
    cut = w_qkv.shape[3] // 256 * 128
    spread_plan(
        plan, "qkv", owners, reps, z, r, c, None, lambda o, p: w_qkv.at[o, p],
        lambda ref: (ref.at[:, pl.ds(0, cut)], ref.at[:, pl.ds(cut, 3 * half - cut)]),
    )
    for j in range(1, owners):
        del plan.made[("qkv", "z", j)]
    tags = []

    def chunk(tag, shard, whole, by_rows, parts):
        n = shard.shape[2 if by_rows else 3] // parts

        def part(ref, k):
            span = pl.ds(k * n, n)
            return ref.at[span] if by_rows else ref.at[:, span]

        def halves(ref):
            middle = ref.shape[1] // 2
            return ref.at[:, pl.ds(0, middle)], ref.at[:, pl.ds(middle, middle)]

        for k in range(parts):
            tags.append((tag, k))
            spread_plan(
                plan, (tag, k), owners, reps, z, r, c,
                lambda k=k: part(shard.at[c, r], k),
                lambda o, p, k=k: part(whole.at[o, c, p], k),
                halves,
                lambda o, k=k: (whole.at[o, c, :, pl.ds(k * n, n)] if by_rows else whole.at[o, c, :, :, pl.ds(k * n, n)]),
            )

    chunk("mix", mix_ref, w_mix, False, 1)
    chunk("up", up_ref, w_up, False, 2)
    chunk("down", down_ref, w_down, True, 2)
    order = [tags[0], tags[1], tags[3], tags[2], tags[4]]
    plan.made = {name: (i,) + rest[1:] for i, (name, rest) in enumerate(plan.made.items())}

    def keep(i):
        copies = [(small_ref, small.at[z])]
        copies += [(qkv_ref.at[:, :, slab(2 * i + c, half)], w_qkv.at[z, :, :, slab(i, half)]) for i in range(3)]
        copies += [(mix_ref, w_mix.at[z]), (up_ref, w_up.at[z]), (down_ref, w_down.at[z])]
        copies += [(w_qkv, w_qkv_out), (first_t, first_t_out), (qkv, qkv_out)]
        return pltpu.make_async_copy(*copies[i], kept.at[i])

    def mixed_place(step):
        m, p = lax.div(step, pairs), lax.rem(step, pairs)
        return mixed.at[m, :, slab(c * pairs + p, lanes)]

    def mixed_sends(k, slot):
        return pltpu.make_async_remote_copy(
            src_ref=heads.at[k, their_rows],
            dst_ref=mixed_place(k),
            send_sem=send.at[slot],
            recv_sem=recv.at[slot],
            device_id={"ctx": 1 - c},
            device_id_type=MESH,
        )

    base = len(plan.made)

    @pl.when(step == 0)
    def _():
        greet(owners, reps)
        for i in range(7):
            keep(i).start()
        plan.start(*[("small", j) for j in range(1, owners)])
        for j in range(1, owners):
            plan.start(*[("qkv", "z", i, j) for i in range(3)])
        keep(0).wait()
        plan.arrive(*[("small", j) for j in range(1, owners)])
        vec_ref[...] = jnp.transpose(small[...].reshape(-1, small.shape[-1]))[:16]
        gain, shift = vec_ref[3:4, :], vec_ref[4:5, :]
        for m in range(mbs):
            for at in range(0, rows, TB):
                normal, _ = norm_stats(x_ref[m, at : at + TB].astype(F32))
                place = pl.ds(pl.multiple_of(c * rows + at, TB), TB)
                first[m, place] = (normal * gain + shift).astype(BF16)
            plan.start(("first", m))
        for j in range(1, owners):
            plan.arrive(*[("qkv", "z", i, j) for i in range(3)])
            plan.start(("qkv", "x", j), ("qkv", "y", j))
        for tag in order:
            spread_step(plan, tag, owners, 0)
        plan.arrive(*[("first", m) for m in range(mbs)])
        for m in range(mbs):
            for at in range(0, 2 * rows, TB):
                first_t[:, m * 2 * rows + at : m * 2 * rows + at + TB] = jnp.transpose(first[m, at : at + TB])
        keep(8).start()
        spread_step(plan, "qkv", owners, 2)
        spread_step(plan, "qkv", owners, 3)
        for i in range(1, 4):
            keep(i).wait()
        keep(7).start()
        weight = w_qkv[...].reshape(-1, w_qkv.shape[-1])
        b_query = vec_ref[0:1, slab(c, half)]
        b_value = vec_ref[1:2, slab(c, half)]
        bias = jnp.concatenate([b_query, jnp.zeros_like(b_query), b_value], axis=1)

        def project_rows(i, _):
            m, at = lax.div(i, 2 * rows // TB), lax.rem(i, 2 * rows // TB)
            place = pl.ds(pl.multiple_of(at * TB, TB), TB)
            joined = (dot_nn(first[m, place], weight) + bias).astype(BF16)
            for s in range(3 * pairs):
                qkv[m, s, place] = joined[:, s * lanes : (s + 1) * lanes]
            return 0

        lax.fori_loop(0, mbs * 2 * rows // TB, project_rows, 0)
        keep(9).start()

    moves = {
        1: [(0, 1)],
        2: [(0, 2), (1, 1)],
        3: [(0, 3), (1, 2), (2, 1)],
        4: [(0, 4), (1, 3), (2, 2), (3, 1)],
        5: [(1, 4), (2, 3), (3, 2), (4, 1)],
        6: [(2, 4), (3, 3), (4, 2)],
    }
    for k, some in moves.items():

        @pl.when(step == k)
        def _():
            for t, stage in some:
                spread_step(plan, order[t], owners, stage)

    @pl.when(step > 0)
    def _():
        k = step - 1
        m, p = lax.div(k, pairs), lax.rem(k, pairs)
        attention_forward_block(
            factor, size, qkv.at[m, p], qkv.at[m, pairs + p], qkv.at[m, 2 * pairs + p], heads.at[k], lse_ref.at[m, p]
        )
        mixed_sends(k, base + k).start()
        pltpu.make_async_copy(heads.at[k, own_rows], mixed_place(k), kept.at[10 + k]).start()

    @pl.when(step == last)
    def _():
        spread_step(plan, order[3], owners, 4)
        spread_step(plan, order[4], owners, 3)
        spread_step(plan, order[4], owners, 4)
        for k in range(mbs * pairs):
            mixed_sends(k, base + k).wait()
            pltpu.make_async_copy(heads.at[k, own_rows], mixed_place(k), kept.at[10 + k]).wait()
        plan.close()
        for i in range(4, 10):
            keep(i).wait()


def forward_block(x, weight_qkv, weight_mix, weight_up, weight_down, small, owners, reps, factor, size):
    own, wide = weight_qkv.shape
    mbs, rows, width = x.shape
    lanes = 2 * size
    pairs = width // 2 // lanes

    def cut(shard):
        return shard.reshape(2, reps, shard.shape[0] // (2 * reps), shard.shape[1])

    shards = (weight_qkv.reshape(reps, own // reps, wide), cut(weight_mix), cut(weight_up), cut(weight_down), small)
    shape = jax.ShapeDtypeStruct
    w_shape = (owners, reps, own // reps, wide // 2)
    qkv_shape = (mbs, 3 * pairs, 2 * rows, lanes)
    anywhere = pl.BlockSpec(memory_space=pl.ANY)
    whole = lambda s: pl.BlockSpec(s, lambda i: (0,) * len(s), pipeline_mode=pl.Buffered(1))
    remotes = 3 + mbs + 9 + 12 + 5 * 18 + mbs * pairs
    area = mbs * pairs * 2 * rows * (2 * rows + QB)
    mixed, qkv, first_t, w_qkv, w_mix, w_up, w_down, vecs, lse = pl.pallas_call(
        partial(forward_kernel, owners, reps, pairs, factor, size),
        grid=(1 + mbs * pairs,),
        in_specs=[whole(x.shape)] + [anywhere] * 5,
        out_specs=[anywhere] * 7 + [whole((16, width)), whole((mbs, pairs, 8, 2 * rows))],
        out_shape=[
            shape((mbs, rows, width), BF16),
            shape(qkv_shape, BF16),
            shape((width, mbs * 2 * rows), BF16),
            shape(w_shape, BF16),
            shape((owners,) + shards[1].shape, BF16),
            shape((owners,) + shards[2].shape, BF16),
            shape((owners,) + shards[3].shape, BF16),
            shape((16, width), F32),
            shape((mbs, pairs, 8, 2 * rows), F32),
        ],
        scratch_shapes=[
            pltpu.VMEM((mbs, 2 * rows, width), BF16),
            pltpu.VMEM((width, mbs * 2 * rows), BF16),
            pltpu.VMEM(w_shape, BF16),
            pltpu.VMEM(qkv_shape, BF16),
            pltpu.VMEM((mbs * pairs, 2 * rows, lanes), BF16),
            pltpu.VMEM((owners,) + small.shape, F32),
            pltpu.SemaphoreType.DMA((remotes,)),
            pltpu.SemaphoreType.DMA((remotes,)),
            pltpu.SemaphoreType.DMA((10 + mbs * pairs,)),
        ],
        compiler_params=pltpu.CompilerParams(
            collective_id=1, has_side_effects=True, vmem_limit_bytes=56 << 20
        ),
        name="forward_block",
    )(x, *shards)
    return (
        mixed,
        qkv,
        first_t,
        w_qkv.reshape(owners * own, -1),
        w_mix.reshape(owners * own, -1),
        w_up.reshape(owners * own, -1),
        w_down.reshape(owners * weight_down.shape[0], -1),
        vecs,
        lse,
    )


def local(
    inputs,
    weight_qkv,
    bias_query,
    bias_value,
    weight_mix,
    bias_mix,
    gain_attn,
    shift_attn,
    gain_mlp,
    shift_mlp,
    weight_up,
    bias_up,
    weight_down,
    bias_down,
    cotangent,
):
    width = weight_qkv.shape[1] // 3
    half = width // 2
    size = width // H
    factor = size ** (-0.5)
    rows = inputs.shape[2]
    owners = lax.axis_size("fsdp")
    reps = lax.axis_size("rep")
    ctx = lax.axis_index("ctx")
    rep = lax.axis_index("rep")
    own = weight_qkv.shape[0]
    direct = own % (16 * reps) == 0 and owners == 4 and reps == 4

    def swap(x):
        return lax.ppermute(x, "ctx", [(0, 1), (1, 0)])

    def order(mine, other, axis):
        return jnp.where(
            ctx == 0,
            jnp.concatenate([mine, other], axis=axis),
            jnp.concatenate([other, mine], axis=axis),
        )

    def columns(x, axis, which):
        return lax.dynamic_slice_in_dim(x, which * half, half, axis)

    direct = own % (16 * reps) == 0 and owners == 4 and reps == 4
    vectors = [bias_query, bias_value, bias_mix, gain_attn, shift_attn, gain_mlp, shift_mlp, bias_down]
    small = jnp.stack(vectors + [v for v in bias_up.reshape(-1, own)], axis=1).astype(F32)
    tokens = inputs[:, 0].astype(F32)
    if direct:
        mixed, qkv, first_t, w_qkv, w_mix, w_up, w_down, vecs, lse = forward_block(
            inputs[:, 0],
            weight_qkv,
            weight_mix,
            weight_up,
            weight_down,
            jnp.pad(small, ((0, 0), (0, 128 - small.shape[1]))),
            owners,
            reps,
            factor,
            size,
        )
        vecs = vecs[:12]
    else:
        part = own // reps
        mine = lax.dynamic_slice_in_dim(weight_qkv, rep * part, part, 0)
        mine = jnp.concatenate([columns(mine[:, i * width : (i + 1) * width], 1, ctx) for i in range(3)], axis=1)
        w_qkv = lax.all_gather(mine, ("fsdp", "rep"), axis=0, tiled=True)

        def gather(shard):
            piece = shard.shape[0] // (2 * reps)
            mine = lax.dynamic_slice_in_dim(shard, (rep * 2 + ctx) * piece, piece, 0)
            return lax.all_gather(mine, ("fsdp", "rep", "ctx"), axis=0, tiled=True)

        w_mix = gather(weight_mix)
        w_up = gather(weight_up)
        w_down = gather(weight_down)
        vecs = lax.all_gather(small, "fsdp", axis=0, tiled=True).T
    b_query, b_value, b_mix, g_attn, s_attn, g_mlp, s_mlp, b_down = (vecs[i] for i in range(8))
    b_up = vecs[8:].reshape(-1, owners, own).swapaxes(0, 1).reshape(-1)

    normal_one, inverse_one = norm_stats(tokens)
    if not direct:
        first_own = (normal_one * g_attn + s_attn).astype(BF16)
        first = order(first_own, swap(first_own), 1)
        joined = project(first, w_qkv)
        query = (joined[..., :half] + columns(b_query, 0, ctx)).astype(BF16)
        key = joined[..., half : 2 * half].astype(BF16)
        value = (joined[..., 2 * half :] + columns(b_value, 0, ctx)).astype(BF16)
        mixed_heads, lse = attention_forward(query, key, value, factor, size)

    def my_rows(x):
        return lax.dynamic_slice_in_dim(x, ctx * rows, rows, 1)

    def their_rows(x):
        return lax.dynamic_slice_in_dim(x, (1 - ctx) * rows, rows, 1)

    if not direct:
        mixed = order(my_rows(mixed_heads), swap(their_rows(mixed_heads)), 2)
    flat = (-1, width)
    result, d_middle, d_mixed, g_wmix, g_wup, g_wdown, g_vecs, g_bup = middle_block(
        inputs.reshape(flat),
        mixed.reshape(flat),
        cotangent.reshape(flat),
        w_mix,
        w_up,
        w_down,
        jnp.stack([b_mix, g_mlp, s_mlp, b_down]),
        b_up.reshape(1, -1),
    )
    g_bmix, g_gmlp, g_smlp, g_bdown = (g_vecs[i] for i in range(4))
    d_mixed = d_mixed.reshape(tokens.shape)
    d_middle = d_middle.reshape(tokens.shape)
    d_heads = order(columns(d_mixed, 2, ctx), swap(columns(d_mixed, 2, 1 - ctx)), 1)
    if direct:
        query, key, value = (
            qkv[:, i * n : (i + 1) * n].swapaxes(1, 2).reshape(d_heads.shape) for n in [qkv.shape[1] // 3] for i in range(3)
        )
        first = first_t.T.reshape(d_heads.shape[:2] + (width,))
    d_query, d_key, d_value = attention_backward(query, key, value, d_heads, lse, factor, size)
    d_joined = jnp.concatenate([d_query, d_key, d_value], axis=-1)
    g_wqkv = outer_sum(first, d_joined)
    g_bquery = jnp.sum(d_query.astype(F32), axis=(0, 1))
    g_bvalue = jnp.sum(d_value.astype(F32), axis=(0, 1))
    d_first = project_back(d_joined, w_qkv)
    d_first = my_rows(d_first) + swap(their_rows(d_first).astype(BF16)).astype(F32)
    g_gattn = jnp.sum(d_first * normal_one, axis=(0, 1))
    g_sattn = jnp.sum(d_first, axis=(0, 1))
    d_tokens = d_middle + norm_back(d_first, normal_one, inverse_one, g_attn)

    zeros = jnp.zeros((width,), F32)

    def place(v):
        return lax.dynamic_update_slice_in_dim(zeros, v, ctx * half, 0)

    vectors = (place(g_bquery), place(g_bvalue), g_bmix, g_gattn, g_sattn, g_gmlp, g_smlp, g_bdown)
    stacked = jnp.concatenate(
        [jnp.stack([v.reshape(owners, own) for v in vectors], axis=1), g_bup.reshape(owners, -1, own), jnp.zeros((owners, 4, own), F32)],
        axis=1,
    )
    if direct:
        o_wdown, o_wup, o_wmix, o_wqkv, summed = reduce_grads(
            owners, reps, g_wdown.astype(BF16), g_wup.astype(BF16), g_wmix.astype(BF16), g_wqkv.astype(BF16), stacked
        )
    else:

        def reduce(grad):
            piece = lax.psum_scatter(
                grad.astype(BF16), ("fsdp", "rep", "ctx"), scatter_dimension=0, tiled=True
            )
            return lax.all_gather(piece, ("rep", "ctx"), axis=0, tiled=True).astype(F32)

        o_wdown = reduce(g_wdown)
        o_wup = reduce(g_wup)
        o_wmix = reduce(g_wmix)
        piece = lax.psum_scatter(g_wqkv.astype(BF16), ("fsdp", "rep"), scatter_dimension=0, tiled=True)
        piece = lax.all_gather(piece, "rep", axis=0, tiled=True)
        other = swap(piece)
        low, high = jnp.where(ctx == 0, piece, other), jnp.where(ctx == 0, other, piece)
        o_wqkv = jnp.concatenate(
            [t for i in range(3) for t in (low[:, i * half : (i + 1) * half], high[:, i * half : (i + 1) * half])],
            axis=1,
        ).astype(F32)
        summed = lax.psum(stacked, ("rep", "fsdp", "ctx"))
        summed = lax.dynamic_index_in_dim(summed, lax.axis_index("fsdp"), 0, keepdims=False)
    o_bq, o_bv, o_bmix, o_ga, o_sa, o_gm, o_sm, o_bd = (summed[i] for i in range(8))
    o_bup = summed[8:-4].reshape(-1)
    return (
        result.reshape(inputs.shape),
        d_tokens[:, None],
        o_wqkv,
        o_bq,
        o_bv,
        o_wmix,
        o_bmix,
        o_ga,
        o_sa,
        o_gm,
        o_sm,
        o_wup,
        o_bup,
        o_wdown,
        o_bd,
    )


def solution(mesh):
    row = P(None, ("rep", "fsdp"), "ctx", None)
    mat = P("fsdp", None)
    vec = P("fsdp")
    params = (mat, vec, vec, mat, vec, vec, vec, vec, vec, mat, vec, mat, vec)
    in_specs = (row,) + params + (row,)
    out_specs = (row, row) + params
    return jax.shard_map(local, mesh=mesh, in_specs=in_specs, out_specs=out_specs, check_vma=False)
```

```python
from functools import partial

import jax
import jax.numpy as jnp
from jax import lax
from jax.experimental import pallas as pl
from jax.experimental.pallas import tpu as pltpu
from jax.sharding import PartitionSpec as P

H = 12
EPS = 1e-05
BF16 = jnp.bfloat16
F32 = jnp.float32
QB = 256
TB = 256
FP = 256
SHARES = 4
GELU_A = 0.7978845608028654
GELU_B = 0.044715


def norm_stats(values):
    center = values - jnp.mean(values, axis=-1, keepdims=True)
    inverse = lax.rsqrt(jnp.mean(center * center, axis=-1, keepdims=True) + EPS)
    return (center * inverse, inverse)


def norm_back(grad_norm, normal, inverse, gain):
    scaled = grad_norm * gain
    return inverse * (
        scaled
        - jnp.mean(scaled, axis=-1, keepdims=True)
        - normal * jnp.mean(scaled * normal, axis=-1, keepdims=True)
    )


def outer_sum(left, right):
    return jnp.einsum("sri,srj->ij", left, right, preferred_element_type=F32)


def project(left, weight):
    return jnp.einsum("sri,ij->srj", left, weight, preferred_element_type=F32)


def project_back(grad_rows, weight):
    return jnp.einsum("srj,ij->sri", grad_rows, weight, preferred_element_type=F32)


def dot_nt(a, b):
    return lax.dot_general(a, b, (((1,), (1,)), ((), ())), preferred_element_type=F32)


def dot_nn(a, b):
    return lax.dot_general(a, b, (((1,), (0,)), ((), ())), preferred_element_type=F32)


def head_mask(x, head, size):
    lane = lax.broadcasted_iota(jnp.int32, x.shape, 1)
    keep = (lane >= head * size) & (lane < (head + 1) * size)
    return jnp.where(keep, x, jnp.zeros_like(x))


def causal(scores_t, qb):
    n = scores_t.shape[0]
    bottom = scores_t[n - QB :]
    key = lax.broadcasted_iota(jnp.int32, bottom.shape, 0)
    query = lax.broadcasted_iota(jnp.int32, bottom.shape, 1)
    bottom = jnp.where(key <= query, bottom, -1e30)
    return bottom if n == QB else jnp.concatenate([scores_t[: n - QB], bottom], axis=0)


def attention_forward_kernel(factor, size, q_ref, k_ref, v_ref, o_ref, lse_ref):
    attention_forward_block(factor, size, q_ref.at[0], k_ref.at[0], v_ref.at[0], o_ref.at[0], lse_ref.at[0, 0])


def attention_forward_block(factor, size, q_ref, k_ref, v_ref, o_ref, lse_ref):
    length = q_ref.shape[0]
    k = k_ref[...]
    vt = jnp.transpose(v_ref[...])
    for qb in range(length // QB):
        n = (qb + 1) * QB
        rows = pl.ds(qb * QB, QB)
        q = q_ref[rows, :]
        outs = []
        for head in range(2):
            s = causal(dot_nt(k[:n], head_mask(q, head, size)) * factor, qb)
            top = jnp.max(s, axis=0, keepdims=True)
            p = jnp.exp(s - top)
            total = jnp.sum(p, axis=0, keepdims=True)
            o = dot_nn(vt[head * size : (head + 1) * size, :n], p.astype(BF16))
            outs.append(o * (1.0 / total))
            lse_ref[head : head + 1, rows] = top + jnp.log(total)
        o_ref[rows, :] = jnp.transpose(jnp.concatenate(outs, axis=0)).astype(o_ref.dtype)


def attention_forward(q, k, v, factor, size):
    mbs, length, width = q.shape
    lanes = 2 * size
    pairs = width // lanes
    block = pl.BlockSpec((1, length, lanes), lambda m, p: (m, 0, p))
    area = mbs * pairs * 2 * length * (length + QB) // 2
    return pl.pallas_call(
        partial(attention_forward_kernel, factor, size),
        grid=(mbs, pairs),
        in_specs=[block] * 3,
        out_specs=[block, pl.BlockSpec((1, 1, 8, length), lambda m, p: (m, p, 0, 0))],
        out_shape=[
            jax.ShapeDtypeStruct(q.shape, BF16),
            jax.ShapeDtypeStruct((mbs, pairs, 8, length), F32),
        ],
        compiler_params=pltpu.CompilerParams(vmem_limit_bytes=48 << 20),
        cost_estimate=pl.CostEstimate(
            flops=16 * area * size, bytes_accessed=8 * q.size, transcendentals=area
        ),
        name="attention_forward",
    )(q, k, v)


def attention_backward_kernel(factor, size, q_ref, k_ref, v_ref, do_ref, lse_ref, dq_ref, dk_ref, dv_ref, dk_sum, dv_sum):
    refs = [ref.at[0] for ref in (q_ref, k_ref, v_ref, do_ref)]
    attention_backward_block(
        factor, size, *refs, lse_ref.at[0, 0], dq_ref.at[0], dk_ref.at[0], dv_ref.at[0], dk_sum, dv_sum, lambda done: None
    )


def attention_backward_block(
    factor, size, q_ref, k_ref, v_ref, do_ref, lse_ref, dq_ref, dk_ref, dv_ref, dk_sum, dv_sum, between
):
    length = q_ref.shape[0]
    k = k_ref[...]
    v = v_ref[...]
    kt = jnp.transpose(k)
    for i, qb in enumerate(reversed(range(length // QB))):
        n = (qb + 1) * QB
        rows = pl.ds(qb * QB, QB)
        q = q_ref[rows, :]
        do = do_ref[rows, :]
        dqs, dk, dv = [], None, None
        for head in range(2):
            qh = head_mask(q, head, size)
            doh = head_mask(do, head, size)
            s = causal(dot_nt(k[:n], qh) * factor, qb)
            p = jnp.exp(s - lse_ref[head : head + 1, rows])
            dp = dot_nt(v[:n], doh)
            mean = jnp.sum(dp * p, axis=0, keepdims=True)
            ds = (p * (dp - mean) * factor).astype(BF16)
            dvh = dot_nn(p.astype(BF16), doh)
            dkh = dot_nn(ds, qh)
            dv = dvh if dv is None else dv + dvh
            dk = dkh if dk is None else dk + dkh
            dqs.append(dot_nn(kt[head * size : (head + 1) * size, :n], ds))
        dq_ref[rows, :] = jnp.transpose(jnp.concatenate(dqs, axis=0)).astype(BF16)
        if n == length:
            dk_sum[...] = dk
            dv_sum[...] = dv
        else:
            dk_sum[:n] += dk
            dv_sum[:n] += dv
        between(i)
    dk_ref[...] = dk_sum[...].astype(BF16)
    dv_ref[...] = dv_sum[...].astype(BF16)


def attention_backward(q, k, v, do, lse, factor, size):
    mbs, length, width = q.shape
    lanes = 2 * size
    pairs = width // lanes
    block = pl.BlockSpec((1, length, lanes), lambda m, p: (m, 0, p))
    area = mbs * pairs * 2 * length * (length + QB) // 2
    return pl.pallas_call(
        partial(attention_backward_kernel, factor, size),
        grid=(mbs, pairs),
        in_specs=[block] * 4 + [pl.BlockSpec((1, 1, 8, length), lambda m, p: (m, p, 0, 0))],
        out_specs=[block] * 3,
        out_shape=[jax.ShapeDtypeStruct(q.shape, BF16)] * 3,
        scratch_shapes=[pltpu.VMEM((length, lanes), F32)] * 2,
        compiler_params=pltpu.CompilerParams(vmem_limit_bytes=48 << 20),
        cost_estimate=pl.CostEstimate(
            flops=40 * area * size, bytes_accessed=14 * q.size, transcendentals=area
        ),
        name="attention_backward",
    )(q, k, v, do, lse)


def gelu_parts(b):
    square = b * b
    inner = GELU_A * b * (1.0 + GELU_B * square)
    t = jnp.tanh(inner)
    rise = 0.5 * (1.0 + t)
    slope = rise + 0.5 * b * (1.0 - t * t) * (GELU_A * (1.0 + 3.0 * GELU_B * square))
    return b * rise, slope


def middle_kernel(
    owners, x_ref, mixed_ref, d_ref, wmix_ref, *refs
):
    wups, (wdown_ref, vec_ref, bup_ref) = refs[:owners], refs[owners : owners + 3]
    (result_ref, dmid_ref, dmixed_ref, gmix_ref, gup_ref, gdown_ref, gvec_ref,
     middle, second, second_t, mixed_t, out_sum, ds_sum, active_t, d_before) = refs[owners + 3 :]
    step = pl.program_id(0)
    last = pl.num_programs(0) - 1
    rows = x_ref.shape[0]
    chunks = [slice(i, i + TB) for i in range(0, rows, TB)]
    b_mix, gain, shift, b_down = (vec_ref[i : i + 1, :] for i in (2, 5, 6, 7))

    @pl.when(step == 0)
    def _():
        gvec_ref[...] = jnp.zeros_like(gvec_ref)
        for at in chunks:
            mixed = mixed_ref[at]
            mixed_t[:, at] = jnp.transpose(mixed)
            mid = x_ref[at].astype(F32) + (dot_nn(mixed, wmix_ref[...]) + b_mix)
            middle[at] = mid
            normal, _ = norm_stats(mid)
            low = (normal * gain + shift).astype(BF16)
            second[at] = low
            second_t[:, at] = jnp.transpose(low)

    wup = jnp.concatenate([w[...] for w in wups], axis=1)
    wdown = wdown_ref[...].reshape(-1, wdown_ref.shape[-1])
    d_bup = None
    for at in chunks:
        act, slope = gelu_parts(dot_nn(second[at], wup) + bup_ref[0])
        act = act.astype(BF16)
        active_t[:, at] = jnp.transpose(act)
        db = (dot_nt(d_ref[at], wdown) * slope).astype(BF16)
        d_before[at] = db
        part = jnp.sum(db.astype(F32), axis=0, keepdims=True)
        d_bup = part if d_bup is None else d_bup + part
        out = dot_nn(act, wdown)
        ds = dot_nt(db, wup)

        @pl.when(step == 0)
        def _():
            out_sum[at] = out
            ds_sum[at] = ds

        @pl.when(step > 0)
        def _():
            out_sum[at] += out
            ds_sum[at] += ds

    part = d_bup.shape[1] // owners
    for k in range(owners):
        gvec_ref[8 + k : 9 + k, slab(step, part)] = d_bup[:, k * part : (k + 1) * part]
    gdown_ref[0] = dot_nn(active_t[...], d_ref[...]).reshape(gdown_ref.shape[1:]).astype(BF16)
    gup_ref[0] = dot_nn(second_t[...], d_before[...]).reshape(gup_ref.shape[1:]).astype(BF16)

    @pl.when(step == last)
    def _():
        sums = [None] * 4
        for at in chunks:
            mid = middle[at]
            result_ref[at] = (mid + (out_sum[at] + b_down)).astype(BF16)
            normal, inverse = norm_stats(mid)
            ds = ds_sum[at]
            grad_out = d_ref[at].astype(F32)
            d_mid = grad_out + norm_back(ds, normal, inverse, gain)
            dmid_ref[at] = d_mid
            branch = d_mid.astype(BF16)
            second[at] = branch
            dmixed_ref[at] = dot_nt(branch, wmix_ref[...]).astype(BF16)
            parts = (branch.astype(F32), ds * normal, ds, grad_out)
            for i, part in enumerate(parts):
                part = jnp.sum(part, axis=0, keepdims=True)
                sums[i] = part if sums[i] is None else sums[i] + part
        for i, k in enumerate((2, 5, 6, 7)):
            gvec_ref[k : k + 1, :] = sums[i]
        gmix_ref[...] = dot_nn(mixed_t[...], second[...]).reshape(gmix_ref.shape).astype(BF16)


def middle_block(x, mixed, d_out, w_mix, w_up, w_down, vecs, b_up, owners, reps):
    rows, width = x.shape
    ff = w_up.shape[1]
    steps = ff // owners // FP
    whole = lambda shape: pl.BlockSpec(shape, lambda f: (0,) * len(shape), pipeline_mode=pl.Buffered(1))
    out = jax.ShapeDtypeStruct
    vmem = pltpu.VMEM
    side = (owners, 2, reps)
    g_mix = side + (width // owners // 2 // reps, width)
    g_up = (steps,) + g_mix[:-1] + (owners * FP,)
    g_down = (steps,) + side + (FP // 2 // reps, width)
    per_step = lambda s: pl.BlockSpec((1,) + s[1:], lambda f: (f,) + (0,) * (len(s) - 1))
    return pl.pallas_call(
        partial(middle_kernel, owners),
        grid=(steps,),
        in_specs=[whole((rows, width))] * 3
        + [whole((width, width))]
        + [pl.BlockSpec((width, FP), lambda f, k=k: (0, k * steps + f)) for k in range(owners)]
        + [
            pl.BlockSpec((owners, 1, FP, width), lambda f: (0, f, 0, 0)),
            whole(vecs.shape),
            pl.BlockSpec((1, 1, owners * FP), lambda f: (f, 0, 0)),
        ],
        out_specs=[
            whole((rows, width)),
            whole((rows, width)),
            whole((rows, width)),
            whole(g_mix),
            per_step(g_up),
            per_step(g_down),
            whole((16, width)),
        ],
        out_shape=[
            out((rows, width), BF16),
            out((rows, width), F32),
            out((rows, width), BF16),
            out(g_mix, BF16),
            out(g_up, BF16),
            out(g_down, BF16),
            out((16, width), F32),
        ],
        scratch_shapes=[
            vmem((rows, width), F32),
            vmem((rows, width), BF16),
            vmem((width, rows), BF16),
            vmem((width, rows), BF16),
            vmem((rows, width), F32),
            vmem((rows, width), F32),
            vmem((owners * FP, rows), BF16),
            vmem((rows, owners * FP), BF16),
        ],
        compiler_params=pltpu.CompilerParams(vmem_limit_bytes=60 << 20),
        cost_estimate=pl.CostEstimate(
            flops=12 * rows * width * ff + 6 * rows * width * width,
            bytes_accessed=8 * width * ff + 16 * rows * width,
            transcendentals=rows * ff,
        ),
        name="middle_block",
    )(x, mixed, d_out, w_mix, *[w_up] * owners, w_down.reshape(owners, steps, FP, width), vecs, b_up)


MESH = pl.DeviceIdType.MESH


def position():
    return lax.axis_index("fsdp"), lax.axis_index("rep"), lax.axis_index("ctx")


def greet(owners, reps):
    z, r, c = position()
    barrier = pltpu.get_barrier_semaphore()
    peers = [{"fsdp": lax.rem(z + j, owners)} for j in range(1, owners)]
    peers += [{"rep": r ^ j} for j in range(1, reps)]
    peers += [{"ctx": 1 - c}]
    for peer in peers:
        pl.semaphore_signal(barrier, inc=1, device_id=peer, device_id_type=MESH)
    pl.semaphore_wait(barrier, len(peers))


def slab(i, half):
    return pl.ds(pl.multiple_of(i * half, 128), half)


def add_blocks(out, parts, dtype):
    lead = out.shape[:-2]
    count = 1
    for n in lead:
        count *= n

    def body(i, _):
        at = []
        for n in reversed(lead):
            at.append(lax.rem(i, n))
            i = lax.div(i, n)
        at = tuple(reversed(at))
        terms = [p[at].astype(F32) for p in parts]
        while len(terms) > 1:
            terms = [terms[0] + terms[1]] + terms[2:]
        out[at] = terms[0].astype(dtype)
        return 0

    lax.fori_loop(0, count, body, 0)


class Plan:
    def __init__(self, send, recv):
        self.send, self.recv = send, recv
        self.made = {}

    def add(self, name, src, dst, peer):
        self.made[name] = (len(self.made), src, dst, peer)

    def copy(self, name):
        slot, src, dst, peer = self.made[name]
        return pltpu.make_async_remote_copy(
            src_ref=src(),
            dst_ref=dst(),
            send_sem=self.send.at[slot],
            recv_sem=self.recv.at[slot],
            device_id=peer,
            device_id_type=MESH,
        )

    def start(self, *names):
        for name in names:
            self.copy(name).start()

    def arrive(self, *names):
        for name in names:
            self.copy(name).wait_recv()

    def close(self):
        for name in self.made:
            self.copy(name).wait_send()


def spread_plan(plan, tag, owners, reps, z, r, c, src, dst, halves, core=None):
    for j in range(1, owners):
        origin = lax.rem(z - j + owners, owners)
        plan.add((tag, "z", j), src, lambda: dst(z, r), {"fsdp": lax.rem(z + j, owners)})
        here = partial(dst, origin, r)
        plan.add((tag, "x", j), here, here, {"rep": r ^ 1})
        plan.add((tag, "y", j), here, here, {"rep": r ^ 2})
        by_y = lambda origin=origin: halves(dst(origin, r ^ 2))[0]
        by_x = lambda origin=origin: halves(dst(origin, r ^ 1))[1]
        plan.add((tag, "xx", j), by_y, by_y, {"rep": r ^ 1})
        plan.add((tag, "yy", j), by_x, by_x, {"rep": r ^ 2})
        if core is not None:
            side = partial(core, origin)
            plan.add((tag, "c", j), side, side, {"ctx": 1 - c})


def spread_step(plan, tag, owners, stage):
    for j in range(1, owners):
        if stage == 0:
            plan.start((tag, "z", j))
        elif stage == 1:
            plan.arrive((tag, "z", j))
            plan.start((tag, "x", j), (tag, "y", j))
        elif stage == 2:
            plan.arrive((tag, "y", j))
            plan.start((tag, "xx", j))
            plan.arrive((tag, "x", j))
            plan.start((tag, "yy", j))
        elif stage == 3:
            plan.arrive((tag, "xx", j), (tag, "yy", j))
            if (tag, "c", j) in plan.made:
                plan.start((tag, "c", j))
        else:
            plan.arrive((tag, "c", j))


def forward_kernel(owners, reps, pairs, factor, size,
                   x_ref, qkv_ref, mix_ref, up_ref, down_ref, small_ref,
                   mixed, qkv_out, first_t_out, w_qkv_out, w_mix, w_up, w_down, vec_ref, lse_ref,
                   first, first_t, w_qkv, qkv, heads, small, send, recv, kept):
    step = pl.program_id(0)
    last = pl.num_programs(0) - 1
    z, r, c = position()
    mbs, rows, width = x_ref.shape
    half = width // 2
    lanes = 2 * size
    plan = Plan(send, recv)
    own_rows = pl.ds(pl.multiple_of(c * rows, rows), rows)
    their_rows = pl.ds(pl.multiple_of((1 - c) * rows, rows), rows)

    for j in range(1, owners):
        plan.add(("small", j), lambda: small_ref, lambda: small.at[z], {"fsdp": lax.rem(z + j, owners)})
    for m in range(mbs):
        plan.add(("first", m), lambda m=m: first.at[m, own_rows], lambda m=m: first.at[m, own_rows], {"ctx": 1 - c})
    for j in range(1, owners):
        for i in range(3):
            plan.add(
                ("qkv", "z", i, j),
                lambda i=i: qkv_ref.at[r, :, slab(2 * i + c, half)],
                lambda i=i: w_qkv.at[z, r, :, slab(i, half)],
                {"fsdp": lax.rem(z + j, owners)},
            )
    cut = w_qkv.shape[3] // 256 * 128
    spread_plan(
        plan, "qkv", owners, reps, z, r, c, None, lambda o, p: w_qkv.at[o, p],
        lambda ref: (ref.at[:, pl.ds(0, cut)], ref.at[:, pl.ds(cut, 3 * half - cut)]),
    )
    for j in range(1, owners):
        del plan.made[("qkv", "z", j)]
    tags = []

    def chunk(tag, shard, whole, by_rows, parts):
        n = shard.shape[2 if by_rows else 3] // parts

        def part(ref, k):
            span = pl.ds(k * n, n)
            return ref.at[span] if by_rows else ref.at[:, span]

        def halves(ref):
            middle = ref.shape[1] // 2
            return ref.at[:, pl.ds(0, middle)], ref.at[:, pl.ds(middle, middle)]

        for k in range(parts):
            tags.append((tag, k))
            spread_plan(
                plan, (tag, k), owners, reps, z, r, c,
                lambda k=k: part(shard.at[c, r], k),
                lambda o, p, k=k: part(whole.at[o, c, p], k),
                halves,
                lambda o, k=k: (whole.at[o, c, :, pl.ds(k * n, n)] if by_rows else whole.at[o, c, :, :, pl.ds(k * n, n)]),
            )

    chunk("mix", mix_ref, w_mix, False, 1)
    chunk("up", up_ref, w_up, False, 2)
    chunk("down", down_ref, w_down, True, 2)
    order = [tags[0], tags[1], tags[3], tags[2], tags[4]]
    plan.made = {name: (i,) + rest[1:] for i, (name, rest) in enumerate(plan.made.items())}

    def keep(i):
        copies = [(small_ref, small.at[z])]
        copies += [(qkv_ref.at[:, :, slab(2 * i + c, half)], w_qkv.at[z, :, :, slab(i, half)]) for i in range(3)]
        copies += [(mix_ref, w_mix.at[z]), (up_ref, w_up.at[z]), (down_ref, w_down.at[z])]
        copies += [(w_qkv, w_qkv_out), (first_t, first_t_out), (qkv, qkv_out)]
        return pltpu.make_async_copy(*copies[i], kept.at[i])

    def mixed_place(step):
        m, p = lax.div(step, pairs), lax.rem(step, pairs)
        return mixed.at[m, :, slab(c * pairs + p, lanes)]

    def mixed_sends(k, slot):
        return pltpu.make_async_remote_copy(
            src_ref=heads.at[k, their_rows],
            dst_ref=mixed_place(k),
            send_sem=send.at[slot],
            recv_sem=recv.at[slot],
            device_id={"ctx": 1 - c},
            device_id_type=MESH,
        )

    base = len(plan.made)

    @pl.when(step == 0)
    def _():
        greet(owners, reps)
        for i in range(7):
            keep(i).start()
        plan.start(*[("small", j) for j in range(1, owners)])
        for j in range(1, owners):
            plan.start(*[("qkv", "z", i, j) for i in range(3)])
        keep(0).wait()
        plan.arrive(*[("small", j) for j in range(1, owners)])
        vec_ref[...] = jnp.transpose(small[...].reshape(-1, small.shape[-1]))[:16]
        gain, shift = vec_ref[3:4, :], vec_ref[4:5, :]
        for m in range(mbs):
            for at in range(0, rows, TB):
                normal, _ = norm_stats(x_ref[m, at : at + TB].astype(F32))
                place = pl.ds(pl.multiple_of(c * rows + at, TB), TB)
                first[m, place] = (normal * gain + shift).astype(BF16)
            plan.start(("first", m))
        for j in range(1, owners):
            plan.arrive(*[("qkv", "z", i, j) for i in range(3)])
            plan.start(("qkv", "x", j), ("qkv", "y", j))
        for tag in order:
            spread_step(plan, tag, owners, 0)
        plan.arrive(*[("first", m) for m in range(mbs)])
        for m in range(mbs):
            for at in range(0, 2 * rows, TB):
                first_t[:, m * 2 * rows + at : m * 2 * rows + at + TB] = jnp.transpose(first[m, at : at + TB])
        keep(8).start()
        spread_step(plan, "qkv", owners, 2)
        spread_step(plan, "qkv", owners, 3)
        for i in range(1, 4):
            keep(i).wait()
        keep(7).start()
        weight = w_qkv[...].reshape(-1, w_qkv.shape[-1])
        b_query = vec_ref[0:1, slab(c, half)]
        b_value = vec_ref[1:2, slab(c, half)]
        bias = jnp.concatenate([b_query, jnp.zeros_like(b_query), b_value], axis=1)

        def project_rows(i, _):
            m, at = lax.div(i, 2 * rows // TB), lax.rem(i, 2 * rows // TB)
            place = pl.ds(pl.multiple_of(at * TB, TB), TB)
            joined = (dot_nn(first[m, place], weight) + bias).astype(BF16)
            for s in range(3 * pairs):
                qkv[m, s, place] = joined[:, s * lanes : (s + 1) * lanes]
            return 0

        lax.fori_loop(0, mbs * 2 * rows // TB, project_rows, 0)
        keep(9).start()

    moves = {
        1: [(0, 1)],
        2: [(0, 2), (1, 1)],
        3: [(0, 3), (1, 2), (2, 1)],
        4: [(0, 4), (1, 3), (2, 2), (3, 1)],
        5: [(1, 4), (2, 3), (3, 2), (4, 1)],
        6: [(2, 4), (3, 3), (4, 2)],
    }
    for k, some in moves.items():

        @pl.when(step == k)
        def _():
            for t, stage in some:
                spread_step(plan, order[t], owners, stage)

    @pl.when(step > 0)
    def _():
        k = step - 1
        m, p = lax.div(k, pairs), lax.rem(k, pairs)
        attention_forward_block(
            factor, size, qkv.at[m, p], qkv.at[m, pairs + p], qkv.at[m, 2 * pairs + p], heads.at[k], lse_ref.at[m, p]
        )
        mixed_sends(k, base + k).start()
        pltpu.make_async_copy(heads.at[k, own_rows], mixed_place(k), kept.at[10 + k]).start()

    @pl.when(step == last)
    def _():
        spread_step(plan, order[3], owners, 4)
        spread_step(plan, order[4], owners, 3)
        spread_step(plan, order[4], owners, 4)
        for k in range(mbs * pairs):
            mixed_sends(k, base + k).wait()
            pltpu.make_async_copy(heads.at[k, own_rows], mixed_place(k), kept.at[10 + k]).wait()
        plan.close()
        for i in range(4, 10):
            keep(i).wait()


def forward_block(x, weight_qkv, weight_mix, weight_up, weight_down, small, owners, reps, factor, size):
    own, wide = weight_qkv.shape
    mbs, rows, width = x.shape
    lanes = 2 * size
    pairs = width // 2 // lanes

    def cut(shard):
        return shard.reshape(2, reps, shard.shape[0] // (2 * reps), shard.shape[1])

    shards = (weight_qkv.reshape(reps, own // reps, wide), cut(weight_mix), cut(weight_up), cut(weight_down), small)
    shape = jax.ShapeDtypeStruct
    w_shape = (owners, reps, own // reps, wide // 2)
    qkv_shape = (mbs, 3 * pairs, 2 * rows, lanes)
    anywhere = pl.BlockSpec(memory_space=pl.ANY)
    whole = lambda s: pl.BlockSpec(s, lambda i: (0,) * len(s), pipeline_mode=pl.Buffered(1))
    remotes = 3 + mbs + 9 + 12 + 5 * 18 + mbs * pairs
    area = mbs * pairs * 2 * rows * (2 * rows + QB)
    mixed, qkv, first_t, w_qkv, w_mix, w_up, w_down, vecs, lse = pl.pallas_call(
        partial(forward_kernel, owners, reps, pairs, factor, size),
        grid=(1 + mbs * pairs,),
        in_specs=[whole(x.shape)] + [anywhere] * 5,
        out_specs=[anywhere] * 7 + [whole((16, width)), whole((mbs, pairs, 8, 2 * rows))],
        out_shape=[
            shape((mbs, rows, width), BF16),
            shape(qkv_shape, BF16),
            shape((width, mbs * 2 * rows), BF16),
            shape(w_shape, BF16),
            shape((owners,) + shards[1].shape, BF16),
            shape((owners,) + shards[2].shape, BF16),
            shape((owners,) + shards[3].shape, BF16),
            shape((16, width), F32),
            shape((mbs, pairs, 8, 2 * rows), F32),
        ],
        scratch_shapes=[
            pltpu.VMEM((mbs, 2 * rows, width), BF16),
            pltpu.VMEM((width, mbs * 2 * rows), BF16),
            pltpu.VMEM(w_shape, BF16),
            pltpu.VMEM(qkv_shape, BF16),
            pltpu.VMEM((mbs * pairs, 2 * rows, lanes), BF16),
            pltpu.VMEM((owners,) + small.shape, F32),
            pltpu.SemaphoreType.DMA((remotes,)),
            pltpu.SemaphoreType.DMA((remotes,)),
            pltpu.SemaphoreType.DMA((10 + mbs * pairs,)),
        ],
        compiler_params=pltpu.CompilerParams(
            collective_id=1, has_side_effects=True, vmem_limit_bytes=56 << 20
        ),
        name="forward_block",
    )(x, *shards)
    return (
        mixed,
        qkv,
        first_t,
        w_qkv.reshape(owners * own, -1),
        w_mix.reshape(owners * own, -1),
        w_up.reshape(owners * own, -1),
        w_down.reshape(owners * weight_down.shape[0], -1),
        vecs,
        lse,
    )


class Flow:
    def __init__(self, plan, name, place, owners, bits, mine, theirs, hops, outs, load=None, core=None):
        z, r, c = place
        first, second = bits
        self.plan, self.name, self.place, self.owners = plan, name, place, owners
        self.mine, self.theirs, self.second = mine, theirs, r ^ second
        self.hop_one, self.hop_two, self.hop_z, self.final = hops
        self.outs = outs
        self.load = load
        peer = {"rep": r ^ first}
        if core is not None:
            plan.add((name, "core"), core, lambda: theirs, {"ctx": 1 - c})
        self.split = core is not None
        plan.add((name, "me"), lambda: mine.at[:, r ^ first], lambda: self.hop_one.at[0], peer)
        plan.add((name, "on"), lambda: mine.at[:, r ^ first ^ second], lambda: self.hop_one.at[1], peer)
        plan.add((name, "two"), lambda: mine.at[:, r ^ second], lambda: self.hop_two, {"rep": r ^ second})
        for j in range(1, owners):
            to = lax.rem(z + j, owners)
            plan.add((name, "z", j), lambda to=to: mine.at[to, r], lambda j=j: self.hop_z.at[j - 1], {"fsdp": to})
        here = lambda: self.final.at[c, r]
        plan.add((name, "x"), here, here, {"rep": r ^ first})
        plan.add((name, "y"), here, here, {"rep": r ^ second})
        far = lambda: self.final.at[c, r ^ second]
        plan.add((name, "xy"), far, far, {"rep": r ^ first})
        side = lambda: self.final.at[c]
        plan.add((name, "back"), side, side, {"ctx": 1 - c})

    def step(self, stage):
        z, r, c = self.place
        plan, name, mine = self.plan, self.name, self.mine
        owners = self.owners
        if stage == 0:
            if self.split:
                plan.start((name, "core"))
            if self.load is not None:
                self.load().start()
        elif stage == 1:
            if self.load is not None:
                self.load().wait()
            if self.split:
                plan.arrive((name, "core"))
                add_blocks(mine, [mine, self.theirs], BF16)
            plan.start((name, "on"), (name, "me"))
        elif stage == 2:
            plan.arrive((name, "on"))
            part = mine.at[:, self.second]
            add_blocks(part, [part, self.hop_one.at[1]], BF16)
            plan.start((name, "two"))
        elif stage == 3:
            plan.arrive((name, "me"), (name, "two"))
            part = mine.at[:, r]
            add_blocks(part, [part, self.hop_one.at[0], self.hop_two], BF16)
            plan.start(*[(name, "z", j) for j in range(1, owners)])
        elif stage == 4:
            plan.arrive(*[(name, "z", j) for j in range(1, owners)])
            terms = [mine[z, r].astype(F32)] + [self.hop_z[j].astype(F32) for j in range(owners - 1)]
            while len(terms) > 1:
                terms = [a + b for a, b in zip(terms[::2], terms[1::2])]
            self.final[c, r] = terms[0].astype(BF16)
            plan.start((name, "x"), (name, "y"))
        elif stage == 5:
            plan.arrive((name, "y"))
            plan.start((name, "xy"))
        elif stage == 6:
            plan.arrive((name, "x"), (name, "xy"))
            plan.start((name, "back"))
        else:
            plan.arrive((name, "back"))
            for copy in self.outs(self.final):
                copy.start()


def flow_scratch(owners, reps, piece, split):
    vmem = lambda *lead: pltpu.VMEM(lead + piece, BF16)
    mine = [vmem(owners, reps)] * (2 if split else 1)
    return mine + [vmem(2, owners), vmem(owners), vmem(owners - 1), vmem(2, reps)]


def timetable(groups, products, gaps=(0, 4, 7, 11, 13, 15, 17), every=5):
    table = [(2 + every * g + gap, g, 1 + i) for g in range(groups) for i, gap in enumerate(gaps)]
    table += [(8 * (p + 1) + 1 + gap, groups + p, 1 + i) for p in range(products) for i, gap in enumerate(gaps) if i]
    return sorted(table)


def backward_kernel(
    owners, reps, pairs, factor, size, shapes,
    q_ref, k_ref, v_ref, lse_ref, x_ref, vec_ref, gvec_ref, dmid_ref, dmixed_ref, first_t_ref, w_ref, *refs
):
    n_in = len(shapes)
    sources, refs = refs[:n_in], refs[n_in:]
    dtok_ref, vec_out, refs = refs[0], refs[1], refs[2:]
    outs, refs = refs[: n_in + 1], refs[n_in + 1 :]
    d_heads, d_joined, first_t, w_pairs, df_send, df_recv, dk_sum, dv_sum, b_sum, vec_one, vec_got, vec_sum, refs = (
        refs[:12] + (refs[12:],)
    )
    flow_refs, (send, recv, kept) = refs[:-3], refs[-3:]
    step = pl.program_id(0)
    last = pl.num_programs(0) - 1
    place = z, r, c = position()
    mbs, rows, width = x_ref.shape
    half = width // 2
    lanes = 2 * size
    plan = Plan(send, recv)
    own_rows = pl.ds(pl.multiple_of(c * rows, rows), rows)

    locals_used = 0

    def local(src, dst):
        nonlocal locals_used
        locals_used += 1
        slot = kept.at[locals_used - 1]
        return lambda: pltpu.make_async_copy(src(), dst(), slot)

    up_step = shapes[1][-1] // owners
    flows, leaving, at = [], [], 0

    def add_flow(name, bits, mine, theirs, hops, places, load=None, core=None):
        final = hops[-1]
        copies = [local(partial(part, final), dst) for part, dst in places]
        leaving.extend(copies)
        flows.append(
            Flow(plan, name, place, owners, bits, mine, theirs, hops, lambda final: [f() for f in copies], load, core)
        )

    for i, shape in enumerate(shapes):
        for f in range(shape[0]):
            wide = shape[-1] // 2
            for s in range(2):
                mine, theirs, *hops = flow_refs[at : at + 6]
                at += 6
                source, out, cols = sources[i], outs[i], pl.ds(s * wide, wide)
                if i == 1:
                    places = []
                    for k in range(wide // up_step):
                        to = pl.ds(((s * wide // up_step + k) * shape[0] + f) * up_step, up_step)
                        places.append((
                            lambda final, k=k: final.at[:, :, :, pl.ds(k * up_step, up_step)],
                            lambda out=out, to=to: out.at[:, :, :, to],
                        ))
                else:
                    places = [(lambda final: final, lambda out=out, f=f, cols=cols: out.at[f, :, :, :, cols])]
                add_flow(
                    (i, f, s), (1, 2) if s == 0 else (2, 1), mine, theirs, hops, places,
                    local(lambda source=source, f=f, cols=cols: source.at[f, :, c, :, :, cols], lambda mine=mine: mine),
                    lambda source=source, f=f, cols=cols: source.at[f, :, 1 - c, :, :, cols],
                )
    for p in range(pairs):
        for s in range(2):
            mine, *hops = flow_refs[at : at + 5]
            at += 5
            places = []
            for side in range(2):
                for i in range(3):
                    to = pl.ds((i * 2 * pairs + side * pairs + p) * lanes, lanes)
                    places.append((
                        lambda final, side=side, i=i: final.at[side, :, :, pl.ds(i * lanes, lanes)],
                        lambda s=s, to=to: outs[-1].at[:, s, :, to],
                    ))
            add_flow((n_in, p, s), (1, 2) if s == 0 else (2, 1), mine, None, hops, places)
    groups = [flows[i : i + 2] for i in range(0, len(flows), 2)]
    products = len(groups) - pairs
    ff_steps = shapes[0][0]
    groups[: 2 * ff_steps] = [groups[k * ff_steps + f] for f in range(ff_steps) for k in range(2)]

    def advance(group, stage):
        for flow in groups[group]:
            flow.step(stage)

    for m in range(mbs):
        for p in range(pairs):
            plan.add(
                ("heads", m, p),
                lambda m=m, p=p: dmixed_ref.at[m, :, slab((1 - c) * pairs + p, lanes)],
                lambda m=m, p=p: d_heads.at[p, m, own_rows],
                {"ctx": 1 - c},
            )
        plan.add(("first", m), lambda m=m: df_send.at[m], lambda m=m: df_recv.at[m], {"ctx": 1 - c})
    for i, peer in enumerate([{"ctx": 1 - c}, {"rep": r ^ 1}, {"rep": r ^ 2}]):
        plan.add(("vec", i), lambda i=i: vec_sum.at[i], lambda i=i: vec_got.at[i], peer)
    for j in range(1, owners):
        plan.add(
            ("vec", "z", j), lambda: vec_sum.at[3], lambda j=j: vec_got.at[2 + j], {"fsdp": lax.rem(z + j, owners)}
        )

    def own_heads(m, p):
        return pltpu.make_async_copy(
            dmixed_ref.at[m, :, slab(c * pairs + p, lanes)], d_heads.at[p, m, own_rows], kept.at[locals_used + m * pairs + p]
        )

    def load_first():
        return pltpu.make_async_copy(first_t_ref, first_t, kept.at[locals_used + mbs * pairs])

    def load_weight(i, p):
        return pltpu.make_async_copy(
            w_ref.at[:, pl.ds((i * pairs + p) * lanes, lanes)],
            w_pairs.at[p, :, pl.ds(i * lanes, lanes)],
            kept.at[locals_used + mbs * pairs + 1 + i * pairs + p],
        )

    @pl.when(step == 0)
    def _():
        greet(owners, reps)
        for p in range(pairs):
            for m in range(mbs):
                plan.start(("heads", m, p))
                own_heads(m, p).start()
        for g in range(products):
            advance(g, 0)
        load_first().start()
        for i in range(3):
            for p in range(pairs):
                load_weight(i, p).start()
        for p in range(pairs):
            for m in range(mbs):
                plan.arrive(("heads", m, p))
                own_heads(m, p).wait()

    table = timetable(products, pairs)
    quarters = 2 * rows // QB
    tail = [entry for entry in table if entry[0] >= quarters * mbs * pairs]

    def between(k, done):
        for i in range(mbs * pairs):
            some = [entry for entry in table if entry[0] == quarters * i + done]
            if some:

                @pl.when(k == i)
                def _():
                    for _, group, stage in some:
                        advance(group, stage)

    def weight_grad(p):
        grad = dot_nn(first_t[...], d_joined[p])
        piece = groups[products][0].mine.shape[2]
        grad = grad.reshape(owners, reps, 2 * piece, grad.shape[1])
        for s in range(2):
            groups[products + p][s].mine[...] = grad[:, :, s * piece : (s + 1) * piece].astype(BF16)

    for p in range(pairs):

        @pl.when(step == mbs * (p + 1))
        def _():
            if p == 0:
                load_first().wait()
            weight_grad(p)
            advance(products + p, 1)

    @pl.when(step < last)
    def _():
        p, m = lax.div(step, mbs), lax.rem(step, mbs)
        start = pl.multiple_of(m * 2 * rows, 2 * rows)
        joined = d_joined.at[p, pl.ds(start, 2 * rows)]
        attention_backward_block(
            factor, size, q_ref.at[0, 0], k_ref.at[0, 0], v_ref.at[0, 0], d_heads.at[p, m], lse_ref.at[m, p],
            joined.at[:, pl.ds(0, lanes)], joined.at[:, pl.ds(lanes, lanes)], joined.at[:, pl.ds(2 * lanes, lanes)],
            dk_sum, dv_sum, partial(between, step),
        )
        for i, k in enumerate((0, 2)):
            part = jnp.sum(joined[:, k * lanes : (k + 1) * lanes].astype(F32), axis=0, keepdims=True)
            before = b_sum[p, i : i + 1, :]
            b_sum[p, i : i + 1, :] = part + jnp.where(m == 0, jnp.zeros_like(before), before)

    def first_part(m, at):
        total = None
        for p in range(pairs):
            term = dot_nt(d_joined[p, pl.ds(pl.multiple_of(m * 2 * rows + at, TB), TB)], w_pairs[p])
            total = term if total is None else total + term
        return total

    @pl.when(step == last)
    def _():
        for i in range(3):
            for p in range(pairs):
                load_weight(i, p).wait()
        gain = vec_ref[3:4, :]
        steps = rows // TB

        def theirs(i, _):
            m, at = lax.div(i, steps), lax.rem(i, steps) * TB
            df_send[m, pl.ds(pl.multiple_of(at, TB), TB)] = first_part(m, (1 - c) * rows + at).astype(BF16)
            return 0

        def go(until):
            while tail and tail[0][0] < until:
                _, group, stage = tail.pop(0)
                advance(group, stage)

        lax.fori_loop(0, mbs * steps, theirs, 0)
        for m in range(mbs):
            plan.start(("first", m))
        go(28)
        for m in range(mbs):
            plan.arrive(("first", m))

        def mine(i, sums):
            m, at = lax.div(i, steps), lax.rem(i, steps) * TB
            here = pl.ds(pl.multiple_of(at, TB), TB)
            total = first_part(m, c * rows + at) + df_recv[m, here].astype(F32)
            normal, inverse = norm_stats(x_ref[m, here].astype(F32))
            dtok_ref[m, here] = dmid_ref[m, here] + norm_back(total, normal, inverse, gain)
            gains = jnp.sum(total * normal, axis=0, keepdims=True)
            return (sums[0] + gains, sums[1] + jnp.sum(total, axis=0, keepdims=True))

        zero = jnp.zeros((1, width), F32)
        g_gain, g_shift = lax.fori_loop(0, mbs * steps, mine, (zero, zero))
        vec_one[...] = gvec_ref[...]
        vec_one[3:4, :] = g_gain
        vec_one[4:5, :] = g_shift
        for p in range(pairs):
            for i in range(2):
                vec_one[i : i + 1, slab(c * pairs + p, lanes)] = b_sum[p, i : i + 1, :]
        vec_sum[0] = vec_one[...]
        plan.start(("vec", 0))
        for i in range(3):
            go(36 + 2 * i)
            plan.arrive(("vec", i))
            vec_sum[i + 1] = vec_sum[i] + vec_got[i]
            if i < 2:
                plan.start(("vec", i + 1))
        plan.start(*[("vec", "z", j) for j in range(1, owners)])
        go(42)
        plan.arrive(*[("vec", "z", j) for j in range(1, owners)])
        vec_out[...] = (vec_sum[3] + vec_got[3]) + (vec_got[4] + vec_got[5])
        go(1000)
        plan.close()
        for copy in leaving:
            copy().wait()


def backward_block(qkv, lse, x, vecs, gvec, d_middle, d_mixed, first_t, w_qkv, grads, owners, reps, factor, size):
    mbs, rows, width = x.shape
    lanes = 2 * size
    pairs = width // 2 // lanes
    shape = jax.ShapeDtypeStruct
    anywhere = pl.BlockSpec(memory_space=pl.ANY)
    whole = lambda s: pl.BlockSpec(s, lambda i: (0,) * len(s), pipeline_mode=pl.Buffered(1))
    final_step = mbs * pairs - 1

    def block(which):
        def index(i):
            k = jnp.minimum(i, final_step)
            return (lax.rem(k, mbs), which * pairs + lax.div(k, mbs), 0, 0)

        return pl.BlockSpec((1, 1, 2 * rows, lanes), index)

    pieces = [(g.shape[4], g.shape[5] // 2) for g in grads for _ in range(2 * g.shape[0])]
    q_piece = (width // owners // reps // 2, 3 * lanes)
    down, up, mix = (g.shape for g in grads)
    finals = [down[:1] + down[2:], up[2:5] + (up[0] * up[5],), mix[:1] + mix[2:], (reps, 2, q_piece[0], 3 * width)]
    scratch = [s for p in pieces for s in flow_scratch(owners, reps, p, True)]
    scratch += [s for _ in range(2 * pairs) for s in flow_scratch(owners, reps, q_piece, False)]
    remotes = 11 * len(pieces) + 10 * 2 * pairs + mbs * pairs + mbs + 6
    vec = (16, width)
    dtok, vec_sum, *outs = pl.pallas_call(
        partial(backward_kernel, owners, reps, pairs, factor, size, [g.shape for g in grads]),
        grid=(mbs * pairs + 1,),
        in_specs=[block(0), block(1), block(2), whole(lse.shape), whole(x.shape), whole(vec), whole(vec), whole(x.shape)]
        + [anywhere] * (3 + len(grads)),
        out_specs=[whole(x.shape), whole(vec)] + [anywhere] * len(finals),
        out_shape=[shape(x.shape, F32), shape(vec, F32)] + [shape(f, BF16) for f in finals],
        scratch_shapes=[
            pltpu.VMEM((pairs, mbs, 2 * rows, lanes), BF16),
            pltpu.VMEM((pairs, mbs * 2 * rows, 3 * lanes), BF16),
            pltpu.VMEM(first_t.shape, BF16),
            pltpu.VMEM((pairs, width, 3 * lanes), BF16),
            pltpu.VMEM(x.shape, BF16),
            pltpu.VMEM(x.shape, BF16),
            pltpu.VMEM((2 * rows, lanes), F32),
            pltpu.VMEM((2 * rows, lanes), F32),
            pltpu.VMEM((pairs, 8, lanes), F32),
            pltpu.VMEM(vec, F32),
            pltpu.VMEM((6,) + vec, F32),
            pltpu.VMEM((4,) + vec, F32),
        ]
        + scratch
        + [
            pltpu.SemaphoreType.DMA((remotes,)),
            pltpu.SemaphoreType.DMA((remotes,)),
            pltpu.SemaphoreType.DMA((len(pieces) * 3 + 12 * pairs + mbs * pairs + 1 + 3 * pairs,)),
        ],
        compiler_params=pltpu.CompilerParams(
            collective_id=2, has_side_effects=True, vmem_limit_bytes=63 << 20
        ),
        name="backward_block",
    )(qkv, qkv, qkv, lse, x, vecs, gvec, d_middle, d_mixed, first_t, w_qkv, *grads)
    return dtok, vec_sum, outs


def local(
    inputs,
    weight_qkv,
    bias_query,
    bias_value,
    weight_mix,
    bias_mix,
    gain_attn,
    shift_attn,
    gain_mlp,
    shift_mlp,
    weight_up,
    bias_up,
    weight_down,
    bias_down,
    cotangent,
):
    width = weight_qkv.shape[1] // 3
    half = width // 2
    size = width // H
    factor = size ** (-0.5)
    rows = inputs.shape[2]
    owners = lax.axis_size("fsdp")
    reps = lax.axis_size("rep")
    ctx = lax.axis_index("ctx")
    rep = lax.axis_index("rep")
    own = weight_qkv.shape[0]
    b_up_rows = bias_up.shape[0]
    direct = own % (16 * reps) == 0 and owners == 4 and reps == 4

    def swap(x):
        return lax.ppermute(x, "ctx", [(0, 1), (1, 0)])

    def order(mine, other, axis):
        return jnp.where(
            ctx == 0,
            jnp.concatenate([mine, other], axis=axis),
            jnp.concatenate([other, mine], axis=axis),
        )

    def columns(x, axis, which):
        return lax.dynamic_slice_in_dim(x, which * half, half, axis)

    direct = own % (16 * reps) == 0 and owners == 4 and reps == 4
    vectors = [bias_query, bias_value, bias_mix, gain_attn, shift_attn, gain_mlp, shift_mlp, bias_down]
    small = jnp.stack(vectors + [v for v in bias_up.reshape(-1, own)], axis=1).astype(F32)
    tokens = inputs[:, 0].astype(F32)
    if direct:
        mixed, qkv, first_t, w_qkv, w_mix, w_up, w_down, vecs, lse = forward_block(
            inputs[:, 0],
            weight_qkv,
            weight_mix,
            weight_up,
            weight_down,
            jnp.pad(small, ((0, 0), (0, 128 - small.shape[1]))),
            owners,
            reps,
            factor,
            size,
        )
        vecs = vecs[:12]
    else:
        part = own // reps
        mine = lax.dynamic_slice_in_dim(weight_qkv, rep * part, part, 0)
        mine = jnp.concatenate([columns(mine[:, i * width : (i + 1) * width], 1, ctx) for i in range(3)], axis=1)
        w_qkv = lax.all_gather(mine, ("fsdp", "rep"), axis=0, tiled=True)

        def gather(shard):
            piece = shard.shape[0] // (2 * reps)
            mine = lax.dynamic_slice_in_dim(shard, (rep * 2 + ctx) * piece, piece, 0)
            return lax.all_gather(mine, ("fsdp", "rep", "ctx"), axis=0, tiled=True)

        w_mix = gather(weight_mix)
        w_up = gather(weight_up)
        w_down = gather(weight_down)
        vecs = lax.all_gather(small, "fsdp", axis=0, tiled=True).T
    b_query, b_value, g_attn, s_attn = (vecs[i] for i in (0, 1, 3, 4))

    if not direct:
        normal_one, inverse_one = norm_stats(tokens)
        first_own = (normal_one * g_attn + s_attn).astype(BF16)
        first = order(first_own, swap(first_own), 1)
        joined = project(first, w_qkv)
        query = (joined[..., :half] + columns(b_query, 0, ctx)).astype(BF16)
        key = joined[..., half : 2 * half].astype(BF16)
        value = (joined[..., 2 * half :] + columns(b_value, 0, ctx)).astype(BF16)
        mixed_heads, lse = attention_forward(query, key, value, factor, size)

    def my_rows(x):
        return lax.dynamic_slice_in_dim(x, ctx * rows, rows, 1)

    def their_rows(x):
        return lax.dynamic_slice_in_dim(x, (1 - ctx) * rows, rows, 1)

    if not direct:
        mixed = order(my_rows(mixed_heads), swap(their_rows(mixed_heads)), 2)
    flat = (-1, width)
    d_out = cotangent.reshape(flat)
    b_up = vecs[8:].reshape(-1, owners, own).swapaxes(0, 1).reshape(SHARES, -1, FP).swapaxes(0, 1)
    result, d_middle, d_mixed, g_wmix, g_wup, g_wdown, gvec = middle_block(
        inputs.reshape(flat),
        mixed.reshape(flat),
        d_out,
        w_mix,
        w_up,
        w_down,
        vecs,
        b_up.reshape(b_up.shape[0], 1, -1),
        SHARES,
        reps,
    )
    steps = g_wup.shape[0]
    if direct:
        d_tokens, summed, outs = backward_block(
            qkv, lse, inputs[:, 0], vecs, gvec, d_middle.reshape(tokens.shape), d_mixed.reshape(tokens.shape),
            first_t, w_qkv, [g_wdown, g_wup, g_wmix[None]], owners, reps, factor, size,
        )
        o_wdown, o_wup, o_wmix, o_wqkv = (
            o.reshape(-1, n).astype(F32) for o, n in zip(outs, (width, w_up.shape[1], width, 3 * width))
        )
    else:
        d_mixed = d_mixed.reshape(tokens.shape)
        d_middle = d_middle.reshape(tokens.shape)
        d_heads = order(columns(d_mixed, 2, ctx), swap(columns(d_mixed, 2, 1 - ctx)), 1)
        d_query, d_key, d_value = attention_backward(query, key, value, d_heads, lse, factor, size)
        d_joined = jnp.concatenate([d_query, d_key, d_value], axis=-1)
        g_wqkv = outer_sum(first, d_joined)
        d_first = project_back(d_joined, w_qkv)
        d_first = my_rows(d_first) + swap(their_rows(d_first).astype(BF16)).astype(F32)
        normal_one, inverse_one = norm_stats(tokens)
        d_tokens = d_middle + norm_back(d_first, normal_one, inverse_one, g_attn)

        def reduce(grad):
            piece = lax.psum_scatter(
                grad.astype(BF16), ("fsdp", "rep", "ctx"), scatter_dimension=0, tiled=True
            )
            return lax.all_gather(piece, ("rep", "ctx"), axis=0, tiled=True).astype(F32)

        g_wdown = jnp.concatenate([g_wdown[f].reshape(SHARES, FP, width) for f in range(steps)], axis=1)
        o_wdown = reduce(g_wdown.reshape(-1, width))
        g_wup = jnp.stack([g_wup[f].reshape(width, SHARES, FP) for f in range(steps)], axis=2)
        o_wup = reduce(g_wup.reshape(width, -1))
        o_wmix = reduce(g_wmix.reshape(width, width))
        piece = lax.psum_scatter(g_wqkv.astype(BF16), ("fsdp", "rep"), scatter_dimension=0, tiled=True)
        piece = lax.all_gather(piece, "rep", axis=0, tiled=True)
        other = swap(piece)
        low, high = jnp.where(ctx == 0, piece, other), jnp.where(ctx == 0, other, piece)
        o_wqkv = jnp.concatenate(
            [t for i in range(3) for t in (low[:, i * half : (i + 1) * half], high[:, i * half : (i + 1) * half])],
            axis=1,
        ).astype(F32)

        def place(v):
            return lax.dynamic_update_slice_in_dim(jnp.zeros((width,), F32), v, ctx * half, 0)

        first_rows = (
            place(jnp.sum(d_query.astype(F32), axis=(0, 1))),
            place(jnp.sum(d_value.astype(F32), axis=(0, 1))),
            jnp.sum(d_first * normal_one, axis=(0, 1)),
            jnp.sum(d_first, axis=(0, 1)),
        )
        summed = jnp.concatenate([jnp.stack(first_rows[:2]), gvec[2:3], jnp.stack(first_rows[2:]), gvec[5:12]], axis=0)
        summed = lax.psum(summed, ("rep", "fsdp", "ctx"))
    owner = lax.axis_index("fsdp")
    o_bup = lax.dynamic_slice_in_dim(summed[8 : 8 + SHARES].reshape(-1), owner * b_up_rows, b_up_rows, 0)
    summed = lax.dynamic_slice_in_dim(summed[:8], owner * own, own, 1)
    o_bq, o_bv, o_bmix, o_ga, o_sa, o_gm, o_sm, o_bd = (summed[i] for i in range(8))
    return (
        result.reshape(inputs.shape),
        d_tokens[:, None],
        o_wqkv,
        o_bq,
        o_bv,
        o_wmix,
        o_bmix,
        o_ga,
        o_sa,
        o_gm,
        o_sm,
        o_wup,
        o_bup,
        o_wdown,
        o_bd,
    )


def solution(mesh):
    row = P(None, ("rep", "fsdp"), "ctx", None)
    mat = P("fsdp", None)
    vec = P("fsdp")
    params = (mat, vec, vec, mat, vec, vec, vec, vec, vec, mat, vec, mat, vec)
    in_specs = (row,) + params + (row,)
    out_specs = (row, row) + params
    return jax.shard_map(local, mesh=mesh, in_specs=in_specs, out_specs=out_specs, check_vma=False)
```

```python
from functools import partial

import jax
import jax.numpy as jnp
from jax import lax
from jax.experimental import pallas as pl
from jax.experimental.pallas import tpu as pltpu
from jax.sharding import PartitionSpec as P

H = 12
EPS = 1e-05
BF16 = jnp.bfloat16
F32 = jnp.float32
QB = 256
TB = 256
FP = 256
SHARES = 4
GELU_A = 0.7978845608028654
GELU_B = 0.044715
LOG2E = 1.4426950408889634


def norm_stats(values):
    center = values - jnp.mean(values, axis=-1, keepdims=True)
    inverse = lax.rsqrt(jnp.mean(center * center, axis=-1, keepdims=True) + EPS)
    return (center * inverse, inverse)


def norm_back(grad_norm, normal, inverse, gain):
    scaled = grad_norm * gain
    return inverse * (
        scaled
        - jnp.mean(scaled, axis=-1, keepdims=True)
        - normal * jnp.mean(scaled * normal, axis=-1, keepdims=True)
    )


def outer_sum(left, right):
    return jnp.einsum("sri,srj->ij", left, right, preferred_element_type=F32)


def project(left, weight):
    return jnp.einsum("sri,ij->srj", left, weight, preferred_element_type=F32)


def project_back(grad_rows, weight):
    return jnp.einsum("srj,ij->sri", grad_rows, weight, preferred_element_type=F32)


def dot_nt(a, b):
    return lax.dot_general(a, b, (((1,), (1,)), ((), ())), preferred_element_type=F32)


def dot_nn(a, b):
    return lax.dot_general(a, b, (((1,), (0,)), ((), ())), preferred_element_type=F32)


def head_mask(x, head, size):
    lane = lax.broadcasted_iota(jnp.int32, x.shape, 1)
    keep = (lane >= head * size) & (lane < (head + 1) * size)
    return jnp.where(keep, x, jnp.zeros_like(x))


def causal(scores_t, qb):
    n = scores_t.shape[0]
    bottom = scores_t[n - QB :]
    key = lax.broadcasted_iota(jnp.int32, bottom.shape, 0)
    query = lax.broadcasted_iota(jnp.int32, bottom.shape, 1)
    bottom = jnp.where(key <= query, bottom, -1e30)
    return bottom if n == QB else jnp.concatenate([scores_t[: n - QB], bottom], axis=0)


def attention_forward_kernel(factor, size, q_ref, k_ref, v_ref, o_ref, lse_ref):
    refs = [ref.at[0] for ref in (q_ref, k_ref, v_ref, o_ref)]
    attention_forward_block(factor, size, *refs, lse_ref.at[0, 0], lambda done: None)


def attention_forward_block(factor, size, q_ref, k_ref, v_ref, o_ref, lse_ref, between):
    length = q_ref.shape[0]
    base_two = factor * LOG2E
    k = k_ref[...]
    vt = jnp.transpose(v_ref[...])
    for qb in range(length // QB):
        n = (qb + 1) * QB
        rows = pl.ds(qb * QB, QB)
        q = q_ref[rows, :]
        outs = []
        for head in range(2):
            s = causal(dot_nt(k[:n], head_mask(q, head, size)), qb)
            top = jnp.max(s, axis=0, keepdims=True) * base_two
            p = jnp.exp2(s * base_two - top)
            total = jnp.sum(p, axis=0, keepdims=True)
            o = dot_nn(vt[head * size : (head + 1) * size, :n], p.astype(BF16))
            outs.append(o * (1.0 / total))
            lse_ref[head : head + 1, rows] = top + jnp.log2(total)
        o_ref[rows, :] = jnp.transpose(jnp.concatenate(outs, axis=0)).astype(o_ref.dtype)
        between(qb)


def attention_forward(q, k, v, factor, size):
    mbs, length, width = q.shape
    lanes = 2 * size
    pairs = width // lanes
    block = pl.BlockSpec((1, length, lanes), lambda m, p: (m, 0, p))
    area = mbs * pairs * 2 * length * (length + QB) // 2
    return pl.pallas_call(
        partial(attention_forward_kernel, factor, size),
        grid=(mbs, pairs),
        in_specs=[block] * 3,
        out_specs=[block, pl.BlockSpec((1, 1, 8, length), lambda m, p: (m, p, 0, 0))],
        out_shape=[
            jax.ShapeDtypeStruct(q.shape, BF16),
            jax.ShapeDtypeStruct((mbs, pairs, 8, length), F32),
        ],
        compiler_params=pltpu.CompilerParams(vmem_limit_bytes=48 << 20),
        cost_estimate=pl.CostEstimate(
            flops=16 * area * size, bytes_accessed=8 * q.size, transcendentals=area
        ),
        name="attention_forward",
    )(q, k, v)


def attention_backward_kernel(factor, size, q_ref, k_ref, v_ref, do_ref, lse_ref, dq_ref, dk_ref, dv_ref, dk_sum, dv_sum):
    refs = [ref.at[0] for ref in (q_ref, k_ref, v_ref, do_ref)]
    attention_backward_block(
        factor, size, *refs, lse_ref.at[0, 0], dq_ref.at[0], dk_ref.at[0], dv_ref.at[0], dk_sum, dv_sum, lambda done: None
    )


def attention_backward_block(
    factor, size, q_ref, k_ref, v_ref, do_ref, lse_ref, dq_ref, dk_ref, dv_ref, dk_sum, dv_sum, between
):
    length = q_ref.shape[0]
    base_two = factor * LOG2E
    k = k_ref[...]
    v = v_ref[...]
    kt = jnp.transpose(k)
    for i, qb in enumerate(reversed(range(length // QB))):
        n = (qb + 1) * QB
        rows = pl.ds(qb * QB, QB)
        q = q_ref[rows, :]
        do = do_ref[rows, :]
        dqs, dk, dv = [], None, None
        for head in range(2):
            qh = head_mask(q, head, size)
            doh = head_mask(do, head, size)
            s = causal(dot_nt(k[:n], qh), qb)
            p = jnp.exp2(s * base_two - lse_ref[head : head + 1, rows])
            dp = dot_nt(v[:n], doh)
            mean = jnp.sum(dp * p, axis=0, keepdims=True)
            ds = (p * (dp - mean)).astype(BF16)
            dvh = dot_nn(p.astype(BF16), doh)
            dkh = dot_nn(ds, qh)
            dv = dvh if dv is None else dv + dvh
            dk = dkh if dk is None else dk + dkh
            dqs.append(dot_nn(kt[head * size : (head + 1) * size, :n], ds))
        dq_ref[rows, :] = jnp.transpose(jnp.concatenate(dqs, axis=0) * factor).astype(BF16)
        if n == length:
            dk_sum[...] = dk
            dv_sum[...] = dv
        else:
            dk_sum[:n] += dk
            dv_sum[:n] += dv
        between(i)
    dk_ref[...] = (dk_sum[...] * factor).astype(BF16)
    dv_ref[...] = dv_sum[...].astype(BF16)


def attention_backward(q, k, v, do, lse, factor, size):
    mbs, length, width = q.shape
    lanes = 2 * size
    pairs = width // lanes
    block = pl.BlockSpec((1, length, lanes), lambda m, p: (m, 0, p))
    area = mbs * pairs * 2 * length * (length + QB) // 2
    return pl.pallas_call(
        partial(attention_backward_kernel, factor, size),
        grid=(mbs, pairs),
        in_specs=[block] * 4 + [pl.BlockSpec((1, 1, 8, length), lambda m, p: (m, p, 0, 0))],
        out_specs=[block] * 3,
        out_shape=[jax.ShapeDtypeStruct(q.shape, BF16)] * 3,
        scratch_shapes=[pltpu.VMEM((length, lanes), F32)] * 2,
        compiler_params=pltpu.CompilerParams(vmem_limit_bytes=48 << 20),
        cost_estimate=pl.CostEstimate(
            flops=40 * area * size, bytes_accessed=14 * q.size, transcendentals=area
        ),
        name="attention_backward",
    )(q, k, v, do, lse)


MESH = pl.DeviceIdType.MESH


def position():
    return lax.axis_index("fsdp"), lax.axis_index("rep"), lax.axis_index("ctx")


def greet(owners, reps):
    z, r, c = position()
    barrier = pltpu.get_barrier_semaphore()
    peers = [{"fsdp": lax.rem(z + j, owners)} for j in range(1, owners)]
    peers += [{"rep": r ^ j} for j in range(1, reps)]
    peers += [{"ctx": 1 - c}]
    for peer in peers:
        pl.semaphore_signal(barrier, inc=1, device_id=peer, device_id_type=MESH)
    pl.semaphore_wait(barrier, len(peers))


def slab(i, half):
    return pl.ds(pl.multiple_of(i * half, 128), half)


def add_blocks(out, parts, dtype):
    lead = out.shape[:-2]
    count = 1
    for n in lead:
        count *= n

    def body(i, _):
        at = []
        for n in reversed(lead):
            at.append(lax.rem(i, n))
            i = lax.div(i, n)
        at = tuple(reversed(at))
        terms = [p[at].astype(F32) for p in parts]
        while len(terms) > 1:
            terms = [terms[0] + terms[1]] + terms[2:]
        out[at] = terms[0].astype(dtype)
        return 0

    lax.fori_loop(0, count, body, 0)


class Plan:
    def __init__(self, send, recv):
        self.send, self.recv = send, recv
        self.made, self.left = {}, set()

    def add(self, name, src, dst, peer):
        self.made[name] = (len(self.made), src, dst, peer)

    def copy(self, name):
        slot, src, dst, peer = self.made[name]
        return pltpu.make_async_remote_copy(
            src_ref=src(),
            dst_ref=dst(),
            send_sem=self.send.at[slot],
            recv_sem=self.recv.at[slot],
            device_id=peer,
            device_id_type=MESH,
        )

    def start(self, *names):
        for name in names:
            self.copy(name).start()

    def arrive(self, *names):
        for name in names:
            self.copy(name).wait_recv()

    def leave(self, *names):
        for name in names:
            self.copy(name).wait_send()
            self.left.add(name)

    def close(self):
        for name in self.made:
            if name not in self.left:
                self.copy(name).wait_send()


def spread_plan(plan, tag, owners, reps, z, r, c, src, dst, halves, core=None):
    for j in range(1, owners):
        origin = lax.rem(z - j + owners, owners)
        if src is not None:
            plan.add((tag, "z", j), src, lambda: dst(z, r), {"fsdp": lax.rem(z + j, owners)})
        here = partial(dst, origin, r)
        plan.add((tag, "x", j), here, here, {"rep": r ^ 1})
        plan.add((tag, "y", j), here, here, {"rep": r ^ 2})
        by_y = lambda origin=origin: halves(dst(origin, r ^ 2))[0]
        by_x = lambda origin=origin: halves(dst(origin, r ^ 1))[1]
        plan.add((tag, "xx", j), by_y, by_y, {"rep": r ^ 1})
        plan.add((tag, "yy", j), by_x, by_x, {"rep": r ^ 2})
        if core is not None:
            side = partial(core, origin)
            plan.add((tag, "c", j), side, side, {"ctx": 1 - c})


def spread_step(plan, tag, owners, stage):
    for j in range(1, owners):
        if stage == 0:
            plan.start((tag, "z", j))
        elif stage == 1:
            if (tag, "z", j) in plan.made:
                plan.arrive((tag, "z", j))
            plan.start((tag, "x", j), (tag, "y", j))
        elif stage == 2:
            plan.arrive((tag, "y", j))
            plan.start((tag, "xx", j))
            plan.arrive((tag, "x", j))
            plan.start((tag, "yy", j))
        elif stage == 3:
            plan.arrive((tag, "xx", j), (tag, "yy", j))
            if (tag, "c", j) in plan.made:
                plan.start((tag, "c", j))
        else:
            plan.arrive((tag, "c", j))


def up_side(ref, c):
    half = ref.shape[-1] // 2
    return ref.at[:, pl.ds(pl.multiple_of(c * half, 128), half)]


def up_piece(ref, c, r):
    return ref.at[:, pl.ds(pl.multiple_of((c * 4 + r) * 128, 128), 128)]


def down_side(ref, c):
    half = ref.shape[0] // 2
    return ref.at[pl.ds(pl.multiple_of(c * half, 32), half)]


def down_piece(ref, c, r):
    piece = ref.shape[0] // 8
    return ref.at[pl.ds(pl.multiple_of((c * 4 + r) * piece, 32), piece)]


def row_halves(ref):
    middle = ref.shape[0] // 2
    return ref.at[pl.ds(0, middle)], ref.at[pl.ds(middle, middle)]


def column_halves(ref):
    middle = ref.shape[-1] // 2
    return ref.at[:, pl.ds(0, middle)], ref.at[:, pl.ds(middle, middle)]


def forward_timetable(weights, gaps=(0, 5, 8, 11), every=7, first=-11):
    return sorted((first + every * t + gap, t, 1 + i) for t in range(weights) for i, gap in enumerate(gaps))


def forward_kernel(owners, reps, pairs, factor, size,
                   x_ref, qkv_ref, mix_ref, up_ref, down_ref, small_ref,
                   mixed, qkv_out, first_t_out, w_qkv_out, w_mix, w_up, w_down, vec_ref, lse_ref,
                   first, first_t, w_qkv, qkv, heads, small, own_mix, own_up, own_down, send, recv, kept):
    step = pl.program_id(0)
    last = pl.num_programs(0) - 1
    z, r, c = position()
    mbs, rows, width = x_ref.shape
    half = width // 2
    lanes = 2 * size
    plan = Plan(send, recv)
    own_rows = pl.ds(pl.multiple_of(c * rows, rows), rows)
    their_rows = pl.ds(pl.multiple_of((1 - c) * rows, rows), rows)

    for j in range(1, owners):
        plan.add(("small", j), lambda: small_ref, lambda: small.at[z], {"fsdp": lax.rem(z + j, owners)})
    for m in range(mbs):
        plan.add(("first", m), lambda m=m: first.at[m, own_rows], lambda m=m: first.at[m, own_rows], {"ctx": 1 - c})
    for j in range(1, owners):
        for i in range(3):
            plan.add(
                ("qkv", "z", i, j),
                lambda i=i: qkv_ref.at[r, :, slab(2 * i + c, half)],
                lambda i=i: w_qkv.at[z, r, :, slab(i, half)],
                {"fsdp": lax.rem(z + j, owners)},
            )
    cut = w_qkv.shape[3] // 256 * 128
    spread_plan(
        plan, "qkv", owners, reps, z, r, c, None, lambda o, p: w_qkv.at[o, p],
        lambda ref: (ref.at[:, pl.ds(0, cut)], ref.at[:, pl.ds(cut, 3 * half - cut)]),
    )
    steps = w_up.shape[0]
    spread_plan(
        plan, ("mix", 0), owners, reps, z, r, c,
        lambda: own_mix.at[c, r], lambda o, p: w_mix.at[o, c, p], column_halves, lambda o: w_mix.at[o, c],
    )
    for tag, own, whole, piece, side in (("up", own_up, w_up, up_piece, up_side), ("down", own_down, w_down, down_piece, down_side)):
        for f in range(steps):
            dst = lambda o, p, whole=whole, piece=piece, f=f: piece(whole.at[f, o], c, p)
            src = lambda own=own, piece=piece, f=f: piece(own.at[f], c, r)
            if f == 0:
                core = lambda o, whole=whole, side=side, f=f: side(whole.at[f, o], c)
                spread_plan(plan, (tag, f), owners, reps, z, r, c, src, dst, row_halves, core)
            else:
                for j in range(1, owners):
                    to = lax.rem(z + j, owners)
                    plan.add(((tag, f), "z", j), src, lambda dst=dst: dst(z, r), {"fsdp": to})
    quarters = 2 * rows // QB
    table = forward_timetable(3)
    order = [("mix", 0)] + [(tag, f) for f in range(steps) for tag in ("up", "down")]

    up_step = own_up.shape[-1] // owners
    pairs_of = [(small_ref, small.at[z])]
    pairs_of += [(qkv_ref.at[:, :, slab(2 * i + c, half)], w_qkv.at[z, :, :, slab(i, half)]) for i in range(3)]
    pairs_of += [(mix_ref, own_mix)]
    early = len(pairs_of)
    for f in range(steps):
        for k in range(owners):
            cols = pl.ds((k * (up_ref.shape[-1] // owners)) + f * up_step, up_step)
            pairs_of += [(up_ref.at[:, cols], own_up.at[f, :, pl.ds(k * up_step, up_step)])]
        pairs_of += [(down_ref.at[pl.ds(f * own_down.shape[1], own_down.shape[1])], own_down.at[f])]
    loads = len(pairs_of)
    pairs_of += [(own_mix, w_mix.at[z])]
    for f in range(steps):
        pairs_of += [(own_up.at[f], w_up.at[f, z]), (own_down.at[f], w_down.at[f, z])]
    stores = len(pairs_of)
    pairs_of += [(w_qkv, w_qkv_out), (first_t, first_t_out), (qkv, qkv_out)]
    ends = len(pairs_of)

    def keep(i):
        return pltpu.make_async_copy(*pairs_of[i], kept.at[i])

    def mixed_place(step):
        m, p = lax.div(step, pairs), lax.rem(step, pairs)
        return mixed.at[m, :, slab(c * pairs + p, lanes)]

    def mixed_sends(k, slot):
        return pltpu.make_async_remote_copy(
            src_ref=heads.at[k, their_rows],
            dst_ref=mixed_place(k),
            send_sem=send.at[slot],
            recv_sem=recv.at[slot],
            device_id={"ctx": 1 - c},
            device_id_type=MESH,
        )

    base = len(plan.made)

    @pl.when(step == 0)
    def _():
        for i in range(loads):
            keep(i).start()
        greet(owners, reps)
        plan.start(*[("small", j) for j in range(1, owners)])
        for j in range(1, owners):
            plan.start(*[("qkv", "z", i, j) for i in range(3)])
        keep(0).wait()
        plan.arrive(*[("small", j) for j in range(1, owners)])
        vec_ref[...] = jnp.concatenate([small[k] for k in range(owners)], axis=1)
        gain, shift = vec_ref[3:4, :], vec_ref[4:5, :]
        for m in range(mbs):
            for at in range(0, rows, TB):
                normal, _ = norm_stats(x_ref[m, at : at + TB].astype(F32))
                place = pl.ds(pl.multiple_of(c * rows + at, TB), TB)
                first[m, place] = (normal * gain + shift).astype(BF16)
            plan.start(("first", m))
        for j in range(1, owners):
            plan.arrive(*[("qkv", "z", i, j) for i in range(3)])
            plan.start(("qkv", "x", j), ("qkv", "y", j))
        for i in range(4, loads):
            keep(i).wait()
        for tag in order:
            spread_step(plan, tag, owners, 0)
        for i in range(loads, stores):
            keep(i).start()
        plan.arrive(*[("first", m) for m in range(mbs)])
        for m in range(mbs):
            for at in range(0, 2 * rows, TB):
                first_t[:, m * 2 * rows + at : m * 2 * rows + at + TB] = jnp.transpose(first[m, at : at + TB])
        keep(stores + 1).start()
        spread_step(plan, "qkv", owners, 2)
        for when, t, stage in table:
            if when < 0:
                spread_step(plan, order[t], owners, stage)
        spread_step(plan, "qkv", owners, 3)
        for i in range(1, 4):
            keep(i).wait()
        keep(stores).start()
        weight = w_qkv[...].reshape(-1, w_qkv.shape[-1])
        b_query = vec_ref[0:1, slab(c, half)]
        b_value = vec_ref[1:2, slab(c, half)]
        bias = jnp.concatenate([b_query, jnp.zeros_like(b_query), b_value], axis=1)

        def project_rows(i, _):
            m, at = lax.div(i, 2 * rows // TB), lax.rem(i, 2 * rows // TB)
            place = pl.ds(pl.multiple_of(at * TB, TB), TB)
            joined = (dot_nn(first[m, place], weight) + bias).astype(BF16)
            for s in range(3 * pairs):
                qkv[m, s, place] = joined[:, s * lanes : (s + 1) * lanes]
            return 0

        lax.fori_loop(0, mbs * 2 * rows // TB, project_rows, 0)
        keep(stores + 2).start()

    def between(k, done):
        for i in range(mbs * pairs):
            some = [entry for entry in table if entry[0] == i * quarters + done]
            if some:

                @pl.when(k == i)
                def _():
                    for _, t, stage in some:
                        spread_step(plan, order[t], owners, stage)

    @pl.when(step > 0)
    def _():
        k = step - 1
        m, p = lax.div(k, pairs), lax.rem(k, pairs)
        attention_forward_block(
            factor, size, qkv.at[m, p], qkv.at[m, pairs + p], qkv.at[m, 2 * pairs + p], heads.at[k], lse_ref.at[m, p],
            partial(between, k),
        )
        mixed_sends(k, base + k).start()
        pltpu.make_async_copy(heads.at[k, own_rows], mixed_place(k), kept.at[ends + k]).start()

    @pl.when(step == last)
    def _():
        for when, t, stage in table:
            if when >= quarters * mbs * pairs:
                spread_step(plan, order[t], owners, stage)
        for k in range(mbs * pairs):
            mixed_sends(k, base + k).wait()
            pltpu.make_async_copy(heads.at[k, own_rows], mixed_place(k), kept.at[ends + k]).wait()
        for tag in order[3:]:
            for j in range(1, owners):
                plan.arrive((tag, "z", j))
        plan.close()
        for i in range(loads, ends):
            keep(i).wait()


def forward_block(x, weight_qkv, weight_mix, weight_up, weight_down, small, owners, reps, factor, size):
    own, wide = weight_qkv.shape
    mbs, rows, width = x.shape
    lanes = 2 * size
    pairs = width // 2 // lanes

    def cut(shard):
        return shard.reshape(2, reps, shard.shape[0] // (2 * reps), shard.shape[1])

    steps = weight_down.shape[0] // FP
    shards = (weight_qkv.reshape(reps, own // reps, wide), cut(weight_mix), weight_up, weight_down, small)
    own_up = (steps, own, owners * FP)
    own_down = (steps, FP, width)
    shape = jax.ShapeDtypeStruct
    w_shape = (owners, reps, own // reps, wide // 2)
    qkv_shape = (mbs, 3 * pairs, 2 * rows, lanes)
    anywhere = pl.BlockSpec(memory_space=pl.ANY)
    whole = lambda s: pl.BlockSpec(s, lambda i: (0,) * len(s), pipeline_mode=pl.Buffered(1))
    remotes = 3 + mbs + 9 + 12 + 3 * 18 + 6 * (steps - 1) + mbs * pairs
    copies = 5 + steps * (owners + 1) + 1 + 2 * steps + 3 + mbs * pairs
    area = mbs * pairs * 2 * rows * (2 * rows + QB)
    mixed, qkv, first_t, w_qkv, w_mix, w_up, w_down, vecs, lse = pl.pallas_call(
        partial(forward_kernel, owners, reps, pairs, factor, size),
        grid=(1 + mbs * pairs,),
        in_specs=[whole(x.shape)] + [anywhere] * 5,
        out_specs=[anywhere] * 7 + [whole((16, width)), whole((mbs, pairs, 8, 2 * rows))],
        out_shape=[
            shape((mbs, rows, width), BF16),
            shape(qkv_shape, BF16),
            shape((width, mbs * 2 * rows), BF16),
            shape(w_shape, BF16),
            shape((owners,) + shards[1].shape, BF16),
            shape(own_up[:1] + (owners,) + own_up[1:], BF16),
            shape(own_down[:1] + (owners,) + own_down[1:], BF16),
            shape((16, width), F32),
            shape((mbs, pairs, 8, 2 * rows), F32),
        ],
        scratch_shapes=[
            pltpu.VMEM((mbs, 2 * rows, width), BF16),
            pltpu.VMEM((width, mbs * 2 * rows), BF16),
            pltpu.VMEM(w_shape, BF16),
            pltpu.VMEM(qkv_shape, BF16),
            pltpu.VMEM((mbs * pairs, 2 * rows, lanes), BF16),
            pltpu.VMEM((owners,) + small.shape, F32),
            pltpu.VMEM(shards[1].shape, BF16),
            pltpu.VMEM(own_up, BF16),
            pltpu.VMEM(own_down, BF16),
            pltpu.SemaphoreType.DMA((remotes,)),
            pltpu.SemaphoreType.DMA((remotes,)),
            pltpu.SemaphoreType.DMA((copies,)),
        ],
        compiler_params=pltpu.CompilerParams(
            collective_id=1, has_side_effects=True, vmem_limit_bytes=56 << 20
        ),
        name="forward_block",
    )(x, *shards)
    return (
        mixed,
        qkv,
        first_t,
        w_qkv.reshape(owners * own, -1),
        w_mix.reshape(owners * own, -1),
        w_up,
        w_down,
        vecs,
        lse,
    )


class Flow:
    def __init__(self, plan, name, place, owners, bits, mine, theirs, hops, outs, load=None, core=None):
        z, r, c = place
        first, second = bits
        self.plan, self.name, self.place, self.owners = plan, name, place, owners
        self.mine, self.theirs, self.second = mine, theirs, r ^ second
        self.hop_one, self.hop_two, self.hop_z, self.final = hops
        self.outs = outs
        self.load = load
        peer = {"rep": r ^ first}
        if core is not None:
            plan.add((name, "core"), core, lambda: theirs, {"ctx": 1 - c})
        self.split = core is not None
        plan.add((name, "me"), lambda: mine.at[:, r ^ first], lambda: self.hop_one.at[0], peer)
        plan.add((name, "on"), lambda: mine.at[:, r ^ first ^ second], lambda: self.hop_one.at[1], peer)
        plan.add((name, "two"), lambda: mine.at[:, r ^ second], lambda: self.hop_two, {"rep": r ^ second})
        for j in range(1, owners):
            to = lax.rem(z + j, owners)
            plan.add((name, "z", j), lambda to=to: mine.at[to, r], lambda j=j: self.hop_z.at[j - 1], {"fsdp": to})
        here = lambda: self.final.at[c, r]
        plan.add((name, "x"), here, here, {"rep": r ^ first})
        plan.add((name, "y"), here, here, {"rep": r ^ second})
        far = lambda: self.final.at[c, r ^ second]
        plan.add((name, "xy"), far, far, {"rep": r ^ first})
        side = lambda: self.final.at[c]
        plan.add((name, "back"), side, side, {"ctx": 1 - c})

    def step(self, stage):
        z, r, c = self.place
        plan, name, mine = self.plan, self.name, self.mine
        owners = self.owners
        if stage == 0:
            if self.split:
                plan.start((name, "core"))
            if self.load is not None:
                self.load().start()
        elif stage == 1:
            if self.load is not None:
                self.load().wait()
            if self.split:
                plan.arrive((name, "core"))
                add_blocks(mine, [mine, self.theirs], BF16)
            plan.start((name, "on"), (name, "me"))
        elif stage == 2:
            plan.arrive((name, "on"))
            part = mine.at[:, self.second]
            add_blocks(part, [part, self.hop_one.at[1]], BF16)
            plan.start((name, "two"))
        elif stage == 3:
            plan.arrive((name, "me"), (name, "two"))
            part = mine.at[:, r]
            add_blocks(part, [part, self.hop_one.at[0], self.hop_two], BF16)
            plan.start(*[(name, "z", j) for j in range(1, owners)])
        elif stage == 4:
            plan.arrive(*[(name, "z", j) for j in range(1, owners)])
            terms = [mine[z, r].astype(F32)] + [self.hop_z[j].astype(F32) for j in range(owners - 1)]
            while len(terms) > 1:
                terms = [a + b for a, b in zip(terms[::2], terms[1::2])]
            self.final[c, r] = terms[0].astype(BF16)
            plan.start((name, "x"), (name, "y"))
        elif stage == 5:
            plan.arrive((name, "y"))
            plan.start((name, "xy"))
        elif stage == 6:
            plan.arrive((name, "x"), (name, "xy"))
            plan.start((name, "back"))
        else:
            plan.arrive((name, "back"))
            for copy in self.outs(self.final):
                copy.start()


def flow_scratch(owners, reps, piece, split):
    vmem = lambda *lead: pltpu.VMEM(lead + piece, BF16)
    mine = [vmem(owners, reps)] * (2 if split else 1)
    return mine + [vmem(2, owners), vmem(owners), vmem(owners - 1), vmem(2, reps)]


def timetable(groups, products, gaps=(0, 4, 7, 11, 13, 15, 17), every=5):
    table = [(2 + every * g + gap, g, 1 + i) for g in range(groups) for i, gap in enumerate(gaps)]
    table += [(8 * (p + 1) + 1 + gap, groups + p, 1 + i) for p in range(products) for i, gap in enumerate(gaps) if i]
    return sorted(table)


def gelu_parts(b):
    square = b * b
    inner = GELU_A * b * (1.0 + GELU_B * square)
    t = jnp.tanh(inner)
    rise = 0.5 * (1.0 + t)
    slope = rise + 0.5 * b * (1.0 - t * t) * (GELU_A * (1.0 + 3.0 * GELU_B * square))
    return b * rise, slope


GATHERS = [
    (1, ("up", 1), 2), (1, ("down", 1), 2), (2, ("up", 1), 3), (2, ("down", 1), 3), (2, ("up", 2), 1), (2, ("down", 2), 1),
    (4, ("up", 1), 4), (4, ("down", 1), 4), (5, ("up", 2), 2), (5, ("down", 2), 2), (6, ("up", 2), 3), (6, ("down", 2), 3),
    (8, ("up", 2), 4), (8, ("down", 2), 4),
]
SUMS = [
    (3, 0, 0), (3, 1, 0), (5, 0, 1), (6, 1, 1), (8, 0, 2), (9, 1, 2), (9, 0, 3), (10, 1, 3), (10, 0, 4), (11, 0, 5),
    (11, 1, 4), (12, 1, 5), (12, 0, 6), (13, 1, 6), (14, 0, 7), (14, 1, 7),
]


def middle_kernel(owners, reps, direct, *refs):
    x_ref, mixed_ref, d_ref, wmix_ref, wup_any, wdown_any, vec_ref, bup_ref = refs[:8]
    result_ref, dmid_ref, dmixed_ref, gmix_ref, gup_ref, gdown_ref, gvec_ref = refs[8:15]
    refs = refs[15:]
    if direct:
        down_out, up_out, refs = refs[0], refs[1], refs[2:]
    middle, second, second_t, mixed_t, out_sum, ds_sum, active_t, d_before, w_up, w_down = refs[:10]
    refs = refs[10:]
    step = pl.program_id(0)
    rows = x_ref.shape[0]
    steps = w_up.shape[0]
    last = steps - 1
    chunks = [slice(i, i + TB) for i in range(0, rows, TB)]
    b_mix, gain, shift, b_down = (vec_ref[i : i + 1, :] for i in (2, 5, 6, 7))
    slots = 4

    if direct:
        flow_refs, (send, recv, kept) = refs[:-3], refs[-3:]
        place = z, r, c = position()
        plan = Plan(send, recv)
        used = 0

        def local(src, dst):
            nonlocal used
            used += 1
            slot = kept.at[used - 1]
            return lambda: pltpu.make_async_copy(src(), dst(), slot)

        own_rows, part = w_up.shape[1] // owners, w_down.shape[1] // owners
        up_of = lambda ref, f, o: ref.at[f, pl.ds(pl.multiple_of(o * own_rows, 32), own_rows)]
        down_of = lambda ref, f, o: ref.at[f, pl.ds(pl.multiple_of(o * part, 32), part)]
        loads, pieces = [], {}
        for tag, source, whole, of, piece, side in (
            ("up", wup_any, w_up, up_of, up_piece, up_side),
            ("down", wdown_any, w_down, down_of, down_piece, down_side),
        ):
            for o in range(owners):
                loads.append(local(lambda o=o, s=source: s.at[0, o], lambda o=o, w=whole, of=of: of(w, 0, o)))
            for f in range(1, steps):
                loads.append(
                    local(lambda f=f, s=source: s.at[f, z], lambda f=f, w=whole, of=of: of(w, f, z))
                )
                pieces[tag, f] = [
                    local(
                        lambda f=f, j=j, s=source, p=piece: p(s.at[f, lax.rem(z + j, owners)], c, r),
                        lambda f=f, j=j, w=whole, of=of, p=piece: p(of(w, f, lax.rem(z + j, owners)), c, r),
                    )
                    for j in range(1, owners)
                ]
                spread_plan(
                    plan, (tag, f), owners, reps, z, r, c, None,
                    lambda o, p, f=f, w=whole, of=of, piece=piece: piece(of(w, f, o), c, p),
                    row_halves,
                    lambda o, f=f, w=whole, of=of, side=side: side(of(w, f, o), c),
                )
        flows, leaving, at = [], [], 0
        for i, (ref, out) in enumerate(((gdown_ref, down_out), (gup_ref, up_out))):
            wide = ref.shape[-1] // 2
            up_step = ref.shape[-1] // owners
            for s in range(2):
                mine, theirs, *hops = flow_refs[at : at + 6]
                at += 6
                cols, final = pl.ds(s * wide, wide), hops[-1]
                if i == 1:
                    places = []
                    for k in range(wide // up_step):
                        to = pl.ds((s * wide // up_step + k) * steps * up_step, up_step)
                        places.append((
                            lambda final=final, k=k: final.at[:, :, :, pl.ds(k * up_step, up_step)],
                            lambda out=out, to=to: out.at[:, :, :, to],
                        ))
                else:
                    places = [(lambda final=final: final, lambda out=out, cols=cols: out.at[0, :, :, :, cols])]
                copies = [local(src, dst) for src, dst in places]
                leaving.extend(copies)
                flows.append(
                    Flow(
                        plan, (i, s), place, owners, (1, 2) if s == 0 else (2, 1), mine, theirs, hops,
                        lambda final, copies=copies: [f() for f in copies],
                        local(lambda ref=ref, cols=cols: ref.at[0, :, c, :, :, cols], lambda mine=mine: mine),
                        lambda ref=ref, cols=cols: ref.at[0, :, 1 - c, :, :, cols],
                    )
                )
    else:
        kept = refs[0]
        loads = [
            lambda: pltpu.make_async_copy(wup_any, w_up, kept.at[0]),
            lambda: pltpu.make_async_copy(wdown_any, w_down, kept.at[1]),
        ]

    def between(slot):
        if not direct:
            return
        for k in range(steps):
            some = [lambda t=t, n=n: spread_step(plan, t, owners, n) for when, t, n in GATHERS if when == k * slots + slot]
            some += [lambda g=g, n=n: [flow.step(n) for flow in flows[2 * g : 2 * g + 2]] for when, g, n in SUMS if when == k * slots + slot]
            if some:

                @pl.when(step == k)
                def _():
                    for act in some:
                        act()

    @pl.when(step == 0)
    def _():
        for copy in loads:
            copy().start()
        if direct:
            for some in pieces.values():
                for copy in some:
                    copy().start()
            greet(owners, reps)
            for f in range(1, steps):
                for tag in ("up", "down"):
                    for copy in pieces[tag, f]:
                        copy().wait()
                    if f == 1:
                        spread_step(plan, (tag, f), owners, 1)
        gvec_ref[...] = jnp.zeros_like(gvec_ref)
        for at in chunks:
            mixed = mixed_ref[at]
            mixed_t[:, at] = jnp.transpose(mixed)
            mid = x_ref[at].astype(F32) + (dot_nn(mixed, wmix_ref[...]) + b_mix)
            middle[at] = mid
            out_sum[at] = mid + b_down
            ds_sum[at] = jnp.zeros_like(mid)
            normal, _ = norm_stats(mid)
            low = (normal * gain + shift).astype(BF16)
            second[at] = low
            second_t[:, at] = jnp.transpose(low)
        for copy in loads:
            copy().wait()

    between(0)
    d_bup = None
    for i, at in enumerate(chunks):
        act, slope = gelu_parts(dot_nn(second[at], w_up[step]) + bup_ref[0])
        act = act.astype(BF16)
        active_t[:, at] = jnp.transpose(act)
        db = (dot_nt(d_ref[at], w_down[step]) * slope).astype(BF16)
        d_before[at] = db
        part_sum = jnp.sum(db.astype(F32), axis=0, keepdims=True)
        d_bup = part_sum if d_bup is None else d_bup + part_sum
        out = dot_nn(act, w_down[step])
        ds = dot_nt(db, w_up[step])
        out_sum[at] += out
        ds_sum[at] += ds
        if i % 2:
            between((i + 1) // 2)

    width = d_bup.shape[1] // owners
    for k in range(owners):
        gvec_ref[8 + k : 9 + k, slab(step, width)] = d_bup[:, k * width : (k + 1) * width]
    if direct:

        @pl.when(step == 1)
        def _():
            plan.leave(*[(flow.name, "core") for flow in flows])

    gdown_ref[0] = dot_nn(active_t[...], d_ref[...]).reshape(gdown_ref.shape[1:]).astype(BF16)
    gup_ref[0] = dot_nn(second_t[...], d_before[...]).reshape(gup_ref.shape[1:]).astype(BF16)
    between(slots - 1)

    @pl.when(step == last)
    def _():
        sums = [None] * 4
        for at in chunks:
            mid = middle[at]
            result_ref[at] = out_sum[at].astype(BF16)
            normal, inverse = norm_stats(mid)
            ds = ds_sum[at]
            grad_out = d_ref[at].astype(F32)
            d_mid = grad_out + norm_back(ds, normal, inverse, gain)
            dmid_ref[at] = d_mid
            branch = d_mid.astype(BF16)
            second[at] = branch
            dmixed_ref[at] = dot_nt(branch, wmix_ref[...]).astype(BF16)
            parts = (branch.astype(F32), ds * normal, ds, grad_out)
            for i, part in enumerate(parts):
                part = jnp.sum(part, axis=0, keepdims=True)
                sums[i] = part if sums[i] is None else sums[i] + part
        for i, k in enumerate((2, 5, 6, 7)):
            gvec_ref[k : k + 1, :] = sums[i]
        gmix_ref[...] = dot_nn(mixed_t[...], second[...]).reshape(gmix_ref.shape).astype(BF16)
        if direct:
            for when, g, n in SUMS:
                if when >= steps * slots:
                    for flow in flows[2 * g : 2 * g + 2]:
                        flow.step(n)
            plan.close()
            for copy in leaving:
                copy().wait()


def middle_block(x, mixed, d_out, w_mix, w_up, w_down, vecs, b_up, owners, reps, direct):
    rows, width = x.shape
    steps = w_up.shape[0]
    ff = steps * owners * FP
    whole = lambda shape: pl.BlockSpec(shape, lambda f: (0,) * len(shape), pipeline_mode=pl.Buffered(1))
    anywhere = pl.BlockSpec(memory_space=pl.ANY)
    out = jax.ShapeDtypeStruct
    vmem = pltpu.VMEM
    side = (owners, 2, reps)
    g_mix = side + (width // owners // 2 // reps, width)
    given = steps - 1 if direct else steps
    g_up = (given,) + g_mix[:-1] + (owners * FP,)
    g_down = (given,) + side + (FP // 2 // reps, width)
    skip = steps - given
    per_step = lambda s: pl.BlockSpec((1,) + s[1:], lambda f: (jnp.maximum(f - skip, 0),) + (0,) * (len(s) - 1))
    scratch = [
        vmem((rows, width), F32),
        vmem((rows, width), BF16),
        vmem((width, rows), BF16),
        vmem((width, rows), BF16),
        vmem((rows, width), F32),
        vmem((rows, width), F32),
        vmem((owners * FP, rows), BF16),
        vmem((rows, owners * FP), BF16),
        vmem((steps, width, owners * FP), BF16),
        vmem((steps, owners * FP, width), BF16),
    ]
    finished = []
    if direct:
        finished = [out((steps,) + g_down[2:], BF16), out(g_up[2:5] + (steps * g_up[5],), BF16)]
        for g in (g_down, g_up):
            for _ in range(2):
                scratch += flow_scratch(owners, reps, (g[4], g[5] // 2), True)
        remotes = (steps - 1) * 2 * 15 + 4 * 11
        scratch += [pltpu.SemaphoreType.DMA((remotes,))] * 2 + [pltpu.SemaphoreType.DMA((2 * owners + 2 * (steps - 1) * owners + 10,))]
        params = dict(collective_id=3, has_side_effects=True)
    else:
        scratch += [pltpu.SemaphoreType.DMA((2,))]
        params = {}
    return pl.pallas_call(
        partial(middle_kernel, owners, reps, direct),
        grid=(steps,),
        in_specs=[whole((rows, width))] * 3
        + [whole((width, width)), anywhere, anywhere, whole(vecs.shape), pl.BlockSpec((1, 1, owners * FP), lambda f: (f, 0, 0))],
        out_specs=[
            whole((rows, width)),
            whole((rows, width)),
            whole((rows, width)),
            whole(g_mix),
            per_step(g_up),
            per_step(g_down),
            whole((16, width)),
        ]
        + [anywhere] * len(finished),
        out_shape=[
            out((rows, width), BF16),
            out((rows, width), F32),
            out((rows, width), BF16),
            out(g_mix, BF16),
            out(g_up, BF16),
            out(g_down, BF16),
            out((16, width), F32),
        ]
        + finished,
        scratch_shapes=scratch,
        compiler_params=pltpu.CompilerParams(vmem_limit_bytes=62 << 20, **params),
        cost_estimate=pl.CostEstimate(
            flops=12 * rows * width * ff + 6 * rows * width * width,
            bytes_accessed=8 * width * ff + 16 * rows * width,
            transcendentals=rows * ff,
        ),
        name="middle_block",
    )(x, mixed, d_out, w_mix, w_up, w_down, vecs, b_up)


def backward_kernel(
    owners, reps, pairs, factor, size, shapes, done,
    q_ref, k_ref, v_ref, lse_ref, x_ref, vec_ref, gvec_ref, dmid_ref, dmixed_ref, first_t_ref, w_ref, *refs
):
    n_in = len(shapes)
    sources, refs = refs[:n_in], refs[n_in + 2 :]
    dtok_ref, vec_out, refs = refs[0], refs[1], refs[2:]
    outs, refs = refs[: n_in + 1], refs[n_in + 1 :]
    d_heads, d_joined, first_t, w_pairs, df_send, df_recv, dk_sum, dv_sum, b_sum, vec_one, vec_got, vec_sum, refs = (
        refs[:12] + (refs[12:],)
    )
    flow_refs, (send, recv, kept) = refs[:-3], refs[-3:]
    step = pl.program_id(0)
    last = pl.num_programs(0) - 1
    place = z, r, c = position()
    mbs, rows, width = x_ref.shape
    half = width // 2
    lanes = 2 * size
    plan = Plan(send, recv)
    own_rows = pl.ds(pl.multiple_of(c * rows, rows), rows)

    locals_used = 0

    def local(src, dst):
        nonlocal locals_used
        locals_used += 1
        slot = kept.at[locals_used - 1]
        return lambda: pltpu.make_async_copy(src(), dst(), slot)

    up_step = shapes[1][-1] // owners
    flows, leaving, at = [], [], 0

    def add_flow(name, bits, mine, theirs, hops, places, load=None, core=None):
        final = hops[-1]
        copies = [local(partial(part, final), dst) for part, dst in places]
        leaving.extend(copies)
        flows.append(
            Flow(plan, name, place, owners, bits, mine, theirs, hops, lambda final: [f() for f in copies], load, core)
        )

    for i, shape in enumerate(shapes):
        for f in range(shape[0]):
            wide = shape[-1] // 2
            for s in range(2):
                mine, theirs, *hops = flow_refs[at : at + 6]
                at += 6
                source, out, cols = sources[i], outs[i], pl.ds(s * wide, wide)
                if i == 1:
                    places = []
                    for k in range(wide // up_step):
                        to = pl.ds(((s * wide // up_step + k) * (shape[0] + done) + done + f) * up_step, up_step)
                        places.append((
                            lambda final, k=k: final.at[:, :, :, pl.ds(k * up_step, up_step)],
                            lambda out=out, to=to: out.at[:, :, :, to],
                        ))
                else:
                    skip = done if i == 0 else 0
                    places = [(lambda final: final, lambda out=out, f=f + skip, cols=cols: out.at[f, :, :, :, cols])]
                add_flow(
                    (i, f, s), (1, 2) if s == 0 else (2, 1), mine, theirs, hops, places,
                    local(lambda source=source, f=f, cols=cols: source.at[f, :, c, :, :, cols], lambda mine=mine: mine),
                    lambda source=source, f=f, cols=cols: source.at[f, :, 1 - c, :, :, cols],
                )
    for p in range(pairs):
        for s in range(2):
            mine, *hops = flow_refs[at : at + 5]
            at += 5
            places = []
            for side in range(2):
                for i in range(3):
                    to = pl.ds((i * 2 * pairs + side * pairs + p) * lanes, lanes)
                    places.append((
                        lambda final, side=side, i=i: final.at[side, :, :, pl.ds(i * lanes, lanes)],
                        lambda s=s, to=to: outs[-1].at[:, s, :, to],
                    ))
            add_flow((n_in, p, s), (1, 2) if s == 0 else (2, 1), mine, None, hops, places)
    groups = [flows[i : i + 2] for i in range(0, len(flows), 2)]
    products = len(groups) - pairs
    ff_steps = shapes[0][0]
    groups[: 2 * ff_steps] = [groups[k * ff_steps + f] for f in range(ff_steps) for k in range(2)]

    def advance(group, stage):
        for flow in groups[group]:
            flow.step(stage)

    for m in range(mbs):
        for p in range(pairs):
            plan.add(
                ("heads", m, p),
                lambda m=m, p=p: dmixed_ref.at[m, :, slab((1 - c) * pairs + p, lanes)],
                lambda m=m, p=p: d_heads.at[p, m, own_rows],
                {"ctx": 1 - c},
            )
        plan.add(("first", m), lambda m=m: df_send.at[m], lambda m=m: df_recv.at[m], {"ctx": 1 - c})
    for i, peer in enumerate([{"ctx": 1 - c}, {"rep": r ^ 1}, {"rep": r ^ 2}]):
        plan.add(("vec", i), lambda i=i: vec_sum.at[i], lambda i=i: vec_got.at[i], peer)
    for j in range(1, owners):
        plan.add(
            ("vec", "z", j), lambda: vec_sum.at[3], lambda j=j: vec_got.at[2 + j], {"fsdp": lax.rem(z + j, owners)}
        )

    def own_heads(m, p):
        return pltpu.make_async_copy(
            dmixed_ref.at[m, :, slab(c * pairs + p, lanes)], d_heads.at[p, m, own_rows], kept.at[locals_used + m * pairs + p]
        )

    def load_first():
        return pltpu.make_async_copy(first_t_ref, first_t, kept.at[locals_used + mbs * pairs])

    def load_weight(i, p):
        return pltpu.make_async_copy(
            w_ref.at[:, pl.ds((i * pairs + p) * lanes, lanes)],
            w_pairs.at[p, :, pl.ds(i * lanes, lanes)],
            kept.at[locals_used + mbs * pairs + 1 + i * pairs + p],
        )

    @pl.when(step == 0)
    def _():
        greet(owners, reps)
        for p in range(pairs):
            for m in range(mbs):
                plan.start(("heads", m, p))
                own_heads(m, p).start()
        for g in range(products):
            advance(g, 0)
        load_first().start()
        for i in range(3):
            for p in range(pairs):
                load_weight(i, p).start()
        for p in range(pairs):
            for m in range(mbs):
                plan.arrive(("heads", m, p))
                own_heads(m, p).wait()

    table = timetable(products, pairs)
    quarters = 2 * rows // QB
    tail = [entry for entry in table if entry[0] >= quarters * mbs * pairs]

    def between(k, done):
        for i in range(mbs * pairs):
            some = [entry for entry in table if entry[0] == quarters * i + done]
            if some:

                @pl.when(k == i)
                def _():
                    for _, group, stage in some:
                        advance(group, stage)

    def weight_grad(p):
        grad = dot_nn(first_t[...], d_joined[p])
        piece = groups[products][0].mine.shape[2]
        grad = grad.reshape(owners, reps, 2 * piece, grad.shape[1])
        for s in range(2):
            groups[products + p][s].mine[...] = grad[:, :, s * piece : (s + 1) * piece].astype(BF16)

    for p in range(pairs):

        @pl.when(step == mbs * (p + 1))
        def _():
            if p == 0:
                load_first().wait()
            weight_grad(p)
            advance(products + p, 1)

    @pl.when(step < last)
    def _():
        p, m = lax.div(step, mbs), lax.rem(step, mbs)
        start = pl.multiple_of(m * 2 * rows, 2 * rows)
        joined = d_joined.at[p, pl.ds(start, 2 * rows)]
        attention_backward_block(
            factor, size, q_ref.at[0, 0], k_ref.at[0, 0], v_ref.at[0, 0], d_heads.at[p, m], lse_ref.at[m, p],
            joined.at[:, pl.ds(0, lanes)], joined.at[:, pl.ds(lanes, lanes)], joined.at[:, pl.ds(2 * lanes, lanes)],
            dk_sum, dv_sum, partial(between, step),
        )
        for i, k in enumerate((0, 2)):
            part = jnp.sum(joined[:, k * lanes : (k + 1) * lanes].astype(F32), axis=0, keepdims=True)
            before = b_sum[p, i : i + 1, :]
            b_sum[p, i : i + 1, :] = part + jnp.where(m == 0, jnp.zeros_like(before), before)

    def first_part(m, at):
        total = None
        for p in range(pairs):
            term = dot_nt(d_joined[p, pl.ds(pl.multiple_of(m * 2 * rows + at, TB), TB)], w_pairs[p])
            total = term if total is None else total + term
        return total

    @pl.when(step == last)
    def _():
        for i in range(3):
            for p in range(pairs):
                load_weight(i, p).wait()
        gain = vec_ref[3:4, :]
        steps = rows // TB

        def theirs(i, _):
            m, at = lax.div(i, steps), lax.rem(i, steps) * TB
            df_send[m, pl.ds(pl.multiple_of(at, TB), TB)] = first_part(m, (1 - c) * rows + at).astype(BF16)
            return 0

        def go(until):
            while tail and tail[0][0] < until:
                _, group, stage = tail.pop(0)
                advance(group, stage)

        lax.fori_loop(0, mbs * steps, theirs, 0)
        for m in range(mbs):
            plan.start(("first", m))
        go(28)
        for m in range(mbs):
            plan.arrive(("first", m))

        def mine(i, sums):
            m, at = lax.div(i, steps), lax.rem(i, steps) * TB
            here = pl.ds(pl.multiple_of(at, TB), TB)
            total = first_part(m, c * rows + at) + df_recv[m, here].astype(F32)
            normal, inverse = norm_stats(x_ref[m, here].astype(F32))
            dtok_ref[m, here] = dmid_ref[m, here] + norm_back(total, normal, inverse, gain)
            gains = jnp.sum(total * normal, axis=0, keepdims=True)
            return (sums[0] + gains, sums[1] + jnp.sum(total, axis=0, keepdims=True))

        zero = jnp.zeros((1, width), F32)
        g_gain, g_shift = lax.fori_loop(0, mbs * steps, mine, (zero, zero))
        vec_one[...] = gvec_ref[...]
        vec_one[3:4, :] = g_gain
        vec_one[4:5, :] = g_shift
        for p in range(pairs):
            for i in range(2):
                vec_one[i : i + 1, slab(c * pairs + p, lanes)] = b_sum[p, i : i + 1, :]
        vec_sum[0] = vec_one[...]
        plan.start(("vec", 0))
        for i in range(3):
            go(36 + 2 * i)
            plan.arrive(("vec", i))
            vec_sum[i + 1] = vec_sum[i] + vec_got[i]
            if i < 2:
                plan.start(("vec", i + 1))
        plan.start(*[("vec", "z", j) for j in range(1, owners)])
        go(42)
        plan.arrive(*[("vec", "z", j) for j in range(1, owners)])
        vec_out[...] = (vec_sum[3] + vec_got[3]) + (vec_got[4] + vec_got[5])
        go(1000)
        plan.close()
        for copy in leaving:
            copy().wait()


def backward_block(
    qkv, lse, x, vecs, gvec, d_middle, d_mixed, first_t, w_qkv, grads, finished, owners, reps, factor, size
):
    mbs, rows, width = x.shape
    lanes = 2 * size
    pairs = width // 2 // lanes
    shape = jax.ShapeDtypeStruct
    anywhere = pl.BlockSpec(memory_space=pl.ANY)
    whole = lambda s: pl.BlockSpec(s, lambda i: (0,) * len(s), pipeline_mode=pl.Buffered(1))
    final_step = mbs * pairs - 1

    def block(which):
        def index(i):
            k = jnp.minimum(i, final_step)
            return (lax.rem(k, mbs), which * pairs + lax.div(k, mbs), 0, 0)

        return pl.BlockSpec((1, 1, 2 * rows, lanes), index)

    pieces = [(g.shape[4], g.shape[5] // 2) for g in grads for _ in range(2 * g.shape[0])]
    q_piece = (width // owners // reps // 2, 3 * lanes)
    down, up, mix = (g.shape for g in grads)
    finals = [f.shape for f in finished] + [mix[:1] + mix[2:], (reps, 2, q_piece[0], 3 * width)]
    scratch = [s for p in pieces for s in flow_scratch(owners, reps, p, True)]
    scratch += [s for _ in range(2 * pairs) for s in flow_scratch(owners, reps, q_piece, False)]
    remotes = 11 * len(pieces) + 10 * 2 * pairs + mbs * pairs + mbs + 6
    vec = (16, width)
    dtok, vec_sum, *outs = pl.pallas_call(
        partial(backward_kernel, owners, reps, pairs, factor, size, [g.shape for g in grads], finished[0].shape[0] - down[0]),
        grid=(mbs * pairs + 1,),
        in_specs=[block(0), block(1), block(2), whole(lse.shape), whole(x.shape), whole(vec), whole(vec), whole(x.shape)]
        + [anywhere] * (3 + len(grads) + 2),
        input_output_aliases={11 + len(grads): 2, 12 + len(grads): 3},
        out_specs=[whole(x.shape), whole(vec)] + [anywhere] * len(finals),
        out_shape=[shape(x.shape, F32), shape(vec, F32)] + [shape(f, BF16) for f in finals],
        scratch_shapes=[
            pltpu.VMEM((pairs, mbs, 2 * rows, lanes), BF16),
            pltpu.VMEM((pairs, mbs * 2 * rows, 3 * lanes), BF16),
            pltpu.VMEM(first_t.shape, BF16),
            pltpu.VMEM((pairs, width, 3 * lanes), BF16),
            pltpu.VMEM(x.shape, BF16),
            pltpu.VMEM(x.shape, BF16),
            pltpu.VMEM((2 * rows, lanes), F32),
            pltpu.VMEM((2 * rows, lanes), F32),
            pltpu.VMEM((pairs, 8, lanes), F32),
            pltpu.VMEM(vec, F32),
            pltpu.VMEM((6,) + vec, F32),
            pltpu.VMEM((4,) + vec, F32),
        ]
        + scratch
        + [
            pltpu.SemaphoreType.DMA((remotes,)),
            pltpu.SemaphoreType.DMA((remotes,)),
            pltpu.SemaphoreType.DMA((len(pieces) * 3 + 12 * pairs + mbs * pairs + 1 + 3 * pairs,)),
        ],
        compiler_params=pltpu.CompilerParams(
            collective_id=2, has_side_effects=True, vmem_limit_bytes=63 << 20
        ),
        name="backward_block",
    )(qkv, qkv, qkv, lse, x, vecs, gvec, d_middle, d_mixed, first_t, w_qkv, *grads, *finished)
    return dtok, vec_sum, outs


def local(
    inputs,
    weight_qkv,
    bias_query,
    bias_value,
    weight_mix,
    bias_mix,
    gain_attn,
    shift_attn,
    gain_mlp,
    shift_mlp,
    weight_up,
    bias_up,
    weight_down,
    bias_down,
    cotangent,
):
    width = weight_qkv.shape[1] // 3
    half = width // 2
    size = width // H
    factor = size ** (-0.5)
    rows = inputs.shape[2]
    owners = lax.axis_size("fsdp")
    reps = lax.axis_size("rep")
    ctx = lax.axis_index("ctx")
    rep = lax.axis_index("rep")
    own = weight_qkv.shape[0]
    b_up_rows = bias_up.shape[0]
    direct = own % (16 * reps) == 0 and owners == 4 and reps == 4

    def swap(x):
        return lax.ppermute(x, "ctx", [(0, 1), (1, 0)])

    def order(mine, other, axis):
        return jnp.where(
            ctx == 0,
            jnp.concatenate([mine, other], axis=axis),
            jnp.concatenate([other, mine], axis=axis),
        )

    def columns(x, axis, which):
        return lax.dynamic_slice_in_dim(x, which * half, half, axis)

    direct = own % (16 * reps) == 0 and owners == 4 and reps == 4
    vectors = [bias_query, bias_value, bias_mix, gain_attn, shift_attn, gain_mlp, shift_mlp, bias_down]
    small = jnp.stack(vectors + [v for v in bias_up.reshape(-1, own)]).astype(F32)
    tokens = inputs[:, 0].astype(F32)
    if direct:
        mixed, qkv, first_t, w_qkv, w_mix, w_up, w_down, vecs, lse = forward_block(
            inputs[:, 0],
            weight_qkv,
            weight_mix,
            weight_up,
            weight_down,
            jnp.pad(small, ((0, 16 - small.shape[0]), (0, 0))),
            owners,
            reps,
            factor,
            size,
        )
        vecs = vecs[:12]
    else:
        part = own // reps
        mine = lax.dynamic_slice_in_dim(weight_qkv, rep * part, part, 0)
        mine = jnp.concatenate([columns(mine[:, i * width : (i + 1) * width], 1, ctx) for i in range(3)], axis=1)
        w_qkv = lax.all_gather(mine, ("fsdp", "rep"), axis=0, tiled=True)

        def gather(shard):
            piece = shard.shape[0] // (2 * reps)
            mine = lax.dynamic_slice_in_dim(shard, (rep * 2 + ctx) * piece, piece, 0)
            return lax.all_gather(mine, ("fsdp", "rep", "ctx"), axis=0, tiled=True)

        w_mix = gather(weight_mix)
        w_up = gather(weight_up)
        w_down = gather(weight_down)
        vecs = lax.all_gather(small, "fsdp", axis=1, tiled=True)
        w_up = w_up.reshape(width, SHARES, -1, FP).transpose(2, 0, 1, 3).reshape(-1, width, SHARES * FP)
        w_down = w_down.reshape(SHARES, -1, FP, width).swapaxes(0, 1).reshape(-1, SHARES * FP, width)
    b_query, b_value, g_attn, s_attn = (vecs[i] for i in (0, 1, 3, 4))

    if not direct:
        normal_one, inverse_one = norm_stats(tokens)
        first_own = (normal_one * g_attn + s_attn).astype(BF16)
        first = order(first_own, swap(first_own), 1)
        joined = project(first, w_qkv)
        query = (joined[..., :half] + columns(b_query, 0, ctx)).astype(BF16)
        key = joined[..., half : 2 * half].astype(BF16)
        value = (joined[..., 2 * half :] + columns(b_value, 0, ctx)).astype(BF16)
        mixed_heads, lse = attention_forward(query, key, value, factor, size)

    def my_rows(x):
        return lax.dynamic_slice_in_dim(x, ctx * rows, rows, 1)

    def their_rows(x):
        return lax.dynamic_slice_in_dim(x, (1 - ctx) * rows, rows, 1)

    if not direct:
        mixed = order(my_rows(mixed_heads), swap(their_rows(mixed_heads)), 2)
    flat = (-1, width)
    d_out = cotangent.reshape(flat)
    b_up = vecs[8:].reshape(-1, owners, own).swapaxes(0, 1).reshape(SHARES, -1, FP).swapaxes(0, 1)
    result, d_middle, d_mixed, g_wmix, g_wup, g_wdown, gvec, *finished = middle_block(
        inputs.reshape(flat),
        mixed.reshape(flat),
        d_out,
        w_mix,
        w_up,
        w_down,
        vecs,
        b_up.reshape(b_up.shape[0], 1, -1),
        SHARES,
        reps,
        direct,
    )
    steps = b_up.shape[0]
    if direct:
        d_tokens, summed, outs = backward_block(
            qkv, lse, inputs[:, 0], vecs, gvec, d_middle.reshape(tokens.shape), d_mixed.reshape(tokens.shape),
            first_t, w_qkv, [g_wdown, g_wup, g_wmix[None]], finished, owners, reps, factor, size,
        )
        o_wdown, o_wup, o_wmix, o_wqkv = (
            o.reshape(-1, n).astype(F32) for o, n in zip(outs, (width, SHARES * steps * FP, width, 3 * width))
        )
    else:
        d_mixed = d_mixed.reshape(tokens.shape)
        d_middle = d_middle.reshape(tokens.shape)
        d_heads = order(columns(d_mixed, 2, ctx), swap(columns(d_mixed, 2, 1 - ctx)), 1)
        d_query, d_key, d_value = attention_backward(query, key, value, d_heads, lse, factor, size)
        d_joined = jnp.concatenate([d_query, d_key, d_value], axis=-1)
        g_wqkv = outer_sum(first, d_joined)
        d_first = project_back(d_joined, w_qkv)
        d_first = my_rows(d_first) + swap(their_rows(d_first).astype(BF16)).astype(F32)
        normal_one, inverse_one = norm_stats(tokens)
        d_tokens = d_middle + norm_back(d_first, normal_one, inverse_one, g_attn)

        def reduce(grad):
            piece = lax.psum_scatter(
                grad.astype(BF16), ("fsdp", "rep", "ctx"), scatter_dimension=0, tiled=True
            )
            return lax.all_gather(piece, ("rep", "ctx"), axis=0, tiled=True).astype(F32)

        g_wdown = jnp.concatenate([g_wdown[f].reshape(SHARES, FP, width) for f in range(steps)], axis=1)
        o_wdown = reduce(g_wdown.reshape(-1, width))
        g_wup = jnp.stack([g_wup[f].reshape(width, SHARES, FP) for f in range(steps)], axis=2)
        o_wup = reduce(g_wup.reshape(width, -1))
        o_wmix = reduce(g_wmix.reshape(width, width))
        piece = lax.psum_scatter(g_wqkv.astype(BF16), ("fsdp", "rep"), scatter_dimension=0, tiled=True)
        piece = lax.all_gather(piece, "rep", axis=0, tiled=True)
        other = swap(piece)
        low, high = jnp.where(ctx == 0, piece, other), jnp.where(ctx == 0, other, piece)
        o_wqkv = jnp.concatenate(
            [t for i in range(3) for t in (low[:, i * half : (i + 1) * half], high[:, i * half : (i + 1) * half])],
            axis=1,
        ).astype(F32)

        def place(v):
            return lax.dynamic_update_slice_in_dim(jnp.zeros((width,), F32), v, ctx * half, 0)

        first_rows = (
            place(jnp.sum(d_query.astype(F32), axis=(0, 1))),
            place(jnp.sum(d_value.astype(F32), axis=(0, 1))),
            jnp.sum(d_first * normal_one, axis=(0, 1)),
            jnp.sum(d_first, axis=(0, 1)),
        )
        summed = jnp.concatenate([jnp.stack(first_rows[:2]), gvec[2:3], jnp.stack(first_rows[2:]), gvec[5:12]], axis=0)
        summed = lax.psum(summed, ("rep", "fsdp", "ctx"))
    owner = lax.axis_index("fsdp")
    o_bup = lax.dynamic_slice_in_dim(summed[8 : 8 + SHARES].reshape(-1), owner * b_up_rows, b_up_rows, 0)
    summed = lax.dynamic_slice_in_dim(summed[:8], owner * own, own, 1)
    o_bq, o_bv, o_bmix, o_ga, o_sa, o_gm, o_sm, o_bd = (summed[i] for i in range(8))
    return (
        result.reshape(inputs.shape),
        d_tokens[:, None],
        o_wqkv,
        o_bq,
        o_bv,
        o_wmix,
        o_bmix,
        o_ga,
        o_sa,
        o_gm,
        o_sm,
        o_wup,
        o_bup,
        o_wdown,
        o_bd,
    )


def solution(mesh):
    row = P(None, ("rep", "fsdp"), "ctx", None)
    mat = P("fsdp", None)
    vec = P("fsdp")
    params = (mat, vec, vec, mat, vec, vec, vec, vec, vec, mat, vec, mat, vec)
    in_specs = (row,) + params + (row,)
    out_specs = (row, row) + params
    return jax.shard_map(local, mesh=mesh, in_specs=in_specs, out_specs=out_specs, check_vma=False)
```

```python
from functools import partial

import jax
import jax.numpy as jnp
from jax import lax
from jax.experimental import pallas as pl
from jax.experimental.pallas import tpu as pltpu
from jax.sharding import PartitionSpec as P

H = 12
EPS = 1e-05
BF16 = jnp.bfloat16
F32 = jnp.float32
QB = 256
TB = 256
FP = 256
SHARES = 4
GELU_A = 0.7978845608028654
GELU_B = 0.044715
LOG2E = 1.4426950408889634


def norm_stats(values):
    center = values - jnp.mean(values, axis=-1, keepdims=True)
    inverse = lax.rsqrt(jnp.mean(center * center, axis=-1, keepdims=True) + EPS)
    return (center * inverse, inverse)


def norm_back(grad_norm, normal, inverse, gain):
    scaled = grad_norm * gain
    return inverse * (
        scaled
        - jnp.mean(scaled, axis=-1, keepdims=True)
        - normal * jnp.mean(scaled * normal, axis=-1, keepdims=True)
    )


def outer_sum(left, right):
    return jnp.einsum("sri,srj->ij", left, right, preferred_element_type=F32)


def project(left, weight):
    return jnp.einsum("sri,ij->srj", left, weight, preferred_element_type=F32)


def project_back(grad_rows, weight):
    return jnp.einsum("srj,ij->sri", grad_rows, weight, preferred_element_type=F32)


def dot_nt(a, b):
    return lax.dot_general(a, b, (((1,), (1,)), ((), ())), preferred_element_type=F32)


def dot_nn(a, b):
    return lax.dot_general(a, b, (((1,), (0,)), ((), ())), preferred_element_type=F32)


def head_mask(x, head, size):
    lane = lax.broadcasted_iota(jnp.int32, x.shape, 1)
    keep = (lane >= head * size) & (lane < (head + 1) * size)
    return jnp.where(keep, x, jnp.zeros_like(x))


def causal(scores_t, qb):
    n = scores_t.shape[0]
    bottom = scores_t[n - QB :]
    key = lax.broadcasted_iota(jnp.int32, bottom.shape, 0)
    query = lax.broadcasted_iota(jnp.int32, bottom.shape, 1)
    bottom = jnp.where(key <= query, bottom, -1e30)
    return bottom if n == QB else jnp.concatenate([scores_t[: n - QB], bottom], axis=0)


def attention_forward_kernel(factor, size, q_ref, k_ref, v_ref, o_ref, lse_ref):
    refs = [ref.at[0] for ref in (q_ref, k_ref, v_ref, o_ref)]
    attention_forward_block(factor, size, *refs, lse_ref.at[0, 0], lambda done: None)


def attention_forward_block(factor, size, q_ref, k_ref, v_ref, o_ref, lse_ref, between):
    length = q_ref.shape[0]
    base_two = factor * LOG2E
    k = k_ref[...]
    vt = jnp.transpose(v_ref[...])
    for qb in range(length // QB):
        n = (qb + 1) * QB
        rows = pl.ds(qb * QB, QB)
        q = q_ref[rows, :]
        outs = []
        for head in range(2):
            s = causal(dot_nt(k[:n], head_mask(q, head, size)), qb)
            top = jnp.max(s, axis=0, keepdims=True) * base_two
            p = jnp.exp2(s * base_two - top)
            total = jnp.sum(p, axis=0, keepdims=True)
            o = dot_nn(vt[head * size : (head + 1) * size, :n], p.astype(BF16))
            outs.append(o * (1.0 / total))
            lse_ref[head : head + 1, rows] = top + jnp.log2(total)
        o_ref[rows, :] = jnp.transpose(jnp.concatenate(outs, axis=0)).astype(o_ref.dtype)
        between(qb)


def attention_forward(q, k, v, factor, size):
    mbs, length, width = q.shape
    lanes = 2 * size
    pairs = width // lanes
    block = pl.BlockSpec((1, length, lanes), lambda m, p: (m, 0, p))
    area = mbs * pairs * 2 * length * (length + QB) // 2
    return pl.pallas_call(
        partial(attention_forward_kernel, factor, size),
        grid=(mbs, pairs),
        in_specs=[block] * 3,
        out_specs=[block, pl.BlockSpec((1, 1, 8, length), lambda m, p: (m, p, 0, 0))],
        out_shape=[
            jax.ShapeDtypeStruct(q.shape, BF16),
            jax.ShapeDtypeStruct((mbs, pairs, 8, length), F32),
        ],
        compiler_params=pltpu.CompilerParams(vmem_limit_bytes=48 << 20),
        cost_estimate=pl.CostEstimate(
            flops=16 * area * size, bytes_accessed=8 * q.size, transcendentals=area
        ),
        name="attention_forward",
    )(q, k, v)


def attention_backward_kernel(factor, size, q_ref, k_ref, v_ref, do_ref, lse_ref, dq_ref, dk_ref, dv_ref, dk_sum, dv_sum):
    refs = [ref.at[0] for ref in (q_ref, k_ref, v_ref, do_ref)]
    attention_backward_block(
        factor, size, *refs, lse_ref.at[0, 0], dq_ref.at[0], dk_ref.at[0], dv_ref.at[0], dk_sum, dv_sum, lambda done: None
    )


def attention_backward_block(
    factor, size, q_ref, k_ref, v_ref, do_ref, lse_ref, dq_ref, dk_ref, dv_ref, dk_sum, dv_sum, between
):
    length = q_ref.shape[0]
    base_two = factor * LOG2E
    k = k_ref[...]
    v = v_ref[...]
    kt = jnp.transpose(k)
    for i, qb in enumerate(reversed(range(length // QB))):
        n = (qb + 1) * QB
        rows = pl.ds(qb * QB, QB)
        q = q_ref[rows, :]
        do = do_ref[rows, :]
        dqs, dk, dv = [], None, None
        for head in range(2):
            qh = head_mask(q, head, size)
            doh = head_mask(do, head, size)
            s = causal(dot_nt(k[:n], qh), qb)
            p = jnp.exp2(s * base_two - lse_ref[head : head + 1, rows])
            dp = dot_nt(v[:n], doh)
            mean = jnp.sum(dp * p, axis=0, keepdims=True)
            ds = (p * (dp - mean)).astype(BF16)
            dvh = dot_nn(p.astype(BF16), doh)
            dkh = dot_nn(ds, qh)
            dv = dvh if dv is None else dv + dvh
            dk = dkh if dk is None else dk + dkh
            dqs.append(dot_nn(kt[head * size : (head + 1) * size, :n], ds))
        dq_ref[rows, :] = jnp.transpose(jnp.concatenate(dqs, axis=0) * factor).astype(BF16)
        if n == length:
            dk_sum[...] = dk
            dv_sum[...] = dv
        else:
            dk_sum[:n] += dk
            dv_sum[:n] += dv
        between(i)
    dk_ref[...] = (dk_sum[...] * factor).astype(BF16)
    dv_ref[...] = dv_sum[...].astype(BF16)


def attention_backward(q, k, v, do, lse, factor, size):
    mbs, length, width = q.shape
    lanes = 2 * size
    pairs = width // lanes
    block = pl.BlockSpec((1, length, lanes), lambda m, p: (m, 0, p))
    area = mbs * pairs * 2 * length * (length + QB) // 2
    return pl.pallas_call(
        partial(attention_backward_kernel, factor, size),
        grid=(mbs, pairs),
        in_specs=[block] * 4 + [pl.BlockSpec((1, 1, 8, length), lambda m, p: (m, p, 0, 0))],
        out_specs=[block] * 3,
        out_shape=[jax.ShapeDtypeStruct(q.shape, BF16)] * 3,
        scratch_shapes=[pltpu.VMEM((length, lanes), F32)] * 2,
        compiler_params=pltpu.CompilerParams(vmem_limit_bytes=48 << 20),
        cost_estimate=pl.CostEstimate(
            flops=40 * area * size, bytes_accessed=14 * q.size, transcendentals=area
        ),
        name="attention_backward",
    )(q, k, v, do, lse)


MESH = pl.DeviceIdType.MESH


def position():
    return lax.axis_index("fsdp"), lax.axis_index("rep"), lax.axis_index("ctx")


def greet(owners, reps):
    z, r, c = position()
    barrier = pltpu.get_barrier_semaphore()
    peers = [{"fsdp": lax.rem(z + j, owners)} for j in range(1, owners)]
    peers += [{"rep": r ^ j} for j in range(1, reps)]
    peers += [{"ctx": 1 - c}]
    for peer in peers:
        pl.semaphore_signal(barrier, inc=1, device_id=peer, device_id_type=MESH)
    pl.semaphore_wait(barrier, len(peers))


def slab(i, half):
    return pl.ds(pl.multiple_of(i * half, 128), half)


def add_blocks(out, parts, dtype):
    lead = out.shape[:-2]
    count = 1
    for n in lead:
        count *= n

    def body(i, _):
        at = []
        for n in reversed(lead):
            at.append(lax.rem(i, n))
            i = lax.div(i, n)
        at = tuple(reversed(at))
        terms = [p[at].astype(F32) for p in parts]
        while len(terms) > 1:
            terms = [terms[0] + terms[1]] + terms[2:]
        out[at] = terms[0].astype(dtype)
        return 0

    lax.fori_loop(0, count, body, 0)


class Plan:
    def __init__(self, send, recv):
        self.send, self.recv = send, recv
        self.made, self.left = {}, set()

    def add(self, name, src, dst, peer):
        self.made[name] = (len(self.made), src, dst, peer)

    def copy(self, name):
        slot, src, dst, peer = self.made[name]
        return pltpu.make_async_remote_copy(
            src_ref=src(),
            dst_ref=dst(),
            send_sem=self.send.at[slot],
            recv_sem=self.recv.at[slot],
            device_id=peer,
            device_id_type=MESH,
        )

    def start(self, *names):
        for name in names:
            self.copy(name).start()

    def arrive(self, *names):
        for name in names:
            self.copy(name).wait_recv()

    def leave(self, *names):
        for name in names:
            self.copy(name).wait_send()
            self.left.add(name)

    def close(self):
        for name in self.made:
            if name not in self.left:
                self.copy(name).wait_send()


def spread_plan(plan, tag, owners, reps, z, r, c, src, dst, halves, core=None):
    for j in range(1, owners):
        origin = lax.rem(z - j + owners, owners)
        if src is not None:
            plan.add((tag, "z", j), src, lambda: dst(z, r), {"fsdp": lax.rem(z + j, owners)})
        here = partial(dst, origin, r)
        plan.add((tag, "x", j), here, here, {"rep": r ^ 1})
        plan.add((tag, "y", j), here, here, {"rep": r ^ 2})
        by_y = lambda origin=origin: halves(dst(origin, r ^ 2))[0]
        by_x = lambda origin=origin: halves(dst(origin, r ^ 1))[1]
        plan.add((tag, "xx", j), by_y, by_y, {"rep": r ^ 1})
        plan.add((tag, "yy", j), by_x, by_x, {"rep": r ^ 2})
        if core is not None:
            side = partial(core, origin)
            plan.add((tag, "c", j), side, side, {"ctx": 1 - c})


def spread_step(plan, tag, owners, stage):
    for j in range(1, owners):
        if stage == 0:
            plan.start((tag, "z", j))
        elif stage == 1:
            if (tag, "z", j) in plan.made:
                plan.arrive((tag, "z", j))
            plan.start((tag, "x", j), (tag, "y", j))
        elif stage == 2:
            plan.arrive((tag, "y", j))
            plan.start((tag, "xx", j))
            plan.arrive((tag, "x", j))
            plan.start((tag, "yy", j))
        elif stage == 3:
            plan.arrive((tag, "xx", j), (tag, "yy", j))
            if (tag, "c", j) in plan.made:
                plan.start((tag, "c", j))
        else:
            plan.arrive((tag, "c", j))


def up_side(ref, c):
    half = ref.shape[-1] // 2
    return ref.at[:, pl.ds(pl.multiple_of(c * half, 128), half)]


def up_piece(ref, c, r):
    return ref.at[:, pl.ds(pl.multiple_of((c * 4 + r) * 128, 128), 128)]


def down_side(ref, c):
    half = ref.shape[0] // 2
    return ref.at[pl.ds(pl.multiple_of(c * half, 32), half)]


def down_piece(ref, c, r):
    piece = ref.shape[0] // 8
    return ref.at[pl.ds(pl.multiple_of((c * 4 + r) * piece, 32), piece)]


def uneven_halves(ref):
    middle = ref.shape[1] // 256 * 128
    return ref.at[:, pl.ds(0, middle)], ref.at[:, pl.ds(middle, ref.shape[1] - middle)]


def row_halves(ref):
    middle = ref.shape[0] // 2
    return ref.at[pl.ds(0, middle)], ref.at[pl.ds(middle, middle)]


def column_halves(ref):
    middle = ref.shape[-1] // 2
    return ref.at[:, pl.ds(0, middle)], ref.at[:, pl.ds(middle, middle)]


SPREADS = [
    (-1, 0, 1), (-1, 1, 1), (2, 2, 1), (5, 0, 2), (9, 1, 2), (9, 0, 3), (14, 2, 2), (14, 1, 3), (15, 0, 4), (18, 1, 4),
    (19, 2, 3), (23, 2, 4),
]


def forward_kernel(owners, reps, pairs, factor, size,
                   x_ref, qkv_ref, mix_ref, up_ref, down_ref, *refs):
    vectors, b_up_ref, refs = refs[:8], refs[8], refs[9:]
    (mixed, qkv_out, first_t_out, w_qkv_out, w_mix, w_up, w_down, vec_ref, bup_ref, lse_ref, small_ref,
                   first, first_t, w_qkv, qkv, heads, small, own_mix, own_up, own_down, send, recv, kept) = refs
    step = pl.program_id(0)
    last = pl.num_programs(0) - 1
    z, r, c = position()
    mbs, rows, width = x_ref.shape
    half = width // 2
    lanes = 2 * size
    plan = Plan(send, recv)
    own_rows = pl.ds(pl.multiple_of(c * rows, rows), rows)
    their_rows = pl.ds(pl.multiple_of((1 - c) * rows, rows), rows)

    for j in range(1, owners):
        plan.add(("small", j), lambda: small_ref, lambda: small.at[z], {"fsdp": lax.rem(z + j, owners)})
    for m in range(mbs):
        plan.add(("first", m), lambda m=m: first.at[m, own_rows], lambda m=m: first.at[m, own_rows], {"ctx": 1 - c})
    for i in range(3):
        spread_plan(
            plan, ("qkv", i), owners, reps, z, r, c,
            lambda i=i: qkv_ref.at[r, :, slab(2 * i + c, half)],
            lambda o, p, i=i: w_qkv.at[o, p, :, slab(i, half)],
            uneven_halves,
        )
    steps = w_up.shape[0]
    spread_plan(
        plan, ("mix", 0), owners, reps, z, r, c,
        lambda: own_mix.at[c, r], lambda o, p: w_mix.at[o, c, p], column_halves, lambda o: w_mix.at[o, c],
    )
    for tag, own, whole, piece, side in (("up", own_up, w_up, up_piece, up_side), ("down", own_down, w_down, down_piece, down_side)):
        for f in range(steps):
            dst = lambda o, p, whole=whole, piece=piece, f=f: piece(whole.at[f, o], c, p)
            src = lambda own=own, piece=piece, f=f: piece(own.at[f], c, r)
            if f == 0:
                core = lambda o, whole=whole, side=side, f=f: side(whole.at[f, o], c)
                spread_plan(plan, (tag, f), owners, reps, z, r, c, src, dst, row_halves, core)
            else:
                for j in range(1, owners):
                    to = lax.rem(z + j, owners)
                    plan.add(((tag, f), "z", j), src, lambda dst=dst: dst(z, r), {"fsdp": to})
    quarters = 2 * rows // QB
    table = SPREADS
    order = [("mix", 0)] + [(tag, f) for f in range(steps) for tag in ("up", "down")]

    up_step = own_up.shape[-1] // owners
    pairs_of = [(small_ref, small.at[z])]
    pairs_of += [(qkv_ref.at[:, :, slab(2 * i + c, half)], w_qkv.at[z, :, :, slab(i, half)]) for i in range(3)]
    pairs_of += [(mix_ref, own_mix)]
    early = len(pairs_of)
    for f in range(steps):
        for k in range(owners):
            cols = pl.ds((k * (up_ref.shape[-1] // owners)) + f * up_step, up_step)
            pairs_of += [(up_ref.at[:, cols], own_up.at[f, :, pl.ds(k * up_step, up_step)])]
        pairs_of += [(down_ref.at[pl.ds(f * own_down.shape[1], own_down.shape[1])], own_down.at[f])]
    loads = len(pairs_of)
    pairs_of += [(own_mix, w_mix.at[z])]
    for f in range(steps):
        pairs_of += [(own_up.at[f], w_up.at[f, z]), (own_down.at[f], w_down.at[f, z])]
    stores = len(pairs_of)
    pairs_of += [(w_qkv, w_qkv_out), (first_t, first_t_out), (qkv, qkv_out)]
    ends = len(pairs_of)

    def keep(i):
        return pltpu.make_async_copy(*pairs_of[i], kept.at[i])

    def mixed_place(step):
        m, p = lax.div(step, pairs), lax.rem(step, pairs)
        return mixed.at[m, :, slab(c * pairs + p, lanes)]

    def mixed_sends(k, slot):
        return pltpu.make_async_remote_copy(
            src_ref=heads.at[k, their_rows],
            dst_ref=mixed_place(k),
            send_sem=send.at[slot],
            recv_sem=recv.at[slot],
            device_id={"ctx": 1 - c},
            device_id_type=MESH,
        )

    base = len(plan.made)

    @pl.when(step == 0)
    def _():
        for i in range(1, loads):
            keep(i).start()
        small_ref[...] = jnp.zeros_like(small_ref)
        own = vectors[0].shape[0]
        for i, vector in enumerate(vectors):
            small_ref[i : i + 1, :own] = vector[...].astype(F32).reshape(1, own)
        for f in range(steps):
            small_ref[8 + f : 9 + f, :] = b_up_ref[f * FP : (f + 1) * FP].astype(F32).reshape(1, FP)
        greet(owners, reps)
        keep(0).start()
        plan.start(*[("small", j) for j in range(1, owners)])
        for i in range(3):
            spread_step(plan, ("qkv", i), owners, 0)
        keep(0).wait()
        plan.arrive(*[("small", j) for j in range(1, owners)])
        vec_ref[...] = jnp.concatenate([small[k, :, :own] for k in range(owners)], axis=1)
        bup_ref[...] = jnp.concatenate([small[k, 8:16] for k in range(owners)], axis=1)
        gain, shift = vec_ref[3:4, :], vec_ref[4:5, :]
        for m in range(mbs):
            for at in range(0, rows, TB):
                normal, _ = norm_stats(x_ref[m, at : at + TB].astype(F32))
                place = pl.ds(pl.multiple_of(c * rows + at, TB), TB)
                first[m, place] = (normal * gain + shift).astype(BF16)
            plan.start(("first", m))
        spread_step(plan, ("qkv", 0), owners, 1)
        for i in range(4, loads):
            keep(i).wait()
        for i in range(loads, stores):
            keep(i).start()
        plan.arrive(*[("first", m) for m in range(mbs)])
        spread_step(plan, ("qkv", 1), owners, 1)
        spread_step(plan, ("qkv", 0), owners, 2)
        spread_step(plan, ("qkv", 2), owners, 1)
        for tag in order[:3]:
            spread_step(plan, tag, owners, 0)

        def turn(i, _):
            m, at = lax.div(i, 2 * rows // TB), lax.rem(i, 2 * rows // TB)
            place = pl.ds(pl.multiple_of(at * TB, TB), TB)
            first_t[:, pl.ds(pl.multiple_of(i * TB, TB), TB)] = jnp.transpose(first[m, place])
            return 0

        lax.fori_loop(0, mbs * 2 * rows // TB, turn, 0)
        keep(stores + 1).start()
        spread_step(plan, ("qkv", 1), owners, 2)

        def project_all(i):
            weight = w_qkv[:, :, :, i * half : (i + 1) * half].reshape(-1, half)
            bias = None if i == 1 else vec_ref[i // 2 : i // 2 + 1, slab(c, half)]

            def project_rows(n, _):
                m, at = lax.div(n, 2 * rows // TB), lax.rem(n, 2 * rows // TB)
                place = pl.ds(pl.multiple_of(at * TB, TB), TB)
                joined = dot_nn(first[m, place], weight)
                joined = (joined if bias is None else joined + bias).astype(BF16)
                for s in range(pairs):
                    qkv[m, i * pairs + s, place] = joined[:, s * lanes : (s + 1) * lanes]
                return 0

            lax.fori_loop(0, mbs * 2 * rows // TB, project_rows, 0)

        for i in range(1, 4):
            keep(i).wait()
        for i in range(3):
            if i == 1:
                spread_step(plan, ("qkv", 2), owners, 2)
            spread_step(plan, ("qkv", i), owners, 3)
            if i == 2:
                for when, t, stage in table:
                    if when < 0:
                        spread_step(plan, order[t], owners, stage)
            project_all(i)
        keep(stores).start()
        keep(stores + 2).start()

    def between(k, done):
        for i in range(mbs * pairs):
            some = [entry for entry in table if entry[0] == i * quarters + done]
            if some:

                @pl.when(k == i)
                def _():
                    for _, t, stage in some:
                        spread_step(plan, order[t], owners, stage)

    @pl.when(step == 1)
    def _():
        for tag in order[3:]:
            spread_step(plan, tag, owners, 0)

    @pl.when(step > 0)
    def _():
        k = step - 1
        m, p = lax.div(k, pairs), lax.rem(k, pairs)
        attention_forward_block(
            factor, size, qkv.at[m, p], qkv.at[m, pairs + p], qkv.at[m, 2 * pairs + p], heads.at[k], lse_ref.at[m, p],
            partial(between, k),
        )
        mixed_sends(k, base + k).start()
        pltpu.make_async_copy(heads.at[k, own_rows], mixed_place(k), kept.at[ends + k]).start()

    @pl.when(step == last)
    def _():
        for when, t, stage in table:
            if when >= quarters * mbs * pairs:
                spread_step(plan, order[t], owners, stage)
        for k in range(mbs * pairs):
            mixed_sends(k, base + k).wait()
            pltpu.make_async_copy(heads.at[k, own_rows], mixed_place(k), kept.at[ends + k]).wait()
        for tag in order[3:]:
            for j in range(1, owners):
                plan.arrive((tag, "z", j))
        plan.close()
        for i in range(loads, ends):
            keep(i).wait()


def forward_block(x, weight_qkv, weight_mix, weight_up, weight_down, vectors, b_up, owners, reps, factor, size):
    own, wide = weight_qkv.shape
    mbs, rows, width = x.shape
    lanes = 2 * size
    pairs = width // 2 // lanes

    def cut(shard):
        return shard.reshape(2, reps, shard.shape[0] // (2 * reps), shard.shape[1])

    steps = weight_down.shape[0] // FP
    shards = (weight_qkv.reshape(reps, own // reps, wide), cut(weight_mix), weight_up, weight_down)
    own_up = (steps, own, owners * FP)
    own_down = (steps, FP, width)
    shape = jax.ShapeDtypeStruct
    w_shape = (owners, reps, own // reps, wide // 2)
    qkv_shape = (mbs, 3 * pairs, 2 * rows, lanes)
    anywhere = pl.BlockSpec(memory_space=pl.ANY)
    whole = lambda s: pl.BlockSpec(s, lambda i: (0,) * len(s), pipeline_mode=pl.Buffered(1))
    remotes = 3 + mbs + 3 * 15 + 3 * 18 + 6 * (steps - 1) + mbs * pairs
    copies = 5 + steps * (owners + 1) + 1 + 2 * steps + 3 + mbs * pairs
    area = mbs * pairs * 2 * rows * (2 * rows + QB)
    mixed, qkv, first_t, w_qkv, w_mix, w_up, w_down, vecs, b_up, lse = pl.pallas_call(
        partial(forward_kernel, owners, reps, pairs, factor, size),
        grid=(1 + mbs * pairs,),
        in_specs=[whole(x.shape)] + [anywhere] * 4 + [whole(v.shape) for v in (*vectors, b_up)],
        out_specs=[anywhere] * 7 + [whole((16, width)), whole((8, owners * FP)), whole((mbs, pairs, 8, 2 * rows))],
        out_shape=[
            shape((mbs, rows, width), BF16),
            shape(qkv_shape, BF16),
            shape((width, mbs * 2 * rows), BF16),
            shape(w_shape, BF16),
            shape((owners,) + shards[1].shape, BF16),
            shape(own_up[:1] + (owners,) + own_up[1:], BF16),
            shape(own_down[:1] + (owners,) + own_down[1:], BF16),
            shape((16, width), F32),
            shape((8, owners * FP), F32),
            shape((mbs, pairs, 8, 2 * rows), F32),
        ],
        scratch_shapes=[
            pltpu.VMEM((16, FP), F32),
            pltpu.VMEM((mbs, 2 * rows, width), BF16),
            pltpu.VMEM((width, mbs * 2 * rows), BF16),
            pltpu.VMEM(w_shape, BF16),
            pltpu.VMEM(qkv_shape, BF16),
            pltpu.VMEM((mbs * pairs, 2 * rows, lanes), BF16),
            pltpu.VMEM((owners, 16, FP), F32),
            pltpu.VMEM(shards[1].shape, BF16),
            pltpu.VMEM(own_up, BF16),
            pltpu.VMEM(own_down, BF16),
            pltpu.SemaphoreType.DMA((remotes,)),
            pltpu.SemaphoreType.DMA((remotes,)),
            pltpu.SemaphoreType.DMA((copies,)),
        ],
        compiler_params=pltpu.CompilerParams(
            collective_id=1, has_side_effects=True, vmem_limit_bytes=56 << 20
        ),
        name="forward_block",
    )(x, *shards, *vectors, b_up)
    return (
        mixed,
        qkv,
        first_t,
        w_qkv.reshape(owners * own, -1),
        w_mix.reshape(owners * own, -1),
        w_up,
        w_down,
        vecs,
        b_up[:steps].reshape(steps, 1, owners * FP),
        lse,
    )


class Flow:
    def __init__(self, plan, name, place, owners, bits, mine, theirs, hops, outs, load=None, core=None):
        z, r, c = place
        first, second = bits
        self.plan, self.name, self.place, self.owners = plan, name, place, owners
        self.mine, self.theirs, self.second = mine, theirs, r ^ second
        self.hop_one, self.hop_two, self.hop_z, self.final = hops
        self.outs = outs
        self.load = load
        peer = {"rep": r ^ first}
        if core is not None:
            plan.add((name, "core"), core, lambda: theirs, {"ctx": 1 - c})
        self.split = core is not None
        plan.add((name, "me"), lambda: mine.at[:, r ^ first], lambda: self.hop_one.at[0], peer)
        plan.add((name, "on"), lambda: mine.at[:, r ^ first ^ second], lambda: self.hop_one.at[1], peer)
        plan.add((name, "two"), lambda: mine.at[:, r ^ second], lambda: self.hop_two, {"rep": r ^ second})
        for j in range(1, owners):
            to = lax.rem(z + j, owners)
            plan.add((name, "z", j), lambda to=to: mine.at[to, r], lambda j=j: self.hop_z.at[j - 1], {"fsdp": to})
        here = lambda: self.final.at[c, r]
        plan.add((name, "x"), here, here, {"rep": r ^ first})
        plan.add((name, "y"), here, here, {"rep": r ^ second})
        far = lambda: self.final.at[c, r ^ second]
        plan.add((name, "xy"), far, far, {"rep": r ^ first})
        side = lambda: self.final.at[c]
        plan.add((name, "back"), side, side, {"ctx": 1 - c})

    def step(self, stage):
        z, r, c = self.place
        plan, name, mine = self.plan, self.name, self.mine
        owners = self.owners
        if stage == 0:
            if self.split:
                plan.start((name, "core"))
            if self.load is not None:
                self.load().start()
        elif stage == 1:
            if self.load is not None:
                self.load().wait()
            if self.split:
                plan.arrive((name, "core"))
                add_blocks(mine, [mine, self.theirs], BF16)
            plan.start((name, "on"), (name, "me"))
        elif stage == 2:
            plan.arrive((name, "on"))
            part = mine.at[:, self.second]
            add_blocks(part, [part, self.hop_one.at[1]], BF16)
            plan.start((name, "two"))
        elif stage == 3:
            plan.arrive((name, "me"), (name, "two"))
            part = mine.at[:, r]
            add_blocks(part, [part, self.hop_one.at[0], self.hop_two], BF16)
            plan.start(*[(name, "z", j) for j in range(1, owners)])
        elif stage == 4:
            plan.arrive(*[(name, "z", j) for j in range(1, owners)])
            terms = [mine[z, r].astype(F32)] + [self.hop_z[j].astype(F32) for j in range(owners - 1)]
            while len(terms) > 1:
                terms = [a + b for a, b in zip(terms[::2], terms[1::2])]
            self.final[c, r] = terms[0].astype(BF16)
            plan.start((name, "x"), (name, "y"))
        elif stage == 5:
            plan.arrive((name, "y"))
            plan.start((name, "xy"))
        elif stage == 6:
            plan.arrive((name, "x"), (name, "xy"))
            plan.start((name, "back"))
        else:
            plan.arrive((name, "back"))
            for copy in self.outs(self.final):
                copy.start()


def flow_scratch(owners, reps, piece, split):
    vmem = lambda *lead: pltpu.VMEM(lead + piece, BF16)
    mine = [vmem(owners, reps)] * (2 if split else 1)
    return mine + [vmem(2, owners), vmem(owners), vmem(owners - 1), vmem(2, reps)]


def timetable(groups, products):
    table = []
    for g in range(groups):
        second = 6 + 4 * g
        times = (1 + 2 * g, second, second + 5, second + 9, second + 11, second + 13, second + 15)
        table += [(t, g, 1 + i) for i, t in enumerate(times)]
    for p, second in zip(range(products), (20, 27, 28)):
        times = (second, second + 4, second + 8, second + 10, second + 12, second + 14)
        table += [(t, groups + p, 2 + i) for i, t in enumerate(times)]
    return sorted(table)


def gelu_parts(b):
    square = b * b
    inner = GELU_A * b * (1.0 + GELU_B * square)
    t = jnp.tanh(inner)
    rise = 0.5 * (1.0 + t)
    slope = rise + 0.5 * b * (1.0 - t * t) * (GELU_A * (1.0 + 3.0 * GELU_B * square))
    return b * rise, slope


GATHERS = [
    (1, ("up", 1), 2), (1, ("down", 1), 2), (2, ("up", 1), 3), (2, ("down", 1), 3), (2, ("up", 2), 1), (2, ("down", 2), 1),
    (4, ("up", 1), 4), (4, ("down", 1), 4), (5, ("up", 2), 2), (5, ("down", 2), 2), (6, ("up", 2), 3), (6, ("down", 2), 3),
    (8, ("up", 2), 4), (8, ("down", 2), 4),
]
SUMS = [
    (3, 0, 0), (3, 1, 0), (5, 0, 1), (6, 1, 1), (8, 0, 2), (9, 1, 2), (9, 0, 3), (10, 1, 3), (10, 0, 4), (11, 0, 5),
    (11, 1, 4), (12, 1, 5), (12, 0, 6), (13, 1, 6), (14, 0, 7), (14, 1, 7),
]


def middle_kernel(owners, reps, direct, *refs):
    x_ref, mixed_ref, d_ref, wmix_ref, wup_any, wdown_any, vec_ref, bup_ref = refs[:8]
    result_ref, dmid_ref, dmixed_ref, gmix_ref, gup_ref, gdown_ref, gvec_ref = refs[8:15]
    refs = refs[15:]
    if direct:
        down_out, up_out, refs = refs[0], refs[1], refs[2:]
    middle, second, second_t, mixed_t, out_sum, ds_sum, active_t, d_before, w_up, w_down = refs[:10]
    refs = refs[10:]
    step = pl.program_id(0)
    rows = x_ref.shape[0]
    steps = w_up.shape[0]
    last = steps - 1
    count = rows // TB
    chunk = lambda i: pl.ds(pl.multiple_of(i * TB, TB), TB)
    b_mix, gain, shift, b_down = (vec_ref[i : i + 1, :] for i in (2, 5, 6, 7))
    slots = 4

    if direct:
        flow_refs, (send, recv, kept) = refs[:-3], refs[-3:]
        place = z, r, c = position()
        plan = Plan(send, recv)
        used = 0

        def local(src, dst):
            nonlocal used
            used += 1
            slot = kept.at[used - 1]
            return lambda: pltpu.make_async_copy(src(), dst(), slot)

        own_rows, part = w_up.shape[1] // owners, w_down.shape[1] // owners
        up_of = lambda ref, f, o: ref.at[f, pl.ds(pl.multiple_of(o * own_rows, 32), own_rows)]
        down_of = lambda ref, f, o: ref.at[f, pl.ds(pl.multiple_of(o * part, 32), part)]
        loads, pieces = [], {}
        for tag, source, whole, of, piece, side in (
            ("up", wup_any, w_up, up_of, up_piece, up_side),
            ("down", wdown_any, w_down, down_of, down_piece, down_side),
        ):
            for o in range(owners):
                loads.append(local(lambda o=o, s=source: s.at[0, o], lambda o=o, w=whole, of=of: of(w, 0, o)))
            for f in range(1, steps):
                loads.append(
                    local(lambda f=f, s=source: s.at[f, z], lambda f=f, w=whole, of=of: of(w, f, z))
                )
                pieces[tag, f] = [
                    local(
                        lambda f=f, j=j, s=source, p=piece: p(s.at[f, lax.rem(z + j, owners)], c, r),
                        lambda f=f, j=j, w=whole, of=of, p=piece: p(of(w, f, lax.rem(z + j, owners)), c, r),
                    )
                    for j in range(1, owners)
                ]
                spread_plan(
                    plan, (tag, f), owners, reps, z, r, c, None,
                    lambda o, p, f=f, w=whole, of=of, piece=piece: piece(of(w, f, o), c, p),
                    row_halves,
                    lambda o, f=f, w=whole, of=of, side=side: side(of(w, f, o), c),
                )
        flows, leaving, at = [], [], 0
        for i, (ref, out) in enumerate(((gdown_ref, down_out), (gup_ref, up_out))):
            wide = ref.shape[-1] // 2
            up_step = ref.shape[-1] // owners
            for s in range(2):
                mine, theirs, *hops = flow_refs[at : at + 6]
                at += 6
                cols, final = pl.ds(s * wide, wide), hops[-1]
                if i == 1:
                    places = []
                    for k in range(wide // up_step):
                        to = pl.ds((s * wide // up_step + k) * steps * up_step, up_step)
                        places.append((
                            lambda final=final, k=k: final.at[:, :, :, pl.ds(k * up_step, up_step)],
                            lambda out=out, to=to: out.at[:, :, :, to],
                        ))
                else:
                    places = [(lambda final=final: final, lambda out=out, cols=cols: out.at[0, :, :, :, cols])]
                copies = [local(src, dst) for src, dst in places]
                leaving.extend(copies)
                flows.append(
                    Flow(
                        plan, (i, s), place, owners, (1, 2) if s == 0 else (2, 1), mine, theirs, hops,
                        lambda final, copies=copies: [f() for f in copies],
                        local(lambda ref=ref, cols=cols: ref.at[0, :, c, :, :, cols], lambda mine=mine: mine),
                        lambda ref=ref, cols=cols: ref.at[0, :, 1 - c, :, :, cols],
                    )
                )
    else:
        kept = refs[0]
        loads = [
            lambda: pltpu.make_async_copy(wup_any, w_up, kept.at[0]),
            lambda: pltpu.make_async_copy(wdown_any, w_down, kept.at[1]),
        ]

    def between(slot, here=True):
        if not direct:
            return
        for k in range(steps):
            some = [lambda t=t, n=n: spread_step(plan, t, owners, n) for when, t, n in GATHERS if when == k * slots + slot]
            some += [lambda g=g, n=n: [flow.step(n) for flow in flows[2 * g : 2 * g + 2]] for when, g, n in SUMS if when == k * slots + slot]
            if some:

                @pl.when((step == k) & here)
                def _():
                    for act in some:
                        act()

    @pl.when(step == 0)
    def _():
        for copy in loads:
            copy().start()
        if direct:
            for some in pieces.values():
                for copy in some:
                    copy().start()
            greet(owners, reps)
            for f in range(1, steps):
                for tag in ("up", "down"):
                    for copy in pieces[tag, f]:
                        copy().wait()
                    if f == 1:
                        spread_step(plan, (tag, f), owners, 1)
        gvec_ref[...] = jnp.zeros_like(gvec_ref)

        def prepare(i, _):
            at = chunk(i)
            mixed = mixed_ref[at]
            mixed_t[:, at] = jnp.transpose(mixed)
            mid = x_ref[at].astype(F32) + (dot_nn(mixed, wmix_ref[...]) + b_mix)
            middle[at] = mid
            out_sum[at] = mid + b_down
            ds_sum[at] = jnp.zeros_like(mid)
            normal, _ = norm_stats(mid)
            low = (normal * gain + shift).astype(BF16)
            second[at] = low
            second_t[:, at] = jnp.transpose(low)
            return 0

        lax.fori_loop(0, count, prepare, 0)
        for copy in loads:
            copy().wait()

    between(0)

    def feed(i, d_bup):
        at = chunk(i)
        act, slope = gelu_parts(dot_nn(second[at], w_up[step]) + bup_ref[0])
        act = act.astype(BF16)
        active_t[:, at] = jnp.transpose(act)
        db = (dot_nt(d_ref[at], w_down[step]) * slope).astype(BF16)
        d_before[at] = db
        out_sum[at] += dot_nn(act, w_down[step])
        ds_sum[at] += dot_nt(db, w_up[step])
        between(1, i == count // 2 - 1)
        return d_bup + jnp.sum(db.astype(F32), axis=0, keepdims=True)

    d_bup = lax.fori_loop(0, count, feed, jnp.zeros(bup_ref.shape[1:], F32))
    between(2)

    width = d_bup.shape[1] // owners
    for k in range(owners):
        gvec_ref[8 + k : 9 + k, slab(step, width)] = d_bup[:, k * width : (k + 1) * width]
    if direct:

        @pl.when(step == 1)
        def _():
            plan.leave(*[(flow.name, "core") for flow in flows])

    share = second_t.shape[0] // owners
    part = active_t.shape[0] // owners

    def weights(o, _):
        lines = pl.ds(pl.multiple_of(o * part, part), part)
        gdown_ref[0, o] = dot_nn(active_t[lines], d_ref[...]).reshape(gdown_ref.shape[2:]).astype(BF16)
        lines = pl.ds(pl.multiple_of(o * share, 64), share)
        gup_ref[0, o] = dot_nn(second_t[lines], d_before[...]).reshape(gup_ref.shape[2:]).astype(BF16)
        return 0

    lax.fori_loop(0, owners, weights, 0)
    between(slots - 1)

    @pl.when(step == last)
    def _():

        def finish(i, sums):
            at = chunk(i)
            result_ref[at] = out_sum[at].astype(BF16)
            normal, inverse = norm_stats(middle[at])
            ds = ds_sum[at]
            grad_out = d_ref[at].astype(F32)
            d_mid = grad_out + norm_back(ds, normal, inverse, gain)
            dmid_ref[at] = d_mid
            branch = d_mid.astype(BF16)
            second[at] = branch
            dmixed_ref[at] = dot_nt(branch, wmix_ref[...]).astype(BF16)
            parts = (branch.astype(F32), ds * normal, ds, grad_out)
            return tuple(s + jnp.sum(p, axis=0, keepdims=True) for s, p in zip(sums, parts))

        zero = jnp.zeros((1, x_ref.shape[1]), F32)
        sums = lax.fori_loop(0, count, finish, (zero,) * 4)
        for i, k in enumerate((2, 5, 6, 7)):
            gvec_ref[k : k + 1, :] = sums[i]

        def mix(o, _):
            lines = pl.ds(pl.multiple_of(o * share, 64), share)
            gmix_ref[o] = dot_nn(mixed_t[lines], second[...]).reshape(gmix_ref.shape[1:]).astype(BF16)
            return 0

        lax.fori_loop(0, owners, mix, 0)
        if direct:
            for when, g, n in SUMS:
                if when >= steps * slots:
                    for flow in flows[2 * g : 2 * g + 2]:
                        flow.step(n)
            plan.close()
            for copy in leaving:
                copy().wait()


def middle_block(x, mixed, d_out, w_mix, w_up, w_down, vecs, b_up, owners, reps, direct):
    rows, width = x.shape
    steps = w_up.shape[0]
    ff = steps * owners * FP
    whole = lambda shape: pl.BlockSpec(shape, lambda f: (0,) * len(shape), pipeline_mode=pl.Buffered(1))
    anywhere = pl.BlockSpec(memory_space=pl.ANY)
    out = jax.ShapeDtypeStruct
    vmem = pltpu.VMEM
    side = (owners, 2, reps)
    g_mix = side + (width // owners // 2 // reps, width)
    given = steps - 1 if direct else steps
    g_up = (given,) + g_mix[:-1] + (owners * FP,)
    g_down = (given,) + side + (FP // 2 // reps, width)
    skip = steps - given
    per_step = lambda s: pl.BlockSpec((1,) + s[1:], lambda f: (jnp.maximum(f - skip, 0),) + (0,) * (len(s) - 1))
    scratch = [
        vmem((rows, width), F32),
        vmem((rows, width), BF16),
        vmem((width, rows), BF16),
        vmem((width, rows), BF16),
        vmem((rows, width), F32),
        vmem((rows, width), F32),
        vmem((owners * FP, rows), BF16),
        vmem((rows, owners * FP), BF16),
        vmem((steps, width, owners * FP), BF16),
        vmem((steps, owners * FP, width), BF16),
    ]
    finished = []
    if direct:
        finished = [out((steps,) + g_down[2:], BF16), out(g_up[2:5] + (steps * g_up[5],), BF16)]
        for g in (g_down, g_up):
            for _ in range(2):
                scratch += flow_scratch(owners, reps, (g[4], g[5] // 2), True)
        remotes = (steps - 1) * 2 * 15 + 4 * 11
        scratch += [pltpu.SemaphoreType.DMA((remotes,))] * 2 + [pltpu.SemaphoreType.DMA((2 * owners + 2 * (steps - 1) * owners + 10,))]
        params = dict(collective_id=3, has_side_effects=True)
    else:
        scratch += [pltpu.SemaphoreType.DMA((2,))]
        params = {}
    return pl.pallas_call(
        partial(middle_kernel, owners, reps, direct),
        grid=(steps,),
        in_specs=[whole((rows, width))] * 3
        + [whole((width, width)), anywhere, anywhere, whole(vecs.shape), pl.BlockSpec((1, 1, owners * FP), lambda f: (f, 0, 0))],
        out_specs=[
            whole((rows, width)),
            whole((rows, width)),
            whole((rows, width)),
            whole(g_mix),
            per_step(g_up),
            per_step(g_down),
            whole((16, width)),
        ]
        + [anywhere] * len(finished),
        out_shape=[
            out((rows, width), BF16),
            out((rows, width), F32),
            out((rows, width), BF16),
            out(g_mix, BF16),
            out(g_up, BF16),
            out(g_down, BF16),
            out((16, width), F32),
        ]
        + finished,
        scratch_shapes=scratch,
        compiler_params=pltpu.CompilerParams(vmem_limit_bytes=62 << 20, **params),
        cost_estimate=pl.CostEstimate(
            flops=12 * rows * width * ff + 6 * rows * width * width,
            bytes_accessed=8 * width * ff + 16 * rows * width,
            transcendentals=rows * ff,
        ),
        name="middle_block",
    )(x, mixed, d_out, w_mix, w_up, w_down, vecs, b_up)


def backward_kernel(
    owners, reps, pairs, factor, size, shapes, done,
    q_ref, k_ref, v_ref, lse_ref, x_ref, vec_ref, gvec_ref, dmid_ref, dmixed_ref, first_t_ref, w_ref, *refs
):
    n_in = len(shapes)
    sources, refs = refs[:n_in], refs[n_in + 2 :]
    dtok_ref, vec_out, refs = refs[0], refs[1], refs[2:]
    outs, refs = refs[: n_in + 1], refs[n_in + 1 :]
    d_heads, d_joined, first_t, w_pairs, df_send, df_recv, dk_sum, dv_sum, b_sum, vec_one, vec_got, vec_sum, refs = (
        refs[:12] + (refs[12:],)
    )
    flow_refs, (send, recv, kept) = refs[:-3], refs[-3:]
    step = pl.program_id(0)
    last = pl.num_programs(0) - 1
    place = z, r, c = position()
    mbs, rows, width = x_ref.shape
    half = width // 2
    lanes = 2 * size
    plan = Plan(send, recv)
    own_rows = pl.ds(pl.multiple_of(c * rows, rows), rows)

    locals_used = 0

    def local(src, dst):
        nonlocal locals_used
        locals_used += 1
        slot = kept.at[locals_used - 1]
        return lambda: pltpu.make_async_copy(src(), dst(), slot)

    up_step = shapes[1][-1] // owners
    flows, leaving, at = [], [], 0

    def add_flow(name, bits, mine, theirs, hops, places, load=None, core=None):
        final = hops[-1]
        copies = [local(partial(part, final), dst) for part, dst in places]
        leaving.extend(copies)
        flows.append(
            Flow(plan, name, place, owners, bits, mine, theirs, hops, lambda final: [f() for f in copies], load, core)
        )

    for i, shape in enumerate(shapes):
        for f in range(shape[0]):
            wide = shape[-1] // 2
            for s in range(2):
                mine, theirs, *hops = flow_refs[at : at + 6]
                at += 6
                source, out, cols = sources[i], outs[i], pl.ds(s * wide, wide)
                if i == 1:
                    places = []
                    for k in range(wide // up_step):
                        to = pl.ds(((s * wide // up_step + k) * (shape[0] + done) + done + f) * up_step, up_step)
                        places.append((
                            lambda final, k=k: final.at[:, :, :, pl.ds(k * up_step, up_step)],
                            lambda out=out, to=to: out.at[:, :, :, to],
                        ))
                else:
                    skip = done if i == 0 else 0
                    places = [(lambda final: final, lambda out=out, f=f + skip, cols=cols: out.at[f, :, :, :, cols])]
                add_flow(
                    (i, f, s), (1, 2) if s == 0 else (2, 1), mine, theirs, hops, places,
                    local(lambda source=source, f=f, cols=cols: source.at[f, :, c, :, :, cols], lambda mine=mine: mine),
                    lambda source=source, f=f, cols=cols: source.at[f, :, 1 - c, :, :, cols],
                )
    for p in range(pairs):
        for s in range(2):
            mine, *hops = flow_refs[at : at + 5]
            at += 5
            places = []
            for side in range(2):
                for i in range(3):
                    to = pl.ds((i * 2 * pairs + side * pairs + p) * lanes, lanes)
                    places.append((
                        lambda final, side=side, i=i: final.at[side, :, :, pl.ds(i * lanes, lanes)],
                        lambda s=s, to=to: outs[-1].at[:, s, :, to],
                    ))
            add_flow((n_in, p, s), (1, 2) if s == 0 else (2, 1), mine, None, hops, places)
    groups = [flows[i : i + 2] for i in range(0, len(flows), 2)]
    products = len(groups) - pairs
    ff_steps = shapes[0][0]
    groups[: 2 * ff_steps] = [groups[k * ff_steps + f] for f in range(ff_steps) for k in range(2)]

    def advance(group, stage):
        for flow in groups[group]:
            flow.step(stage)

    for m in range(mbs):
        for p in range(pairs):
            plan.add(
                ("heads", m, p),
                lambda m=m, p=p: dmixed_ref.at[m, :, slab((1 - c) * pairs + p, lanes)],
                lambda m=m, p=p: d_heads.at[p, m, own_rows],
                {"ctx": 1 - c},
            )
        plan.add(("first", m), lambda m=m: df_send.at[m], lambda m=m: df_recv.at[m], {"ctx": 1 - c})
    for i, peer in enumerate([{"ctx": 1 - c}, {"rep": r ^ 1}, {"rep": r ^ 2}]):
        plan.add(("vec", i), lambda i=i: vec_sum.at[i], lambda i=i: vec_got.at[i], peer)
    for j in range(1, owners):
        plan.add(
            ("vec", "z", j), lambda: vec_sum.at[3], lambda j=j: vec_got.at[2 + j], {"fsdp": lax.rem(z + j, owners)}
        )

    def own_heads(m, p):
        return pltpu.make_async_copy(
            dmixed_ref.at[m, :, slab(c * pairs + p, lanes)], d_heads.at[p, m, own_rows], kept.at[locals_used + m * pairs + p]
        )

    def load_first():
        return pltpu.make_async_copy(first_t_ref, first_t, kept.at[locals_used + mbs * pairs])

    def load_weight(i, p):
        return pltpu.make_async_copy(
            w_ref.at[:, pl.ds((i * pairs + p) * lanes, lanes)],
            w_pairs.at[p, :, pl.ds(i * lanes, lanes)],
            kept.at[locals_used + mbs * pairs + 1 + i * pairs + p],
        )

    @pl.when(step == 0)
    def _():
        greet(owners, reps)
        for p in range(pairs):
            for m in range(mbs):
                plan.start(("heads", m, p))
                own_heads(m, p).start()
        for g in range(products):
            advance(g, 0)
        load_first().start()
        for i in range(3):
            for p in range(pairs):
                load_weight(i, p).start()
        for p in range(pairs):
            for m in range(mbs):
                plan.arrive(("heads", m, p))
                own_heads(m, p).wait()

    table = timetable(products, pairs)
    quarters = 2 * rows // QB
    tail = [entry for entry in table if entry[0] >= quarters * mbs * pairs]

    def between(k, done):
        for i in range(mbs * pairs):
            some = [entry for entry in table if entry[0] == quarters * i + done]
            if some:

                @pl.when(k == i)
                def _():
                    for _, group, stage in some:
                        advance(group, stage)

    def weight_grad(p):
        grad = dot_nn(first_t[...], d_joined[p])
        piece = groups[products][0].mine.shape[2]
        grad = grad.reshape(owners, reps, 2 * piece, grad.shape[1])
        for s in range(2):
            groups[products + p][s].mine[...] = grad[:, :, s * piece : (s + 1) * piece].astype(BF16)

    for p in range(pairs):

        @pl.when(step == mbs * (p + 1))
        def _():
            if p == 0:
                load_first().wait()
            weight_grad(p)
            advance(products + p, 1)

    @pl.when(step < last)
    def _():
        p, m = lax.div(step, mbs), lax.rem(step, mbs)
        start = pl.multiple_of(m * 2 * rows, 2 * rows)
        joined = d_joined.at[p, pl.ds(start, 2 * rows)]
        attention_backward_block(
            factor, size, q_ref.at[0, 0], k_ref.at[0, 0], v_ref.at[0, 0], d_heads.at[p, m], lse_ref.at[m, p],
            joined.at[:, pl.ds(0, lanes)], joined.at[:, pl.ds(lanes, lanes)], joined.at[:, pl.ds(2 * lanes, lanes)],
            dk_sum, dv_sum, partial(between, step),
        )
        for i, k in enumerate((0, 2)):
            part = jnp.sum(joined[:, k * lanes : (k + 1) * lanes].astype(F32), axis=0, keepdims=True)
            before = b_sum[p, i : i + 1, :]
            b_sum[p, i : i + 1, :] = part + jnp.where(m == 0, jnp.zeros_like(before), before)

    def first_part(m, at):
        total = None
        for p in range(pairs):
            term = dot_nt(d_joined[p, pl.ds(pl.multiple_of(m * 2 * rows + at, TB), TB)], w_pairs[p])
            total = term if total is None else total + term
        return total

    @pl.when(step == last)
    def _():
        for i in range(3):
            for p in range(pairs):
                load_weight(i, p).wait()
        gain = vec_ref[3:4, :]
        steps = rows // TB

        def theirs(i, _):
            m, at = lax.div(i, steps), lax.rem(i, steps) * TB
            df_send[m, pl.ds(pl.multiple_of(at, TB), TB)] = first_part(m, (1 - c) * rows + at).astype(BF16)
            return 0

        def go(until):
            while tail and tail[0][0] < until:
                _, group, stage = tail.pop(0)
                advance(group, stage)

        lax.fori_loop(0, mbs * steps, theirs, 0)
        for m in range(mbs):
            plan.start(("first", m))
        go(28)
        for m in range(mbs):
            plan.arrive(("first", m))

        def mine(i, sums):
            m, at = lax.div(i, steps), lax.rem(i, steps) * TB
            here = pl.ds(pl.multiple_of(at, TB), TB)
            total = first_part(m, c * rows + at) + df_recv[m, here].astype(F32)
            normal, inverse = norm_stats(x_ref[m, here].astype(F32))
            dtok_ref[m, here] = dmid_ref[m, here] + norm_back(total, normal, inverse, gain)
            gains = jnp.sum(total * normal, axis=0, keepdims=True)
            return (sums[0] + gains, sums[1] + jnp.sum(total, axis=0, keepdims=True))

        zero = jnp.zeros((1, width), F32)
        g_gain, g_shift = lax.fori_loop(0, mbs * steps, mine, (zero, zero))
        vec_one[...] = gvec_ref[...]
        vec_one[3:4, :] = g_gain
        vec_one[4:5, :] = g_shift
        for p in range(pairs):
            for i in range(2):
                vec_one[i : i + 1, slab(c * pairs + p, lanes)] = b_sum[p, i : i + 1, :]
        vec_sum[0] = vec_one[...]
        plan.start(("vec", 0))
        for i in range(3):
            go(36 + 2 * i)
            plan.arrive(("vec", i))
            vec_sum[i + 1] = vec_sum[i] + vec_got[i]
            if i < 2:
                plan.start(("vec", i + 1))
        plan.start(*[("vec", "z", j) for j in range(1, owners)])
        go(42)
        plan.arrive(*[("vec", "z", j) for j in range(1, owners)])
        vec_out[...] = (vec_sum[3] + vec_got[3]) + (vec_got[4] + vec_got[5])
        go(1000)
        plan.close()
        for copy in leaving:
            copy().wait()


def backward_block(
    qkv, lse, x, vecs, gvec, d_middle, d_mixed, first_t, w_qkv, grads, finished, owners, reps, factor, size
):
    mbs, rows, width = x.shape
    lanes = 2 * size
    pairs = width // 2 // lanes
    shape = jax.ShapeDtypeStruct
    anywhere = pl.BlockSpec(memory_space=pl.ANY)
    whole = lambda s: pl.BlockSpec(s, lambda i: (0,) * len(s), pipeline_mode=pl.Buffered(1))
    final_step = mbs * pairs - 1

    def block(which):
        def index(i):
            k = jnp.minimum(i, final_step)
            return (lax.rem(k, mbs), which * pairs + lax.div(k, mbs), 0, 0)

        return pl.BlockSpec((1, 1, 2 * rows, lanes), index)

    pieces = [(g.shape[4], g.shape[5] // 2) for g in grads for _ in range(2 * g.shape[0])]
    q_piece = (width // owners // reps // 2, 3 * lanes)
    down, up, mix = (g.shape for g in grads)
    finals = [f.shape for f in finished] + [mix[:1] + mix[2:], (reps, 2, q_piece[0], 3 * width)]
    scratch = [s for p in pieces for s in flow_scratch(owners, reps, p, True)]
    scratch += [s for _ in range(2 * pairs) for s in flow_scratch(owners, reps, q_piece, False)]
    remotes = 11 * len(pieces) + 10 * 2 * pairs + mbs * pairs + mbs + 6
    vec = (16, width)
    dtok, vec_sum, *outs = pl.pallas_call(
        partial(backward_kernel, owners, reps, pairs, factor, size, [g.shape for g in grads], finished[0].shape[0] - down[0]),
        grid=(mbs * pairs + 1,),
        in_specs=[block(0), block(1), block(2), whole(lse.shape), whole(x.shape), whole(vec), whole(vec), whole(x.shape)]
        + [anywhere] * (3 + len(grads) + 2),
        input_output_aliases={11 + len(grads): 2, 12 + len(grads): 3},
        out_specs=[whole(x.shape), whole(vec)] + [anywhere] * len(finals),
        out_shape=[shape(x.shape, F32), shape(vec, F32)] + [shape(f, BF16) for f in finals],
        scratch_shapes=[
            pltpu.VMEM((pairs, mbs, 2 * rows, lanes), BF16),
            pltpu.VMEM((pairs, mbs * 2 * rows, 3 * lanes), BF16),
            pltpu.VMEM(first_t.shape, BF16),
            pltpu.VMEM((pairs, width, 3 * lanes), BF16),
            pltpu.VMEM(x.shape, BF16),
            pltpu.VMEM(x.shape, BF16),
            pltpu.VMEM((2 * rows, lanes), F32),
            pltpu.VMEM((2 * rows, lanes), F32),
            pltpu.VMEM((pairs, 8, lanes), F32),
            pltpu.VMEM(vec, F32),
            pltpu.VMEM((6,) + vec, F32),
            pltpu.VMEM((4,) + vec, F32),
        ]
        + scratch
        + [
            pltpu.SemaphoreType.DMA((remotes,)),
            pltpu.SemaphoreType.DMA((remotes,)),
            pltpu.SemaphoreType.DMA((len(pieces) * 3 + 12 * pairs + mbs * pairs + 1 + 3 * pairs,)),
        ],
        compiler_params=pltpu.CompilerParams(
            collective_id=2, has_side_effects=True, vmem_limit_bytes=63 << 20
        ),
        name="backward_block",
    )(qkv, qkv, qkv, lse, x, vecs, gvec, d_middle, d_mixed, first_t, w_qkv, *grads, *finished)
    return dtok, vec_sum, outs


def local(
    inputs,
    weight_qkv,
    bias_query,
    bias_value,
    weight_mix,
    bias_mix,
    gain_attn,
    shift_attn,
    gain_mlp,
    shift_mlp,
    weight_up,
    bias_up,
    weight_down,
    bias_down,
    cotangent,
):
    width = weight_qkv.shape[1] // 3
    half = width // 2
    size = width // H
    factor = size ** (-0.5)
    rows = inputs.shape[2]
    owners = lax.axis_size("fsdp")
    reps = lax.axis_size("rep")
    ctx = lax.axis_index("ctx")
    rep = lax.axis_index("rep")
    own = weight_qkv.shape[0]
    b_up_rows = bias_up.shape[0]
    direct = own % (16 * reps) == 0 and owners == 4 and reps == 4

    def swap(x):
        return lax.ppermute(x, "ctx", [(0, 1), (1, 0)])

    def order(mine, other, axis):
        return jnp.where(
            ctx == 0,
            jnp.concatenate([mine, other], axis=axis),
            jnp.concatenate([other, mine], axis=axis),
        )

    def columns(x, axis, which):
        return lax.dynamic_slice_in_dim(x, which * half, half, axis)

    direct = own % (16 * reps) == 0 and owners == 4 and reps == 4
    vectors = [bias_query, bias_value, bias_mix, gain_attn, shift_attn, gain_mlp, shift_mlp, bias_down]
    tokens = inputs[:, 0].astype(F32)
    if direct:
        mixed, qkv, first_t, w_qkv, w_mix, w_up, w_down, vecs, b_up, lse = forward_block(
            inputs[:, 0],
            weight_qkv,
            weight_mix,
            weight_up,
            weight_down,
            vectors,
            bias_up,
            owners,
            reps,
            factor,
            size,
        )
    else:
        part = own // reps
        mine = lax.dynamic_slice_in_dim(weight_qkv, rep * part, part, 0)
        mine = jnp.concatenate([columns(mine[:, i * width : (i + 1) * width], 1, ctx) for i in range(3)], axis=1)
        w_qkv = lax.all_gather(mine, ("fsdp", "rep"), axis=0, tiled=True)

        def gather(shard):
            piece = shard.shape[0] // (2 * reps)
            mine = lax.dynamic_slice_in_dim(shard, (rep * 2 + ctx) * piece, piece, 0)
            return lax.all_gather(mine, ("fsdp", "rep", "ctx"), axis=0, tiled=True)

        w_mix = gather(weight_mix)
        w_up = gather(weight_up)
        w_down = gather(weight_down)
        vecs = lax.all_gather(jnp.stack(vectors).astype(F32), "fsdp", axis=1, tiled=True)
        b_up = lax.all_gather(bias_up.astype(F32), "fsdp", axis=0, tiled=True)
        b_up = b_up.reshape(SHARES, -1, FP).swapaxes(0, 1)
        b_up = b_up.reshape(b_up.shape[0], 1, -1)
        w_up = w_up.reshape(width, SHARES, -1, FP).transpose(2, 0, 1, 3).reshape(-1, width, SHARES * FP)
        w_down = w_down.reshape(SHARES, -1, FP, width).swapaxes(0, 1).reshape(-1, SHARES * FP, width)
    b_query, b_value, g_attn, s_attn = (vecs[i] for i in (0, 1, 3, 4))

    if not direct:
        normal_one, inverse_one = norm_stats(tokens)
        first_own = (normal_one * g_attn + s_attn).astype(BF16)
        first = order(first_own, swap(first_own), 1)
        joined = project(first, w_qkv)
        query = (joined[..., :half] + columns(b_query, 0, ctx)).astype(BF16)
        key = joined[..., half : 2 * half].astype(BF16)
        value = (joined[..., 2 * half :] + columns(b_value, 0, ctx)).astype(BF16)
        mixed_heads, lse = attention_forward(query, key, value, factor, size)

    def my_rows(x):
        return lax.dynamic_slice_in_dim(x, ctx * rows, rows, 1)

    def their_rows(x):
        return lax.dynamic_slice_in_dim(x, (1 - ctx) * rows, rows, 1)

    if not direct:
        mixed = order(my_rows(mixed_heads), swap(their_rows(mixed_heads)), 2)
    flat = (-1, width)
    d_out = cotangent.reshape(flat)
    result, d_middle, d_mixed, g_wmix, g_wup, g_wdown, gvec, *finished = middle_block(
        inputs.reshape(flat),
        mixed.reshape(flat),
        d_out,
        w_mix,
        w_up,
        w_down,
        vecs,
        b_up,
        SHARES,
        reps,
        direct,
    )
    steps = b_up.shape[0]
    if direct:
        d_tokens, summed, outs = backward_block(
            qkv, lse, inputs[:, 0], vecs, gvec, d_middle.reshape(tokens.shape), d_mixed.reshape(tokens.shape),
            first_t, w_qkv, [g_wdown, g_wup, g_wmix[None]], finished, owners, reps, factor, size,
        )
        o_wdown, o_wup, o_wmix, o_wqkv = (
            o.reshape(-1, n).astype(F32) for o, n in zip(outs, (width, SHARES * steps * FP, width, 3 * width))
        )
    else:
        d_mixed = d_mixed.reshape(tokens.shape)
        d_middle = d_middle.reshape(tokens.shape)
        d_heads = order(columns(d_mixed, 2, ctx), swap(columns(d_mixed, 2, 1 - ctx)), 1)
        d_query, d_key, d_value = attention_backward(query, key, value, d_heads, lse, factor, size)
        d_joined = jnp.concatenate([d_query, d_key, d_value], axis=-1)
        g_wqkv = outer_sum(first, d_joined)
        d_first = project_back(d_joined, w_qkv)
        d_first = my_rows(d_first) + swap(their_rows(d_first).astype(BF16)).astype(F32)
        normal_one, inverse_one = norm_stats(tokens)
        d_tokens = d_middle + norm_back(d_first, normal_one, inverse_one, g_attn)

        def reduce(grad):
            piece = lax.psum_scatter(
                grad.astype(BF16), ("fsdp", "rep", "ctx"), scatter_dimension=0, tiled=True
            )
            return lax.all_gather(piece, ("rep", "ctx"), axis=0, tiled=True).astype(F32)

        g_wdown = jnp.concatenate([g_wdown[f].reshape(SHARES, FP, width) for f in range(steps)], axis=1)
        o_wdown = reduce(g_wdown.reshape(-1, width))
        g_wup = jnp.stack([g_wup[f].reshape(width, SHARES, FP) for f in range(steps)], axis=2)
        o_wup = reduce(g_wup.reshape(width, -1))
        o_wmix = reduce(g_wmix.reshape(width, width))
        piece = lax.psum_scatter(g_wqkv.astype(BF16), ("fsdp", "rep"), scatter_dimension=0, tiled=True)
        piece = lax.all_gather(piece, "rep", axis=0, tiled=True)
        other = swap(piece)
        low, high = jnp.where(ctx == 0, piece, other), jnp.where(ctx == 0, other, piece)
        o_wqkv = jnp.concatenate(
            [t for i in range(3) for t in (low[:, i * half : (i + 1) * half], high[:, i * half : (i + 1) * half])],
            axis=1,
        ).astype(F32)

        def place(v):
            return lax.dynamic_update_slice_in_dim(jnp.zeros((width,), F32), v, ctx * half, 0)

        first_rows = (
            place(jnp.sum(d_query.astype(F32), axis=(0, 1))),
            place(jnp.sum(d_value.astype(F32), axis=(0, 1))),
            jnp.sum(d_first * normal_one, axis=(0, 1)),
            jnp.sum(d_first, axis=(0, 1)),
        )
        summed = jnp.concatenate([jnp.stack(first_rows[:2]), gvec[2:3], jnp.stack(first_rows[2:]), gvec[5:12]], axis=0)
        summed = lax.psum(summed, ("rep", "fsdp", "ctx"))
    owner = lax.axis_index("fsdp")
    o_bup = lax.dynamic_slice_in_dim(summed[8 : 8 + SHARES].reshape(-1), owner * b_up_rows, b_up_rows, 0)
    summed = lax.dynamic_slice_in_dim(summed[:8], owner * own, own, 1)
    o_bq, o_bv, o_bmix, o_ga, o_sa, o_gm, o_sm, o_bd = (summed[i] for i in range(8))
    return (
        result.reshape(inputs.shape),
        d_tokens[:, None],
        o_wqkv,
        o_bq,
        o_bv,
        o_wmix,
        o_bmix,
        o_ga,
        o_sa,
        o_gm,
        o_sm,
        o_wup,
        o_bup,
        o_wdown,
        o_bd,
    )


def solution(mesh):
    row = P(None, ("rep", "fsdp"), "ctx", None)
    mat = P("fsdp", None)
    vec = P("fsdp")
    params = (mat, vec, vec, mat, vec, vec, vec, vec, vec, mat, vec, mat, vec)
    in_specs = (row,) + params + (row,)
    out_specs = (row, row) + params
    return jax.shard_map(local, mesh=mesh, in_specs=in_specs, out_specs=out_specs, check_vma=False)
```

```python
from functools import partial

import jax
import jax.numpy as jnp
from jax import lax
from jax.experimental import pallas as pl
from jax.experimental.pallas import tpu as pltpu
from jax.sharding import PartitionSpec as P

H = 12
EPS = 1e-05
BF16 = jnp.bfloat16
F32 = jnp.float32
QB = 256
TB = 256
RB = 512
FP = 256
SHARES = 4
GELU_A = 0.7978845608028654
GELU_B = 0.044715
LOG2E = 1.4426950408889634


def norm_stats(values):
    center = values - jnp.mean(values, axis=-1, keepdims=True)
    inverse = lax.rsqrt(jnp.mean(center * center, axis=-1, keepdims=True) + EPS)
    return (center * inverse, inverse)


def norm_back(grad_norm, normal, inverse, gain):
    scaled = grad_norm * gain
    return inverse * (
        scaled
        - jnp.mean(scaled, axis=-1, keepdims=True)
        - normal * jnp.mean(scaled * normal, axis=-1, keepdims=True)
    )


def outer_sum(left, right):
    return jnp.einsum("sri,srj->ij", left, right, preferred_element_type=F32)


def project(left, weight):
    return jnp.einsum("sri,ij->srj", left, weight, preferred_element_type=F32)


def project_back(grad_rows, weight):
    return jnp.einsum("srj,ij->sri", grad_rows, weight, preferred_element_type=F32)


def dot_nt(a, b):
    return lax.dot_general(a, b, (((1,), (1,)), ((), ())), preferred_element_type=F32)


def dot_nn(a, b):
    return lax.dot_general(a, b, (((1,), (0,)), ((), ())), preferred_element_type=F32)


def head_mask(x, head, size):
    lane = lax.broadcasted_iota(jnp.int32, x.shape, 1)
    keep = (lane >= head * size) & (lane < (head + 1) * size)
    return jnp.where(keep, x, jnp.zeros_like(x))


def causal(scores_t, qb):
    n = scores_t.shape[0]
    bottom = scores_t[n - QB :]
    key = lax.broadcasted_iota(jnp.int32, bottom.shape, 0)
    query = lax.broadcasted_iota(jnp.int32, bottom.shape, 1)
    bottom = jnp.where(key <= query, bottom, -1e30)
    return bottom if n == QB else jnp.concatenate([scores_t[: n - QB], bottom], axis=0)


def attention_forward_kernel(factor, size, q_ref, k_ref, v_ref, o_ref, lse_ref):
    refs = [ref.at[0] for ref in (q_ref, k_ref, v_ref, o_ref)]
    attention_forward_block(factor, size, *refs, lse_ref.at[0, 0], lambda done: None)


def attention_forward_block(factor, size, q_ref, k_ref, v_ref, o_ref, lse_ref, between):
    length = q_ref.shape[0]
    base_two = factor * LOG2E
    k = k_ref[...]
    vt = jnp.transpose(v_ref[...])
    for qb in range(length // QB):
        n = (qb + 1) * QB
        rows = pl.ds(qb * QB, QB)
        q = q_ref[rows, :]
        outs = []
        for head in range(2):
            s = causal(dot_nt(k[:n], head_mask(q, head, size)), qb)
            top = jnp.max(s, axis=0, keepdims=True) * base_two
            p = jnp.exp2(s * base_two - top)
            total = jnp.sum(p, axis=0, keepdims=True)
            o = dot_nn(vt[head * size : (head + 1) * size, :n], p.astype(BF16))
            outs.append(o * (1.0 / total))
            lse_ref[head : head + 1, rows] = top + jnp.log2(total)
        o_ref[rows, :] = jnp.transpose(jnp.concatenate(outs, axis=0)).astype(o_ref.dtype)
        between(qb)


def attention_forward(q, k, v, factor, size):
    mbs, length, width = q.shape
    lanes = 2 * size
    pairs = width // lanes
    block = pl.BlockSpec((1, length, lanes), lambda m, p: (m, 0, p))
    area = mbs * pairs * 2 * length * (length + QB) // 2
    return pl.pallas_call(
        partial(attention_forward_kernel, factor, size),
        grid=(mbs, pairs),
        in_specs=[block] * 3,
        out_specs=[block, pl.BlockSpec((1, 1, 8, length), lambda m, p: (m, p, 0, 0))],
        out_shape=[
            jax.ShapeDtypeStruct(q.shape, BF16),
            jax.ShapeDtypeStruct((mbs, pairs, 8, length), F32),
        ],
        compiler_params=pltpu.CompilerParams(vmem_limit_bytes=48 << 20),
        cost_estimate=pl.CostEstimate(
            flops=16 * area * size, bytes_accessed=8 * q.size, transcendentals=area
        ),
        name="attention_forward",
    )(q, k, v)


def attention_backward_kernel(factor, size, q_ref, k_ref, v_ref, do_ref, lse_ref, dq_ref, dk_ref, dv_ref, dk_sum, dv_sum):
    refs = [ref.at[0] for ref in (q_ref, k_ref, v_ref, do_ref)]
    attention_backward_block(
        factor, size, *refs, lse_ref.at[0, 0], dq_ref.at[0], dk_ref.at[0], dv_ref.at[0], dk_sum, dv_sum, lambda done: None
    )


def attention_backward_block(
    factor, size, q_ref, k_ref, v_ref, do_ref, lse_ref, dq_ref, dk_ref, dv_ref, dk_sum, dv_sum, between
):
    length = q_ref.shape[0]
    base_two = factor * LOG2E
    k = k_ref[...]
    v = v_ref[...]
    kt = jnp.transpose(k)
    for i, qb in enumerate(reversed(range(length // QB))):
        n = (qb + 1) * QB
        rows = pl.ds(qb * QB, QB)
        q = q_ref[rows, :]
        do = do_ref[rows, :]
        dqs, dk, dv = [], None, None
        for head in range(2):
            qh = head_mask(q, head, size)
            doh = head_mask(do, head, size)
            s = causal(dot_nt(k[:n], qh), qb)
            p = jnp.exp2(s * base_two - lse_ref[head : head + 1, rows])
            dp = dot_nt(v[:n], doh)
            mean = jnp.sum(dp * p, axis=0, keepdims=True)
            ds = (p * (dp - mean)).astype(BF16)
            dvh = dot_nn(p.astype(BF16), doh)
            dkh = dot_nn(ds, qh)
            dv = dvh if dv is None else dv + dvh
            dk = dkh if dk is None else dk + dkh
            dqs.append(dot_nn(kt[head * size : (head + 1) * size, :n], ds))
        dq_ref[rows, :] = jnp.transpose(jnp.concatenate(dqs, axis=0) * factor).astype(BF16)
        if n == length:
            dk_sum[...] = dk
            dv_sum[...] = dv
        else:
            dk_sum[:n] += dk
            dv_sum[:n] += dv
        between(i)
    dk_ref[...] = (dk_sum[...] * factor).astype(BF16)
    dv_ref[...] = dv_sum[...].astype(BF16)


def attention_backward(q, k, v, do, lse, factor, size):
    mbs, length, width = q.shape
    lanes = 2 * size
    pairs = width // lanes
    block = pl.BlockSpec((1, length, lanes), lambda m, p: (m, 0, p))
    area = mbs * pairs * 2 * length * (length + QB) // 2
    return pl.pallas_call(
        partial(attention_backward_kernel, factor, size),
        grid=(mbs, pairs),
        in_specs=[block] * 4 + [pl.BlockSpec((1, 1, 8, length), lambda m, p: (m, p, 0, 0))],
        out_specs=[block] * 3,
        out_shape=[jax.ShapeDtypeStruct(q.shape, BF16)] * 3,
        scratch_shapes=[pltpu.VMEM((length, lanes), F32)] * 2,
        compiler_params=pltpu.CompilerParams(vmem_limit_bytes=48 << 20),
        cost_estimate=pl.CostEstimate(
            flops=40 * area * size, bytes_accessed=14 * q.size, transcendentals=area
        ),
        name="attention_backward",
    )(q, k, v, do, lse)


MESH = pl.DeviceIdType.MESH


def position():
    return lax.axis_index("fsdp"), lax.axis_index("rep"), lax.axis_index("ctx")


def greet(owners, reps, across=False):
    z, r, c = position()
    barrier = pltpu.get_barrier_semaphore()
    peers = [{"fsdp": lax.rem(z + j, owners)} for j in range(1, owners)]
    peers += [{"rep": r ^ j} for j in range(1, reps)]
    peers += [{"ctx": 1 - c}]
    if across:
        peers += [{"rep": r ^ j, "ctx": 1 - c} for j in range(1, reps)]
    for peer in peers:
        pl.semaphore_signal(barrier, inc=1, device_id=peer, device_id_type=MESH)
    pl.semaphore_wait(barrier, len(peers))


def slab(i, half):
    return pl.ds(pl.multiple_of(i * half, 128), half)


def add_blocks(out, parts, dtype):
    lead = out.shape[:-2]
    count = 1
    for n in lead:
        count *= n

    def body(i, _):
        at = []
        for n in reversed(lead):
            at.append(lax.rem(i, n))
            i = lax.div(i, n)
        at = tuple(reversed(at))
        terms = [p[at].astype(F32) for p in parts]
        while len(terms) > 1:
            terms = [terms[0] + terms[1]] + terms[2:]
        out[at] = terms[0].astype(dtype)
        return 0

    lax.fori_loop(0, count, body, 0)


class Plan:
    def __init__(self, send, recv):
        self.send, self.recv = send, recv
        self.made, self.left = {}, set()

    def add(self, name, src, dst, peer):
        self.made[name] = (len(self.made), src, dst, peer)

    def copy(self, name):
        slot, src, dst, peer = self.made[name]
        return pltpu.make_async_remote_copy(
            src_ref=src(),
            dst_ref=dst(),
            send_sem=self.send.at[slot],
            recv_sem=self.recv.at[slot],
            device_id=peer,
            device_id_type=MESH,
        )

    def start(self, *names):
        for name in names:
            self.copy(name).start()

    def arrive(self, *names):
        for name in names:
            self.copy(name).wait_recv()

    def leave(self, *names):
        for name in names:
            self.copy(name).wait_send()
            self.left.add(name)

    def close(self):
        for name in self.made:
            if name not in self.left:
                self.copy(name).wait_send()


def spread_plan(plan, tag, owners, reps, z, r, c, src, dst, halves, core=None):
    for j in range(1, owners):
        origin = lax.rem(z - j + owners, owners)
        if src is not None:
            plan.add((tag, "z", j), src, lambda: dst(z, r), {"fsdp": lax.rem(z + j, owners)})
        here = partial(dst, origin, r)
        plan.add((tag, "x", j), here, here, {"rep": r ^ 1})
        plan.add((tag, "y", j), here, here, {"rep": r ^ 2})
        by_y = lambda origin=origin: halves(dst(origin, r ^ 2))[0]
        by_x = lambda origin=origin: halves(dst(origin, r ^ 1))[1]
        plan.add((tag, "xx", j), by_y, by_y, {"rep": r ^ 1})
        plan.add((tag, "yy", j), by_x, by_x, {"rep": r ^ 2})
        if core is not None:
            side = partial(core, origin)
            plan.add((tag, "c", j), side, side, {"ctx": 1 - c})


def spread_step(plan, tag, owners, stage):
    for j in range(1, owners):
        if stage == 0:
            plan.start((tag, "z", j))
        elif stage == 1:
            if (tag, "z", j) in plan.made:
                plan.arrive((tag, "z", j))
            plan.start((tag, "x", j), (tag, "y", j))
        elif stage == 2:
            plan.arrive((tag, "y", j))
            plan.start((tag, "xx", j))
            plan.arrive((tag, "x", j))
            plan.start((tag, "yy", j))
        elif stage == 3:
            plan.arrive((tag, "xx", j), (tag, "yy", j))
            if (tag, "c", j) in plan.made:
                plan.start((tag, "c", j))
        else:
            plan.arrive((tag, "c", j))


def up_side(ref, c):
    half = ref.shape[-1] // 2
    return ref.at[:, pl.ds(pl.multiple_of(c * half, 128), half)]


def up_piece(ref, c, r):
    return ref.at[:, pl.ds(pl.multiple_of((c * 4 + r) * 128, 128), 128)]


def down_side(ref, c):
    half = ref.shape[0] // 2
    return ref.at[pl.ds(pl.multiple_of(c * half, 32), half)]


def down_piece(ref, c, r):
    piece = ref.shape[0] // 8
    return ref.at[pl.ds(pl.multiple_of((c * 4 + r) * piece, 32), piece)]


def uneven_halves(ref):
    middle = ref.shape[1] // 256 * 128
    return ref.at[:, pl.ds(0, middle)], ref.at[:, pl.ds(middle, ref.shape[1] - middle)]


def row_halves(ref):
    middle = ref.shape[0] // 2
    return ref.at[pl.ds(0, middle)], ref.at[pl.ds(middle, middle)]


def column_halves(ref):
    middle = ref.shape[-1] // 2
    return ref.at[:, pl.ds(0, middle)], ref.at[:, pl.ds(middle, middle)]


SPREADS = [
    (-1, 0, 1), (-1, 1, 1), (2, 2, 1), (5, 0, 2), (9, 1, 2), (9, 0, 3), (14, 2, 2), (14, 1, 3), (15, 0, 4), (18, 1, 4),
    (19, 2, 3), (23, 2, 4),
]


def forward_kernel(owners, reps, pairs, factor, size,
                   x_ref, qkv_ref, mix_ref, up_ref, down_ref, *refs):
    vectors, b_up_ref, refs = refs[:8], refs[8], refs[9:]
    (mixed, qkv_out, first_t_out, w_qkv_out, w_mix, w_up, w_down, vec_ref, bup_ref, lse_ref, small_ref,
                   first, first_t, w_qkv, qkv, heads, small, own_mix, own_up, own_down, send, recv, kept) = refs
    step = pl.program_id(0)
    last = pl.num_programs(0) - 1
    z, r, c = position()
    mbs, rows, width = x_ref.shape
    half = width // 2
    lanes = 2 * size
    plan = Plan(send, recv)
    own_rows = pl.ds(pl.multiple_of(c * rows, rows), rows)
    their_rows = pl.ds(pl.multiple_of((1 - c) * rows, rows), rows)

    for j in range(1, owners):
        plan.add(("small", j), lambda: small_ref, lambda: small.at[z], {"fsdp": lax.rem(z + j, owners)})
    for m in range(mbs):
        plan.add(("first", m), lambda m=m: first.at[m, own_rows], lambda m=m: first.at[m, own_rows], {"ctx": 1 - c})
    for i in range(3):
        spread_plan(
            plan, ("qkv", i), owners, reps, z, r, c,
            lambda i=i: qkv_ref.at[r, :, slab(2 * i + c, half)],
            lambda o, p, i=i: w_qkv.at[o, p, :, slab(i, half)],
            uneven_halves,
        )
    steps = w_up.shape[0]
    spread_plan(
        plan, ("mix", 0), owners, reps, z, r, c,
        lambda: own_mix.at[c, r], lambda o, p: w_mix.at[o, c, p], column_halves, lambda o: w_mix.at[o, c],
    )
    for tag, own, whole, piece, side in (("up", own_up, w_up, up_piece, up_side), ("down", own_down, w_down, down_piece, down_side)):
        for f in range(steps):
            dst = lambda o, p, whole=whole, piece=piece, f=f: piece(whole.at[f, o], c, p)
            src = lambda own=own, piece=piece, f=f: piece(own.at[f], c, r)
            if f == 0:
                core = lambda o, whole=whole, side=side, f=f: side(whole.at[f, o], c)
                spread_plan(plan, (tag, f), owners, reps, z, r, c, src, dst, row_halves, core)
            else:
                for j in range(1, owners):
                    to = lax.rem(z + j, owners)
                    plan.add(((tag, f), "z", j), src, lambda dst=dst: dst(z, r), {"fsdp": to})
    quarters = 2 * rows // QB
    table = SPREADS
    order = [("mix", 0)] + [(tag, f) for f in range(steps) for tag in ("up", "down")]

    up_step = own_up.shape[-1] // owners
    pairs_of = [(small_ref, small.at[z])]
    pairs_of += [(qkv_ref.at[:, :, slab(2 * i + c, half)], w_qkv.at[z, :, :, slab(i, half)]) for i in range(3)]
    pairs_of += [(mix_ref, own_mix)]
    early = len(pairs_of)
    for f in range(steps):
        for k in range(owners):
            cols = pl.ds((k * (up_ref.shape[-1] // owners)) + f * up_step, up_step)
            pairs_of += [(up_ref.at[:, cols], own_up.at[f, :, pl.ds(k * up_step, up_step)])]
        pairs_of += [(down_ref.at[pl.ds(f * own_down.shape[1], own_down.shape[1])], own_down.at[f])]
    loads = len(pairs_of)
    pairs_of += [(own_mix, w_mix.at[z])]
    for f in range(steps):
        pairs_of += [(own_up.at[f], w_up.at[f, z]), (own_down.at[f], w_down.at[f, z])]
    stores = len(pairs_of)
    pairs_of += [(w_qkv, w_qkv_out), (first_t, first_t_out), (qkv, qkv_out)]
    ends = len(pairs_of)

    def keep(i):
        return pltpu.make_async_copy(*pairs_of[i], kept.at[i])

    def mixed_place(step):
        m, p = lax.div(step, pairs), lax.rem(step, pairs)
        return mixed.at[m, :, slab(c * pairs + p, lanes)]

    def mixed_sends(k, slot):
        return pltpu.make_async_remote_copy(
            src_ref=heads.at[k, their_rows],
            dst_ref=mixed_place(k),
            send_sem=send.at[slot],
            recv_sem=recv.at[slot],
            device_id={"ctx": 1 - c},
            device_id_type=MESH,
        )

    base = len(plan.made)

    @pl.when(step == 0)
    def _():
        for i in range(1, loads):
            keep(i).start()
        small_ref[...] = jnp.zeros_like(small_ref)
        own = vectors[0].shape[0]
        for i, vector in enumerate(vectors):
            small_ref[i : i + 1, :own] = vector[...].astype(F32).reshape(1, own)
        for f in range(steps):
            small_ref[8 + f : 9 + f, :] = b_up_ref[f * FP : (f + 1) * FP].astype(F32).reshape(1, FP)
        greet(owners, reps)
        keep(0).start()
        plan.start(*[("small", j) for j in range(1, owners)])
        for i in range(3):
            spread_step(plan, ("qkv", i), owners, 0)
        keep(0).wait()
        plan.arrive(*[("small", j) for j in range(1, owners)])
        vec_ref[...] = jnp.concatenate([small[k, :, :own] for k in range(owners)], axis=1)
        bup_ref[...] = jnp.concatenate([small[k, 8:16] for k in range(owners)], axis=1)
        gain, shift = vec_ref[3:4, :], vec_ref[4:5, :]
        for m in range(mbs):
            for at in range(0, rows, TB):
                normal, _ = norm_stats(x_ref[m, at : at + TB].astype(F32))
                place = pl.ds(pl.multiple_of(c * rows + at, TB), TB)
                first[m, place] = (normal * gain + shift).astype(BF16)
            plan.start(("first", m))
        spread_step(plan, ("qkv", 0), owners, 1)
        for i in range(4, loads):
            keep(i).wait()
        for i in range(loads, stores):
            keep(i).start()
        plan.arrive(*[("first", m) for m in range(mbs)])
        spread_step(plan, ("qkv", 1), owners, 1)
        spread_step(plan, ("qkv", 0), owners, 2)
        spread_step(plan, ("qkv", 2), owners, 1)
        for tag in order[:3]:
            spread_step(plan, tag, owners, 0)

        def turn(i, _):
            m, at = lax.div(i, 2 * rows // TB), lax.rem(i, 2 * rows // TB)
            place = pl.ds(pl.multiple_of(at * TB, TB), TB)
            first_t[:, pl.ds(pl.multiple_of(i * TB, TB), TB)] = jnp.transpose(first[m, place])
            return 0

        lax.fori_loop(0, mbs * 2 * rows // TB, turn, 0)
        keep(stores + 1).start()
        spread_step(plan, ("qkv", 1), owners, 2)

        def project_all(i):
            weight = w_qkv[:, :, :, i * half : (i + 1) * half].reshape(-1, half)
            bias = None if i == 1 else vec_ref[i // 2 : i // 2 + 1, slab(c, half)]

            def project_rows(n, _):
                m, at = lax.div(n, 2 * rows // TB), lax.rem(n, 2 * rows // TB)
                place = pl.ds(pl.multiple_of(at * TB, TB), TB)
                joined = dot_nn(first[m, place], weight)
                joined = (joined if bias is None else joined + bias).astype(BF16)
                for s in range(pairs):
                    qkv[m, i * pairs + s, place] = joined[:, s * lanes : (s + 1) * lanes]
                return 0

            lax.fori_loop(0, mbs * 2 * rows // TB, project_rows, 0)

        for i in range(1, 4):
            keep(i).wait()
        for i in range(3):
            if i == 1:
                spread_step(plan, ("qkv", 2), owners, 2)
            spread_step(plan, ("qkv", i), owners, 3)
            if i == 2:
                for when, t, stage in table:
                    if when < 0:
                        spread_step(plan, order[t], owners, stage)
            project_all(i)
        keep(stores).start()
        keep(stores + 2).start()

    def between(k, done):
        for i in range(mbs * pairs):
            some = [entry for entry in table if entry[0] == i * quarters + done]
            if some:

                @pl.when(k == i)
                def _():
                    for _, t, stage in some:
                        spread_step(plan, order[t], owners, stage)

    @pl.when(step == 1)
    def _():
        for tag in order[3:]:
            spread_step(plan, tag, owners, 0)

    @pl.when(step > 0)
    def _():
        k = step - 1
        m, p = lax.div(k, pairs), lax.rem(k, pairs)
        attention_forward_block(
            factor, size, qkv.at[m, p], qkv.at[m, pairs + p], qkv.at[m, 2 * pairs + p], heads.at[k], lse_ref.at[m, p],
            partial(between, k),
        )
        mixed_sends(k, base + k).start()
        pltpu.make_async_copy(heads.at[k, own_rows], mixed_place(k), kept.at[ends + k]).start()

    @pl.when(step == last)
    def _():
        for when, t, stage in table:
            if when >= quarters * mbs * pairs:
                spread_step(plan, order[t], owners, stage)
        for k in range(mbs * pairs):
            mixed_sends(k, base + k).wait()
            pltpu.make_async_copy(heads.at[k, own_rows], mixed_place(k), kept.at[ends + k]).wait()
        for tag in order[3:]:
            for j in range(1, owners):
                plan.arrive((tag, "z", j))
        plan.close()
        for i in range(loads, ends):
            keep(i).wait()


def forward_block(x, weight_qkv, weight_mix, weight_up, weight_down, vectors, b_up, owners, reps, factor, size):
    own, wide = weight_qkv.shape
    mbs, rows, width = x.shape
    lanes = 2 * size
    pairs = width // 2 // lanes

    def cut(shard):
        return shard.reshape(2, reps, shard.shape[0] // (2 * reps), shard.shape[1])

    steps = weight_down.shape[0] // FP
    shards = (weight_qkv.reshape(reps, own // reps, wide), cut(weight_mix), weight_up, weight_down)
    own_up = (steps, own, owners * FP)
    own_down = (steps, FP, width)
    shape = jax.ShapeDtypeStruct
    w_shape = (owners, reps, own // reps, wide // 2)
    qkv_shape = (mbs, 3 * pairs, 2 * rows, lanes)
    anywhere = pl.BlockSpec(memory_space=pl.ANY)
    whole = lambda s: pl.BlockSpec(s, lambda i: (0,) * len(s), pipeline_mode=pl.Buffered(1))
    remotes = 3 + mbs + 3 * 15 + 3 * 18 + 6 * (steps - 1) + mbs * pairs
    copies = 5 + steps * (owners + 1) + 1 + 2 * steps + 3 + mbs * pairs
    area = mbs * pairs * 2 * rows * (2 * rows + QB)
    mixed, qkv, first_t, w_qkv, w_mix, w_up, w_down, vecs, b_up, lse = pl.pallas_call(
        partial(forward_kernel, owners, reps, pairs, factor, size),
        grid=(1 + mbs * pairs,),
        in_specs=[whole(x.shape)] + [anywhere] * 4 + [whole(v.shape) for v in (*vectors, b_up)],
        out_specs=[anywhere] * 7 + [whole((16, width)), whole((8, owners * FP)), whole((mbs, pairs, 8, 2 * rows))],
        out_shape=[
            shape((mbs, rows, width), BF16),
            shape(qkv_shape, BF16),
            shape((width, mbs * 2 * rows), BF16),
            shape(w_shape, BF16),
            shape((owners,) + shards[1].shape, BF16),
            shape(own_up[:1] + (owners,) + own_up[1:], BF16),
            shape(own_down[:1] + (owners,) + own_down[1:], BF16),
            shape((16, width), F32),
            shape((8, owners * FP), F32),
            shape((mbs, pairs, 8, 2 * rows), F32),
        ],
        scratch_shapes=[
            pltpu.VMEM((16, FP), F32),
            pltpu.VMEM((mbs, 2 * rows, width), BF16),
            pltpu.VMEM((width, mbs * 2 * rows), BF16),
            pltpu.VMEM(w_shape, BF16),
            pltpu.VMEM(qkv_shape, BF16),
            pltpu.VMEM((mbs * pairs, 2 * rows, lanes), BF16),
            pltpu.VMEM((owners, 16, FP), F32),
            pltpu.VMEM(shards[1].shape, BF16),
            pltpu.VMEM(own_up, BF16),
            pltpu.VMEM(own_down, BF16),
            pltpu.SemaphoreType.DMA((remotes,)),
            pltpu.SemaphoreType.DMA((remotes,)),
            pltpu.SemaphoreType.DMA((copies,)),
        ],
        compiler_params=pltpu.CompilerParams(
            collective_id=1, has_side_effects=True, vmem_limit_bytes=56 << 20
        ),
        name="forward_block",
    )(x, *shards, *vectors, b_up)
    return (
        mixed,
        qkv,
        first_t,
        w_qkv.reshape(owners * own, -1),
        w_mix.reshape(owners * own, -1),
        w_up,
        w_down,
        vecs,
        b_up[:steps].reshape(steps, 1, owners * FP),
        lse,
    )


class Flow:
    def __init__(self, plan, name, place, owners, bits, mine, theirs, hops, outs, load=None, core=None):
        z, r, c = place
        first, second = bits
        self.plan, self.name, self.place, self.owners = plan, name, place, owners
        self.mine, self.theirs, self.second = mine, theirs, r ^ second
        self.hop_one, self.hop_two, self.hop_z, self.final = hops
        self.outs = outs
        self.load = load
        peer = {"rep": r ^ first}
        if core is not None:
            plan.add((name, "core"), core, lambda: theirs, {"ctx": 1 - c})
        self.split = core is not None
        plan.add((name, "me"), lambda: mine.at[:, r ^ first], lambda: self.hop_one.at[0], peer)
        plan.add((name, "on"), lambda: mine.at[:, r ^ first ^ second], lambda: self.hop_one.at[1], peer)
        plan.add((name, "two"), lambda: mine.at[:, r ^ second], lambda: self.hop_two, {"rep": r ^ second})
        for j in range(1, owners):
            to = lax.rem(z + j, owners)
            plan.add((name, "z", j), lambda to=to: mine.at[to, r], lambda j=j: self.hop_z.at[j - 1], {"fsdp": to})
        here = lambda: self.final.at[c, r]
        plan.add((name, "x"), here, here, {"rep": r ^ first})
        plan.add((name, "y"), here, here, {"rep": r ^ second})
        far = lambda: self.final.at[c, r ^ second]
        plan.add((name, "xy"), far, far, {"rep": r ^ first})
        side = lambda: self.final.at[c]
        plan.add((name, "back"), side, side, {"ctx": 1 - c})

    def step(self, stage):
        z, r, c = self.place
        plan, name, mine = self.plan, self.name, self.mine
        owners = self.owners
        if stage == 0:
            if self.split:
                plan.start((name, "core"))
            if self.load is not None:
                self.load().start()
        elif stage == 1:
            if self.load is not None:
                self.load().wait()
            if self.split:
                plan.arrive((name, "core"))
                add_blocks(mine, [mine, self.theirs], BF16)
            plan.start((name, "on"), (name, "me"))
        elif stage == 2:
            plan.arrive((name, "on"))
            part = mine.at[:, self.second]
            add_blocks(part, [part, self.hop_one.at[1]], BF16)
            plan.start((name, "two"))
        elif stage == 3:
            plan.arrive((name, "me"), (name, "two"))
            part = mine.at[:, r]
            add_blocks(part, [part, self.hop_one.at[0], self.hop_two], BF16)
            plan.start(*[(name, "z", j) for j in range(1, owners)])
        elif stage == 4:
            plan.arrive(*[(name, "z", j) for j in range(1, owners)])
            terms = [mine[z, r].astype(F32)] + [self.hop_z[j].astype(F32) for j in range(owners - 1)]
            while len(terms) > 1:
                terms = [a + b for a, b in zip(terms[::2], terms[1::2])]
            self.final[c, r] = terms[0].astype(BF16)
            plan.start((name, "x"), (name, "y"))
        elif stage == 5:
            plan.arrive((name, "y"))
            plan.start((name, "xy"))
        elif stage == 6:
            plan.arrive((name, "x"), (name, "xy"))
            plan.start((name, "back"))
        else:
            plan.arrive((name, "back"))
            for copy in self.outs(self.final):
                copy.start()


def flow_scratch(owners, reps, piece, split):
    vmem = lambda *lead: pltpu.VMEM(lead + piece, BF16)
    mine = [vmem(owners, reps)] * (2 if split else 1)
    return mine + [vmem(2, owners), vmem(owners), vmem(owners - 1), vmem(2, reps)]


def timetable(groups, products):
    table = []
    for g in range(groups):
        second = 4 + 5 * g
        times = (2 * g - 1, second, second + 5, second + 9, second + 11, second + 13, second + 15)
        table += [(t, g, 1 + i) for i, t in enumerate(times)]
    for p, second in zip(range(products), (25, 27, 28)):
        times = (second, second + 4, second + 8, second + 10, second + 12, second + 14)
        table += [(t, groups + p, 2 + i) for i, t in enumerate(times)]
    return sorted(table)


def gelu_parts(b):
    cubic = (GELU_A * GELU_B) * (b * b)
    t = jnp.tanh(b * (cubic + GELU_A))
    rise = 0.5 * t + 0.5
    active = b * rise
    return active, rise + active * (1.0 - t) * (3.0 * cubic + GELU_A)


GATHERS = [
    (1, ("up", 1), 2), (1, ("down", 1), 2), (2, ("up", 1), 3), (2, ("down", 1), 3), (2, ("up", 2), 1), (2, ("down", 2), 1),
    (4, ("up", 1), 4), (4, ("down", 1), 4), (5, ("up", 2), 2), (5, ("down", 2), 2), (6, ("up", 2), 3), (6, ("down", 2), 3),
    (8, ("up", 2), 4), (8, ("down", 2), 4),
]
SUMS = [
    (3, 0, 0), (3, 1, 0), (5, 0, 1), (6, 1, 1), (8, 0, 2), (9, 1, 2), (9, 0, 3), (10, 1, 3), (10, 0, 4), (11, 0, 5),
    (11, 1, 4), (12, 1, 5), (12, 0, 6), (13, 1, 6), (14, 0, 7), (14, 1, 7),
]


def middle_kernel(owners, reps, direct, *refs):
    x_ref, mixed_ref, d_ref, wmix_ref, wup_any, wdown_any, vec_ref, bup_ref = refs[:8]
    result_ref, dmid_ref, gmix_ref, gvec_ref = refs[8:12]
    refs = refs[12:]
    if direct:
        heads_out, up_sums, down_sums, down_out, up_out, dmixed_ref, gup_ref, gdown_ref, up_got, down_got = refs[:10]
        refs = refs[10:]
    else:
        dmixed_ref, gup_ref, gdown_ref = refs[:3]
        refs = refs[3:]
    middle, second, second_t, mixed_t, out_sum, ds_sum, active_t, d_before, w_up, w_down = refs[:10]
    refs = refs[10:]
    step = pl.program_id(0)
    rows = x_ref.shape[0]
    steps = w_up.shape[0]
    last = steps - 1
    count = rows // RB
    chunk = lambda i: pl.ds(pl.multiple_of(i * RB, RB), RB)
    b_mix, gain, shift, b_down = (vec_ref[i : i + 1, :] for i in (2, 5, 6, 7))
    slots = 4

    if direct:
        flow_refs, (send, recv, kept) = refs[:-3], refs[-3:]
        place = z, r, c = position()
        plan = Plan(send, recv)
        used = 0

        def local(src, dst):
            nonlocal used
            used += 1
            slot = kept.at[used - 1]
            return lambda: pltpu.make_async_copy(src(), dst(), slot)

        own_rows, part = w_up.shape[1] // owners, w_down.shape[1] // owners
        up_of = lambda ref, f, o: ref.at[f, pl.ds(pl.multiple_of(o * own_rows, 32), own_rows)]
        down_of = lambda ref, f, o: ref.at[f, pl.ds(pl.multiple_of(o * part, 32), part)]
        loads, pieces = [], {}
        for tag, source, whole, of, piece, side in (
            ("up", wup_any, w_up, up_of, up_piece, up_side),
            ("down", wdown_any, w_down, down_of, down_piece, down_side),
        ):
            for o in range(owners):
                loads.append(local(lambda o=o, s=source: s.at[0, o], lambda o=o, w=whole, of=of: of(w, 0, o)))
            for f in range(1, steps):
                loads.append(
                    local(lambda f=f, s=source: s.at[f, z], lambda f=f, w=whole, of=of: of(w, f, z))
                )
                pieces[tag, f] = [
                    local(
                        lambda f=f, j=j, s=source, p=piece: p(s.at[f, lax.rem(z + j, owners)], c, r),
                        lambda f=f, j=j, w=whole, of=of, p=piece: p(of(w, f, lax.rem(z + j, owners)), c, r),
                    )
                    for j in range(1, owners)
                ]
                spread_plan(
                    plan, (tag, f), owners, reps, z, r, c, None,
                    lambda o, p, f=f, w=whole, of=of, piece=piece: piece(of(w, f, o), c, p),
                    row_halves,
                    lambda o, f=f, w=whole, of=of, side=side: side(of(w, f, o), c),
                )
        cores = []
        for f in range(1, steps):
            for tag, ref, got, sums in (("d", gdown_ref, down_got, down_sums), ("u", gup_ref, up_got, up_sums)):
                there = lambda got=got, f=f: got.at[f - 1]
                plan.add(("core", tag, f), lambda ref=ref: ref.at[0, :, 1 - c], there, {"ctx": 1 - c})
                cores.append((f, ("core", tag, f), ref, there, local(there, lambda sums=sums, f=f: sums.at[f - 1])))
        mbs, pairs, lanes = heads_out.shape[1], heads_out.shape[0], heads_out.shape[3]
        seq = rows // mbs
        seq_rows = pl.ds(pl.multiple_of(c * seq, seq), seq)
        kept_heads = []
        for m in range(mbs):
            for p in range(pairs):
                part_of = lambda side, m=m, p=p: dmixed_ref.at[pl.ds(m * seq, seq), slab(side * pairs + p, lanes)]
                to = lambda m=m, p=p: heads_out.at[p, m, seq_rows]
                plan.add(("heads", m, p), partial(part_of, 1 - c), to, {"ctx": 1 - c})
                kept_heads.append(local(partial(part_of, c), to))
        flows, leaving, at = [], [], 0
        for i, (ref, out) in enumerate(((gdown_ref, down_out), (gup_ref, up_out))):
            wide = ref.shape[-1] // 2
            up_step = ref.shape[-1] // owners
            for s in range(2):
                mine, theirs, *hops = flow_refs[at : at + 6]
                at += 6
                cols, final = pl.ds(s * wide, wide), hops[-1]
                if i == 1:
                    places = []
                    for k in range(wide // up_step):
                        to = pl.ds((s * wide // up_step + k) * steps * up_step, up_step)
                        places.append((
                            lambda final=final, k=k: final.at[:, :, :, pl.ds(k * up_step, up_step)],
                            lambda out=out, to=to: out.at[:, :, :, to],
                        ))
                else:
                    places = [(lambda final=final: final, lambda out=out, cols=cols: out.at[0, :, :, :, cols])]
                copies = [local(src, dst) for src, dst in places]
                leaving.extend(copies)
                flows.append(
                    Flow(
                        plan, (i, s), place, owners, (1, 2) if s == 0 else (2, 1), mine, theirs, hops,
                        lambda final, copies=copies: [f() for f in copies],
                        local(lambda ref=ref, cols=cols: ref.at[0, :, c, :, :, cols], lambda mine=mine: mine),
                        lambda ref=ref, cols=cols: ref.at[0, :, 1 - c, :, :, cols],
                    )
                )
    else:
        kept = refs[0]
        loads = [
            lambda: pltpu.make_async_copy(wup_any, w_up, kept.at[0]),
            lambda: pltpu.make_async_copy(wdown_any, w_down, kept.at[1]),
        ]

    def core_sums(step):
        for f, name, ref, there, out in cores:
            if f == step:
                plan.arrive(name)
                add_blocks(there(), [there(), ref.at[0, :, c]], BF16)
                out().start()
                plan.leave(name)

    def between(slot, here=True):
        if not direct:
            return
        for k in range(steps):
            some = [lambda t=t, n=n: spread_step(plan, t, owners, n) for when, t, n in GATHERS if when == k * slots + slot]
            some += [lambda g=g, n=n: [flow.step(n) for flow in flows[2 * g : 2 * g + 2]] for when, g, n in SUMS if when == k * slots + slot]
            if some:

                @pl.when((step == k) & here)
                def _():
                    for act in some:
                        act()

    @pl.when(step == 0)
    def _():
        for copy in loads:
            copy().start()
        if direct:
            for some in pieces.values():
                for copy in some:
                    copy().start()
            greet(owners, reps)
            for f in range(1, steps):
                for tag in ("up", "down"):
                    for copy in pieces[tag, f]:
                        copy().wait()
                    if f == 1:
                        spread_step(plan, (tag, f), owners, 1)
        gvec_ref[...] = jnp.zeros_like(gvec_ref)

        def prepare(i, _):
            at = chunk(i)
            mixed = mixed_ref[at]
            mixed_t[:, at] = jnp.transpose(mixed)
            mid = x_ref[at].astype(F32) + (dot_nn(mixed, wmix_ref[...]) + b_mix)
            middle[at] = mid
            out_sum[at] = mid + b_down
            ds_sum[at] = jnp.zeros_like(mid)
            normal, _ = norm_stats(mid)
            low = (normal * gain + shift).astype(BF16)
            second[at] = low
            second_t[:, at] = jnp.transpose(low)
            return 0

        lax.fori_loop(0, count, prepare, 0)
        for copy in loads:
            copy().wait()

    between(0)

    def feed(i, d_bup):
        at = chunk(i)
        act, slope = gelu_parts(dot_nn(second[at], w_up[step]) + bup_ref[0])
        act = act.astype(BF16)
        active_t[:, at] = jnp.transpose(act)
        db = (dot_nt(d_ref[at], w_down[step]) * slope).astype(BF16)
        d_before[at] = db
        out_sum[at] += dot_nn(act, w_down[step])
        ds_sum[at] += dot_nt(db, w_up[step])
        between(1, i == count // 2 - 1)
        return d_bup + jnp.sum(db.astype(F32), axis=0, keepdims=True)

    d_bup = lax.fori_loop(0, count, feed, jnp.zeros(bup_ref.shape[1:], F32))
    between(2)

    width = d_bup.shape[1] // owners
    for k in range(owners):
        gvec_ref[8 + k : 9 + k, slab(step, width)] = d_bup[:, k * width : (k + 1) * width]
    if direct:

        @pl.when(step == 1)
        def _():
            plan.leave(*[(flow.name, "core") for flow in flows])

        @pl.when(step == 2)
        def _():
            core_sums(1)

    share = second_t.shape[0] // owners
    part = active_t.shape[0] // owners

    def weights(o, _):
        two = pl.ds(2 * o, 2)
        lines = pl.ds(pl.multiple_of(o * 2 * part, part), 2 * part)
        gdown_ref[0, two] = dot_nn(active_t[lines], d_ref[...]).reshape((2,) + gdown_ref.shape[2:]).astype(BF16)
        lines = pl.ds(pl.multiple_of(o * 2 * share, 64), 2 * share)
        gup_ref[0, two] = dot_nn(second_t[lines], d_before[...]).reshape((2,) + gup_ref.shape[2:]).astype(BF16)
        return 0

    lax.fori_loop(0, owners // 2, weights, 0)
    if direct:
        for f in range(1, steps):

            @pl.when(step == f)
            def _():
                for when, name, *_ in cores:
                    if when == f:
                        plan.start(name)

    between(slots - 1)

    @pl.when(step == last)
    def _():

        def finish(i, sums):
            at = chunk(i)
            result_ref[at] = out_sum[at].astype(BF16)
            normal, inverse = norm_stats(middle[at])
            ds = ds_sum[at]
            grad_out = d_ref[at].astype(F32)
            d_mid = grad_out + norm_back(ds, normal, inverse, gain)
            dmid_ref[at] = d_mid
            branch = d_mid.astype(BF16)
            second[at] = branch
            dmixed_ref[at] = dot_nt(branch, wmix_ref[...]).astype(BF16)
            parts = (branch.astype(F32), ds * normal, ds, grad_out)
            return tuple(s + jnp.sum(p, axis=0, keepdims=True) for s, p in zip(sums, parts))

        zero = jnp.zeros((1, x_ref.shape[1]), F32)
        sums = lax.fori_loop(0, count, finish, (zero,) * 4)
        for i, k in enumerate((2, 5, 6, 7)):
            gvec_ref[k : k + 1, :] = sums[i]

        if direct:
            plan.start(*[("heads", m, p) for m in range(mbs) for p in range(pairs)])
            for copy in kept_heads:
                copy().start()

        def mix(o, _):
            lines = pl.ds(pl.multiple_of(o * share, 64), share)
            gmix_ref[o] = dot_nn(mixed_t[lines], second[...]).reshape(gmix_ref.shape[1:]).astype(BF16)
            return 0

        lax.fori_loop(0, owners, mix, 0)
        if direct:
            core_sums(last)
            for when, g, n in SUMS:
                if when >= steps * slots:
                    for flow in flows[2 * g : 2 * g + 2]:
                        flow.step(n)
            plan.arrive(*[("heads", m, p) for m in range(mbs) for p in range(pairs)])
            plan.close()
            for copy in kept_heads + [out for *_, out in cores]:
                copy().wait()
            for copy in leaving:
                copy().wait()


def middle_block(x, mixed, d_out, w_mix, w_up, w_down, vecs, b_up, owners, reps, direct, heads):
    rows, width = x.shape
    steps = w_up.shape[0]
    ff = steps * owners * FP
    whole = lambda shape: pl.BlockSpec(shape, lambda f: (0,) * len(shape), pipeline_mode=pl.Buffered(1))
    anywhere = pl.BlockSpec(memory_space=pl.ANY)
    out = jax.ShapeDtypeStruct
    vmem = pltpu.VMEM
    side = (owners, 2, reps)
    g_mix = side + (width // owners // 2 // reps, width)
    g_up = (1,) + g_mix[:-1] + (owners * FP,)
    g_down = (1,) + side + (FP // 2 // reps, width)
    scratch = [
        vmem((rows, width), F32),
        vmem((rows, width), BF16),
        vmem((width, rows), BF16),
        vmem((width, rows), BF16),
        vmem((rows, width), F32),
        vmem((rows, width), F32),
        vmem((owners * FP, rows), BF16),
        vmem((rows, owners * FP), BF16),
        vmem((steps, width, owners * FP), BF16),
        vmem((steps, owners * FP, width), BF16),
    ]
    grads = [vmem((rows, width), BF16), vmem(g_up, BF16), vmem(g_down, BF16)]
    if direct:
        later = [(steps - 1, g[1]) + g[3:] for g in (g_up, g_down)]
        extra = [out(heads, BF16)] + [out(s, BF16) for s in later]
        extra += [out((steps,) + g_down[2:], BF16), out(g_up[2:5] + (steps * g_up[5],), BF16)]
        extra_specs = [anywhere] * 5
        scratch = grads + [vmem(s, BF16) for s in later] + scratch
        for g in (g_down, g_up):
            for _ in range(2):
                scratch += flow_scratch(owners, reps, (g[4], g[5] // 2), True)
        remotes = (steps - 1) * 2 * 15 + 4 * 11 + 2 * (steps - 1) + heads[0] * heads[1]
        scratch += [pltpu.SemaphoreType.DMA((remotes,))] * 2 + [
            pltpu.SemaphoreType.DMA((2 * owners + 2 * (steps - 1) * owners + 10 + 2 * (steps - 1) + heads[0] * heads[1],))
        ]
        params = dict(collective_id=3, has_side_effects=True)
    else:
        per_step = lambda s: pl.BlockSpec(s, lambda f: (f,) + (0,) * (len(s) - 1))
        extra = [out((rows, width), BF16)] + [out((steps,) + g[1:], BF16) for g in (g_up, g_down)]
        extra_specs = [whole((rows, width)), per_step(g_up), per_step(g_down)]
        scratch += [pltpu.SemaphoreType.DMA((2,))]
        params = {}
    return pl.pallas_call(
        partial(middle_kernel, owners, reps, direct),
        grid=(steps,),
        in_specs=[whole((rows, width))] * 3
        + [whole((width, width)), anywhere, anywhere, whole(vecs.shape), pl.BlockSpec((1, 1, owners * FP), lambda f: (f, 0, 0))],
        out_specs=[whole((rows, width)), whole((rows, width)), whole(g_mix), whole((16, width))] + extra_specs,
        out_shape=[out((rows, width), BF16), out((rows, width), F32), out(g_mix, BF16), out((16, width), F32)] + extra,
        scratch_shapes=scratch,
        compiler_params=pltpu.CompilerParams(vmem_limit_bytes=62 << 20, **params),
        cost_estimate=pl.CostEstimate(
            flops=12 * rows * width * ff + 6 * rows * width * width,
            bytes_accessed=8 * width * ff + 16 * rows * width,
            transcendentals=rows * ff,
        ),
        name="middle_block",
    )(x, mixed, d_out, w_mix, w_up, w_down, vecs, b_up)


def backward_kernel(
    owners, reps, pairs, factor, size, shapes, done,
    q_ref, k_ref, v_ref, d_heads, lse_ref, x_ref, vec_ref, gvec_ref, dmid_ref, first_t_ref, w_ref, *refs
):
    n_in = len(shapes)
    sources, refs = refs[:n_in], refs[n_in + 2 :]
    dtok_ref, vec_out, refs = refs[0], refs[1], refs[2:]
    outs, refs = refs[: n_in + 1], refs[n_in + 1 :]
    d_joined, first_t, w_pairs, df_send, df_recv, dk_sum, dv_sum, b_sum, vec_one, vec_got, vec_sum, refs = (
        refs[:11] + (refs[11:],)
    )
    flow_refs, (send, recv, kept) = refs[:-3], refs[-3:]
    step = pl.program_id(0)
    last = pl.num_programs(0) - 1
    place = z, r, c = position()
    mbs, rows, width = x_ref.shape
    half = width // 2
    lanes = 2 * size
    plan = Plan(send, recv)
    own_rows = pl.ds(pl.multiple_of(c * rows, rows), rows)

    locals_used = 0

    def local(src, dst):
        nonlocal locals_used
        locals_used += 1
        slot = kept.at[locals_used - 1]
        return lambda: pltpu.make_async_copy(src(), dst(), slot)

    up_step = shapes[1][-1] // owners
    flows, leaving, at = [], [], 0

    def add_flow(name, bits, mine, theirs, hops, places, load=None, core=None):
        final = hops[-1]
        copies = [local(partial(part, final), dst) for part, dst in places]
        leaving.extend(copies)
        flows.append(
            Flow(plan, name, place, owners, bits, mine, theirs, hops, lambda final: [f() for f in copies], load, core)
        )

    for i, shape in enumerate(shapes):
        for f in range(shape[0]):
            wide = shape[-1] // 2
            for s in range(2):
                split = len(shape) == 6
                mine, *hops = flow_refs[at : at + 5 + split]
                at += 5 + split
                theirs = hops.pop(0) if split else None
                source, out, cols = sources[i], outs[i], pl.ds(s * wide, wide)
                if i == 1:
                    places = []
                    for k in range(wide // up_step):
                        to = pl.ds(((s * wide // up_step + k) * (shape[0] + done) + done + f) * up_step, up_step)
                        places.append((
                            lambda final, k=k: final.at[:, :, :, pl.ds(k * up_step, up_step)],
                            lambda out=out, to=to: out.at[:, :, :, to],
                        ))
                else:
                    skip = done if i == 0 else 0
                    places = [(lambda final: final, lambda out=out, f=f + skip, cols=cols: out.at[f, :, :, :, cols])]
                add_flow(
                    (i, f, s), (1, 2) if s == 0 else (2, 1), mine, theirs, hops, places,
                    local(
                        lambda source=source, f=f, cols=cols, split=split: (
                            source.at[f, :, c, :, :, cols] if split else source.at[f, :, :, :, cols]
                        ),
                        lambda mine=mine: mine,
                    ),
                    (lambda source=source, f=f, cols=cols: source.at[f, :, 1 - c, :, :, cols]) if split else None,
                )
    for p in range(pairs):
        for s in range(2):
            mine, *hops = flow_refs[at : at + 5]
            at += 5
            places = []
            for side in range(2):
                for i in range(3):
                    to = pl.ds((i * 2 * pairs + side * pairs + p) * lanes, lanes)
                    places.append((
                        lambda final, side=side, i=i: final.at[side, :, :, pl.ds(i * lanes, lanes)],
                        lambda s=s, to=to: outs[-1].at[:, s, :, to],
                    ))
            add_flow((n_in, p, s), (1, 2) if s == 0 else (2, 1), mine, None, hops, places)
    groups = [flows[i : i + 2] for i in range(0, len(flows), 2)]
    products = len(groups) - pairs
    ff_steps = shapes[0][0]
    groups[: 2 * ff_steps] = [groups[k * ff_steps + f] for f in range(ff_steps) for k in range(2)]

    def advance(group, stage):
        for flow in groups[group]:
            flow.step(stage)

    for m in range(mbs):
        plan.add(("first", m), lambda m=m: df_send.at[m], lambda m=m: df_recv.at[m], {"ctx": 1 - c})
    around = [(k, side) for k in range(reps) for side in range(2) if k or side]
    for k, side in around:
        peer = {"rep": r ^ k, "ctx": 1 - c if side else c}
        plan.add(("vec", k, side), lambda: vec_sum.at[0], lambda k=k, side=side: vec_got.at[2 * k + side], peer)
    for j in range(1, owners):
        plan.add(
            ("vec", "z", j), lambda: vec_sum.at[1], lambda j=j: vec_got.at[2 * reps + j - 1], {"fsdp": lax.rem(z + j, owners)}
        )

    table = timetable(products, pairs)
    quarters = 2 * rows // QB
    tail = [entry for entry in table if entry[0] >= quarters * mbs * pairs]

    def load_first():
        return pltpu.make_async_copy(first_t_ref, first_t, kept.at[locals_used])

    def load_weight(i, p):
        return pltpu.make_async_copy(
            w_ref.at[:, pl.ds((i * pairs + p) * lanes, lanes)],
            w_pairs.at[p, :, pl.ds(i * lanes, lanes)],
            kept.at[locals_used + 1 + i * pairs + p],
        )

    @pl.when(step == 0)
    def _():
        greet(owners, reps, across=True)
        for g in range(products):
            advance(g, 0)
        load_first().start()
        for i in range(3):
            for p in range(pairs):
                load_weight(i, p).start()
        for when, group, stage in table:
            if when < 0:
                advance(group, stage)


    def between(k, done):
        for i in range(mbs * pairs):
            some = [entry for entry in table if entry[0] == quarters * i + done]
            if some:

                @pl.when(k == i)
                def _():
                    for _, group, stage in some:
                        advance(group, stage)

    def weight_grad(p):
        grad = dot_nn(first_t[...], d_joined[p])
        piece = groups[products][0].mine.shape[2]
        grad = grad.reshape(owners, reps, 2 * piece, grad.shape[1])
        for s in range(2):
            groups[products + p][s].mine[...] = grad[:, :, s * piece : (s + 1) * piece].astype(BF16)

    for p in range(pairs):

        @pl.when(step == mbs * (p + 1))
        def _():
            if p == 0:
                load_first().wait()
            weight_grad(p)
            advance(products + p, 1)

    @pl.when(step < last)
    def _():
        p, m = lax.div(step, mbs), lax.rem(step, mbs)
        start = pl.multiple_of(m * 2 * rows, 2 * rows)
        joined = d_joined.at[p, pl.ds(start, 2 * rows)]
        attention_backward_block(
            factor, size, q_ref.at[0, 0], k_ref.at[0, 0], v_ref.at[0, 0], d_heads.at[0, 0], lse_ref.at[m, p],
            joined.at[:, pl.ds(0, lanes)], joined.at[:, pl.ds(lanes, lanes)], joined.at[:, pl.ds(2 * lanes, lanes)],
            dk_sum, dv_sum, partial(between, step),
        )
        for i, k in enumerate((0, 2)):
            part = jnp.sum(joined[:, k * lanes : (k + 1) * lanes].astype(F32), axis=0, keepdims=True)
            before = b_sum[p, i : i + 1, :]
            b_sum[p, i : i + 1, :] = part + jnp.where(m == 0, jnp.zeros_like(before), before)

    def first_part(m, at):
        total = None
        for p in range(pairs):
            term = dot_nt(d_joined[p, pl.ds(pl.multiple_of(m * 2 * rows + at, TB), TB)], w_pairs[p])
            total = term if total is None else total + term
        return total

    @pl.when(step == last)
    def _():
        for i in range(3):
            for p in range(pairs):
                load_weight(i, p).wait()
        gain = vec_ref[3:4, :]
        steps = rows // TB

        def theirs(i, _):
            m, at = lax.div(i, steps), lax.rem(i, steps) * TB
            df_send[m, pl.ds(pl.multiple_of(at, TB), TB)] = first_part(m, (1 - c) * rows + at).astype(BF16)
            return 0

        def go(until):
            while tail and tail[0][0] < until:
                _, group, stage = tail.pop(0)
                advance(group, stage)

        lax.fori_loop(0, mbs * steps, theirs, 0)
        for m in range(mbs):
            plan.start(("first", m))
        go(28)
        for m in range(mbs):
            plan.arrive(("first", m))

        def mine(i, sums):
            m, at = lax.div(i, steps), lax.rem(i, steps) * TB
            here = pl.ds(pl.multiple_of(at, TB), TB)
            total = first_part(m, c * rows + at) + df_recv[m, here].astype(F32)
            normal, inverse = norm_stats(x_ref[m, here].astype(F32))
            dtok_ref[m, here] = dmid_ref[m, here] + norm_back(total, normal, inverse, gain)
            gains = jnp.sum(total * normal, axis=0, keepdims=True)
            return (sums[0] + gains, sums[1] + jnp.sum(total, axis=0, keepdims=True))

        zero = jnp.zeros((1, width), F32)
        g_gain, g_shift = lax.fori_loop(0, mbs * steps, mine, (zero, zero))
        vec_one[...] = gvec_ref[...]
        vec_one[3:4, :] = g_gain
        vec_one[4:5, :] = g_shift
        for p in range(pairs):
            for i in range(2):
                vec_one[i : i + 1, slab(c * pairs + p, lanes)] = b_sum[p, i : i + 1, :]
        vec_sum[0] = vec_one[...]
        plan.start(*[("vec", k, side) for k, side in around])
        go(37)
        plan.arrive(*[("vec", k, side) for k, side in around])
        vec_got[0] = vec_one[...]
        cores = [vec_got[2 * k] + vec_got[2 * k + 1] for k in range(reps)]
        vec_sum[1] = (cores[0] + cores[1]) + (cores[2] + cores[3])
        plan.start(*[("vec", "z", j) for j in range(1, owners)])
        go(41)
        plan.arrive(*[("vec", "z", j) for j in range(1, owners)])
        n = 2 * reps
        vec_out[...] = (vec_sum[1] + vec_got[n]) + (vec_got[n + 1] + vec_got[n + 2])
        go(1000)
        plan.close()
        for copy in leaving:
            copy().wait()


def backward_block(
    qkv, heads, lse, x, vecs, gvec, d_middle, first_t, w_qkv, grads, finished, owners, reps, factor, size
):
    mbs, rows, width = x.shape
    lanes = 2 * size
    pairs = width // 2 // lanes
    shape = jax.ShapeDtypeStruct
    anywhere = pl.BlockSpec(memory_space=pl.ANY)
    whole = lambda s: pl.BlockSpec(s, lambda i: (0,) * len(s), pipeline_mode=pl.Buffered(1))
    final_step = mbs * pairs - 1

    def block(which):
        def index(i):
            k = jnp.minimum(i, final_step)
            return (lax.rem(k, mbs), which * pairs + lax.div(k, mbs), 0, 0)

        return pl.BlockSpec((1, 1, 2 * rows, lanes), index)

    def heads_index(i):
        k = jnp.minimum(i, final_step)
        return (lax.div(k, mbs), lax.rem(k, mbs), 0, 0)

    heads_spec = pl.BlockSpec((1, 1, 2 * rows, lanes), heads_index)
    pieces = [(len(g.shape) == 6, (g.shape[-2], g.shape[-1] // 2)) for g in grads for _ in range(2 * g.shape[0])]
    q_piece = (width // owners // reps // 2, 3 * lanes)
    down, up, mix = (g.shape for g in grads)
    finals = [f.shape for f in finished] + [mix[:1] + mix[2:], (reps, 2, q_piece[0], 3 * width)]
    scratch = [s for split, p in pieces for s in flow_scratch(owners, reps, p, split)]
    scratch += [s for _ in range(2 * pairs) for s in flow_scratch(owners, reps, q_piece, False)]
    remotes = 11 * len(pieces) + 10 * 2 * pairs + mbs * pairs + mbs + 2 * reps + owners
    vec = (16, width)
    dtok, vec_sum, *outs = pl.pallas_call(
        partial(backward_kernel, owners, reps, pairs, factor, size, [g.shape for g in grads], finished[0].shape[0] - down[0]),
        grid=(mbs * pairs + 1,),
        in_specs=[block(0), block(1), block(2), heads_spec, whole(lse.shape), whole(x.shape), whole(vec), whole(vec)]
        + [whole(x.shape)]
        + [anywhere] * (2 + len(grads) + 2),
        input_output_aliases={11 + len(grads): 2, 12 + len(grads): 3},
        out_specs=[whole(x.shape), whole(vec)] + [anywhere] * len(finals),
        out_shape=[shape(x.shape, F32), shape(vec, F32)] + [shape(f, BF16) for f in finals],
        scratch_shapes=[
            pltpu.VMEM((pairs, mbs * 2 * rows, 3 * lanes), BF16),
            pltpu.VMEM(first_t.shape, BF16),
            pltpu.VMEM((pairs, width, 3 * lanes), BF16),
            pltpu.VMEM(x.shape, BF16),
            pltpu.VMEM(x.shape, BF16),
            pltpu.VMEM((2 * rows, lanes), F32),
            pltpu.VMEM((2 * rows, lanes), F32),
            pltpu.VMEM((pairs, 8, lanes), F32),
            pltpu.VMEM(vec, F32),
            pltpu.VMEM((2 * reps + owners - 1,) + vec, F32),
            pltpu.VMEM((2,) + vec, F32),
        ]
        + scratch
        + [
            pltpu.SemaphoreType.DMA((remotes,)),
            pltpu.SemaphoreType.DMA((remotes,)),
            pltpu.SemaphoreType.DMA((len(pieces) * 3 + 12 * pairs + mbs * pairs + 1 + 3 * pairs,)),
        ],
        compiler_params=pltpu.CompilerParams(
            collective_id=2, has_side_effects=True, vmem_limit_bytes=63 << 20
        ),
        name="backward_block",
    )(qkv, qkv, qkv, heads, lse, x, vecs, gvec, d_middle, first_t, w_qkv, *grads, *finished)
    return dtok, vec_sum, outs


def local(
    inputs,
    weight_qkv,
    bias_query,
    bias_value,
    weight_mix,
    bias_mix,
    gain_attn,
    shift_attn,
    gain_mlp,
    shift_mlp,
    weight_up,
    bias_up,
    weight_down,
    bias_down,
    cotangent,
):
    width = weight_qkv.shape[1] // 3
    half = width // 2
    size = width // H
    factor = size ** (-0.5)
    rows = inputs.shape[2]
    owners = lax.axis_size("fsdp")
    reps = lax.axis_size("rep")
    ctx = lax.axis_index("ctx")
    rep = lax.axis_index("rep")
    own = weight_qkv.shape[0]
    b_up_rows = bias_up.shape[0]
    direct = own % (16 * reps) == 0 and owners == 4 and reps == 4

    def swap(x):
        return lax.ppermute(x, "ctx", [(0, 1), (1, 0)])

    def order(mine, other, axis):
        return jnp.where(
            ctx == 0,
            jnp.concatenate([mine, other], axis=axis),
            jnp.concatenate([other, mine], axis=axis),
        )

    def columns(x, axis, which):
        return lax.dynamic_slice_in_dim(x, which * half, half, axis)

    direct = own % (16 * reps) == 0 and owners == 4 and reps == 4
    vectors = [bias_query, bias_value, bias_mix, gain_attn, shift_attn, gain_mlp, shift_mlp, bias_down]
    tokens = inputs[:, 0].astype(F32)
    if direct:
        mixed, qkv, first_t, w_qkv, w_mix, w_up, w_down, vecs, b_up, lse = forward_block(
            inputs[:, 0],
            weight_qkv,
            weight_mix,
            weight_up,
            weight_down,
            vectors,
            bias_up,
            owners,
            reps,
            factor,
            size,
        )
    else:
        part = own // reps
        mine = lax.dynamic_slice_in_dim(weight_qkv, rep * part, part, 0)
        mine = jnp.concatenate([columns(mine[:, i * width : (i + 1) * width], 1, ctx) for i in range(3)], axis=1)
        w_qkv = lax.all_gather(mine, ("fsdp", "rep"), axis=0, tiled=True)

        def gather(shard):
            piece = shard.shape[0] // (2 * reps)
            mine = lax.dynamic_slice_in_dim(shard, (rep * 2 + ctx) * piece, piece, 0)
            return lax.all_gather(mine, ("fsdp", "rep", "ctx"), axis=0, tiled=True)

        w_mix = gather(weight_mix)
        w_up = gather(weight_up)
        w_down = gather(weight_down)
        vecs = lax.all_gather(jnp.stack(vectors).astype(F32), "fsdp", axis=1, tiled=True)
        b_up = lax.all_gather(bias_up.astype(F32), "fsdp", axis=0, tiled=True)
        b_up = b_up.reshape(SHARES, -1, FP).swapaxes(0, 1)
        b_up = b_up.reshape(b_up.shape[0], 1, -1)
        w_up = w_up.reshape(width, SHARES, -1, FP).transpose(2, 0, 1, 3).reshape(-1, width, SHARES * FP)
        w_down = w_down.reshape(SHARES, -1, FP, width).swapaxes(0, 1).reshape(-1, SHARES * FP, width)
    b_query, b_value, g_attn, s_attn = (vecs[i] for i in (0, 1, 3, 4))

    if not direct:
        normal_one, inverse_one = norm_stats(tokens)
        first_own = (normal_one * g_attn + s_attn).astype(BF16)
        first = order(first_own, swap(first_own), 1)
        joined = project(first, w_qkv)
        query = (joined[..., :half] + columns(b_query, 0, ctx)).astype(BF16)
        key = joined[..., half : 2 * half].astype(BF16)
        value = (joined[..., 2 * half :] + columns(b_value, 0, ctx)).astype(BF16)
        mixed_heads, lse = attention_forward(query, key, value, factor, size)

    def my_rows(x):
        return lax.dynamic_slice_in_dim(x, ctx * rows, rows, 1)

    def their_rows(x):
        return lax.dynamic_slice_in_dim(x, (1 - ctx) * rows, rows, 1)

    if not direct:
        mixed = order(my_rows(mixed_heads), swap(their_rows(mixed_heads)), 2)
    flat = (-1, width)
    d_out = cotangent.reshape(flat)
    result, d_middle, g_wmix, gvec, d_mixed, g_wup, g_wdown, *finished = middle_block(
        inputs.reshape(flat),
        mixed.reshape(flat),
        d_out,
        w_mix,
        w_up,
        w_down,
        vecs,
        b_up,
        SHARES,
        reps,
        direct,
        (half // (2 * size), inputs.shape[0], 2 * rows, 2 * size),
    )
    steps = b_up.shape[0]
    if direct:
        d_tokens, summed, outs = backward_block(
            qkv, d_mixed, lse, inputs[:, 0], vecs, gvec, d_middle.reshape(tokens.shape), first_t, w_qkv, [g_wdown, g_wup, g_wmix[None]], finished, owners, reps, factor, size,
        )
        o_wdown, o_wup, o_wmix, o_wqkv = (
            o.reshape(-1, n).astype(F32) for o, n in zip(outs, (width, SHARES * steps * FP, width, 3 * width))
        )
    else:
        d_mixed = d_mixed.reshape(tokens.shape)
        d_middle = d_middle.reshape(tokens.shape)
        d_heads = order(columns(d_mixed, 2, ctx), swap(columns(d_mixed, 2, 1 - ctx)), 1)
        d_query, d_key, d_value = attention_backward(query, key, value, d_heads, lse, factor, size)
        d_joined = jnp.concatenate([d_query, d_key, d_value], axis=-1)
        g_wqkv = outer_sum(first, d_joined)
        d_first = project_back(d_joined, w_qkv)
        d_first = my_rows(d_first) + swap(their_rows(d_first).astype(BF16)).astype(F32)
        normal_one, inverse_one = norm_stats(tokens)
        d_tokens = d_middle + norm_back(d_first, normal_one, inverse_one, g_attn)

        def reduce(grad):
            piece = lax.psum_scatter(
                grad.astype(BF16), ("fsdp", "rep", "ctx"), scatter_dimension=0, tiled=True
            )
            return lax.all_gather(piece, ("rep", "ctx"), axis=0, tiled=True).astype(F32)

        g_wdown = jnp.concatenate([g_wdown[f].reshape(SHARES, FP, width) for f in range(steps)], axis=1)
        o_wdown = reduce(g_wdown.reshape(-1, width))
        g_wup = jnp.stack([g_wup[f].reshape(width, SHARES, FP) for f in range(steps)], axis=2)
        o_wup = reduce(g_wup.reshape(width, -1))
        o_wmix = reduce(g_wmix.reshape(width, width))
        piece = lax.psum_scatter(g_wqkv.astype(BF16), ("fsdp", "rep"), scatter_dimension=0, tiled=True)
        piece = lax.all_gather(piece, "rep", axis=0, tiled=True)
        other = swap(piece)
        low, high = jnp.where(ctx == 0, piece, other), jnp.where(ctx == 0, other, piece)
        o_wqkv = jnp.concatenate(
            [t for i in range(3) for t in (low[:, i * half : (i + 1) * half], high[:, i * half : (i + 1) * half])],
            axis=1,
        ).astype(F32)

        def place(v):
            return lax.dynamic_update_slice_in_dim(jnp.zeros((width,), F32), v, ctx * half, 0)

        first_rows = (
            place(jnp.sum(d_query.astype(F32), axis=(0, 1))),
            place(jnp.sum(d_value.astype(F32), axis=(0, 1))),
            jnp.sum(d_first * normal_one, axis=(0, 1)),
            jnp.sum(d_first, axis=(0, 1)),
        )
        summed = jnp.concatenate([jnp.stack(first_rows[:2]), gvec[2:3], jnp.stack(first_rows[2:]), gvec[5:12]], axis=0)
        summed = lax.psum(summed, ("rep", "fsdp", "ctx"))
    owner = lax.axis_index("fsdp")
    o_bup = lax.dynamic_slice_in_dim(summed[8 : 8 + SHARES].reshape(-1), owner * b_up_rows, b_up_rows, 0)
    summed = lax.dynamic_slice_in_dim(summed[:8], owner * own, own, 1)
    o_bq, o_bv, o_bmix, o_ga, o_sa, o_gm, o_sm, o_bd = (summed[i] for i in range(8))
    return (
        result.reshape(inputs.shape),
        d_tokens[:, None],
        o_wqkv,
        o_bq,
        o_bv,
        o_wmix,
        o_bmix,
        o_ga,
        o_sa,
        o_gm,
        o_sm,
        o_wup,
        o_bup,
        o_wdown,
        o_bd,
    )


def solution(mesh):
    row = P(None, ("rep", "fsdp"), "ctx", None)
    mat = P("fsdp", None)
    vec = P("fsdp")
    params = (mat, vec, vec, mat, vec, vec, vec, vec, vec, mat, vec, mat, vec)
    in_specs = (row,) + params + (row,)
    out_specs = (row, row) + params
    return jax.shard_map(local, mesh=mesh, in_specs=in_specs, out_specs=out_specs, check_vma=False)
```

```python
from functools import partial

import jax
import jax.numpy as jnp
from jax import lax
from jax.experimental import pallas as pl
from jax.experimental.pallas import tpu as pltpu
from jax.sharding import PartitionSpec as P

H = 12
EPS = 1e-05
BF16 = jnp.bfloat16
F32 = jnp.float32
QB = 256
TB = 256
RB = 512
FP = 256
SHARES = 4
GELU_A = 0.7978845608028654
GELU_B = 0.044715
LOG2E = 1.4426950408889634


def norm_stats(values):
    center = values - jnp.mean(values, axis=-1, keepdims=True)
    inverse = lax.rsqrt(jnp.mean(center * center, axis=-1, keepdims=True) + EPS)
    return (center * inverse, inverse)


def norm_back(grad_norm, normal, inverse, gain):
    scaled = grad_norm * gain
    return inverse * (
        scaled
        - jnp.mean(scaled, axis=-1, keepdims=True)
        - normal * jnp.mean(scaled * normal, axis=-1, keepdims=True)
    )


def outer_sum(left, right):
    return jnp.einsum("sri,srj->ij", left, right, preferred_element_type=F32)


def project(left, weight):
    return jnp.einsum("sri,ij->srj", left, weight, preferred_element_type=F32)


def project_back(grad_rows, weight):
    return jnp.einsum("srj,ij->sri", grad_rows, weight, preferred_element_type=F32)


def dot_nt(a, b):
    return lax.dot_general(a, b, (((1,), (1,)), ((), ())), preferred_element_type=F32)


def dot_nn(a, b):
    return lax.dot_general(a, b, (((1,), (0,)), ((), ())), preferred_element_type=F32)


def head_mask(x, head, size):
    lane = lax.broadcasted_iota(jnp.int32, x.shape, 1)
    keep = (lane >= head * size) & (lane < (head + 1) * size)
    return jnp.where(keep, x, jnp.zeros_like(x))


def causal(scores_t, qb):
    n = scores_t.shape[0]
    bottom = scores_t[n - QB :]
    key = lax.broadcasted_iota(jnp.int32, bottom.shape, 0)
    query = lax.broadcasted_iota(jnp.int32, bottom.shape, 1)
    bottom = jnp.where(key <= query, bottom, -1e30)
    return bottom if n == QB else jnp.concatenate([scores_t[: n - QB], bottom], axis=0)


def attention_forward_kernel(factor, size, q_ref, k_ref, v_ref, o_ref, lse_ref):
    refs = [ref.at[0] for ref in (q_ref, k_ref, v_ref, o_ref)]
    attention_forward_block(factor, size, *refs, lse_ref.at[0, 0], lambda done: None)


def attention_forward_block(factor, size, q_ref, k_ref, v_ref, o_ref, lse_ref, between):
    length = q_ref.shape[0]
    base_two = factor * LOG2E
    k = k_ref[...]
    vt = jnp.transpose(v_ref[...])
    for qb in range(length // QB):
        n = (qb + 1) * QB
        rows = pl.ds(qb * QB, QB)
        q = q_ref[rows, :]
        outs = []
        for head in range(2):
            s = causal(dot_nt(k[:n], head_mask(q, head, size)), qb)
            top = jnp.max(s, axis=0, keepdims=True) * base_two
            p = jnp.exp2(s * base_two - top)
            total = jnp.sum(p, axis=0, keepdims=True)
            o = dot_nn(vt[head * size : (head + 1) * size, :n], p.astype(BF16))
            outs.append(o * (1.0 / total))
            lse_ref[head : head + 1, rows] = top + jnp.log2(total)
        o_ref[rows, :] = jnp.transpose(jnp.concatenate(outs, axis=0)).astype(o_ref.dtype)
        between(qb)


def attention_forward(q, k, v, factor, size):
    mbs, length, width = q.shape
    lanes = 2 * size
    pairs = width // lanes
    block = pl.BlockSpec((1, length, lanes), lambda m, p: (m, 0, p))
    area = mbs * pairs * 2 * length * (length + QB) // 2
    return pl.pallas_call(
        partial(attention_forward_kernel, factor, size),
        grid=(mbs, pairs),
        in_specs=[block] * 3,
        out_specs=[block, pl.BlockSpec((1, 1, 8, length), lambda m, p: (m, p, 0, 0))],
        out_shape=[
            jax.ShapeDtypeStruct(q.shape, BF16),
            jax.ShapeDtypeStruct((mbs, pairs, 8, length), F32),
        ],
        compiler_params=pltpu.CompilerParams(vmem_limit_bytes=48 << 20),
        cost_estimate=pl.CostEstimate(
            flops=16 * area * size, bytes_accessed=8 * q.size, transcendentals=area
        ),
        name="attention_forward",
    )(q, k, v)


def attention_backward_kernel(factor, size, q_ref, k_ref, v_ref, do_ref, lse_ref, dq_ref, dk_ref, dv_ref, dk_sum, dv_sum):
    refs = [ref.at[0] for ref in (q_ref, k_ref, v_ref, do_ref)]
    attention_backward_block(
        factor, size, *refs, lse_ref.at[0, 0], dq_ref.at[0], dk_ref.at[0], dv_ref.at[0], dk_sum, dv_sum, lambda done: None
    )


def attention_backward_block(
    factor, size, q_ref, k_ref, v_ref, do_ref, lse_ref, dq_ref, dk_ref, dv_ref, dk_sum, dv_sum, between
):
    length = q_ref.shape[0]
    base_two = factor * LOG2E
    k = k_ref[...]
    v = v_ref[...]
    kt = jnp.transpose(k)
    for i, qb in enumerate(reversed(range(length // QB))):
        n = (qb + 1) * QB
        rows = pl.ds(qb * QB, QB)
        q = q_ref[rows, :]
        do = do_ref[rows, :]
        dqs, dk, dv = [], None, None
        for head in range(2):
            qh = head_mask(q, head, size)
            doh = head_mask(do, head, size)
            s = causal(dot_nt(k[:n], qh), qb)
            p = jnp.exp2(s * base_two - lse_ref[head : head + 1, rows])
            dp = dot_nt(v[:n], doh)
            mean = jnp.sum(dp * p, axis=0, keepdims=True)
            ds = (p * (dp - mean)).astype(BF16)
            dvh = dot_nn(p.astype(BF16), doh)
            dkh = dot_nn(ds, qh)
            dv = dvh if dv is None else dv + dvh
            dk = dkh if dk is None else dk + dkh
            dqs.append(dot_nn(kt[head * size : (head + 1) * size, :n], ds))
        dq_ref[rows, :] = jnp.transpose(jnp.concatenate(dqs, axis=0) * factor).astype(BF16)
        if n == length:
            dk_sum[...] = dk
            dv_sum[...] = dv
        else:
            dk_sum[:n] += dk
            dv_sum[:n] += dv
        between(i)
    dk_ref[...] = (dk_sum[...] * factor).astype(BF16)
    dv_ref[...] = dv_sum[...].astype(BF16)


def attention_backward(q, k, v, do, lse, factor, size):
    mbs, length, width = q.shape
    lanes = 2 * size
    pairs = width // lanes
    block = pl.BlockSpec((1, length, lanes), lambda m, p: (m, 0, p))
    area = mbs * pairs * 2 * length * (length + QB) // 2
    return pl.pallas_call(
        partial(attention_backward_kernel, factor, size),
        grid=(mbs, pairs),
        in_specs=[block] * 4 + [pl.BlockSpec((1, 1, 8, length), lambda m, p: (m, p, 0, 0))],
        out_specs=[block] * 3,
        out_shape=[jax.ShapeDtypeStruct(q.shape, BF16)] * 3,
        scratch_shapes=[pltpu.VMEM((length, lanes), F32)] * 2,
        compiler_params=pltpu.CompilerParams(vmem_limit_bytes=48 << 20),
        cost_estimate=pl.CostEstimate(
            flops=40 * area * size, bytes_accessed=14 * q.size, transcendentals=area
        ),
        name="attention_backward",
    )(q, k, v, do, lse)


MESH = pl.DeviceIdType.MESH


def position():
    return lax.axis_index("fsdp"), lax.axis_index("rep"), lax.axis_index("ctx")


def greet(owners, reps, across=False):
    z, r, c = position()
    barrier = pltpu.get_barrier_semaphore()
    peers = [{"fsdp": lax.rem(z + j, owners)} for j in range(1, owners)]
    peers += [{"rep": r ^ j} for j in range(1, reps)]
    peers += [{"ctx": 1 - c}]
    if across:
        peers += [{"rep": r ^ j, "ctx": 1 - c} for j in range(1, reps)]
    for peer in peers:
        pl.semaphore_signal(barrier, inc=1, device_id=peer, device_id_type=MESH)
    pl.semaphore_wait(barrier, len(peers))


def slab(i, half):
    return pl.ds(pl.multiple_of(i * half, 128), half)


def add_blocks(out, parts, dtype):
    lead = out.shape[:-2]
    count = 1
    for n in lead:
        count *= n

    def body(i, _):
        at = []
        for n in reversed(lead):
            at.append(lax.rem(i, n))
            i = lax.div(i, n)
        at = tuple(reversed(at))
        terms = [p[at].astype(F32) for p in parts]
        while len(terms) > 1:
            terms = [terms[0] + terms[1]] + terms[2:]
        out[at] = terms[0].astype(dtype)
        return 0

    lax.fori_loop(0, count, body, 0)


class Plan:
    def __init__(self, send, recv):
        self.send, self.recv = send, recv
        self.made, self.left = {}, set()

    def add(self, name, src, dst, peer):
        self.made[name] = (len(self.made), src, dst, peer)

    def copy(self, name):
        slot, src, dst, peer = self.made[name]
        return pltpu.make_async_remote_copy(
            src_ref=src(),
            dst_ref=dst(),
            send_sem=self.send.at[slot],
            recv_sem=self.recv.at[slot],
            device_id=peer,
            device_id_type=MESH,
        )

    def start(self, *names):
        for name in names:
            self.copy(name).start()

    def arrive(self, *names):
        for name in names:
            self.copy(name).wait_recv()

    def leave(self, *names):
        for name in names:
            self.copy(name).wait_send()
            self.left.add(name)

    def close(self):
        for name in self.made:
            if name not in self.left:
                self.copy(name).wait_send()


def spread_plan(plan, tag, owners, reps, z, r, c, src, dst, halves, core=None):
    for j in range(1, owners):
        origin = lax.rem(z - j + owners, owners)
        if src is not None:
            plan.add((tag, "z", j), src, lambda: dst(z, r), {"fsdp": lax.rem(z + j, owners)})
        here = partial(dst, origin, r)
        plan.add((tag, "x", j), here, here, {"rep": r ^ 1})
        plan.add((tag, "y", j), here, here, {"rep": r ^ 2})
        by_y = lambda origin=origin: halves(dst(origin, r ^ 2))[0]
        by_x = lambda origin=origin: halves(dst(origin, r ^ 1))[1]
        plan.add((tag, "xx", j), by_y, by_y, {"rep": r ^ 1})
        plan.add((tag, "yy", j), by_x, by_x, {"rep": r ^ 2})
        if core is not None:
            side = partial(core, origin)
            plan.add((tag, "c", j), side, side, {"ctx": 1 - c})


def spread_step(plan, tag, owners, stage):
    for j in range(1, owners):
        if stage == 0:
            plan.start((tag, "z", j))
        elif stage == 1:
            if (tag, "z", j) in plan.made:
                plan.arrive((tag, "z", j))
            plan.start((tag, "x", j), (tag, "y", j))
        elif stage == 2:
            plan.arrive((tag, "y", j))
            plan.start((tag, "xx", j))
            plan.arrive((tag, "x", j))
            plan.start((tag, "yy", j))
        elif stage == 3:
            plan.arrive((tag, "xx", j), (tag, "yy", j))
            if (tag, "c", j) in plan.made:
                plan.start((tag, "c", j))
        else:
            plan.arrive((tag, "c", j))


def up_side(ref, c):
    half = ref.shape[-1] // 2
    return ref.at[:, pl.ds(pl.multiple_of(c * half, 128), half)]


def up_piece(ref, c, r):
    return ref.at[:, pl.ds(pl.multiple_of((c * 4 + r) * 128, 128), 128)]


def down_side(ref, c):
    half = ref.shape[0] // 2
    return ref.at[pl.ds(pl.multiple_of(c * half, 32), half)]


def down_piece(ref, c, r):
    piece = ref.shape[0] // 8
    return ref.at[pl.ds(pl.multiple_of((c * 4 + r) * piece, 32), piece)]


def uneven_halves(ref):
    middle = ref.shape[1] // 256 * 128
    return ref.at[:, pl.ds(0, middle)], ref.at[:, pl.ds(middle, ref.shape[1] - middle)]


def row_halves(ref):
    middle = ref.shape[0] // 2
    return ref.at[pl.ds(0, middle)], ref.at[pl.ds(middle, middle)]


def column_halves(ref):
    middle = ref.shape[-1] // 2
    return ref.at[:, pl.ds(0, middle)], ref.at[:, pl.ds(middle, middle)]


SPREADS = [
    (-1, 0, 1), (-1, 1, 1), (2, 2, 1), (5, 0, 2), (9, 1, 2), (9, 0, 3), (14, 2, 2), (14, 1, 3), (15, 0, 4), (18, 1, 4),
    (19, 2, 3), (23, 2, 4),
]


def forward_kernel(owners, reps, pairs, factor, size,
                   x_ref, qkv_ref, mix_ref, up_ref, down_ref, *refs):
    vectors, b_up_ref, refs = refs[:8], refs[8], refs[9:]
    (mixed, qkv_out, first_t_out, w_qkv_out, w_mix, w_up, w_down, vec_ref, bup_ref, lse_ref, small_ref,
                   first, first_t, w_qkv, qkv, heads, small, own_mix, own_up, own_down, send, recv, kept) = refs
    step = pl.program_id(0)
    last = pl.num_programs(0) - 1
    z, r, c = position()
    mbs, rows, width = x_ref.shape
    half = width // 2
    lanes = 2 * size
    plan = Plan(send, recv)
    own_rows = pl.ds(pl.multiple_of(c * rows, rows), rows)
    their_rows = pl.ds(pl.multiple_of((1 - c) * rows, rows), rows)

    for j in range(1, owners):
        plan.add(("small", j), lambda: small_ref, lambda: small.at[z], {"fsdp": lax.rem(z + j, owners)})
    for m in range(mbs):
        plan.add(("first", m), lambda m=m: first.at[m, own_rows], lambda m=m: first.at[m, own_rows], {"ctx": 1 - c})
    for i in range(3):
        spread_plan(
            plan, ("qkv", i), owners, reps, z, r, c,
            lambda i=i: qkv_ref.at[r, :, slab(2 * i + c, half)],
            lambda o, p, i=i: w_qkv.at[o, p, :, slab(i, half)],
            uneven_halves,
        )
    steps = w_up.shape[0]
    spread_plan(
        plan, ("mix", 0), owners, reps, z, r, c,
        lambda: own_mix.at[c, r], lambda o, p: w_mix.at[o, c, p], column_halves, lambda o: w_mix.at[o, c],
    )
    for tag, own, whole, piece, side in (("up", own_up, w_up, up_piece, up_side), ("down", own_down, w_down, down_piece, down_side)):
        for f in range(steps):
            dst = lambda o, p, whole=whole, piece=piece, f=f: piece(whole.at[f, o], c, p)
            src = lambda own=own, piece=piece, f=f: piece(own.at[f], c, r)
            if f == 0:
                core = lambda o, whole=whole, side=side, f=f: side(whole.at[f, o], c)
                spread_plan(plan, (tag, f), owners, reps, z, r, c, src, dst, row_halves, core)
            else:
                for j in range(1, owners):
                    to = lax.rem(z + j, owners)
                    plan.add(((tag, f), "z", j), src, lambda dst=dst: dst(z, r), {"fsdp": to})
    quarters = 2 * rows // QB
    table = SPREADS
    order = [("mix", 0)] + [(tag, f) for f in range(steps) for tag in ("up", "down")]

    up_step = own_up.shape[-1] // owners
    pairs_of = [(small_ref, small.at[z])]
    pairs_of += [(qkv_ref.at[:, :, slab(2 * i + c, half)], w_qkv.at[z, :, :, slab(i, half)]) for i in range(3)]
    pairs_of += [(mix_ref, own_mix)]
    early = len(pairs_of)
    for f in range(steps):
        for k in range(owners):
            cols = pl.ds((k * (up_ref.shape[-1] // owners)) + f * up_step, up_step)
            pairs_of += [(up_ref.at[:, cols], own_up.at[f, :, pl.ds(k * up_step, up_step)])]
        pairs_of += [(down_ref.at[pl.ds(f * own_down.shape[1], own_down.shape[1])], own_down.at[f])]
    loads = len(pairs_of)
    pairs_of += [(own_mix, w_mix.at[z])]
    for f in range(steps):
        pairs_of += [(own_up.at[f], w_up.at[f, z]), (own_down.at[f], w_down.at[f, z])]
    stores = len(pairs_of)
    pairs_of += [(w_qkv, w_qkv_out), (first_t, first_t_out), (qkv, qkv_out)]
    ends = len(pairs_of)

    def keep(i):
        return pltpu.make_async_copy(*pairs_of[i], kept.at[i])

    def mixed_place(step):
        m, p = lax.div(step, pairs), lax.rem(step, pairs)
        return mixed.at[m, :, slab(c * pairs + p, lanes)]

    def mixed_sends(k, slot):
        return pltpu.make_async_remote_copy(
            src_ref=heads.at[k, their_rows],
            dst_ref=mixed_place(k),
            send_sem=send.at[slot],
            recv_sem=recv.at[slot],
            device_id={"ctx": 1 - c},
            device_id_type=MESH,
        )

    base = len(plan.made)

    @pl.when(step == 0)
    def _():
        for i in range(1, loads):
            keep(i).start()
        small_ref[...] = jnp.zeros_like(small_ref)
        own = vectors[0].shape[0]
        for i, vector in enumerate(vectors):
            small_ref[i : i + 1, :own] = vector[...].astype(F32).reshape(1, own)
        for f in range(steps):
            small_ref[8 + f : 9 + f, :] = b_up_ref[f * FP : (f + 1) * FP].astype(F32).reshape(1, FP)
        greet(owners, reps)
        keep(0).start()
        plan.start(*[("small", j) for j in range(1, owners)])
        for i in range(3):
            spread_step(plan, ("qkv", i), owners, 0)
        keep(0).wait()
        plan.arrive(*[("small", j) for j in range(1, owners)])
        vec_ref[...] = jnp.concatenate([small[k, :, :own] for k in range(owners)], axis=1)
        bup_ref[...] = jnp.concatenate([small[k, 8:16] for k in range(owners)], axis=1)
        gain, shift = vec_ref[3:4, :], vec_ref[4:5, :]
        for m in range(mbs):
            for at in range(0, rows, TB):
                normal, _ = norm_stats(x_ref[m, at : at + TB].astype(F32))
                place = pl.ds(pl.multiple_of(c * rows + at, TB), TB)
                first[m, place] = (normal * gain + shift).astype(BF16)
            plan.start(("first", m))
        spread_step(plan, ("qkv", 0), owners, 1)
        for i in range(4, loads):
            keep(i).wait()
        for i in range(loads, stores):
            keep(i).start()
        plan.arrive(*[("first", m) for m in range(mbs)])
        spread_step(plan, ("qkv", 1), owners, 1)
        spread_step(plan, ("qkv", 0), owners, 2)
        spread_step(plan, ("qkv", 2), owners, 1)
        for tag in order[:3]:
            spread_step(plan, tag, owners, 0)

        def turn(i, _):
            m, at = lax.div(i, 2 * rows // TB), lax.rem(i, 2 * rows // TB)
            place = pl.ds(pl.multiple_of(at * TB, TB), TB)
            first_t[:, pl.ds(pl.multiple_of(i * TB, TB), TB)] = jnp.transpose(first[m, place])
            return 0

        lax.fori_loop(0, mbs * 2 * rows // TB, turn, 0)
        keep(stores + 1).start()
        spread_step(plan, ("qkv", 1), owners, 2)

        def project_all(i):
            weight = w_qkv[:, :, :, i * half : (i + 1) * half].reshape(-1, half)
            bias = None if i == 1 else vec_ref[i // 2 : i // 2 + 1, slab(c, half)]

            def project_rows(n, _):
                m, at = lax.div(n, 2 * rows // TB), lax.rem(n, 2 * rows // TB)
                place = pl.ds(pl.multiple_of(at * TB, TB), TB)
                joined = dot_nn(first[m, place], weight)
                joined = (joined if bias is None else joined + bias).astype(BF16)
                for s in range(pairs):
                    qkv[m, i * pairs + s, place] = joined[:, s * lanes : (s + 1) * lanes]
                return 0

            lax.fori_loop(0, mbs * 2 * rows // TB, project_rows, 0)

        for i in range(1, 4):
            keep(i).wait()
        for i in range(3):
            if i == 1:
                spread_step(plan, ("qkv", 2), owners, 2)
            spread_step(plan, ("qkv", i), owners, 3)
            if i == 2:
                for when, t, stage in table:
                    if when < 0:
                        spread_step(plan, order[t], owners, stage)
            project_all(i)
        keep(stores).start()
        keep(stores + 2).start()

    def between(k, done):
        for i in range(mbs * pairs):
            some = [entry for entry in table if entry[0] == i * quarters + done]
            if some:

                @pl.when(k == i)
                def _():
                    for _, t, stage in some:
                        spread_step(plan, order[t], owners, stage)

    @pl.when(step == 1)
    def _():
        for tag in order[3:]:
            spread_step(plan, tag, owners, 0)

    @pl.when(step > 0)
    def _():
        k = step - 1
        m, p = lax.div(k, pairs), lax.rem(k, pairs)
        attention_forward_block(
            factor, size, qkv.at[m, p], qkv.at[m, pairs + p], qkv.at[m, 2 * pairs + p], heads.at[k], lse_ref.at[m, p],
            partial(between, k),
        )
        mixed_sends(k, base + k).start()
        pltpu.make_async_copy(heads.at[k, own_rows], mixed_place(k), kept.at[ends + k]).start()

    @pl.when(step == last)
    def _():
        for when, t, stage in table:
            if when >= quarters * mbs * pairs:
                spread_step(plan, order[t], owners, stage)
        for k in range(mbs * pairs):
            mixed_sends(k, base + k).wait()
            pltpu.make_async_copy(heads.at[k, own_rows], mixed_place(k), kept.at[ends + k]).wait()
        for tag in order[3:]:
            for j in range(1, owners):
                plan.arrive((tag, "z", j))
        plan.close()
        for i in range(loads, ends):
            keep(i).wait()


def forward_block(x, weight_qkv, weight_mix, weight_up, weight_down, vectors, b_up, owners, reps, factor, size):
    own, wide = weight_qkv.shape
    mbs, rows, width = x.shape
    lanes = 2 * size
    pairs = width // 2 // lanes

    def cut(shard):
        return shard.reshape(2, reps, shard.shape[0] // (2 * reps), shard.shape[1])

    steps = weight_down.shape[0] // FP
    shards = (weight_qkv.reshape(reps, own // reps, wide), cut(weight_mix), weight_up, weight_down)
    own_up = (steps, own, owners * FP)
    own_down = (steps, FP, width)
    shape = jax.ShapeDtypeStruct
    w_shape = (owners, reps, own // reps, wide // 2)
    qkv_shape = (mbs, 3 * pairs, 2 * rows, lanes)
    anywhere = pl.BlockSpec(memory_space=pl.ANY)
    whole = lambda s: pl.BlockSpec(s, lambda i: (0,) * len(s), pipeline_mode=pl.Buffered(1))
    remotes = 3 + mbs + 3 * 15 + 3 * 18 + 6 * (steps - 1) + mbs * pairs
    copies = 5 + steps * (owners + 1) + 1 + 2 * steps + 3 + mbs * pairs
    area = mbs * pairs * 2 * rows * (2 * rows + QB)
    mixed, qkv, first_t, w_qkv, w_mix, w_up, w_down, vecs, b_up, lse = pl.pallas_call(
        partial(forward_kernel, owners, reps, pairs, factor, size),
        grid=(1 + mbs * pairs,),
        in_specs=[whole(x.shape)] + [anywhere] * 4 + [whole(v.shape) for v in (*vectors, b_up)],
        out_specs=[anywhere] * 7 + [whole((16, width)), whole((8, owners * FP)), whole((mbs, pairs, 8, 2 * rows))],
        out_shape=[
            shape((mbs, rows, width), BF16),
            shape(qkv_shape, BF16),
            shape((width, mbs * 2 * rows), BF16),
            shape(w_shape, BF16),
            shape((owners,) + shards[1].shape, BF16),
            shape(own_up[:1] + (owners,) + own_up[1:], BF16),
            shape(own_down[:1] + (owners,) + own_down[1:], BF16),
            shape((16, width), F32),
            shape((8, owners * FP), F32),
            shape((mbs, pairs, 8, 2 * rows), F32),
        ],
        scratch_shapes=[
            pltpu.VMEM((16, FP), F32),
            pltpu.VMEM((mbs, 2 * rows, width), BF16),
            pltpu.VMEM((width, mbs * 2 * rows), BF16),
            pltpu.VMEM(w_shape, BF16),
            pltpu.VMEM(qkv_shape, BF16),
            pltpu.VMEM((mbs * pairs, 2 * rows, lanes), BF16),
            pltpu.VMEM((owners, 16, FP), F32),
            pltpu.VMEM(shards[1].shape, BF16),
            pltpu.VMEM(own_up, BF16),
            pltpu.VMEM(own_down, BF16),
            pltpu.SemaphoreType.DMA((remotes,)),
            pltpu.SemaphoreType.DMA((remotes,)),
            pltpu.SemaphoreType.DMA((copies,)),
        ],
        compiler_params=pltpu.CompilerParams(
            collective_id=1, has_side_effects=True, vmem_limit_bytes=56 << 20
        ),
        name="forward_block",
    )(x, *shards, *vectors, b_up)
    return (
        mixed,
        qkv,
        first_t,
        w_qkv.reshape(owners * own, -1),
        w_mix.reshape(owners * own, -1),
        w_up,
        w_down,
        vecs,
        b_up[:steps].reshape(steps, 1, owners * FP),
        lse,
    )


class Flow:
    def __init__(self, plan, name, place, owners, bits, mine, theirs, hops, outs, load=None, core=None):
        z, r, c = place
        first, second = bits
        self.plan, self.name, self.place, self.owners = plan, name, place, owners
        self.mine, self.theirs, self.second = mine, theirs, r ^ second
        self.hop_one, self.hop_two, self.hop_z, self.final = hops
        self.outs = outs
        self.load = load
        peer = {"rep": r ^ first}
        if core is not None:
            plan.add((name, "core"), core, lambda: theirs, {"ctx": 1 - c})
        self.split = core is not None
        plan.add((name, "me"), lambda: mine.at[:, r ^ first], lambda: self.hop_one.at[0], peer)
        plan.add((name, "on"), lambda: mine.at[:, r ^ first ^ second], lambda: self.hop_one.at[1], peer)
        plan.add((name, "two"), lambda: mine.at[:, r ^ second], lambda: self.hop_two, {"rep": r ^ second})
        for j in range(1, owners):
            to = lax.rem(z + j, owners)
            plan.add((name, "z", j), lambda to=to: mine.at[to, r], lambda j=j: self.hop_z.at[j - 1], {"fsdp": to})
        here = lambda: self.final.at[c, r]
        plan.add((name, "x"), here, here, {"rep": r ^ first})
        plan.add((name, "y"), here, here, {"rep": r ^ second})
        far = lambda: self.final.at[c, r ^ second]
        plan.add((name, "xy"), far, far, {"rep": r ^ first})
        side = lambda: self.final.at[c]
        plan.add((name, "back"), side, side, {"ctx": 1 - c})

    def step(self, stage):
        z, r, c = self.place
        plan, name, mine = self.plan, self.name, self.mine
        owners = self.owners
        if stage == 0:
            if self.split:
                plan.start((name, "core"))
            if self.load is not None:
                self.load().start()
        elif stage == 1:
            if self.load is not None:
                self.load().wait()
            if self.split:
                plan.arrive((name, "core"))
                add_blocks(mine, [mine, self.theirs], BF16)
            plan.start((name, "on"), (name, "me"))
        elif stage == 2:
            plan.arrive((name, "on"))
            part = mine.at[:, self.second]
            add_blocks(part, [part, self.hop_one.at[1]], BF16)
            plan.start((name, "two"))
        elif stage == 3:
            plan.arrive((name, "me"), (name, "two"))
            part = mine.at[:, r]
            add_blocks(part, [part, self.hop_one.at[0], self.hop_two], BF16)
            plan.start(*[(name, "z", j) for j in range(1, owners)])
        elif stage == 4:
            plan.arrive(*[(name, "z", j) for j in range(1, owners)])
            terms = [mine[z, r].astype(F32)] + [self.hop_z[j].astype(F32) for j in range(owners - 1)]
            while len(terms) > 1:
                terms = [a + b for a, b in zip(terms[::2], terms[1::2])]
            self.final[c, r] = terms[0].astype(BF16)
            plan.start((name, "x"), (name, "y"))
        elif stage == 5:
            plan.arrive((name, "y"))
            plan.start((name, "xy"))
        elif stage == 6:
            plan.arrive((name, "x"), (name, "xy"))
            plan.start((name, "back"))
        else:
            plan.arrive((name, "back"))
            for copy in self.outs(self.final):
                copy.start()


def flow_scratch(owners, reps, piece, split):
    vmem = lambda *lead: pltpu.VMEM(lead + piece, BF16)
    mine = [vmem(owners, reps)] * (2 if split else 1)
    return mine + [vmem(2, owners), vmem(owners), vmem(owners - 1), vmem(2, reps)]


def timetable(groups, products):
    table = []
    for g in range(groups):
        second = 4 + 5 * g
        times = (2 * g - 1, second, second + 5, second + 9, second + 11, second + 13, second + 15)
        table += [(t, g, 1 + i) for i, t in enumerate(times)]
    for p, second in zip(range(products), (25, 27, 28)):
        times = (second, second + 4, second + 8, second + 10, second + 12, second + 14)
        table += [(t, groups + p, 2 + i) for i, t in enumerate(times)]
    return sorted(table)


def gelu_parts(b):
    cubic = (GELU_A * GELU_B) * (b * b)
    t = jnp.tanh(b * (cubic + GELU_A))
    rise = 0.5 * t + 0.5
    active = b * rise
    return active, rise + active * (1.0 - t) * (3.0 * cubic + GELU_A)


GATHERS = [
    (1, ("up", 1), 2), (1, ("down", 1), 2), (2, ("up", 1), 3), (2, ("down", 1), 3), (2, ("up", 2), 1), (2, ("down", 2), 1),
    (4, ("up", 1), 4), (4, ("down", 1), 4), (5, ("up", 2), 2), (5, ("down", 2), 2), (6, ("up", 2), 3), (6, ("down", 2), 3),
    (8, ("up", 2), 4), (8, ("down", 2), 4),
]
SUMS = [
    (3, 0, 0), (3, 1, 0), (5, 0, 1), (6, 1, 1), (8, 0, 2), (9, 1, 2), (9, 0, 3), (10, 1, 3), (10, 0, 4), (11, 0, 5),
    (11, 1, 4), (12, 1, 5), (12, 0, 6), (13, 1, 6), (14, 0, 7), (14, 1, 7),
]


def middle_kernel(owners, reps, direct, *refs):
    x_ref, mixed_ref, d_ref, wmix_ref, wup_any, wdown_any, vec_ref, bup_ref = refs[:8]
    result_ref, dmid_ref, gmix_ref, gvec_ref = refs[8:12]
    refs = refs[12:]
    if direct:
        heads_out, up_sums, down_sums, down_out, up_out, dmixed_ref, gup_ref, gdown_ref, up_got, down_got = refs[:10]
        refs = refs[10:]
    else:
        dmixed_ref, gup_ref, gdown_ref = refs[:3]
        refs = refs[3:]
    middle, second, second_t, mixed_t, out_sum, ds_sum, active_t, d_before, w_up, w_down = refs[:10]
    refs = refs[10:]
    step = pl.program_id(0)
    rows = x_ref.shape[0]
    steps = w_up.shape[0]
    last = steps - 1
    count = rows // RB
    chunk = lambda i: pl.ds(pl.multiple_of(i * RB, RB), RB)
    b_mix, gain, shift, b_down = (vec_ref[i : i + 1, :] for i in (2, 5, 6, 7))
    slots = 4

    if direct:
        flow_refs, (send, recv, kept) = refs[:-3], refs[-3:]
        place = z, r, c = position()
        plan = Plan(send, recv)
        used = 0

        def local(src, dst):
            nonlocal used
            used += 1
            slot = kept.at[used - 1]
            return lambda: pltpu.make_async_copy(src(), dst(), slot)

        own_rows, part = w_up.shape[1] // owners, w_down.shape[1] // owners
        up_of = lambda ref, f, o: ref.at[f, pl.ds(pl.multiple_of(o * own_rows, 32), own_rows)]
        down_of = lambda ref, f, o: ref.at[f, pl.ds(pl.multiple_of(o * part, 32), part)]
        loads, pieces = [], {}
        for tag, source, whole, of, piece, side in (
            ("up", wup_any, w_up, up_of, up_piece, up_side),
            ("down", wdown_any, w_down, down_of, down_piece, down_side),
        ):
            for o in range(owners):
                loads.append(local(lambda o=o, s=source: s.at[0, o], lambda o=o, w=whole, of=of: of(w, 0, o)))
            for f in range(1, steps):
                loads.append(
                    local(lambda f=f, s=source: s.at[f, z], lambda f=f, w=whole, of=of: of(w, f, z))
                )
                pieces[tag, f] = [
                    local(
                        lambda f=f, j=j, s=source, p=piece: p(s.at[f, lax.rem(z + j, owners)], c, r),
                        lambda f=f, j=j, w=whole, of=of, p=piece: p(of(w, f, lax.rem(z + j, owners)), c, r),
                    )
                    for j in range(1, owners)
                ]
                spread_plan(
                    plan, (tag, f), owners, reps, z, r, c, None,
                    lambda o, p, f=f, w=whole, of=of, piece=piece: piece(of(w, f, o), c, p),
                    row_halves,
                    lambda o, f=f, w=whole, of=of, side=side: side(of(w, f, o), c),
                )
        cores = []
        for f in range(1, steps):
            for tag, ref, got, sums in (("d", gdown_ref, down_got, down_sums), ("u", gup_ref, up_got, up_sums)):
                there = lambda got=got, f=f: got.at[f - 1]
                plan.add(("core", tag, f), lambda ref=ref: ref.at[0, :, 1 - c], there, {"ctx": 1 - c})
                cores.append((f, ("core", tag, f), ref, there, local(there, lambda sums=sums, f=f: sums.at[f - 1])))
        mbs, pairs, lanes = heads_out.shape[1], heads_out.shape[0], heads_out.shape[3]
        seq = rows // mbs
        seq_rows = pl.ds(pl.multiple_of(c * seq, seq), seq)
        kept_heads = []
        for m in range(mbs):
            for p in range(pairs):
                part_of = lambda side, m=m, p=p: dmixed_ref.at[pl.ds(m * seq, seq), slab(side * pairs + p, lanes)]
                to = lambda m=m, p=p: heads_out.at[p, m, seq_rows]
                plan.add(("heads", m, p), partial(part_of, 1 - c), to, {"ctx": 1 - c})
                kept_heads.append(local(partial(part_of, c), to))
        flows, leaving, at = [], [], 0
        for i, (ref, out) in enumerate(((gdown_ref, down_out), (gup_ref, up_out))):
            wide = ref.shape[-1] // 2
            up_step = ref.shape[-1] // owners
            for s in range(2):
                mine, theirs, *hops = flow_refs[at : at + 6]
                at += 6
                cols, final = pl.ds(s * wide, wide), hops[-1]
                if i == 1:
                    places = []
                    for k in range(wide // up_step):
                        to = pl.ds((s * wide // up_step + k) * steps * up_step, up_step)
                        places.append((
                            lambda final=final, k=k: final.at[:, :, :, pl.ds(k * up_step, up_step)],
                            lambda out=out, to=to: out.at[:, :, :, to],
                        ))
                else:
                    places = [(lambda final=final: final, lambda out=out, cols=cols: out.at[0, :, :, :, cols])]
                copies = [local(src, dst) for src, dst in places]
                leaving.extend(copies)
                flows.append(
                    Flow(
                        plan, (i, s), place, owners, (1, 2) if s == 0 else (2, 1), mine, theirs, hops,
                        lambda final, copies=copies: [f() for f in copies],
                        local(lambda ref=ref, cols=cols: ref.at[0, :, c, :, :, cols], lambda mine=mine: mine),
                        lambda ref=ref, cols=cols: ref.at[0, :, 1 - c, :, :, cols],
                    )
                )
    else:
        kept = refs[0]
        loads = [
            lambda: pltpu.make_async_copy(wup_any, w_up, kept.at[0]),
            lambda: pltpu.make_async_copy(wdown_any, w_down, kept.at[1]),
        ]

    def core_sums(step):
        for f, name, ref, there, out in cores:
            if f == step:
                plan.arrive(name)
                add_blocks(there(), [there(), ref.at[0, :, c]], BF16)
                out().start()
                plan.leave(name)

    def between(slot, here=True):
        if not direct:
            return
        for k in range(steps):
            some = [lambda t=t, n=n: spread_step(plan, t, owners, n) for when, t, n in GATHERS if when == k * slots + slot]
            some += [lambda g=g, n=n: [flow.step(n) for flow in flows[2 * g : 2 * g + 2]] for when, g, n in SUMS if when == k * slots + slot]
            if some:

                @pl.when((step == k) & here)
                def _():
                    for act in some:
                        act()

    @pl.when(step == 0)
    def _():
        for copy in loads:
            copy().start()
        if direct:
            for some in pieces.values():
                for copy in some:
                    copy().start()
            greet(owners, reps)
            for f in range(1, steps):
                for tag in ("up", "down"):
                    for copy in pieces[tag, f]:
                        copy().wait()
                    if f == 1:
                        spread_step(plan, (tag, f), owners, 1)
        gvec_ref[...] = jnp.zeros_like(gvec_ref)

        def prepare(i, _):
            at = chunk(i)
            mixed = mixed_ref[at]
            mixed_t[:, at] = jnp.transpose(mixed)
            mid = x_ref[at].astype(F32) + (dot_nn(mixed, wmix_ref[...]) + b_mix)
            middle[at] = mid
            out_sum[at] = mid + b_down
            ds_sum[at] = jnp.zeros_like(mid)
            normal, _ = norm_stats(mid)
            low = (normal * gain + shift).astype(BF16)
            second[at] = low
            second_t[:, at] = jnp.transpose(low)
            return 0

        lax.fori_loop(0, count, prepare, 0)
        for copy in loads:
            copy().wait()

    between(0)

    def feed(i, d_bup):
        at = chunk(i)
        act, slope = gelu_parts(dot_nn(second[at], w_up[step]) + bup_ref[0])
        act = act.astype(BF16)
        active_t[:, at] = jnp.transpose(act)
        db = (dot_nt(d_ref[at], w_down[step]) * slope).astype(BF16)
        d_before[at] = db
        out_sum[at] += dot_nn(act, w_down[step])
        ds_sum[at] += dot_nt(db, w_up[step])
        between(1, i == count // 2 - 1)
        return d_bup + jnp.sum(db.astype(F32), axis=0, keepdims=True)

    d_bup = lax.fori_loop(0, count, feed, jnp.zeros(bup_ref.shape[1:], F32))
    between(2)

    width = d_bup.shape[1] // owners
    for k in range(owners):
        gvec_ref[8 + k : 9 + k, slab(step, width)] = d_bup[:, k * width : (k + 1) * width]
    if direct:

        @pl.when(step == 1)
        def _():
            plan.leave(*[(flow.name, "core") for flow in flows])

        @pl.when(step == 2)
        def _():
            core_sums(1)

    share = second_t.shape[0] // owners
    part = active_t.shape[0] // owners

    def weights(o, _):
        two = pl.ds(2 * o, 2)
        lines = pl.ds(pl.multiple_of(o * 2 * part, part), 2 * part)
        gdown_ref[0, two] = dot_nn(active_t[lines], d_ref[...]).reshape((2,) + gdown_ref.shape[2:]).astype(BF16)
        lines = pl.ds(pl.multiple_of(o * 2 * share, 64), 2 * share)
        gup_ref[0, two] = dot_nn(second_t[lines], d_before[...]).reshape((2,) + gup_ref.shape[2:]).astype(BF16)
        return 0

    lax.fori_loop(0, owners // 2, weights, 0)
    if direct:
        for f in range(1, steps):

            @pl.when(step == f)
            def _():
                for when, name, *_ in cores:
                    if when == f:
                        plan.start(name)

    between(slots - 1)

    @pl.when(step == last)
    def _():

        def finish(i, sums):
            at = chunk(i)
            result_ref[at] = out_sum[at].astype(BF16)
            normal, inverse = norm_stats(middle[at])
            ds = ds_sum[at]
            grad_out = d_ref[at].astype(F32)
            d_mid = grad_out + norm_back(ds, normal, inverse, gain)
            dmid_ref[at] = d_mid
            branch = d_mid.astype(BF16)
            second[at] = branch
            dmixed_ref[at] = dot_nt(branch, wmix_ref[...]).astype(BF16)
            parts = (branch.astype(F32), ds * normal, ds, grad_out)
            return tuple(s + jnp.sum(p, axis=0, keepdims=True) for s, p in zip(sums, parts))

        zero = jnp.zeros((1, x_ref.shape[1]), F32)
        sums = lax.fori_loop(0, count, finish, (zero,) * 4)
        for i, k in enumerate((2, 5, 6, 7)):
            gvec_ref[k : k + 1, :] = sums[i]

        if direct:
            plan.start(*[("heads", m, p) for m in range(mbs) for p in range(pairs)])
            for copy in kept_heads:
                copy().start()

        def mix(o, _):
            lines = pl.ds(pl.multiple_of(o * share, 64), share)
            gmix_ref[o] = dot_nn(mixed_t[lines], second[...]).reshape(gmix_ref.shape[1:]).astype(BF16)
            return 0

        lax.fori_loop(0, owners, mix, 0)
        if direct:
            core_sums(last)
            for when, g, n in SUMS:
                if when >= steps * slots:
                    for flow in flows[2 * g : 2 * g + 2]:
                        flow.step(n)
            plan.arrive(*[("heads", m, p) for m in range(mbs) for p in range(pairs)])
            plan.close()
            for copy in kept_heads + [out for *_, out in cores]:
                copy().wait()
            for copy in leaving:
                copy().wait()


def middle_block(x, mixed, d_out, w_mix, w_up, w_down, vecs, b_up, owners, reps, direct, heads):
    rows, width = x.shape
    steps = w_up.shape[0]
    ff = steps * owners * FP
    whole = lambda shape: pl.BlockSpec(shape, lambda f: (0,) * len(shape), pipeline_mode=pl.Buffered(1))
    anywhere = pl.BlockSpec(memory_space=pl.ANY)
    out = jax.ShapeDtypeStruct
    vmem = pltpu.VMEM
    side = (owners, 2, reps)
    g_mix = side + (width // owners // 2 // reps, width)
    g_up = (1,) + g_mix[:-1] + (owners * FP,)
    g_down = (1,) + side + (FP // 2 // reps, width)
    scratch = [
        vmem((rows, width), F32),
        vmem((rows, width), BF16),
        vmem((width, rows), BF16),
        vmem((width, rows), BF16),
        vmem((rows, width), F32),
        vmem((rows, width), F32),
        vmem((owners * FP, rows), BF16),
        vmem((rows, owners * FP), BF16),
        vmem((steps, width, owners * FP), BF16),
        vmem((steps, owners * FP, width), BF16),
    ]
    grads = [vmem((rows, width), BF16), vmem(g_up, BF16), vmem(g_down, BF16)]
    if direct:
        later = [(steps - 1, g[1]) + g[3:] for g in (g_up, g_down)]
        extra = [out(heads, BF16)] + [out(s, BF16) for s in later]
        extra += [out((steps,) + g_down[2:], BF16), out(g_up[2:5] + (steps * g_up[5],), BF16)]
        extra_specs = [anywhere] * 5
        scratch = grads + [vmem(s, BF16) for s in later] + scratch
        for g in (g_down, g_up):
            for _ in range(2):
                scratch += flow_scratch(owners, reps, (g[4], g[5] // 2), True)
        remotes = (steps - 1) * 2 * 15 + 4 * 11 + 2 * (steps - 1) + heads[0] * heads[1]
        scratch += [pltpu.SemaphoreType.DMA((remotes,))] * 2 + [
            pltpu.SemaphoreType.DMA((2 * owners + 2 * (steps - 1) * owners + 10 + 2 * (steps - 1) + heads[0] * heads[1],))
        ]
        params = dict(collective_id=3, has_side_effects=True)
    else:
        per_step = lambda s: pl.BlockSpec(s, lambda f: (f,) + (0,) * (len(s) - 1))
        extra = [out((rows, width), BF16)] + [out((steps,) + g[1:], BF16) for g in (g_up, g_down)]
        extra_specs = [whole((rows, width)), per_step(g_up), per_step(g_down)]
        scratch += [pltpu.SemaphoreType.DMA((2,))]
        params = {}
    return pl.pallas_call(
        partial(middle_kernel, owners, reps, direct),
        grid=(steps,),
        in_specs=[whole((rows, width))] * 3
        + [whole((width, width)), anywhere, anywhere, whole(vecs.shape), pl.BlockSpec((1, 1, owners * FP), lambda f: (f, 0, 0))],
        out_specs=[whole((rows, width)), whole((rows, width)), whole(g_mix), whole((16, width))] + extra_specs,
        out_shape=[out((rows, width), BF16), out((rows, width), F32), out(g_mix, BF16), out((16, width), F32)] + extra,
        scratch_shapes=scratch,
        compiler_params=pltpu.CompilerParams(vmem_limit_bytes=62 << 20, **params),
        cost_estimate=pl.CostEstimate(
            flops=12 * rows * width * ff + 6 * rows * width * width,
            bytes_accessed=8 * width * ff + 16 * rows * width,
            transcendentals=rows * ff,
        ),
        name="middle_block",
    )(x, mixed, d_out, w_mix, w_up, w_down, vecs, b_up)


def backward_kernel(
    owners, reps, pairs, factor, size, shapes, done,
    q_ref, k_ref, v_ref, d_heads, lse_ref, x_ref, vec_ref, gvec_ref, dmid_ref, first_t_ref, w_ref, *refs
):
    n_in = len(shapes)
    sources, refs = refs[:n_in], refs[n_in + 2 :]
    dtok_ref, vec_out, refs = refs[0], refs[1], refs[2:]
    outs, refs = refs[: n_in + 1], refs[n_in + 1 :]
    d_joined, first_t, w_pairs, df_send, df_recv, dk_sum, dv_sum, b_sum, vec_one, vec_got, vec_sum, refs = (
        refs[:11] + (refs[11:],)
    )
    flow_refs, (send, recv, kept) = refs[:-3], refs[-3:]
    step = pl.program_id(0)
    last = pl.num_programs(0) - 1
    place = z, r, c = position()
    mbs, rows, width = x_ref.shape
    half = width // 2
    lanes = 2 * size
    plan = Plan(send, recv)
    own_rows = pl.ds(pl.multiple_of(c * rows, rows), rows)

    locals_used = 0

    def local(src, dst):
        nonlocal locals_used
        locals_used += 1
        slot = kept.at[locals_used - 1]
        return lambda: pltpu.make_async_copy(src(), dst(), slot)

    up_step = shapes[1][-1] // owners
    flows, leaving, at = [], [], 0

    def add_flow(name, bits, mine, theirs, hops, places, load=None, core=None):
        final = hops[-1]
        copies = [local(partial(part, final), dst) for part, dst in places]
        leaving.extend(copies)
        flows.append(
            Flow(plan, name, place, owners, bits, mine, theirs, hops, lambda final: [f() for f in copies], load, core)
        )

    for i, shape in enumerate(shapes):
        for f in range(shape[0]):
            wide = shape[-1] // 2
            for s in range(2):
                split = len(shape) == 6
                mine, *hops = flow_refs[at : at + 5 + split]
                at += 5 + split
                theirs = hops.pop(0) if split else None
                source, out, cols = sources[i], outs[i], pl.ds(s * wide, wide)
                if i == 1:
                    places = []
                    for k in range(wide // up_step):
                        to = pl.ds(((s * wide // up_step + k) * (shape[0] + done) + done + f) * up_step, up_step)
                        places.append((
                            lambda final, k=k: final.at[:, :, :, pl.ds(k * up_step, up_step)],
                            lambda out=out, to=to: out.at[:, :, :, to],
                        ))
                else:
                    skip = done if i == 0 else 0
                    places = [(lambda final: final, lambda out=out, f=f + skip, cols=cols: out.at[f, :, :, :, cols])]
                add_flow(
                    (i, f, s), (1, 2) if s == 0 else (2, 1), mine, theirs, hops, places,
                    local(
                        lambda source=source, f=f, cols=cols, split=split: (
                            source.at[f, :, c, :, :, cols] if split else source.at[f, :, :, :, cols]
                        ),
                        lambda mine=mine: mine,
                    ),
                    (lambda source=source, f=f, cols=cols: source.at[f, :, 1 - c, :, :, cols]) if split else None,
                )
    for p in range(pairs):
        for s in range(2):
            mine, *hops = flow_refs[at : at + 5]
            at += 5
            places = []
            for side in range(2):
                for i in range(3):
                    to = pl.ds((i * 2 * pairs + side * pairs + p) * lanes, lanes)
                    places.append((
                        lambda final, side=side, i=i: final.at[side, :, :, pl.ds(i * lanes, lanes)],
                        lambda s=s, to=to: outs[-1].at[:, s, :, to],
                    ))
            add_flow((n_in, p, s), (1, 2) if s == 0 else (2, 1), mine, None, hops, places)
    groups = [flows[i : i + 2] for i in range(0, len(flows), 2)]
    products = len(groups) - pairs
    ff_steps = shapes[0][0]
    groups[: 2 * ff_steps] = [groups[k * ff_steps + f] for f in range(ff_steps) for k in range(2)]

    def advance(group, stage):
        for flow in groups[group]:
            flow.step(stage)

    for m in range(mbs):
        plan.add(("first", m), lambda m=m: df_send.at[m], lambda m=m: df_recv.at[m], {"ctx": 1 - c})
    around = [(k, side) for k in range(reps) for side in range(2) if k or side]
    for k, side in around:
        peer = {"rep": r ^ k, "ctx": 1 - c if side else c}
        plan.add(("vec", k, side), lambda: vec_sum.at[0], lambda k=k, side=side: vec_got.at[2 * k + side], peer)
    for j in range(1, owners):
        plan.add(
            ("vec", "z", j), lambda: vec_sum.at[1], lambda j=j: vec_got.at[2 * reps + j - 1], {"fsdp": lax.rem(z + j, owners)}
        )

    table = timetable(products, pairs)
    quarters = 2 * rows // QB
    tail = [entry for entry in table if entry[0] >= quarters * mbs * pairs]

    def load_first():
        return pltpu.make_async_copy(first_t_ref, first_t, kept.at[locals_used])

    def load_weight(i, p):
        return pltpu.make_async_copy(
            w_ref.at[:, pl.ds((i * pairs + p) * lanes, lanes)],
            w_pairs.at[p, :, pl.ds(i * lanes, lanes)],
            kept.at[locals_used + 1 + i * pairs + p],
        )

    @pl.when(step == 0)
    def _():
        within = [g for g in range(products) if not groups[g][0].split]
        for g in within:
            advance(g, 0)
        load_first().start()
        for i in range(3):
            for p in range(pairs):
                load_weight(i, p).start()
        greet(owners, reps, across=True)
        for g in range(products):
            if g not in within:
                advance(g, 0)
        for when, group, stage in table:
            if when < 0:
                advance(group, stage)


    def between(k, done):
        for i in range(mbs * pairs):
            some = [entry for entry in table if entry[0] == quarters * i + done]
            if some:

                @pl.when(k == i)
                def _():
                    for _, group, stage in some:
                        advance(group, stage)

    def weight_grad(p):
        grad = dot_nn(first_t[...], d_joined[p])
        piece = groups[products][0].mine.shape[2]
        grad = grad.reshape(owners, reps, 2 * piece, grad.shape[1])
        for s in range(2):
            groups[products + p][s].mine[...] = grad[:, :, s * piece : (s + 1) * piece].astype(BF16)

    for p in range(pairs):

        @pl.when(step == mbs * (p + 1))
        def _():
            if p == 0:
                load_first().wait()
            weight_grad(p)
            advance(products + p, 1)

    @pl.when(step < last)
    def _():
        p, m = lax.div(step, mbs), lax.rem(step, mbs)
        start = pl.multiple_of(m * 2 * rows, 2 * rows)
        joined = d_joined.at[p, pl.ds(start, 2 * rows)]
        attention_backward_block(
            factor, size, q_ref.at[0, 0], k_ref.at[0, 0], v_ref.at[0, 0], d_heads.at[0, 0], lse_ref.at[m, p],
            joined.at[:, pl.ds(0, lanes)], joined.at[:, pl.ds(lanes, lanes)], joined.at[:, pl.ds(2 * lanes, lanes)],
            dk_sum, dv_sum, partial(between, step),
        )
        for i, k in enumerate((0, 2)):
            part = jnp.sum(joined[:, k * lanes : (k + 1) * lanes].astype(F32), axis=0, keepdims=True)
            before = b_sum[p, i : i + 1, :]
            b_sum[p, i : i + 1, :] = part + jnp.where(m == 0, jnp.zeros_like(before), before)

    def first_part(m, at):
        total = None
        for p in range(pairs):
            term = dot_nt(d_joined[p, pl.ds(pl.multiple_of(m * 2 * rows + at, TB), TB)], w_pairs[p])
            total = term if total is None else total + term
        return total

    @pl.when(step == last)
    def _():
        for i in range(3):
            for p in range(pairs):
                load_weight(i, p).wait()
        gain = vec_ref[3:4, :]
        steps = rows // TB

        def theirs(i, _):
            m, at = lax.div(i, steps), lax.rem(i, steps) * TB
            df_send[m, pl.ds(pl.multiple_of(at, TB), TB)] = first_part(m, (1 - c) * rows + at).astype(BF16)
            return 0

        def go(until):
            while tail and tail[0][0] < until:
                _, group, stage = tail.pop(0)
                advance(group, stage)

        lax.fori_loop(0, mbs * steps, theirs, 0)
        for m in range(mbs):
            plan.start(("first", m))
        go(28)
        for m in range(mbs):
            plan.arrive(("first", m))

        def mine(i, sums):
            m, at = lax.div(i, steps), lax.rem(i, steps) * TB
            here = pl.ds(pl.multiple_of(at, TB), TB)
            total = first_part(m, c * rows + at) + df_recv[m, here].astype(F32)
            normal, inverse = norm_stats(x_ref[m, here].astype(F32))
            dtok_ref[m, here] = dmid_ref[m, here] + norm_back(total, normal, inverse, gain)
            gains = jnp.sum(total * normal, axis=0, keepdims=True)
            return (sums[0] + gains, sums[1] + jnp.sum(total, axis=0, keepdims=True))

        zero = jnp.zeros((1, width), F32)
        g_gain, g_shift = lax.fori_loop(0, mbs * steps, mine, (zero, zero))
        vec_one[...] = gvec_ref[...]
        vec_one[3:4, :] = g_gain
        vec_one[4:5, :] = g_shift
        for p in range(pairs):
            for i in range(2):
                vec_one[i : i + 1, slab(c * pairs + p, lanes)] = b_sum[p, i : i + 1, :]
        vec_sum[0] = vec_one[...]
        plan.start(*[("vec", k, side) for k, side in around])
        go(37)
        plan.arrive(*[("vec", k, side) for k, side in around])
        vec_got[0] = vec_one[...]
        cores = [vec_got[2 * k] + vec_got[2 * k + 1] for k in range(reps)]
        vec_sum[1] = (cores[0] + cores[1]) + (cores[2] + cores[3])
        plan.start(*[("vec", "z", j) for j in range(1, owners)])
        go(41)
        plan.arrive(*[("vec", "z", j) for j in range(1, owners)])
        n = 2 * reps
        vec_out[...] = (vec_sum[1] + vec_got[n]) + (vec_got[n + 1] + vec_got[n + 2])
        go(1000)
        plan.close()
        for copy in leaving:
            copy().wait()


def backward_block(
    qkv, heads, lse, x, vecs, gvec, d_middle, first_t, w_qkv, grads, finished, owners, reps, factor, size
):
    mbs, rows, width = x.shape
    lanes = 2 * size
    pairs = width // 2 // lanes
    shape = jax.ShapeDtypeStruct
    anywhere = pl.BlockSpec(memory_space=pl.ANY)
    whole = lambda s: pl.BlockSpec(s, lambda i: (0,) * len(s), pipeline_mode=pl.Buffered(1))
    final_step = mbs * pairs - 1

    def block(which):
        def index(i):
            k = jnp.minimum(i, final_step)
            return (lax.rem(k, mbs), which * pairs + lax.div(k, mbs), 0, 0)

        return pl.BlockSpec((1, 1, 2 * rows, lanes), index)

    def heads_index(i):
        k = jnp.minimum(i, final_step)
        return (lax.div(k, mbs), lax.rem(k, mbs), 0, 0)

    heads_spec = pl.BlockSpec((1, 1, 2 * rows, lanes), heads_index)
    pieces = [(len(g.shape) == 6, (g.shape[-2], g.shape[-1] // 2)) for g in grads for _ in range(2 * g.shape[0])]
    q_piece = (width // owners // reps // 2, 3 * lanes)
    down, up, mix = (g.shape for g in grads)
    finals = [f.shape for f in finished] + [mix[:1] + mix[2:], (reps, 2, q_piece[0], 3 * width)]
    scratch = [s for split, p in pieces for s in flow_scratch(owners, reps, p, split)]
    scratch += [s for _ in range(2 * pairs) for s in flow_scratch(owners, reps, q_piece, False)]
    remotes = 11 * len(pieces) + 10 * 2 * pairs + mbs * pairs + mbs + 2 * reps + owners
    vec = (16, width)
    dtok, vec_sum, *outs = pl.pallas_call(
        partial(backward_kernel, owners, reps, pairs, factor, size, [g.shape for g in grads], finished[0].shape[0] - down[0]),
        grid=(mbs * pairs + 1,),
        in_specs=[block(0), block(1), block(2), heads_spec, whole(lse.shape), whole(x.shape), whole(vec), whole(vec)]
        + [whole(x.shape)]
        + [anywhere] * (2 + len(grads) + 2),
        input_output_aliases={11 + len(grads): 2, 12 + len(grads): 3},
        out_specs=[whole(x.shape), whole(vec)] + [anywhere] * len(finals),
        out_shape=[shape(x.shape, F32), shape(vec, F32)] + [shape(f, BF16) for f in finals],
        scratch_shapes=[
            pltpu.VMEM((pairs, mbs * 2 * rows, 3 * lanes), BF16),
            pltpu.VMEM(first_t.shape, BF16),
            pltpu.VMEM((pairs, width, 3 * lanes), BF16),
            pltpu.VMEM(x.shape, BF16),
            pltpu.VMEM(x.shape, BF16),
            pltpu.VMEM((2 * rows, lanes), F32),
            pltpu.VMEM((2 * rows, lanes), F32),
            pltpu.VMEM((pairs, 8, lanes), F32),
            pltpu.VMEM(vec, F32),
            pltpu.VMEM((2 * reps + owners - 1,) + vec, F32),
            pltpu.VMEM((2,) + vec, F32),
        ]
        + scratch
        + [
            pltpu.SemaphoreType.DMA((remotes,)),
            pltpu.SemaphoreType.DMA((remotes,)),
            pltpu.SemaphoreType.DMA((len(pieces) * 3 + 12 * pairs + mbs * pairs + 1 + 3 * pairs,)),
        ],
        compiler_params=pltpu.CompilerParams(
            collective_id=2, has_side_effects=True, vmem_limit_bytes=63 << 20
        ),
        name="backward_block",
    )(qkv, qkv, qkv, heads, lse, x, vecs, gvec, d_middle, first_t, w_qkv, *grads, *finished)
    return dtok, vec_sum, outs


def local(
    inputs,
    weight_qkv,
    bias_query,
    bias_value,
    weight_mix,
    bias_mix,
    gain_attn,
    shift_attn,
    gain_mlp,
    shift_mlp,
    weight_up,
    bias_up,
    weight_down,
    bias_down,
    cotangent,
):
    width = weight_qkv.shape[1] // 3
    half = width // 2
    size = width // H
    factor = size ** (-0.5)
    rows = inputs.shape[2]
    owners = lax.axis_size("fsdp")
    reps = lax.axis_size("rep")
    ctx = lax.axis_index("ctx")
    rep = lax.axis_index("rep")
    own = weight_qkv.shape[0]
    b_up_rows = bias_up.shape[0]
    direct = own % (16 * reps) == 0 and owners == 4 and reps == 4

    def swap(x):
        return lax.ppermute(x, "ctx", [(0, 1), (1, 0)])

    def order(mine, other, axis):
        return jnp.where(
            ctx == 0,
            jnp.concatenate([mine, other], axis=axis),
            jnp.concatenate([other, mine], axis=axis),
        )

    def columns(x, axis, which):
        return lax.dynamic_slice_in_dim(x, which * half, half, axis)

    direct = own % (16 * reps) == 0 and owners == 4 and reps == 4
    vectors = [bias_query, bias_value, bias_mix, gain_attn, shift_attn, gain_mlp, shift_mlp, bias_down]
    tokens = inputs[:, 0].astype(F32)
    if direct:
        mixed, qkv, first_t, w_qkv, w_mix, w_up, w_down, vecs, b_up, lse = forward_block(
            inputs[:, 0],
            weight_qkv,
            weight_mix,
            weight_up,
            weight_down,
            vectors,
            bias_up,
            owners,
            reps,
            factor,
            size,
        )
    else:
        part = own // reps
        mine = lax.dynamic_slice_in_dim(weight_qkv, rep * part, part, 0)
        mine = jnp.concatenate([columns(mine[:, i * width : (i + 1) * width], 1, ctx) for i in range(3)], axis=1)
        w_qkv = lax.all_gather(mine, ("fsdp", "rep"), axis=0, tiled=True)

        def gather(shard):
            piece = shard.shape[0] // (2 * reps)
            mine = lax.dynamic_slice_in_dim(shard, (rep * 2 + ctx) * piece, piece, 0)
            return lax.all_gather(mine, ("fsdp", "rep", "ctx"), axis=0, tiled=True)

        w_mix = gather(weight_mix)
        w_up = gather(weight_up)
        w_down = gather(weight_down)
        vecs = lax.all_gather(jnp.stack(vectors).astype(F32), "fsdp", axis=1, tiled=True)
        b_up = lax.all_gather(bias_up.astype(F32), "fsdp", axis=0, tiled=True)
        b_up = b_up.reshape(SHARES, -1, FP).swapaxes(0, 1)
        b_up = b_up.reshape(b_up.shape[0], 1, -1)
        w_up = w_up.reshape(width, SHARES, -1, FP).transpose(2, 0, 1, 3).reshape(-1, width, SHARES * FP)
        w_down = w_down.reshape(SHARES, -1, FP, width).swapaxes(0, 1).reshape(-1, SHARES * FP, width)
    b_query, b_value, g_attn, s_attn = (vecs[i] for i in (0, 1, 3, 4))

    if not direct:
        normal_one, inverse_one = norm_stats(tokens)
        first_own = (normal_one * g_attn + s_attn).astype(BF16)
        first = order(first_own, swap(first_own), 1)
        joined = project(first, w_qkv)
        query = (joined[..., :half] + columns(b_query, 0, ctx)).astype(BF16)
        key = joined[..., half : 2 * half].astype(BF16)
        value = (joined[..., 2 * half :] + columns(b_value, 0, ctx)).astype(BF16)
        mixed_heads, lse = attention_forward(query, key, value, factor, size)

    def my_rows(x):
        return lax.dynamic_slice_in_dim(x, ctx * rows, rows, 1)

    def their_rows(x):
        return lax.dynamic_slice_in_dim(x, (1 - ctx) * rows, rows, 1)

    if not direct:
        mixed = order(my_rows(mixed_heads), swap(their_rows(mixed_heads)), 2)
    flat = (-1, width)
    d_out = cotangent.reshape(flat)
    result, d_middle, g_wmix, gvec, d_mixed, g_wup, g_wdown, *finished = middle_block(
        inputs.reshape(flat),
        mixed.reshape(flat),
        d_out,
        w_mix,
        w_up,
        w_down,
        vecs,
        b_up,
        SHARES,
        reps,
        direct,
        (half // (2 * size), inputs.shape[0], 2 * rows, 2 * size),
    )
    steps = b_up.shape[0]
    if direct:
        d_tokens, summed, outs = backward_block(
            qkv, d_mixed, lse, inputs[:, 0], vecs, gvec, d_middle.reshape(tokens.shape), first_t, w_qkv, [g_wdown, g_wup, g_wmix[None]], finished, owners, reps, factor, size,
        )
        o_wdown, o_wup, o_wmix, o_wqkv = (
            o.reshape(-1, n).astype(F32) for o, n in zip(outs, (width, SHARES * steps * FP, width, 3 * width))
        )
    else:
        d_mixed = d_mixed.reshape(tokens.shape)
        d_middle = d_middle.reshape(tokens.shape)
        d_heads = order(columns(d_mixed, 2, ctx), swap(columns(d_mixed, 2, 1 - ctx)), 1)
        d_query, d_key, d_value = attention_backward(query, key, value, d_heads, lse, factor, size)
        d_joined = jnp.concatenate([d_query, d_key, d_value], axis=-1)
        g_wqkv = outer_sum(first, d_joined)
        d_first = project_back(d_joined, w_qkv)
        d_first = my_rows(d_first) + swap(their_rows(d_first).astype(BF16)).astype(F32)
        normal_one, inverse_one = norm_stats(tokens)
        d_tokens = d_middle + norm_back(d_first, normal_one, inverse_one, g_attn)

        def reduce(grad):
            piece = lax.psum_scatter(
                grad.astype(BF16), ("fsdp", "rep", "ctx"), scatter_dimension=0, tiled=True
            )
            return lax.all_gather(piece, ("rep", "ctx"), axis=0, tiled=True).astype(F32)

        g_wdown = jnp.concatenate([g_wdown[f].reshape(SHARES, FP, width) for f in range(steps)], axis=1)
        o_wdown = reduce(g_wdown.reshape(-1, width))
        g_wup = jnp.stack([g_wup[f].reshape(width, SHARES, FP) for f in range(steps)], axis=2)
        o_wup = reduce(g_wup.reshape(width, -1))
        o_wmix = reduce(g_wmix.reshape(width, width))
        piece = lax.psum_scatter(g_wqkv.astype(BF16), ("fsdp", "rep"), scatter_dimension=0, tiled=True)
        piece = lax.all_gather(piece, "rep", axis=0, tiled=True)
        other = swap(piece)
        low, high = jnp.where(ctx == 0, piece, other), jnp.where(ctx == 0, other, piece)
        o_wqkv = jnp.concatenate(
            [t for i in range(3) for t in (low[:, i * half : (i + 1) * half], high[:, i * half : (i + 1) * half])],
            axis=1,
        ).astype(F32)

        def place(v):
            return lax.dynamic_update_slice_in_dim(jnp.zeros((width,), F32), v, ctx * half, 0)

        first_rows = (
            place(jnp.sum(d_query.astype(F32), axis=(0, 1))),
            place(jnp.sum(d_value.astype(F32), axis=(0, 1))),
            jnp.sum(d_first * normal_one, axis=(0, 1)),
            jnp.sum(d_first, axis=(0, 1)),
        )
        summed = jnp.concatenate([jnp.stack(first_rows[:2]), gvec[2:3], jnp.stack(first_rows[2:]), gvec[5:12]], axis=0)
        summed = lax.psum(summed, ("rep", "fsdp", "ctx"))
    owner = lax.axis_index("fsdp")
    o_bup = lax.dynamic_slice_in_dim(summed[8 : 8 + SHARES].reshape(-1), owner * b_up_rows, b_up_rows, 0)
    summed = lax.dynamic_slice_in_dim(summed[:8], owner * own, own, 1)
    o_bq, o_bv, o_bmix, o_ga, o_sa, o_gm, o_sm, o_bd = (summed[i] for i in range(8))
    return (
        result.reshape(inputs.shape),
        d_tokens[:, None],
        o_wqkv,
        o_bq,
        o_bv,
        o_wmix,
        o_bmix,
        o_ga,
        o_sa,
        o_gm,
        o_sm,
        o_wup,
        o_bup,
        o_wdown,
        o_bd,
    )


def solution(mesh):
    row = P(None, ("rep", "fsdp"), "ctx", None)
    mat = P("fsdp", None)
    vec = P("fsdp")
    params = (mat, vec, vec, mat, vec, vec, vec, vec, vec, mat, vec, mat, vec)
    in_specs = (row,) + params + (row,)
    out_specs = (row, row) + params
    return jax.shard_map(local, mesh=mesh, in_specs=in_specs, out_specs=out_specs, check_vma=False)
```
